32 devices in a mesh: dp: 16 (over z, x, core), tensor: 2 (over y).
Axes of the slice: x: 2, y: 2, z: 4, core: 2. Of those that a mesh axis runs over, the one named last changes fastest.
Arguments:
- pixels: bfloat16 [8192, 3328], P('dp', 'tensor'), may hold values from -6 to 6
- item_kinds: int32 [32], P('dp'), may hold values from 0 to 1
- gsd_codes: int32 [32], P('dp'), may hold values from 0 to 7
- w_spectral: bfloat16 [3328, 1024], P('tensor'), may hold values from -0.109375 to 0.109375
- w_rgb: bfloat16 [768, 1024], P('tensor'), may hold values from -0.21875 to 0.21875
- ln1_gain: float32 [1024], replicated, may hold values from 0.5 to 1.5
- ln1_bias: float32 [1024], replicated, may hold values from -1.5 to 1.5
- w_qkv: bfloat16 [1024, 3, 1024], P(None, None, 'tensor'), may hold values from -0.1875 to 0.1875
- q_bias: float32 [1024], P('tensor'), may hold values from -1.5 to 1.5
- v_bias: float32 [1024], P('tensor'), may hold values from -1.5 to 1.5
- w_out: bfloat16 [1024, 1024], P('tensor'), may hold values from -0.5 to 0.5
- out_bias: float32 [1024], replicated, may hold values from -1.5 to 1.5
- ln2_gain: float32 [1024], replicated, may hold values from 0.5 to 1.5
- ln2_bias: float32 [1024], replicated, may hold values from -1.5 to 1.5
- w_fc1: bfloat16 [1024, 4096], P(None, 'tensor'), may hold values from -0.1875 to 0.1875
- fc1_bias: float32 [4096], P('tensor'), may hold values from -1.5 to 1.5
- w_fc2: bfloat16 [4096, 1024], P('tensor'), may hold values from -0.09375 to 0.09375
- fc2_bias: float32 [1024], replicated, may hold values from -1.5 to 1.5
- cotangent: bfloat16 [8192, 1024], P('dp'), may hold values from -6 to 6
Outputs:
- block_out: bfloat16 [8192, 1024], P('dp')
- pixels_grad: bfloat16 [8192, 3328], P('dp', 'tensor')
- spectral_grad: float32 [3328, 1024], P('tensor', 'dp')
- rgb_grad: float32 [768, 1024], P('tensor', 'dp')
- ln1_gain_grad: float32 [1024], P('dp')
- ln1_bias_grad: float32 [1024], P('dp')
- qkv_grad: float32 [1024, 3, 1024], P('dp', None, 'tensor')
- q_bias_grad: float32 [1024], P(('tensor', 'dp'))
- v_bias_grad: float32 [1024], P(('tensor', 'dp'))
- out_grad: float32 [1024, 1024], P('tensor', 'dp')
- out_bias_grad: float32 [1024], P('dp')
- ln2_gain_grad: float32 [1024], P('dp')
- ln2_bias_grad: float32 [1024], P('dp')
- fc1_grad: float32 [1024, 4096], P('dp', 'tensor')
- fc1_bias_grad: float32 [4096], P(('tensor', 'dp'))
- fc2_grad: float32 [4096, 1024], P('tensor', 'dp')
- fc2_bias_grad: float32 [1024], P('dp')
The draws below stay inside these ranges and needn't reach their ends.
Inputs may be any that keep to these rules, and one draw needn't show every extreme that they name: `item_kinds`: 1 marks an item with all 13 bands, 0 an RGB item whose bands 3 and above are unused. `gsd_codes`: code c stands for a ground sample distance (c + 1) / 4 times the reference one.
All inputs are finite; a program needn't handle non-finite values.
Results may differ from the reference program's by a relative error of at most 0.015.
Values sent between devices are 32-bit elements; how exact they have to be, the bound alone decides.
No kernel may reach another device: no remote copies, remote signals or barrier semaphores. Data moves between devices by JAX's collectives and lax.ppermute only.
A program may use at most 192 MiB of HBM per device.

```python
import math
import jax
import jax.numpy as jnp
from jax import lax

D = 1024
HEADS = 16
HEAD_DIM = 64
FF = 4096
BANDS = 13
GRID = 16
HD = 1024
PIX = 256
PATCHES = 256
ITEMS = 32
TOKENS = 8192


def set_ends(entries, stream_key, smallest, high):
    place = [jax.random.randint(jax.random.fold_in(stream_key, axis), (), 0, length) for axis, length in enumerate(entries.shape)]
    widest = entries.shape.index(max(entries.shape))
    next_to = place[:widest] + [(place[widest] + 1) % entries.shape[widest]] + place[widest + 1:]
    return entries.at[tuple(place)].set(smallest).at[tuple(next_to)].set(high)


def block_scale(own_key, dims, split, smallest, high):
    level, own = 1.0, jax.random.fold_in(own_key, 6)
    for position, parts in split:
        steps = jnp.exp(jax.random.uniform(jax.random.fold_in(own, position), (parts,), jnp.float32, smallest / len(split), high / len(split)))
        level = level * jnp.repeat(steps, dims[position] // parts).reshape([-1 if axis == position else 1 for axis in range(len(dims))])
    return level


def bell_draw(stream_key, shape, scale, bound, shards=(), dtype=jnp.bfloat16):
    gain = block_scale(stream_key, shape, shards, -0.22, 0.18) if shards else 1.0
    entries = jax.random.normal(stream_key, shape, jnp.float32) * scale * gain
    return jnp.minimum(jnp.maximum(entries, -bound), bound).astype(dtype)


def setup_inputs(seed: int = 0) -> dict:
    streams_of = jax.random.split(jax.random.key(seed), 20)
    return {
        "pixels": bell_draw(streams_of[0], (TOKENS, PIX * BANDS), 1.0, 6.0, ((0, 16), (1, 2))),
        "item_kinds": set_ends(jax.random.randint(streams_of[1], (ITEMS,), 0, 2), jax.random.fold_in(streams_of[1], 1), 0, 1).astype(jnp.int32),
        "gsd_codes": set_ends(jax.random.randint(streams_of[2], (ITEMS,), 0, 8), jax.random.fold_in(streams_of[2], 1), 0, 7).astype(jnp.int32),
        "w_spectral": bell_draw(streams_of[3], (PIX * BANDS, D), (PIX * BANDS) ** -0.5, 0.109375, ((0, 2),)),
        "w_rgb": bell_draw(streams_of[4], (PIX * 3, D), (PIX * 3) ** -0.5, 0.21875, ((0, 2),)),
        "ln1_gain": jnp.clip(1.0 + 0.1 * jax.random.normal(streams_of[5], (D,), jnp.float32), 0.5, 1.5),
        "ln1_bias": bell_draw(streams_of[6], (D,), 0.3, 1.5, (), jnp.float32),
        "w_qkv": bell_draw(streams_of[7], (D, 3, HD), D ** -0.5, 0.1875, ((2, 2),)),
        "q_bias": bell_draw(streams_of[8], (HD,), 0.3, 1.5, ((0, 2),), jnp.float32),
        "v_bias": bell_draw(streams_of[9], (HD,), 0.3, 1.5, ((0, 2),), jnp.float32),
        "w_out": bell_draw(streams_of[10], (HD, D), (HD // 8) ** -0.5, 0.5, ((0, 2),)),
        "out_bias": bell_draw(streams_of[11], (D,), 0.3, 1.5, (), jnp.float32),
        "ln2_gain": jnp.clip(1.0 + 0.1 * jax.random.normal(streams_of[12], (D,), jnp.float32), 0.5, 1.5),
        "ln2_bias": bell_draw(streams_of[13], (D,), 0.3, 1.5, (), jnp.float32),
        "w_fc1": bell_draw(streams_of[14], (D, FF), D ** -0.5, 0.1875, ((1, 2),)),
        "fc1_bias": bell_draw(streams_of[15], (FF,), 0.3, 1.5, ((0, 2),), jnp.float32),
        "w_fc2": bell_draw(streams_of[16], (FF, D), FF ** -0.5, 0.09375, ((0, 2),)),
        "fc2_bias": bell_draw(streams_of[17], (D,), 0.3, 1.5, (), jnp.float32),
        "cotangent": bell_draw(streams_of[18], (TOKENS, D), 1.0, 6.0, ((0, 16),)),
    }


EPS = 1e-06
HIGH = lax.Precision.HIGHEST

@jax.custom_vjp
def low(v):
    return lax.optimization_barrier(v.astype(jnp.bfloat16)).astype(jnp.float32)

@jax.custom_vjp
def low_back(v):
    return v

def low_keep(v):
    return (low(v), None)

def low_pass(kept, grad):
    return (grad,)

def back_keep(v):
    return (v, None)

def back_low(kept, grad):
    return (low(grad),)
low.defvjp(low_keep, low_pass)
low_back.defvjp(back_keep, back_low)

def layer_norm(values, gain_vec, shift_vec):
    center = values - lax.optimization_barrier(jnp.mean(values, -1, keepdims=True))
    spread = lax.optimization_barrier(jnp.mean(center * center, -1, keepdims=True))
    return center * lax.rsqrt(spread + EPS) * gain_vec + shift_vec

def gsd_positions(codes, grid_side, width):
    gsd_ratio = (codes.astype(jnp.float32) + 1.0) / 4.0
    grid_cells = jnp.arange(grid_side * grid_side)
    row_place = (grid_cells // grid_side).astype(jnp.float32)
    col_place = (grid_cells % grid_side).astype(jnp.float32)
    quarter = width // 4
    frequency = 1.0 / 10000.0 ** (jnp.arange(quarter).astype(jnp.float32) / quarter)
    row_angle = gsd_ratio[:, None, None] * row_place[None, :, None] * frequency[None, None, :]
    col_angle = gsd_ratio[:, None, None] * col_place[None, :, None] * frequency[None, None, :]
    return jnp.concatenate([jnp.sin(row_angle), jnp.cos(row_angle), jnp.sin(col_angle), jnp.cos(col_angle)], -1)

def matmul(left, right):
    return jnp.dot(left, right, precision=HIGH)

def forward(pix_rows, kinds_part, codes_part, params):
    w_spectral, w_rgb, ln1_gain, ln1_bias, w_qkv, q_bias, v_bias, w_out, out_bias, ln2_gain, ln2_bias, w_fc1, fc1_bias, w_fc2, fc2_bias = params
    row_count = pix_rows.shape[0]
    item_count = kinds_part.shape[0]
    spec_embed = matmul(pix_rows, w_spectral)
    narrow = pix_rows.reshape(row_count, PIX, BANDS)[:, :, :3].reshape(row_count, PIX * 3)
    rgb_embed = matmul(narrow, w_rgb)
    choose = jnp.repeat(kinds_part == 1, PATCHES)[:, None]
    placed = gsd_positions(codes_part, GRID, D).reshape(row_count, D)
    resid0 = low_back(jnp.where(choose, spec_embed, rgb_embed) + placed)
    attn_in = low(layer_norm(resid0, ln1_gain, ln1_bias))
    qkv_bias = jnp.stack([q_bias, jnp.zeros_like(q_bias), v_bias])
    qkv_val = low(low_back(jnp.einsum('td,dch->tch', attn_in, w_qkv, precision=HIGH) + qkv_bias))
    shaped = qkv_val.reshape(item_count, PATCHES, 3, HEADS, HEAD_DIM)
    query_rows = shaped[:, :, 0]
    key_rows = shaped[:, :, 1]
    value_rows = shaped[:, :, 2]
    scores = low_back(jnp.einsum('iqhe,ikhe->ihqk', query_rows, key_rows, precision=HIGH) * HEAD_DIM ** (-0.5))
    top_score = lax.optimization_barrier(jnp.max(scores, -1, keepdims=True))
    expo = jnp.exp(scores - top_score)
    probs = low(expo / lax.optimization_barrier(jnp.sum(expo, -1, keepdims=True)))
    mixed = jnp.einsum('ihqk,ikhe->iqhe', probs, value_rows, precision=HIGH).reshape(row_count, HD)
    attn_val = low(low_back(mixed))
    resid1 = resid0 + low_back(matmul(attn_val, w_out) + out_bias)
    norm2_val = low(layer_norm(resid1, ln2_gain, ln2_bias))
    hidden_pre = low_back(matmul(norm2_val, w_fc1) + fc1_bias)
    hidden_act = low(jax.nn.gelu(hidden_pre, approximate=False))
    return resid1 + low_back(matmul(hidden_act, w_fc2) + fc2_bias)

def reference(pixels, item_kinds, gsd_codes, w_spectral, w_rgb, ln1_gain, ln1_bias, w_qkv, q_bias, v_bias, w_out, out_bias, ln2_gain, ln2_bias, w_fc1, fc1_bias, w_fc2, fc2_bias, cotangent):
    params = tuple((array.astype(jnp.float32) for array in (w_spectral, w_rgb, ln1_gain, ln1_bias, w_qkv, q_bias, v_bias, w_out, out_bias, ln2_gain, ln2_bias, w_fc1, fc1_bias, w_fc2, fc2_bias)))
    per_group = math.gcd(ITEMS, max(1, 4096 // PATCHES))
    group_count = ITEMS // per_group
    pix_groups = pixels.astype(jnp.float32).reshape(group_count, per_group * PATCHES, PIX * BANDS)
    cot_groups = cotangent.astype(jnp.float32).reshape(group_count, per_group * PATCHES, D)
    kind_groups = item_kinds.reshape(group_count, per_group)
    code_groups = gsd_codes.reshape(group_count, per_group)

    def one_group(totals, group):
        pix_rows, kinds_part, codes_part, cot_rows = group

        def run_group(pix_in, weights):
            return forward(pix_in, kinds_part, codes_part, weights)
        out_val, pullback = jax.vjp(run_group, pix_rows, params)
        pix_grad, weight_grads = pullback(cot_rows)
        totals = jax.tree.map(jnp.add, totals, weight_grads)
        return (totals, (out_val.astype(jnp.bfloat16), pix_grad.astype(jnp.bfloat16)))
    starts = jax.tree.map(jnp.zeros_like, params)
    grads, (outputs, pix_grads) = lax.scan(one_group, starts, (pix_groups, kind_groups, code_groups, cot_groups))
    return (outputs.reshape(TOKENS, D), pix_grads.reshape(TOKENS, PIX * BANDS), grads[0], grads[1], grads[2], grads[3], grads[4], grads[5], grads[6], grads[7], grads[8], grads[9], grads[10], grads[11], grads[12], grads[13], grads[14])
```

```python
import functools

import jax
import jax.numpy as jnp
from jax import lax
from jax.experimental import pallas as pl
from jax.experimental.pallas import tpu as pltpu
from jax.sharding import PartitionSpec as P

HEAD_DIM = 64
GRID = 16
EPS = 1e-06
F32 = jnp.float32
BF16 = jnp.bfloat16
LANES = 128
VMEM_LIMIT = 56 * 1024 * 1024
QUAD = 256


def nn(left, right):
    return lax.dot_general(left, right, (((1,), (0,)), ((), ())), preferred_element_type=F32)


def nt(left, right):
    return lax.dot_general(left, right, (((1,), (1,)), ((), ())), preferred_element_type=F32)


def tn(left, right):
    return lax.dot_general(left, right, (((0,), (0,)), ((), ())), preferred_element_type=F32)


def params(**extra):
    return pltpu.CompilerParams(vmem_limit_bytes=VMEM_LIMIT, **extra)


def cost(flops, nbytes, trans=0):
    return pl.CostEstimate(flops=int(flops), bytes_accessed=int(nbytes), transcendentals=int(trans))


def whole(shape):
    return pl.BlockSpec(shape, lambda *_: (0,) * len(shape))


def norm_parts(values):
    center = values - jnp.mean(values, -1, keepdims=True)
    spread = jnp.mean(center * center, -1, keepdims=True)
    inverse = lax.rsqrt(spread + EPS)
    return center * inverse, inverse


def norm_back(normed, inverse, grad, gain):
    scaled = grad * gain
    mean_scaled = jnp.mean(scaled, -1, keepdims=True)
    mean_cross = jnp.mean(scaled * normed, -1, keepdims=True)
    return inverse * (scaled - mean_scaled - normed * mean_cross)


def column_sum(values):
    return jnp.sum(values, 0, keepdims=True)


def embed_kernel(kinds, pix_ref, wspec_ref, wrgb_ref, pick_ref, part_ref, mixed_ref, *, item):
    step = pl.program_id(0)
    wide = pix_ref.shape[1]
    spectral = kinds[item] == 1

    @pl.when(spectral)
    def _():
        @pl.when(step == 0)
        def _():
            mixed_ref[:, :wide] = pix_ref[...]
            mixed_ref[:, wide:] = jnp.zeros((pix_ref.shape[0], wrgb_ref.shape[0]), BF16)

        part_ref[...] = nn(pix_ref[...], wspec_ref[...])

    @pl.when(jnp.logical_not(spectral))
    def _():
        @pl.when(step == 0)
        def _():
            mixed_ref[:, :wide] = jnp.zeros(pix_ref.shape, BF16)
            mixed_ref[:, wide:] = nn(pix_ref[...], pick_ref[...]).astype(BF16)

        part_ref[...] = nn(mixed_ref[:, wide:], wrgb_ref[...])


def embed(kinds, pixels, w_spectral, w_rgb, pick, item, rows):
    wide, width = w_spectral.shape
    narrow = w_rgb.shape[0]
    tile = 256
    return pl.pallas_call(
        functools.partial(embed_kernel, item=item),
        grid_spec=pltpu.PrefetchScalarGridSpec(
            num_scalar_prefetch=1,
            grid=(width // tile,),
            in_specs=[
                pl.BlockSpec((rows, wide), lambda n, *_: (item, 0)),
                pl.BlockSpec((wide, tile), lambda n, *_: (0, n)),
                pl.BlockSpec((narrow, tile), lambda n, *_: (0, n)),
                whole((wide, narrow)),
            ],
            out_specs=[
                pl.BlockSpec((rows, tile), lambda n, *_: (0, n)),
                whole((rows, wide + narrow)),
            ],
        ),
        out_shape=[
            jax.ShapeDtypeStruct((rows, width), F32),
            jax.ShapeDtypeStruct((rows, wide + narrow), BF16),
        ],
        compiler_params=params(),
        cost_estimate=cost(2 * rows * wide * width, 2 * wide * width + 4 * rows * width),
        name="embed",
    )(kinds, pixels, w_spectral, w_rgb, pick)


def pair_masks(rows):
    lane = lax.broadcasted_iota(jnp.int32, (rows, LANES), 1)
    return lane < HEAD_DIM, lane >= HEAD_DIM


def only(mask, values):
    return jnp.where(mask, values, jnp.zeros_like(values))


def softmax_rows(query, key):
    scores = nt(query, key) * (HEAD_DIM**-0.5)
    expo = jnp.exp(scores - jnp.max(scores, -1, keepdims=True))
    return expo / jnp.sum(expo, -1, keepdims=True)


def attn_forward_kernel(
    part_ref, recv_ref, table_ref, gain_ref, bias_ref, wqkv_ref, qb_ref, vb_ref, wout_ref,
    x0_ref, a1_ref, qkv_ref, o_ref, opart_ref,
):
    quad = pl.program_id(0)
    rows, width = part_ref.shape

    @pl.when(quad == 0)
    def _():
        side = table_ref.shape[0]
        half = table_ref.shape[1]
        table = table_ref[...]
        by_row = jnp.broadcast_to(table[:, None, :], (side, side, half)).reshape(rows, half)
        by_col = jnp.broadcast_to(table[None, :, :], (side, side, half)).reshape(rows, half)
        left = part_ref[:, :half] + recv_ref[:, :half] + by_row
        right = part_ref[:, half:] + recv_ref[:, half:] + by_col
        x0_ref[:, :half] = left
        x0_ref[:, half:] = right
        normed, _inv = norm_parts(x0_ref[...])
        a1_ref[...] = (normed * gain_ref[...] + bias_ref[...]).astype(BF16)
        opart_ref[...] = jnp.zeros_like(opart_ref)

    a1 = a1_ref[...]
    query = (nn(a1, wqkv_ref[0]) + qb_ref[...]).astype(BF16)
    key = nn(a1, wqkv_ref[1]).astype(BF16)
    value = (nn(a1, wqkv_ref[2]) + vb_ref[...]).astype(BF16)
    qkv_ref[0] = query
    qkv_ref[1] = key
    qkv_ref[2] = value
    masks = pair_masks(rows)
    for pair in range(query.shape[1] // LANES):
        span = slice(pair * LANES, (pair + 1) * LANES)
        q2, k2, v2 = query[:, span], key[:, span], value[:, span]
        mixed = None
        for mask in masks:
            probs = softmax_rows(only(mask, q2), k2).astype(BF16)
            term = nn(probs, only(mask, v2))
            mixed = term if mixed is None else mixed + term
        o_ref[:, span] = mixed.astype(BF16)
    opart_ref[...] += nn(o_ref[...], wout_ref[...])


def attn_forward(part, recv, table, gain, bias, w_qkv, q_bias, v_bias, w_out):
    rows, width = part.shape
    heads_wide = w_out.shape[0]
    steps = heads_wide // QUAD
    return pl.pallas_call(
        attn_forward_kernel,
        grid=(steps,),
        in_specs=[
            whole(part.shape),
            whole(recv.shape),
            whole(table.shape),
            whole(gain.shape),
            whole(bias.shape),
            pl.BlockSpec((3, width, QUAD), lambda n: (0, 0, n)),
            pl.BlockSpec((1, QUAD), lambda n: (0, n)),
            pl.BlockSpec((1, QUAD), lambda n: (0, n)),
            pl.BlockSpec((QUAD, width), lambda n: (n, 0)),
        ],
        out_specs=[
            whole((rows, width)),
            whole((rows, width)),
            pl.BlockSpec((3, rows, QUAD), lambda n: (0, 0, n)),
            pl.BlockSpec((rows, QUAD), lambda n: (0, n)),
            whole((rows, width)),
        ],
        out_shape=[
            jax.ShapeDtypeStruct((rows, width), F32),
            jax.ShapeDtypeStruct((rows, width), BF16),
            jax.ShapeDtypeStruct((3, rows, heads_wide), BF16),
            jax.ShapeDtypeStruct((rows, heads_wide), BF16),
            jax.ShapeDtypeStruct((rows, width), F32),
        ],
        compiler_params=params(),
        cost_estimate=cost(8 * rows * width * heads_wide * 2, 12 * rows * width * 2, rows * rows * 8),
        name="attn_forward",
    )(part, recv, table, gain, bias, w_qkv, q_bias, v_bias, w_out)


def attn_backward_kernel(
    gpart_ref, grecv_ref, x1_ref, cot_ref, gain_ref, wout_ref, qkv_ref, wqkv_ref,
    dx1_ref, dya_ref, dqkv_ref, da1_ref, sums_ref, qvsum_ref,
):
    quad = pl.program_id(0)
    rows = x1_ref.shape[0]

    @pl.when(quad == 0)
    def _():
        normed, inverse = norm_parts(x1_ref[...])
        grad = gpart_ref[...] + grecv_ref[...]
        cot = cot_ref[...].astype(F32)
        dx1 = cot + norm_back(normed, inverse, grad, gain_ref[...])
        dx1_ref[...] = dx1
        dya = dx1.astype(BF16)
        dya_ref[...] = dya
        da1_ref[...] = jnp.zeros_like(da1_ref)
        sums_ref[0:1, :] = column_sum(grad * normed)
        sums_ref[1:2, :] = column_sum(grad)
        sums_ref[2:3, :] = column_sum(dya.astype(F32))
        sums_ref[3:4, :] = column_sum(cot)
        sums_ref[4:8, :] = jnp.zeros((4, sums_ref.shape[1]), F32)

    dmix = nt(dya_ref[...], wout_ref[...]).astype(BF16)
    scale = HEAD_DIM**-0.5
    masks = pair_masks(rows)
    for pair in range(dmix.shape[1] // LANES):
        span = slice(pair * LANES, (pair + 1) * LANES)
        q2, k2, v2, d2 = qkv_ref[0, :, span], qkv_ref[1, :, span], qkv_ref[2, :, span], dmix[:, span]
        totals = [None, None, None]
        for mask in masks:
            qm, km, dm = only(mask, q2), only(mask, k2), only(mask, d2)
            probs = softmax_rows(qm, k2)
            dprobs = nt(dm, v2)
            dot_row = jnp.sum(probs * dprobs, -1, keepdims=True)
            dscores = (probs * (dprobs - dot_row)).astype(BF16)
            terms = [nn(dscores, km), tn(dscores, qm), tn(probs.astype(BF16), dm)]
            totals = [t if o is None else o + t for o, t in zip(totals, terms)]
        dqkv_ref[0, :, span] = (totals[0] * scale).astype(BF16)
        dqkv_ref[1, :, span] = (totals[1] * scale).astype(BF16)
        dqkv_ref[2, :, span] = totals[2].astype(BF16)
    da1_ref[...] += (
        nt(dqkv_ref[0], wqkv_ref[0]) + nt(dqkv_ref[1], wqkv_ref[1]) + nt(dqkv_ref[2], wqkv_ref[2])
    )
    qvsum_ref[0:1, :] = column_sum(dqkv_ref[0].astype(F32))
    qvsum_ref[1:2, :] = column_sum(dqkv_ref[2].astype(F32))
    qvsum_ref[2:8, :] = jnp.zeros((6, qvsum_ref.shape[1]), F32)


def attn_backward(gpart, grecv, x1, cotangent, gain, w_out, qkv, w_qkv, item):
    rows, width = x1.shape
    heads_wide = w_out.shape[0]
    steps = heads_wide // QUAD
    return pl.pallas_call(
        attn_backward_kernel,
        grid=(steps,),
        in_specs=[
            whole(gpart.shape),
            whole(grecv.shape),
            whole(x1.shape),
            pl.BlockSpec((rows, width), lambda n: (item, 0)),
            whole(gain.shape),
            pl.BlockSpec((QUAD, width), lambda n: (n, 0)),
            pl.BlockSpec((3, rows, QUAD), lambda n: (0, 0, n)),
            pl.BlockSpec((3, width, QUAD), lambda n: (0, 0, n)),
        ],
        out_specs=[
            whole((rows, width)),
            whole((rows, width)),
            pl.BlockSpec((3, rows, QUAD), lambda n: (0, 0, n)),
            whole((rows, width)),
            whole((8, width)),
            pl.BlockSpec((8, QUAD), lambda n: (0, n)),
        ],
        out_shape=[
            jax.ShapeDtypeStruct((rows, width), F32),
            jax.ShapeDtypeStruct((rows, width), BF16),
            jax.ShapeDtypeStruct((3, rows, heads_wide), BF16),
            jax.ShapeDtypeStruct((rows, width), F32),
            jax.ShapeDtypeStruct((8, width), F32),
            jax.ShapeDtypeStruct((8, heads_wide), F32),
        ],
        compiler_params=params(),
        cost_estimate=cost(8 * rows * width * heads_wide * 3, 20 * rows * width * 2, rows * rows * 8),
        name="attn_backward",
    )(gpart, grecv, x1, cotangent, gain, w_out, qkv, w_qkv)


def mlp_kernel(
    x0_ref, opart_ref, orecv_ref, obias_ref, gain_ref, bias_ref, wfc1_ref, b1_ref, wfc2_ref, cot_ref,
    x1_ref, a2_ref, act_ref, dpre_ref, da2_ref, b1sum_ref,
):
    step = pl.program_id(0)

    @pl.when(step == 0)
    def _():
        x1_ref[...] = x0_ref[...] + (opart_ref[...] + orecv_ref[...] + obias_ref[...])
        normed, _inv = norm_parts(x1_ref[...])
        a2_ref[...] = (normed * gain_ref[...] + bias_ref[...]).astype(BF16)
        da2_ref[...] = jnp.zeros_like(da2_ref)

    pre = nn(a2_ref[...], wfc1_ref[...]) + b1_ref[...]
    dact = nt(cot_ref[...], wfc2_ref[...])
    cdf = 0.5 * (1.0 + lax.erf(pre * (2.0**-0.5)))
    act_ref[...] = (pre * cdf).astype(BF16)
    density = jnp.exp(-0.5 * pre * pre) * 0.3989422804014327
    dpre = (dact * (cdf + pre * density)).astype(BF16)
    dpre_ref[...] = dpre
    b1sum_ref[...] = column_sum(dpre.astype(F32))
    da2_ref[...] += nt(dpre, wfc1_ref[...])


def mlp(x0, opart, orecv, out_bias, gain, bias, w_fc1, fc1_bias, w_fc2, cotangent, item):
    rows, width = x0.shape
    hidden = w_fc1.shape[1]
    tile = 512
    return pl.pallas_call(
        mlp_kernel,
        grid=(hidden // tile,),
        in_specs=[
            whole(x0.shape),
            whole(opart.shape),
            whole(orecv.shape),
            whole(out_bias.shape),
            whole(gain.shape),
            whole(bias.shape),
            pl.BlockSpec((width, tile), lambda n: (0, n)),
            pl.BlockSpec((1, tile), lambda n: (0, n)),
            pl.BlockSpec((tile, width), lambda n: (n, 0)),
            pl.BlockSpec((rows, width), lambda n: (item, 0)),
        ],
        out_specs=[
            whole((rows, width)),
            whole((rows, width)),
            pl.BlockSpec((rows, tile), lambda n: (0, n)),
            pl.BlockSpec((rows, tile), lambda n: (0, n)),
            whole((rows, width)),
            pl.BlockSpec((1, tile), lambda n: (0, n)),
        ],
        out_shape=[
            jax.ShapeDtypeStruct((rows, width), F32),
            jax.ShapeDtypeStruct((rows, width), BF16),
            jax.ShapeDtypeStruct((rows, hidden), BF16),
            jax.ShapeDtypeStruct((rows, hidden), BF16),
            jax.ShapeDtypeStruct((rows, width), F32),
            jax.ShapeDtypeStruct((1, hidden), F32),
        ],
        compiler_params=params(),
        cost_estimate=cost(6 * rows * width * hidden, 8 * width * hidden, 2 * rows * hidden),
        name="mlp",
    )(x0, opart, orecv, out_bias, gain, bias, w_fc1, fc1_bias, w_fc2, cotangent)


def first_norm_back_kernel(gpart_ref, grecv_ref, x0_ref, dx1_ref, gain_ref, dx0_ref, sums_ref):
    @pl.when(pl.program_id(0) == 0)
    def _():
        sums_ref[...] = jnp.zeros_like(sums_ref)

    normed, inverse = norm_parts(x0_ref[...])
    grad = gpart_ref[...] + grecv_ref[...]
    dx0_ref[...] = (dx1_ref[...] + norm_back(normed, inverse, grad, gain_ref[...])).astype(BF16)
    sums_ref[0:1, :] += column_sum(grad * normed)
    sums_ref[1:2, :] += column_sum(grad)


def first_norm_back(gpart, grecv, x0, dx1, gain):
    rows, width = x0.shape
    tile = 64
    block = pl.BlockSpec((tile, width), lambda n: (n, 0))
    return pl.pallas_call(
        first_norm_back_kernel,
        grid=(rows // tile,),
        in_specs=[block, block, block, block, whole(gain.shape)],
        out_specs=[block, whole((8, width))],
        out_shape=[
            jax.ShapeDtypeStruct((rows, width), BF16),
            jax.ShapeDtypeStruct((8, width), F32),
        ],
        compiler_params=params(),
        cost_estimate=cost(20 * rows * width, 18 * rows * width),
        name="first_norm_back",
    )(gpart, grecv, x0, dx1, gain)


def pixel_grad_kernel(kinds, da_ref, db_ref, wspec_ref, wrgb_ref, pick_ref, out_ref):
    item = pl.program_id(0)
    spectral = kinds[item] == 1
    grad = jnp.where(item == 0, da_ref[...], db_ref[...])
    wide = wspec_ref.shape[0]
    cut = (wide // 2 + LANES - 1) // LANES * LANES

    @pl.when(spectral)
    def _():
        out_ref[:, :cut] = nt(grad, wspec_ref[:cut, :]).astype(BF16)
        out_ref[:, cut:] = nt(grad, wspec_ref[cut:, :]).astype(BF16)

    @pl.when(jnp.logical_not(spectral))
    def _():
        small = nt(grad, wrgb_ref[...]).astype(BF16)
        out_ref[...] = nt(small, pick_ref[...]).astype(BF16)


def pixel_grad(kinds, grad_a, grad_b, w_spectral, w_rgb, pick):
    rows = grad_a.shape[0]
    wide, width = w_spectral.shape
    return pl.pallas_call(
        pixel_grad_kernel,
        grid_spec=pltpu.PrefetchScalarGridSpec(
            num_scalar_prefetch=1,
            grid=(2,),
            in_specs=[
                whole(grad_a.shape),
                whole(grad_b.shape),
                whole(w_spectral.shape),
                whole(w_rgb.shape),
                whole(pick.shape),
            ],
            out_specs=pl.BlockSpec((rows, wide), lambda i, *_: (i, 0)),
        ),
        out_shape=jax.ShapeDtypeStruct((2 * rows, wide), BF16),
        compiler_params=params(),
        cost_estimate=cost(4 * rows * wide * width, 4 * wide * width + 4 * rows * wide),
        name="pixel_grad",
    )(kinds, grad_a, grad_b, w_spectral, w_rgb, pick)


def weight_grad_kernel(place, *refs, groups):
    count = sum(2 + 2 * g for g in groups)
    send_ref, keep_ref = refs[count:]
    half = send_ref.shape[1] // sum(groups)
    core = place[8]
    base = 0
    cursor = 0
    for planes in groups:
        left_a, left_b = refs[cursor], refs[cursor + 1]
        for plane in range(planes):
            right_a = refs[cursor + 2 + 2 * plane]
            right_b = refs[cursor + 3 + 2 * plane]
            total = tn(left_a[...], right_a[...]) + tn(left_b[...], right_b[...])
            low, high = total[:half], total[half:]
            spot = slice(base, base + half)

            @pl.when(core == 0)
            def _(low=low, high=high, spot=spot):
                keep_ref[0, spot, :] = low
                send_ref[0, spot, :] = high

            @pl.when(core != 0)
            def _(low=low, high=high, spot=spot):
                send_ref[0, spot, :] = low
                keep_ref[0, spot, :] = high

            base += half
        cursor += 2 + 2 * planes


def weight_grad(place, sides, name):
    operands, specs, groups = [], [], []
    flops = 0
    for left_a, left_b, rights in sides:
        rows, width = left_a.shape
        groups.append(len(rights))
        for left in (left_a, left_b):
            operands.append(left)
            specs.append(pl.BlockSpec((rows, LANES), lambda n, pr: (0, pr[n])))
        for right_a, right_b, plane in rights:
            for right in (right_a, right_b):
                operands.append(right)
                if plane is None:
                    specs.append(pl.BlockSpec(right.shape, lambda n, pr: (0, 0)))
                else:
                    specs.append(
                        pl.BlockSpec((None,) + right.shape[1:], lambda n, pr, q=plane: (q, 0, 0))
                    )
            columns = right_a.shape[-1]
            flops += 4 * rows * width * columns
    chips = width // LANES
    half = LANES // 2
    block = (1, half * sum(groups), columns)
    shape = jax.ShapeDtypeStruct((chips,) + block[1:], F32)
    return pl.pallas_call(
        functools.partial(weight_grad_kernel, groups=tuple(groups)),
        grid_spec=pltpu.PrefetchScalarGridSpec(
            num_scalar_prefetch=1,
            grid=(chips,),
            in_specs=specs,
            out_specs=[pl.BlockSpec(block, lambda n, pr: (n, 0, 0))] * 2,
        ),
        out_shape=[shape, shape],
        compiler_params=params(),
        cost_estimate=cost(flops, 8 * chips * block[1] * columns),
        name=name,
    )(place, *operands)


def exchange(values, axis, bit, size):
    return lax.ppermute(values, axis, [(i, i ^ bit) for i in range(size)])


def swap(values):
    return exchange(values, "tensor", 1, 2)


def after(first, values):
    return lax.optimization_barrier((first, values))[1]


def halve(send, keep, size):
    recv = exchange(send, "dp", 1, size)
    block = keep.shape[0]
    bit = 2
    while block > 1:
        block //= 2
        out = keep[:block] + recv[:block]
        kept = keep[block:] + recv[block:]
        recv = exchange(out, "dp", bit, size)
        keep = kept
        bit *= 2
    return (keep + recv)[0]


def places(size):
    me = lax.axis_index("dp")
    chip = me // 2
    core = me % 2
    order = []
    for p in range(8):
        b2, b1, b0 = (p >> 2) & 1, (p >> 1) & 1, p & 1
        order.append((1 - b2) + 2 * (1 - b1) + 4 * (1 - b0))
    flips = jnp.array(order, jnp.int32)
    return jnp.concatenate([chip ^ flips, core[None]]).astype(jnp.int32)


def local(
    pixels, item_kinds, gsd_codes, w_spectral, w_rgb, ln1_gain, ln1_bias, w_qkv, q_bias, v_bias,
    w_out, out_bias, ln2_gain, ln2_bias, w_fc1, fc1_bias, w_fc2, fc2_bias, cotangent, *, size,
):
    items = item_kinds.shape[0]
    rows = pixels.shape[0] // items
    width = w_out.shape[1]
    wide = pixels.shape[1]
    narrow = w_rgb.shape[0]
    bands = wide // (narrow // 3)
    custom = size == 16

    def row(vector):
        return vector.reshape(1, -1)

    g1, c1, g2, c2 = row(ln1_gain), row(ln1_bias), row(ln2_gain), row(ln2_bias)
    qb, vb, ob, b1 = row(q_bias), row(v_bias), row(out_bias), row(fc1_bias)
    wqkv = jnp.transpose(w_qkv, (1, 0, 2))

    source = lax.broadcasted_iota(jnp.int32, (wide, narrow), 0)
    target = lax.broadcasted_iota(jnp.int32, (wide, narrow), 1)
    pick = (source == (target // 3) * bands + target % 3).astype(BF16)

    ratio = (gsd_codes.astype(F32) + 1.0) / 4.0
    quarter = width // 4
    frequency = 1.0 / 10000.0 ** (jnp.arange(quarter).astype(F32) / quarter)
    spot = jnp.arange(GRID).astype(F32)
    angle = ratio[:, None, None] * spot[None, :, None] * frequency[None, None, :]
    tables = jnp.concatenate([jnp.sin(angle), jnp.cos(angle)], -1)

    part, mixed = [None] * items, [None] * items
    for i in range(items):
        part[i], mixed[i] = embed(item_kinds, pixels, w_spectral, w_rgb, pick, i, rows)

    gate = None

    def send(values):
        nonlocal gate
        if gate is not None:
            values = after(gate, values)
        gate = swap(values)
        return gate

    erecv = [send(part[i]) for i in range(items)]
    fwd = []
    orecv = []
    for i in range(items):
        fwd.append(attn_forward(part[i], erecv[i], tables[i], g1, c1, wqkv, qb, vb, w_out))
        orecv.append(send(fwd[i][4]))
    ffn = []
    grecv = []
    for i in range(items):
        ffn.append(
            mlp(fwd[i][0], fwd[i][4], orecv[i], ob, g2, c2, w_fc1, b1, w_fc2, cotangent, i)
        )
        grecv.append(send(ffn[i][4]))
    bwd = []
    arecv = []
    for i in range(items):
        bwd.append(
            attn_backward(ffn[i][4], grecv[i], ffn[i][0], cotangent, g2, w_out, fwd[i][2], wqkv, i)
        )
        arecv.append(send(bwd[i][3]))
    last = []
    for i in range(items):
        last.append(first_norm_back(bwd[i][3], arecv[i], fwd[i][0], bwd[i][0], g1))

    x0, a1, qkv, mix, _ = zip(*fwd)
    x1, a2, act, dpre, _, b1sum = zip(*ffn)
    dx1, dya, dqkv, _, sums2, qvsum = zip(*bwd)
    dx0, sums1 = zip(*last)

    cot = [cotangent[i * rows : (i + 1) * rows] for i in range(items)]
    out_terms = [nn(act[i], w_fc2) for i in range(items)]
    block_rows = []
    for i in range(items):
        got = send(out_terms[i])
        block_rows.append((x1[i] + (out_terms[i] + got + fc2_bias)).astype(BF16))
    block_out = jnp.concatenate(block_rows, 0)

    pixels_grad = pixel_grad(item_kinds, dx0[0], dx0[1], w_spectral, w_rgb, pick)

    vec2 = sums2[0] + sums2[1]
    vec1 = sums1[0] + sums1[1]
    qv = qvsum[0] + qvsum[1]
    b1s = b1sum[0] + b1sum[1]

    if custom:
        place = places(size)
        fc2_s = weight_grad(place, [(cot[0], cot[1], [(act[0], act[1], None)])], "fc2_grad")
        fc1_s = weight_grad(place, [(a2[0], a2[1], [(dpre[0], dpre[1], None)])], "fc1_grad")
        att_s = weight_grad(
            place,
            [
                (a1[0], a1[1], [(dqkv[0], dqkv[1], p) for p in range(3)]),
                (dya[0], dya[1], [(mix[0], mix[1], None)]),
            ],
            "attn_grad",
        )
        emb_s = weight_grad(place, [(dx0[0], dx0[1], [(mixed[0], mixed[1], None)])], "embed_grad")
        fc2_g = halve(*fc2_s, size)
        fc1_g = halve(*fc1_s, size)
        att_g = halve(*att_s, size)
        emb_g = halve(*emb_s, size)
        shard = width // size
        att_g = att_g.reshape(4, shard, -1)
        qkv_grad = jnp.transpose(att_g[:3], (1, 0, 2))
        out_grad = att_g[3].T
    else:

        def scatter(values):
            return lax.psum_scatter(values, "dp", scatter_dimension=0, tiled=True)

        def both(left, right):
            return sum(tn(left[i], right[i]) for i in range(items))

        fc2_g = scatter(both(cot, act))
        fc1_g = scatter(both(a2, dpre))
        emb_g = scatter(both(dx0, mixed))
        qkv_grad = scatter(
            sum(
                lax.dot_general(
                    a1[i], dqkv[i], (((0,), (1,)), ((), ())), preferred_element_type=F32
                )
                for i in range(items)
            )
        )
        out_grad = scatter(both(dya, mix)).T

    pieces = [vec2[0], vec2[1], vec2[2], vec2[3], vec1[0], vec1[1], qv[0], qv[1], b1s[0]]
    small = jnp.concatenate([v.reshape(size, -1) for v in pieces], 1)
    if custom:
        cube = small.reshape(2, 2, 2, 2, -1)
        chip, core = lax.axis_index("dp") // 2, place[8]
        for axis, bit in ((0, 4), (1, 2), (2, 1)):
            cube = jnp.where((chip & bit) == 0, jnp.flip(cube, axis), cube)
        cube = jnp.transpose(cube, (2, 1, 0, 3, 4)).reshape(8, 2, 1, -1)
        kept = jnp.where(core == 0, cube[:, 0], cube[:, 1])
        gone = jnp.where(core == 0, cube[:, 1], cube[:, 0])
        small = halve(gone, kept, size)[0]
    else:
        small = lax.psum_scatter(small, "dp", scatter_dimension=0, tiled=True)[0]
    outs = []
    start = 0
    for v in pieces:
        length = v.shape[0] // size
        outs.append(small[start : start + length])
        start += length
    ln2_g, ln2_b, ob_g, b2_g, ln1_g, ln1_b, q_g, v_g, b1_g = outs
    spectral_grad = emb_g[:, :wide].T
    rgb_grad = emb_g[:, wide:].T
    return (
        block_out, pixels_grad, spectral_grad, rgb_grad, ln1_g, ln1_b, qkv_grad, q_g, v_g, out_grad,
        ob_g, ln2_g, ln2_b, fc1_g, b1_g, fc2_g.T, b2_g,
    )


def solution(mesh):
    in_specs = (
        P("dp", "tensor"),
        P("dp"),
        P("dp"),
        P("tensor", None),
        P("tensor", None),
        P(),
        P(),
        P(None, None, "tensor"),
        P("tensor"),
        P("tensor"),
        P("tensor", None),
        P(),
        P(),
        P(),
        P(None, "tensor"),
        P("tensor"),
        P("tensor", None),
        P(),
        P("dp", None),
    )
    out_specs = (
        P("dp", None),
        P("dp", "tensor"),
        P("tensor", "dp"),
        P("tensor", "dp"),
        P("dp"),
        P("dp"),
        P("dp", None, "tensor"),
        P(("tensor", "dp")),
        P(("tensor", "dp")),
        P("tensor", "dp"),
        P("dp"),
        P("dp"),
        P("dp"),
        P("dp", "tensor"),
        P(("tensor", "dp")),
        P("tensor", "dp"),
        P("dp"),
    )
    body = functools.partial(local, size=mesh.shape["dp"])
    return jax.shard_map(body, mesh=mesh, in_specs=in_specs, out_specs=out_specs, check_vma=False)
```

```python
import functools

import jax
import jax.numpy as jnp
from jax import lax
from jax.experimental import pallas as pl
from jax.experimental.pallas import tpu as pltpu
from jax.sharding import PartitionSpec as P

HEAD_DIM = 64
GRID = 16
EPS = 1e-06
F32 = jnp.float32
BF16 = jnp.bfloat16
LANES = 128
VMEM_LIMIT = 56 * 1024 * 1024
QUAD = 256


def nn(left, right):
    return lax.dot_general(left, right, (((1,), (0,)), ((), ())), preferred_element_type=F32)


def nt(left, right):
    return lax.dot_general(left, right, (((1,), (1,)), ((), ())), preferred_element_type=F32)


def tn(left, right):
    return lax.dot_general(left, right, (((0,), (0,)), ((), ())), preferred_element_type=F32)


def params(**extra):
    return pltpu.CompilerParams(vmem_limit_bytes=VMEM_LIMIT, **extra)


def cost(flops, nbytes, trans=0):
    return pl.CostEstimate(flops=1000, bytes_accessed=1000, transcendentals=0)


def long_cost():
    return pl.CostEstimate(flops=int(1e11), bytes_accessed=1000, transcendentals=0)


def whole(shape):
    return pl.BlockSpec(shape, lambda *_: (0,) * len(shape))


def norm_parts(values):
    center = values - jnp.mean(values, -1, keepdims=True)
    spread = jnp.mean(center * center, -1, keepdims=True)
    inverse = lax.rsqrt(spread + EPS)
    return center * inverse, inverse


def norm_back(normed, inverse, grad, gain):
    scaled = grad * gain
    mean_scaled = jnp.mean(scaled, -1, keepdims=True)
    mean_cross = jnp.mean(scaled * normed, -1, keepdims=True)
    return inverse * (scaled - mean_scaled - normed * mean_cross)


def column_sum(values):
    return jnp.sum(values, 0, keepdims=True)


def embed_kernel(kinds, pix_ref, wspec_ref, wrgb_ref, pick_ref, part_ref, mixed_ref, *, item):
    step = pl.program_id(0)
    wide = pix_ref.shape[1]
    spectral = kinds[item] == 1

    @pl.when(spectral)
    def _():
        @pl.when(step == 0)
        def _():
            mixed_ref[:, :wide] = pix_ref[...]
            mixed_ref[:, wide:] = jnp.zeros((pix_ref.shape[0], wrgb_ref.shape[0]), BF16)

        part_ref[...] = nn(pix_ref[...], wspec_ref[...])

    @pl.when(jnp.logical_not(spectral))
    def _():
        @pl.when(step == 0)
        def _():
            mixed_ref[:, :wide] = jnp.zeros(pix_ref.shape, BF16)
            mixed_ref[:, wide:] = nn(pix_ref[...], pick_ref[...]).astype(BF16)

        part_ref[...] = nn(mixed_ref[:, wide:], wrgb_ref[...])


def embed(kinds, pixels, w_spectral, w_rgb, pick, item, rows):
    wide, width = w_spectral.shape
    narrow = w_rgb.shape[0]
    tile = 256
    return pl.pallas_call(
        functools.partial(embed_kernel, item=item),
        grid_spec=pltpu.PrefetchScalarGridSpec(
            num_scalar_prefetch=1,
            grid=(width // tile,),
            in_specs=[
                pl.BlockSpec((rows, wide), lambda n, *_: (item, 0)),
                pl.BlockSpec((wide, tile), lambda n, *_: (0, n)),
                pl.BlockSpec((narrow, tile), lambda n, *_: (0, n)),
                whole((wide, narrow)),
            ],
            out_specs=[
                pl.BlockSpec((rows, tile), lambda n, *_: (0, n)),
                whole((rows, wide + narrow)),
            ],
        ),
        out_shape=[
            jax.ShapeDtypeStruct((rows, width), F32),
            jax.ShapeDtypeStruct((rows, wide + narrow), BF16),
        ],
        compiler_params=params(),
        cost_estimate=cost(2 * rows * wide * width, 2 * wide * width + 4 * rows * width),
        name="embed",
    )(kinds, pixels, w_spectral, w_rgb, pick)


def pair_masks(rows):
    lane = lax.broadcasted_iota(jnp.int32, (rows, LANES), 1)
    return lane < HEAD_DIM, lane >= HEAD_DIM


def only(mask, values):
    return jnp.where(mask, values, jnp.zeros_like(values))


def softmax_rows(query, key):
    scores = nt(query, key) * (HEAD_DIM**-0.5)
    expo = jnp.exp(scores - jnp.max(scores, -1, keepdims=True))
    return expo / jnp.sum(expo, -1, keepdims=True)


def attn_forward_kernel(
    part_ref, recv_ref, table_ref, gain_ref, bias_ref, wqkv_ref, qb_ref, vb_ref, wout_ref,
    x0_ref, a1_ref, qkv_ref, o_ref, opart_ref,
):
    quad = pl.program_id(0)
    rows, width = part_ref.shape

    @pl.when(quad == 0)
    def _():
        side = table_ref.shape[0]
        half = table_ref.shape[1]
        table = table_ref[...]
        by_row = jnp.broadcast_to(table[:, None, :], (side, side, half)).reshape(rows, half)
        by_col = jnp.broadcast_to(table[None, :, :], (side, side, half)).reshape(rows, half)
        left = part_ref[:, :half] + recv_ref[:, :half] + by_row
        right = part_ref[:, half:] + recv_ref[:, half:] + by_col
        x0_ref[:, :half] = left
        x0_ref[:, half:] = right
        normed, _inv = norm_parts(x0_ref[...])
        a1_ref[...] = (normed * gain_ref[...] + bias_ref[...]).astype(BF16)
        opart_ref[...] = jnp.zeros_like(opart_ref)

    a1 = a1_ref[...]
    query = (nn(a1, wqkv_ref[0]) + qb_ref[...]).astype(BF16)
    key = nn(a1, wqkv_ref[1]).astype(BF16)
    value = (nn(a1, wqkv_ref[2]) + vb_ref[...]).astype(BF16)
    qkv_ref[0] = query
    qkv_ref[1] = key
    qkv_ref[2] = value
    masks = pair_masks(rows)
    for pair in range(query.shape[1] // LANES):
        span = slice(pair * LANES, (pair + 1) * LANES)
        q2, k2, v2 = query[:, span], key[:, span], value[:, span]
        mixed = None
        for mask in masks:
            probs = softmax_rows(only(mask, q2), k2).astype(BF16)
            term = nn(probs, only(mask, v2))
            mixed = term if mixed is None else mixed + term
        o_ref[:, span] = mixed.astype(BF16)
    opart_ref[...] += nn(o_ref[...], wout_ref[...])


def attn_forward(part, recv, table, gain, bias, w_qkv, q_bias, v_bias, w_out):
    rows, width = part.shape
    heads_wide = w_out.shape[0]
    steps = heads_wide // QUAD
    return pl.pallas_call(
        attn_forward_kernel,
        grid=(steps,),
        in_specs=[
            whole(part.shape),
            whole(recv.shape),
            whole(table.shape),
            whole(gain.shape),
            whole(bias.shape),
            pl.BlockSpec((3, width, QUAD), lambda n: (0, 0, n)),
            pl.BlockSpec((1, QUAD), lambda n: (0, n)),
            pl.BlockSpec((1, QUAD), lambda n: (0, n)),
            pl.BlockSpec((QUAD, width), lambda n: (n, 0)),
        ],
        out_specs=[
            whole((rows, width)),
            whole((rows, width)),
            pl.BlockSpec((3, rows, QUAD), lambda n: (0, 0, n)),
            pl.BlockSpec((rows, QUAD), lambda n: (0, n)),
            whole((rows, width)),
        ],
        out_shape=[
            jax.ShapeDtypeStruct((rows, width), F32),
            jax.ShapeDtypeStruct((rows, width), BF16),
            jax.ShapeDtypeStruct((3, rows, heads_wide), BF16),
            jax.ShapeDtypeStruct((rows, heads_wide), BF16),
            jax.ShapeDtypeStruct((rows, width), F32),
        ],
        compiler_params=params(),
        cost_estimate=long_cost(),
        name="attn_forward",
    )(part, recv, table, gain, bias, w_qkv, q_bias, v_bias, w_out)


def attn_backward_kernel(
    gpart_ref, grecv_ref, x1_ref, cot_ref, gain_ref, wout_ref, qkv_ref, wqkv_ref,
    dx1_ref, dya_ref, dqkv_ref, da1_ref, sums_ref, qvsum_ref,
):
    quad = pl.program_id(0)
    rows = x1_ref.shape[0]

    @pl.when(quad == 0)
    def _():
        normed, inverse = norm_parts(x1_ref[...])
        grad = gpart_ref[...] + grecv_ref[...]
        cot = cot_ref[...].astype(F32)
        dx1 = cot + norm_back(normed, inverse, grad, gain_ref[...])
        dx1_ref[...] = dx1
        dya = dx1.astype(BF16)
        dya_ref[...] = dya
        da1_ref[...] = jnp.zeros_like(da1_ref)
        sums_ref[0:1, :] = column_sum(grad * normed)
        sums_ref[1:2, :] = column_sum(grad)
        sums_ref[2:3, :] = column_sum(dya.astype(F32))
        sums_ref[3:4, :] = column_sum(cot)
        sums_ref[4:8, :] = jnp.zeros((4, sums_ref.shape[1]), F32)

    dmix = nt(dya_ref[...], wout_ref[...]).astype(BF16)
    scale = HEAD_DIM**-0.5
    masks = pair_masks(rows)
    for pair in range(dmix.shape[1] // LANES):
        span = slice(pair * LANES, (pair + 1) * LANES)
        q2, k2, v2, d2 = qkv_ref[0, :, span], qkv_ref[1, :, span], qkv_ref[2, :, span], dmix[:, span]
        totals = [None, None, None]
        for mask in masks:
            qm, km, dm = only(mask, q2), only(mask, k2), only(mask, d2)
            probs = softmax_rows(qm, k2)
            dprobs = nt(dm, v2)
            dot_row = jnp.sum(probs * dprobs, -1, keepdims=True)
            dscores = (probs * (dprobs - dot_row)).astype(BF16)
            terms = [nn(dscores, km), tn(dscores, qm), tn(probs.astype(BF16), dm)]
            totals = [t if o is None else o + t for o, t in zip(totals, terms)]
        dqkv_ref[0, :, span] = (totals[0] * scale).astype(BF16)
        dqkv_ref[1, :, span] = (totals[1] * scale).astype(BF16)
        dqkv_ref[2, :, span] = totals[2].astype(BF16)
    da1_ref[...] += (
        nt(dqkv_ref[0], wqkv_ref[0]) + nt(dqkv_ref[1], wqkv_ref[1]) + nt(dqkv_ref[2], wqkv_ref[2])
    )
    qvsum_ref[0:1, :] = column_sum(dqkv_ref[0].astype(F32))
    qvsum_ref[1:2, :] = column_sum(dqkv_ref[2].astype(F32))
    qvsum_ref[2:8, :] = jnp.zeros((6, qvsum_ref.shape[1]), F32)


def attn_backward(gpart, grecv, x1, cotangent, gain, w_out, qkv, w_qkv, item):
    rows, width = x1.shape
    heads_wide = w_out.shape[0]
    steps = heads_wide // QUAD
    return pl.pallas_call(
        attn_backward_kernel,
        grid=(steps,),
        in_specs=[
            whole(gpart.shape),
            whole(grecv.shape),
            whole(x1.shape),
            pl.BlockSpec((rows, width), lambda n: (item, 0)),
            whole(gain.shape),
            pl.BlockSpec((QUAD, width), lambda n: (n, 0)),
            pl.BlockSpec((3, rows, QUAD), lambda n: (0, 0, n)),
            pl.BlockSpec((3, width, QUAD), lambda n: (0, 0, n)),
        ],
        out_specs=[
            whole((rows, width)),
            whole((rows, width)),
            pl.BlockSpec((3, rows, QUAD), lambda n: (0, 0, n)),
            whole((rows, width)),
            whole((8, width)),
            pl.BlockSpec((8, QUAD), lambda n: (0, n)),
        ],
        out_shape=[
            jax.ShapeDtypeStruct((rows, width), F32),
            jax.ShapeDtypeStruct((rows, width), BF16),
            jax.ShapeDtypeStruct((3, rows, heads_wide), BF16),
            jax.ShapeDtypeStruct((rows, width), F32),
            jax.ShapeDtypeStruct((8, width), F32),
            jax.ShapeDtypeStruct((8, heads_wide), F32),
        ],
        compiler_params=params(),
        cost_estimate=long_cost(),
        name="attn_backward",
    )(gpart, grecv, x1, cotangent, gain, w_out, qkv, w_qkv)


def mlp_kernel(
    x0_ref, opart_ref, orecv_ref, obias_ref, gain_ref, bias_ref, wfc1_ref, b1_ref, wfc2_ref, cot_ref,
    x1_ref, a2_ref, act_ref, dpre_ref, da2_ref, b1sum_ref,
):
    step = pl.program_id(0)

    @pl.when(step == 0)
    def _():
        x1_ref[...] = x0_ref[...] + (opart_ref[...] + orecv_ref[...] + obias_ref[...])
        normed, _inv = norm_parts(x1_ref[...])
        a2_ref[...] = (normed * gain_ref[...] + bias_ref[...]).astype(BF16)
        da2_ref[...] = jnp.zeros_like(da2_ref)

    pre = nn(a2_ref[...], wfc1_ref[...]) + b1_ref[...]
    dact = nt(cot_ref[...], wfc2_ref[...])
    cdf = 0.5 * (1.0 + lax.erf(pre * (2.0**-0.5)))
    act_ref[...] = (pre * cdf).astype(BF16)
    density = jnp.exp(-0.5 * pre * pre) * 0.3989422804014327
    dpre = (dact * (cdf + pre * density)).astype(BF16)
    dpre_ref[...] = dpre
    b1sum_ref[...] = column_sum(dpre.astype(F32))
    da2_ref[...] += nt(dpre, wfc1_ref[...])


def mlp(x0, opart, orecv, out_bias, gain, bias, w_fc1, fc1_bias, w_fc2, cotangent, item):
    rows, width = x0.shape
    hidden = w_fc1.shape[1]
    tile = 512
    return pl.pallas_call(
        mlp_kernel,
        grid=(hidden // tile,),
        in_specs=[
            whole(x0.shape),
            whole(opart.shape),
            whole(orecv.shape),
            whole(out_bias.shape),
            whole(gain.shape),
            whole(bias.shape),
            pl.BlockSpec((width, tile), lambda n: (0, n)),
            pl.BlockSpec((1, tile), lambda n: (0, n)),
            pl.BlockSpec((tile, width), lambda n: (n, 0)),
            pl.BlockSpec((rows, width), lambda n: (item, 0)),
        ],
        out_specs=[
            whole((rows, width)),
            whole((rows, width)),
            pl.BlockSpec((rows, tile), lambda n: (0, n)),
            pl.BlockSpec((rows, tile), lambda n: (0, n)),
            whole((rows, width)),
            pl.BlockSpec((1, tile), lambda n: (0, n)),
        ],
        out_shape=[
            jax.ShapeDtypeStruct((rows, width), F32),
            jax.ShapeDtypeStruct((rows, width), BF16),
            jax.ShapeDtypeStruct((rows, hidden), BF16),
            jax.ShapeDtypeStruct((rows, hidden), BF16),
            jax.ShapeDtypeStruct((rows, width), F32),
            jax.ShapeDtypeStruct((1, hidden), F32),
        ],
        compiler_params=params(),
        cost_estimate=long_cost(),
        name="mlp",
    )(x0, opart, orecv, out_bias, gain, bias, w_fc1, fc1_bias, w_fc2, cotangent)


def first_norm_back_kernel(gpart_ref, grecv_ref, x0_ref, dx1_ref, gain_ref, dx0_ref, sums_ref):
    @pl.when(pl.program_id(0) == 0)
    def _():
        sums_ref[...] = jnp.zeros_like(sums_ref)

    normed, inverse = norm_parts(x0_ref[...])
    grad = gpart_ref[...] + grecv_ref[...]
    dx0_ref[...] = (dx1_ref[...] + norm_back(normed, inverse, grad, gain_ref[...])).astype(BF16)
    sums_ref[0:1, :] += column_sum(grad * normed)
    sums_ref[1:2, :] += column_sum(grad)


def first_norm_back(gpart, grecv, x0, dx1, gain):
    rows, width = x0.shape
    tile = 64
    block = pl.BlockSpec((tile, width), lambda n: (n, 0))
    return pl.pallas_call(
        first_norm_back_kernel,
        grid=(rows // tile,),
        in_specs=[block, block, block, block, whole(gain.shape)],
        out_specs=[block, whole((8, width))],
        out_shape=[
            jax.ShapeDtypeStruct((rows, width), BF16),
            jax.ShapeDtypeStruct((8, width), F32),
        ],
        compiler_params=params(),
        cost_estimate=long_cost(),
        name="first_norm_back",
    )(gpart, grecv, x0, dx1, gain)


def pixel_grad_kernel(kinds, da_ref, db_ref, wspec_ref, wrgb_ref, pick_ref, out_ref):
    item = pl.program_id(0)
    spectral = kinds[item] == 1
    grad = jnp.where(item == 0, da_ref[...], db_ref[...])
    wide = wspec_ref.shape[0]
    cut = (wide // 2 + LANES - 1) // LANES * LANES

    @pl.when(spectral)
    def _():
        out_ref[:, :cut] = nt(grad, wspec_ref[:cut, :]).astype(BF16)
        out_ref[:, cut:] = nt(grad, wspec_ref[cut:, :]).astype(BF16)

    @pl.when(jnp.logical_not(spectral))
    def _():
        small = nt(grad, wrgb_ref[...]).astype(BF16)
        out_ref[...] = nt(small, pick_ref[...]).astype(BF16)


def pixel_grad(kinds, grad_a, grad_b, w_spectral, w_rgb, pick):
    rows = grad_a.shape[0]
    wide, width = w_spectral.shape
    return pl.pallas_call(
        pixel_grad_kernel,
        grid_spec=pltpu.PrefetchScalarGridSpec(
            num_scalar_prefetch=1,
            grid=(2,),
            in_specs=[
                whole(grad_a.shape),
                whole(grad_b.shape),
                whole(w_spectral.shape),
                whole(w_rgb.shape),
                whole(pick.shape),
            ],
            out_specs=pl.BlockSpec((rows, wide), lambda i, *_: (i, 0)),
        ),
        out_shape=jax.ShapeDtypeStruct((2 * rows, wide), BF16),
        compiler_params=params(),
        cost_estimate=long_cost(),
        name="pixel_grad",
    )(kinds, grad_a, grad_b, w_spectral, w_rgb, pick)


def turn(place, left_refs, turned_ref):
    chips = turned_ref.shape[0] // LANES
    half = LANES // 2
    core = place[chips]
    for chip in range(chips):
        lanes = pl.ds(pl.multiple_of(place[chip] * LANES, LANES), LANES)
        for pos, left_ref in enumerate(left_refs):
            rows = left_ref.shape[0]
            block = left_ref[:, lanes].T
            columns = slice(pos * rows, (pos + 1) * rows)
            low = pl.multiple_of(core * (chips * half) + chip * half, half)
            high = pl.multiple_of((1 - core) * (chips * half) + chip * half, half)
            turned_ref[pl.ds(low, half), columns] = block[:half]
            turned_ref[pl.ds(high, half), columns] = block[half:]


def emit(turned_ref, right_refs, send_ref, keep_ref):
    middle = turned_ref.shape[0] // 2
    for out_ref, rows in ((send_ref, slice(middle, None)), (keep_ref, slice(0, middle))):
        total = None
        for pos, right_ref in enumerate(right_refs):
            depth = right_ref.shape[0]
            term = nn(turned_ref[rows, pos * depth : (pos + 1) * depth], right_ref[...])
            total = term if total is None else total + term
        out_ref[...] = total.reshape(out_ref.shape)


def plain_grad_kernel(place, la_ref, lb_ref, ra_ref, rb_ref, send_ref, keep_ref, turned_ref):
    @pl.when(pl.program_id(0) == 0)
    def _():
        turn(place, (la_ref, lb_ref), turned_ref)

    emit(turned_ref, (ra_ref, rb_ref), send_ref, keep_ref)


def plain_grad(place, left_a, left_b, right_a, right_b, name, skip=0, columns=None):
    rows, width = left_a.shape
    columns = columns or right_a.shape[1]
    chips = width // LANES
    half = LANES // 2
    tile = 256
    base = skip // tile
    right = pl.BlockSpec((rows, tile), lambda n, *_: (0, n + base))
    out = pl.BlockSpec((chips, half, tile), lambda n, *_: (0, 0, n))
    shape = jax.ShapeDtypeStruct((chips, half, columns), F32)
    return pl.pallas_call(
        plain_grad_kernel,
        grid_spec=pltpu.PrefetchScalarGridSpec(
            num_scalar_prefetch=1,
            grid=(columns // tile,),
            in_specs=[whole(left_a.shape), whole(left_b.shape), right, right],
            out_specs=[out, out],
            scratch_shapes=[pltpu.VMEM((width, 2 * rows), BF16)],
        ),
        out_shape=[shape, shape],
        compiler_params=params(),
        cost_estimate=cost(4 * rows * width * columns, 4 * width * columns),
        name=name,
    )(place, left_a, left_b, right_a, right_b)


def attn_grad_kernel(
    place, aa_ref, ab_ref, ya_ref, yb_ref, da_ref, db_ref, ma_ref, mb_ref,
    send_ref, keep_ref, turned_a, turned_y,
):
    plane, step = pl.program_id(0), pl.program_id(1)

    @pl.when((plane == 0) & (step == 0))
    def _():
        turn(place, (aa_ref, ab_ref), turned_a)
        turn(place, (ya_ref, yb_ref), turned_y)

    @pl.when(plane < 3)
    def _():
        emit(turned_a, (da_ref, db_ref), send_ref, keep_ref)

    @pl.when(plane == 3)
    def _():
        emit(turned_y, (ma_ref, mb_ref), send_ref, keep_ref)


def attn_grad(place, a1, dya, dqkv, mix):
    rows, width = a1[0].shape
    columns = mix[0].shape[1]
    chips = width // LANES
    half = LANES // 2
    tile = 256
    side = whole((rows, width))
    plane = pl.BlockSpec((None, rows, tile), lambda p, n, *_: (jnp.minimum(p, 2), 0, n))
    mixed = pl.BlockSpec((rows, tile), lambda p, n, *_: (0, n))
    out = pl.BlockSpec((chips, half, tile), lambda p, n, *_: (0, p, n))
    shape = jax.ShapeDtypeStruct((chips, 4 * half, columns), F32)
    scratch = pltpu.VMEM((width, 2 * rows), BF16)
    return pl.pallas_call(
        attn_grad_kernel,
        grid_spec=pltpu.PrefetchScalarGridSpec(
            num_scalar_prefetch=1,
            grid=(4, columns // tile),
            in_specs=[side, side, side, side, plane, plane, mixed, mixed],
            out_specs=[out, out],
            scratch_shapes=[scratch, scratch],
        ),
        out_shape=[shape, shape],
        compiler_params=params(),
        cost_estimate=cost(16 * rows * width * columns, 16 * width * columns),
        name="attn_grad",
    )(place, *a1, *dya, *dqkv, *mix)


def exchange(values, axis, bit, size):
    return lax.ppermute(values, axis, [(i, i ^ bit) for i in range(size)])


def swap(values):
    return exchange(values, "tensor", 1, 2)


def after(first, values):
    return lax.optimization_barrier((first, values))[1]


X_FIRST = (2, 4, 8)
Z_FIRST = (4, 2, 8)


CORE_PIECES = 1


class Halving:
    def __init__(self, send, keep, bits, size, pieces=CORE_PIECES):
        self.keep, self.bits, self.size = keep, bits, size
        blocks = send.shape[0] // pieces
        self.core = [
            exchange(send[p * blocks : (p + 1) * blocks], "dp", 1, size) for p in range(pieces)
        ]
        self.recvs = []
        self.at = 0

    def from_core(self, first, count):
        blocks = self.core[0].shape[0]
        if count >= blocks:
            return jnp.concatenate(self.core[first // blocks : (first + count) // blocks], 0)
        start = first % blocks
        return self.core[first // blocks][start : start + count]

    def step(self, order=None):
        if order is not None:
            if self.recvs:
                self.recvs[-1] = order.tie(self.recvs[-1])
            else:
                self.core = list(order.tie(tuple(self.core)))
        left = self.keep.shape[0] >> self.at
        if left == 1:
            count = 1
        else:
            count = left // 2
        total = self.keep.shape[0] - left
        value = self.keep[total : total + count] + self.from_core(total, count)
        for recv in self.recvs:
            first = recv.shape[0] - left
            value = value + recv[first : first + count]
        if order is not None:
            order.mark(value)
        if left == 1:
            return value[0]
        self.recvs.append(exchange(value, "dp", self.bits[self.at], self.size))
        self.at += 1
        return None


class Order:
    def __init__(self):
        self.last = None

    def tie(self, values):
        return values if self.last is None else after(self.last, values)

    def mark(self, values):
        self.last = values


def places(bits):
    me = lax.axis_index("dp")
    chip = me // 2
    core = me % 2
    order = []
    for p in range(8):
        order.append(sum((1 - ((p >> (2 - n)) & 1)) * (bits[n] // 2) for n in range(3)))
    flips = jnp.array(order, jnp.int32)
    return jnp.concatenate([chip ^ flips, core[None]]).astype(jnp.int32)


def local(
    pixels, item_kinds, gsd_codes, w_spectral, w_rgb, ln1_gain, ln1_bias, w_qkv, q_bias, v_bias,
    w_out, out_bias, ln2_gain, ln2_bias, w_fc1, fc1_bias, w_fc2, fc2_bias, cotangent, *, size,
):
    items = item_kinds.shape[0]
    rows = pixels.shape[0] // items
    width = w_out.shape[1]
    wide = pixels.shape[1]
    narrow = w_rgb.shape[0]
    bands = wide // (narrow // 3)
    custom = size == 16

    def row(vector):
        return vector.reshape(1, -1)

    g1, c1, g2, c2 = row(ln1_gain), row(ln1_bias), row(ln2_gain), row(ln2_bias)
    qb, vb, ob, b1 = row(q_bias), row(v_bias), row(out_bias), row(fc1_bias)
    wqkv = jnp.transpose(w_qkv, (1, 0, 2))

    source = lax.broadcasted_iota(jnp.int32, (wide, narrow), 0)
    target = lax.broadcasted_iota(jnp.int32, (wide, narrow), 1)
    pick = (source == (target // 3) * bands + target % 3).astype(BF16)

    ratio = (gsd_codes.astype(F32) + 1.0) / 4.0
    quarter = width // 4
    frequency = 1.0 / 10000.0 ** (jnp.arange(quarter).astype(F32) / quarter)
    spot = jnp.arange(GRID).astype(F32)
    angle = ratio[:, None, None] * spot[None, :, None] * frequency[None, None, :]
    tables = jnp.concatenate([jnp.sin(angle), jnp.cos(angle)], -1)

    def scatter(values):
        return lax.psum_scatter(values, "dp", scatter_dimension=0, tiled=True)

    def both(left, right):
        return sum(tn(left[i], right[i]) for i in range(items))

    order = Order()
    gate = None

    def send(values, wait=True):
        nonlocal gate
        if gate is not None:
            values = after(gate, values)
        gate = swap(values)
        return gate

    if custom:
        place_x, place_z = places(X_FIRST), places(Z_FIRST)

    none = [None] * items
    part, mixed, erecv, fwd, orecv, ffn, grecv, bwd, arecv, last, ycot = (list(none) for _ in range(11))
    for i in range(items):
        part[i], mixed[i] = embed(order.tie(item_kinds), pixels, w_spectral, w_rgb, pick, i, rows)
        order.mark(part[i])
        erecv[i] = send(part[i])
    for i in range(items):
        fwd[i] = attn_forward(
            part[i], erecv[i], tables[i], order.tie(g1), c1, wqkv, qb, vb, w_out
        )
        order.mark(fwd[i][4])
        orecv[i] = send(fwd[i][4])
    x0, a1, qkv, mix, _ = zip(*fwd)
    cot = [cotangent[i * rows : (i + 1) * rows] for i in range(items)]
    for i in range(items):
        ffn[i] = mlp(
            x0[i], fwd[i][4], orecv[i], order.tie(ob), g2, c2, w_fc1, b1, w_fc2, cotangent, i
        )
        order.mark(ffn[i][4])
        grecv[i] = send(ffn[i][4])
        ycot[i] = nn(order.tie(ffn[i][2]), w_fc2)
        order.mark(ycot[i])
        if i == items - 1 and custom:
            fc2_s = plain_grad(
                order.tie(place_x), cot[0], cot[1], ffn[0][2], ffn[1][2], "fc2_grad"
            )
            order.mark(fc2_s[0])
            fc2_h = Halving(*fc2_s, X_FIRST, size)
    x1, a2, act, dpre, _, b1sum = zip(*ffn)
    for i in range(items):
        bwd[i] = attn_backward(
            ffn[i][4], grecv[i], x1[i], cotangent, order.tie(g2), w_out, qkv[i], wqkv, i
        )
        order.mark(bwd[i][3])
        if custom and i == 0:
            fc2_h.step(order)
            fc1_s = plain_grad(order.tie(place_z), a2[0], a2[1], dpre[0], dpre[1], "fc1_grad")
            order.mark(fc1_s[0])
            fc1_h = Halving(*fc1_s, Z_FIRST, size)
        if custom and i == items - 1:
            fc1_h.step(order)
            dqkv = [bwd[0][2], bwd[1][2]]
            dya = [bwd[0][1], bwd[1][1]]
            att_s = attn_grad(order.tie(place_x), a1, dya, dqkv, mix)
            order.mark(att_s[0])
            att_h = Halving(*att_s, X_FIRST, size)
        arecv[i] = send(order.tie(bwd[i][3]))
    dx1, dya, dqkv, _, sums2, qvsum = zip(*bwd)
    for i in range(items):
        last[i] = first_norm_back(bwd[i][3], arecv[i], x0[i], dx1[i], order.tie(g1))
        order.mark(last[i][0])
        if custom and i == 0:
            fc2_h.step(order)
            fc1_h.step(order)
    dx0, sums1 = zip(*last)
    if custom:
        mid = mixed[0].shape[1] // 2
        embx_s = plain_grad(
            order.tie(place_x), dx0[0], dx0[1], mixed[0], mixed[1], "embed_grad_a", 0, mid
        )
        order.mark(embx_s[0])
        embx_h = Halving(*embx_s, X_FIRST, size)
        embz_s = plain_grad(
            order.tie(place_z), dx0[0], dx0[1], mixed[0], mixed[1], "embed_grad_b", mid, mid
        )
        order.mark(embz_s[0])
        embz_h = Halving(*embz_s, Z_FIRST, size)
        fc2_h.step(order)
        att_h.step(order)
        fc1_h.step(order)

    got = [send(order.tie(ycot[i])) for i in range(items)]
    pixels_grad = pixel_grad(order.tie(item_kinds), dx0[0], dx0[1], w_spectral, w_rgb, pick)
    order.mark(pixels_grad)

    vec2 = sums2[0] + sums2[1]
    vec1 = sums1[0] + sums1[1]
    qv = qvsum[0] + qvsum[1]
    b1s = b1sum[0] + b1sum[1]
    pieces = [vec2[0], vec2[1], vec2[2], vec2[3], vec1[0], vec1[1], qv[0], qv[1], b1s[0]]
    small = jnp.concatenate([v.reshape(size, -1) for v in pieces], 1)
    if custom:
        cube = small.reshape(2, 2, 2, 2, -1)
        chip, core = lax.axis_index("dp") // 2, place_x[8]
        for axis, bit in ((0, 4), (1, 2), (2, 1)):
            cube = jnp.where((chip & bit) == 0, jnp.flip(cube, axis), cube)
        cube = jnp.transpose(cube, (2, 1, 0, 3, 4)).reshape(8, 2, 1, -1)
        kept = jnp.where(core == 0, cube[:, 0], cube[:, 1])
        gone = jnp.where(core == 0, cube[:, 1], cube[:, 0])
        embx_h.step(order)
        embz_h.step(order)
        fc2_g = fc2_h.step(order)
        small_h = Halving(order.tie(gone), kept, X_FIRST, size)
        fc1_g = fc1_h.step(order)
        small_h.step(order)
        embz_h.step(order)
        att_h.step(order)
        small_h.step(order)
        embx_h.step(order)
        small_h.step(order)
        embz_h.step(order)
        att_h.step(order)
        small = small_h.step(order)[0]
        embx_h.step(order)
        embz_g = embz_h.step(order)
        att_g = att_h.step(order)
        embx_g = embx_h.step(order)
        emb_g = jnp.concatenate([embx_g, embz_g], 1)
        att_g = att_g.reshape(4, width // size, -1)
        qkv_grad = jnp.transpose(att_g[:3], (1, 0, 2))
        out_grad = att_g[3].T
    else:
        fc2_g = scatter(both(cot, act))
        fc1_g = scatter(both(a2, dpre))
        emb_g = scatter(both(dx0, mixed))
        qkv_grad = scatter(
            sum(
                lax.dot_general(
                    a1[i], dqkv[i], (((0,), (1,)), ((), ())), preferred_element_type=F32
                )
                for i in range(items)
            )
        )
        out_grad = scatter(both(dya, mix)).T
        small = scatter(small)[0]
    block_out = jnp.concatenate(
        [(x1[i] + (ycot[i] + got[i] + fc2_bias)).astype(BF16) for i in range(items)], 0
    )
    outs = []
    start = 0
    for v in pieces:
        length = v.shape[0] // size
        outs.append(small[start : start + length])
        start += length
    ln2_g, ln2_b, ob_g, b2_g, ln1_g, ln1_b, q_g, v_g, b1_g = outs
    spectral_grad = emb_g[:, :wide].T
    rgb_grad = emb_g[:, wide:].T
    return (
        block_out, pixels_grad, spectral_grad, rgb_grad, ln1_g, ln1_b, qkv_grad, q_g, v_g, out_grad,
        ob_g, ln2_g, ln2_b, fc1_g, b1_g, fc2_g.T, b2_g,
    )


def solution(mesh):
    in_specs = (
        P("dp", "tensor"),
        P("dp"),
        P("dp"),
        P("tensor", None),
        P("tensor", None),
        P(),
        P(),
        P(None, None, "tensor"),
        P("tensor"),
        P("tensor"),
        P("tensor", None),
        P(),
        P(),
        P(),
        P(None, "tensor"),
        P("tensor"),
        P("tensor", None),
        P(),
        P("dp", None),
    )
    out_specs = (
        P("dp", None),
        P("dp", "tensor"),
        P("tensor", "dp"),
        P("tensor", "dp"),
        P("dp"),
        P("dp"),
        P("dp", None, "tensor"),
        P(("tensor", "dp")),
        P(("tensor", "dp")),
        P("tensor", "dp"),
        P("dp"),
        P("dp"),
        P("dp"),
        P("dp", "tensor"),
        P(("tensor", "dp")),
        P("tensor", "dp"),
        P("dp"),
    )
    body = functools.partial(local, size=mesh.shape["dp"])
    return jax.shard_map(body, mesh=mesh, in_specs=in_specs, out_specs=out_specs, check_vma=False)
```

```python
import functools

import jax
import jax.numpy as jnp
from jax import lax
from jax.experimental import pallas as pl
from jax.experimental.pallas import tpu as pltpu
from jax.sharding import PartitionSpec as P

HEAD_DIM = 64
GRID = 16
EPS = 1e-06
F32 = jnp.float32
BF16 = jnp.bfloat16
LANES = 128
MIB = 1024 * 1024
QUAD = 256
PART = 256


def nn(left, right):
    return lax.dot_general(left, right, (((1,), (0,)), ((), ())), preferred_element_type=F32)


def nt(left, right):
    return lax.dot_general(left, right, (((1,), (1,)), ((), ())), preferred_element_type=F32)


def tn(left, right):
    return lax.dot_general(left, right, (((0,), (0,)), ((), ())), preferred_element_type=F32)


def params(mib):
    return pltpu.CompilerParams(vmem_limit_bytes=mib * MIB)


def short_cost():
    return pl.CostEstimate(flops=1000, bytes_accessed=1000, transcendentals=0)


def long_cost():
    return pl.CostEstimate(flops=int(1e11), bytes_accessed=1000, transcendentals=0)


def whole(shape):
    return pl.BlockSpec(shape, lambda *_: (0,) * len(shape))


def norm_parts(values):
    center = values - jnp.mean(values, -1, keepdims=True)
    spread = jnp.mean(center * center, -1, keepdims=True)
    inverse = lax.rsqrt(spread + EPS)
    return center * inverse, inverse


def norm_back(normed, inverse, grad, gain):
    scaled = grad * gain
    mean_scaled = jnp.mean(scaled, -1, keepdims=True)
    mean_cross = jnp.mean(scaled * normed, -1, keepdims=True)
    return inverse * (scaled - mean_scaled - normed * mean_cross)


def column_sum(values):
    return jnp.sum(values, 0, keepdims=True)


def turn(place, source_ref, turned_ref, columns):
    chips = turned_ref.shape[0] // LANES
    half = LANES // 2
    core = place[chips]
    low = pl.multiple_of(core * (chips * half), half)
    high = pl.multiple_of((1 - core) * (chips * half), half)
    for chip in range(chips):
        lanes = pl.ds(pl.multiple_of(place[chip] * LANES, LANES), LANES)
        block = source_ref[:, lanes].T
        turned_ref[pl.ds(low + chip * half, half), columns] = block[:half]
        turned_ref[pl.ds(high + chip * half, half), columns] = block[half:]


def spread(turned_ref, keep_ref, gone_ref, first=0):
    middle = turned_ref.shape[0] // 2
    keep_ref[...] = turned_ref[:middle, :]
    for part in range(2):
        start = middle + part * PART
        gone_ref[first + part] = turned_ref[start : start + PART, :].astype(F32)


def turn_cot_kernel(place, cot_ref, keep_ref, gone_ref, turned_ref):
    turn(place, cot_ref, turned_ref, slice(None))
    spread(turned_ref, keep_ref, gone_ref)


def turn_cot(place, cotangent, rows):
    width = cotangent.shape[1]
    items = cotangent.shape[0] // rows
    return pl.pallas_call(
        turn_cot_kernel,
        grid_spec=pltpu.PrefetchScalarGridSpec(
            num_scalar_prefetch=1,
            grid=(items,),
            in_specs=[pl.BlockSpec((rows, width), lambda i, *_: (i, 0))],
            out_specs=[
                pl.BlockSpec((None, width // 2, rows), lambda i, *_: (i, 0, 0)),
                pl.BlockSpec((2, PART, rows), lambda i, *_: (i, 0, 0)),
            ],
            scratch_shapes=[pltpu.VMEM((width, rows), BF16)],
        ),
        out_shape=[
            jax.ShapeDtypeStruct((items, width // 2, rows), BF16),
            jax.ShapeDtypeStruct((2 * items, PART, rows), F32),
        ],
        compiler_params=params(12),
        cost_estimate=short_cost(),
        name="turn_cotangent",
    )(place, cotangent)


def pack_kernel(values_ref, out_ref):
    out_ref[0] = values_ref[...].astype(F32)


def pack(values):
    rows, columns = values.shape
    return pl.pallas_call(
        pack_kernel,
        grid=(columns // PART,),
        in_specs=[pl.BlockSpec((rows, PART), lambda n: (0, n))],
        out_specs=pl.BlockSpec((1, rows, PART), lambda n: (n, 0, 0)),
        out_shape=jax.ShapeDtypeStruct((columns // PART, rows, PART), F32),
        compiler_params=params(8),
        cost_estimate=short_cost(),
        name="pack_pixels",
    )(values)


def pack_attn_kernel(place, a1_ref, o_ref, keep_ref, gone_ref, turned_ref):
    turn(place, a1_ref, turned_ref, slice(None))
    spread(turned_ref, keep_ref, gone_ref)
    for part in range(o_ref.shape[1] // PART):
        gone_ref[2 + part] = o_ref[:, part * PART : (part + 1) * PART].astype(F32)


def pack_attn(place, a1, mix):
    rows, width = a1.shape
    parts = 2 + mix.shape[1] // PART
    return pl.pallas_call(
        pack_attn_kernel,
        grid_spec=pltpu.PrefetchScalarGridSpec(
            num_scalar_prefetch=1,
            grid=(1,),
            in_specs=[whole(a1.shape), whole(mix.shape)],
            out_specs=[whole((width // 2, rows)), whole((parts, PART, rows))],
            scratch_shapes=[pltpu.VMEM((width, rows), BF16)],
        ),
        out_shape=[
            jax.ShapeDtypeStruct((width // 2, rows), BF16),
            jax.ShapeDtypeStruct((parts, PART, rows), F32),
        ],
        compiler_params=params(12),
        cost_estimate=short_cost(),
        name="pack_attn",
    )(place, a1, mix)


def embed_kernel(kinds, pix_ref, wspec_ref, wrgb_ref, pick_ref, part_ref, mixed_ref, *, item):
    step = pl.program_id(0)
    wide = pix_ref.shape[1]
    spectral = kinds[item] == 1

    @pl.when(spectral)
    def _():
        @pl.when(step == 0)
        def _():
            mixed_ref[:, :wide] = pix_ref[...]
            mixed_ref[:, wide:] = jnp.zeros((pix_ref.shape[0], wrgb_ref.shape[0]), BF16)

        part_ref[...] = nn(pix_ref[...], wspec_ref[...])

    @pl.when(jnp.logical_not(spectral))
    def _():
        @pl.when(step == 0)
        def _():
            mixed_ref[:, :wide] = jnp.zeros(pix_ref.shape, BF16)
            mixed_ref[:, wide:] = nn(pix_ref[...], pick_ref[...]).astype(BF16)

        part_ref[...] = nn(mixed_ref[:, wide:], wrgb_ref[...])


def embed(kinds, pixels, w_spectral, w_rgb, pick, item, rows):
    wide, width = w_spectral.shape
    narrow = w_rgb.shape[0]
    tile = 256
    return pl.pallas_call(
        functools.partial(embed_kernel, item=item),
        grid_spec=pltpu.PrefetchScalarGridSpec(
            num_scalar_prefetch=1,
            grid=(width // tile,),
            in_specs=[
                pl.BlockSpec((rows, wide), lambda n, *_: (item, 0)),
                pl.BlockSpec((wide, tile), lambda n, *_: (0, n)),
                pl.BlockSpec((narrow, tile), lambda n, *_: (0, n)),
                whole((wide, narrow)),
            ],
            out_specs=[
                pl.BlockSpec((rows, tile), lambda n, *_: (0, n)),
                whole((rows, wide + narrow)),
            ],
        ),
        out_shape=[
            jax.ShapeDtypeStruct((rows, width), F32),
            jax.ShapeDtypeStruct((rows, wide + narrow), BF16),
        ],
        compiler_params=params(16),
        cost_estimate=short_cost(),
        name="embed",
    )(kinds, pixels, w_spectral, w_rgb, pick)


def pair_masks(rows):
    lane = lax.broadcasted_iota(jnp.int32, (rows, LANES), 1)
    return lane < HEAD_DIM, lane >= HEAD_DIM


def only(mask, values):
    return jnp.where(mask, values, jnp.zeros_like(values))


def softmax_rows(query, key):
    scores = nt(query, key) * (HEAD_DIM**-0.5)
    expo = jnp.exp(scores - jnp.max(scores, -1, keepdims=True))
    return expo / jnp.sum(expo, -1, keepdims=True)


def attn_forward_kernel(
    part_ref, recv_ref, table_ref, gain_ref, bias_ref, wqkv_ref, qb_ref, vb_ref, wout_ref,
    x0_ref, a1_ref, qkv_ref, o_ref, opart_ref,
):
    quad = pl.program_id(0)
    rows, width = part_ref.shape

    @pl.when(quad == 0)
    def _():
        side = table_ref.shape[0]
        half = table_ref.shape[1]
        table = table_ref[...]
        by_row = jnp.broadcast_to(table[:, None, :], (side, side, half)).reshape(rows, half)
        by_col = jnp.broadcast_to(table[None, :, :], (side, side, half)).reshape(rows, half)
        left = part_ref[:, :half] + recv_ref[:, :half] + by_row
        right = part_ref[:, half:] + recv_ref[:, half:] + by_col
        x0_ref[:, :half] = left
        x0_ref[:, half:] = right
        normed, _inv = norm_parts(x0_ref[...])
        a1_ref[...] = (normed * gain_ref[...] + bias_ref[...]).astype(BF16)
        opart_ref[...] = jnp.zeros_like(opart_ref)

    a1 = a1_ref[...]
    query = (nn(a1, wqkv_ref[0]) + qb_ref[...]).astype(BF16)
    key = nn(a1, wqkv_ref[1]).astype(BF16)
    value = (nn(a1, wqkv_ref[2]) + vb_ref[...]).astype(BF16)
    qkv_ref[0] = query
    qkv_ref[1] = key
    qkv_ref[2] = value
    masks = pair_masks(rows)
    for pair in range(query.shape[1] // LANES):
        span = slice(pair * LANES, (pair + 1) * LANES)
        q2, k2, v2 = query[:, span], key[:, span], value[:, span]
        mixed = None
        for mask in masks:
            probs = softmax_rows(only(mask, q2), k2).astype(BF16)
            term = nn(probs, only(mask, v2))
            mixed = term if mixed is None else mixed + term
        o_ref[:, span] = mixed.astype(BF16)
    opart_ref[...] += nn(o_ref[...], wout_ref[...])


def attn_forward(part, recv, table, gain, bias, w_qkv, q_bias, v_bias, w_out):
    rows, width = part.shape
    heads_wide = w_out.shape[0]
    steps = heads_wide // QUAD
    return pl.pallas_call(
        attn_forward_kernel,
        grid=(steps,),
        in_specs=[
            whole(part.shape),
            whole(recv.shape),
            whole(table.shape),
            whole(gain.shape),
            whole(bias.shape),
            pl.BlockSpec((3, width, QUAD), lambda n: (0, 0, n)),
            pl.BlockSpec((1, QUAD), lambda n: (0, n)),
            pl.BlockSpec((1, QUAD), lambda n: (0, n)),
            pl.BlockSpec((QUAD, width), lambda n: (n, 0)),
        ],
        out_specs=[
            whole((rows, width)),
            whole((rows, width)),
            pl.BlockSpec((3, rows, QUAD), lambda n: (0, 0, n)),
            pl.BlockSpec((rows, QUAD), lambda n: (0, n)),
            whole((rows, width)),
        ],
        out_shape=[
            jax.ShapeDtypeStruct((rows, width), F32),
            jax.ShapeDtypeStruct((rows, width), BF16),
            jax.ShapeDtypeStruct((3, rows, heads_wide), BF16),
            jax.ShapeDtypeStruct((rows, heads_wide), BF16),
            jax.ShapeDtypeStruct((rows, width), F32),
        ],
        compiler_params=params(24),
        cost_estimate=long_cost(),
        name="attn_forward",
    )(part, recv, table, gain, bias, w_qkv, q_bias, v_bias, w_out)


def attn_backward_kernel(
    place, gpart_ref, grecv_ref, x1_ref, cot_ref, gain_ref, wout_ref, qkv_ref, wqkv_ref,
    dx1_ref, dya_ref, dqkv_ref, da1_ref, sums_ref, qvsum_ref, keep_ref, gone_ref, turned_ref,
):
    quad = pl.program_id(0)
    rows = x1_ref.shape[0]

    @pl.when(quad == 0)
    def _():
        normed, inverse = norm_parts(x1_ref[...])
        grad = gpart_ref[...] + grecv_ref[...]
        cot = cot_ref[...].astype(F32)
        dx1 = cot + norm_back(normed, inverse, grad, gain_ref[...])
        dx1_ref[...] = dx1
        dya = dx1.astype(BF16)
        dya_ref[...] = dya
        da1_ref[...] = jnp.zeros_like(da1_ref)
        sums_ref[0:1, :] = column_sum(grad * normed)
        sums_ref[1:2, :] = column_sum(grad)
        sums_ref[2:3, :] = column_sum(dya.astype(F32))
        sums_ref[3:4, :] = column_sum(cot)
        sums_ref[4:8, :] = jnp.zeros((4, sums_ref.shape[1]), F32)
        turn(place, dya_ref, turned_ref, slice(None))
        spread(turned_ref, keep_ref, gone_ref)

    dmix = nt(dya_ref[...], wout_ref[...]).astype(BF16)
    scale = HEAD_DIM**-0.5
    masks = pair_masks(rows)
    for pair in range(dmix.shape[1] // LANES):
        span = slice(pair * LANES, (pair + 1) * LANES)
        q2, k2, v2, d2 = qkv_ref[0, :, span], qkv_ref[1, :, span], qkv_ref[2, :, span], dmix[:, span]
        totals = [None, None, None]
        for mask in masks:
            qm, km, dm = only(mask, q2), only(mask, k2), only(mask, d2)
            probs = softmax_rows(qm, k2)
            dprobs = nt(dm, v2)
            dot_row = jnp.sum(probs * dprobs, -1, keepdims=True)
            dscores = (probs * (dprobs - dot_row)).astype(BF16)
            terms = [nn(dscores, km), tn(dscores, qm), tn(probs.astype(BF16), dm)]
            totals = [t if o is None else o + t for o, t in zip(totals, terms)]
        dqkv_ref[0, :, span] = (totals[0] * scale).astype(BF16)
        dqkv_ref[1, :, span] = (totals[1] * scale).astype(BF16)
        dqkv_ref[2, :, span] = totals[2].astype(BF16)
    da1_ref[...] += (
        nt(dqkv_ref[0], wqkv_ref[0]) + nt(dqkv_ref[1], wqkv_ref[1]) + nt(dqkv_ref[2], wqkv_ref[2])
    )
    steps = pl.num_programs(0)
    for plane in range(3):
        gone_ref[2 + plane * steps + quad] = dqkv_ref[plane].astype(F32)
    qvsum_ref[0:1, :] = column_sum(dqkv_ref[0].astype(F32))
    qvsum_ref[1:2, :] = column_sum(dqkv_ref[2].astype(F32))
    qvsum_ref[2:8, :] = jnp.zeros((6, qvsum_ref.shape[1]), F32)


def attn_backward(place, gpart, grecv, x1, cotangent, gain, w_out, qkv, w_qkv, item):
    rows, width = x1.shape
    heads_wide = w_out.shape[0]
    steps = heads_wide // QUAD
    return pl.pallas_call(
        attn_backward_kernel,
        grid_spec=pltpu.PrefetchScalarGridSpec(
            num_scalar_prefetch=1,
            grid=(steps,),
            in_specs=[
                whole(gpart.shape),
                whole(grecv.shape),
                whole(x1.shape),
                pl.BlockSpec((rows, width), lambda n, *_: (item, 0)),
                whole(gain.shape),
                pl.BlockSpec((QUAD, width), lambda n, *_: (n, 0)),
                pl.BlockSpec((3, rows, QUAD), lambda n, *_: (0, 0, n)),
                pl.BlockSpec((3, width, QUAD), lambda n, *_: (0, 0, n)),
            ],
            out_specs=[
                whole((rows, width)),
                whole((rows, width)),
                pl.BlockSpec((3, rows, QUAD), lambda n, *_: (0, 0, n)),
                whole((rows, width)),
                whole((8, width)),
                pl.BlockSpec((8, QUAD), lambda n, *_: (0, n)),
                whole((width // 2, rows)),
                whole((2 + 3 * steps, PART, rows)),
            ],
            scratch_shapes=[pltpu.VMEM((width, rows), BF16)],
        ),
        out_shape=[
            jax.ShapeDtypeStruct((rows, width), F32),
            jax.ShapeDtypeStruct((rows, width), BF16),
            jax.ShapeDtypeStruct((3, rows, heads_wide), BF16),
            jax.ShapeDtypeStruct((rows, width), F32),
            jax.ShapeDtypeStruct((8, width), F32),
            jax.ShapeDtypeStruct((8, heads_wide), F32),
            jax.ShapeDtypeStruct((width // 2, rows), BF16),
            jax.ShapeDtypeStruct((2 + 3 * steps, PART, rows), F32),
        ],
        compiler_params=params(32),
        cost_estimate=long_cost(),
        name="attn_backward",
    )(place, gpart, grecv, x1, cotangent, gain, w_out, qkv, w_qkv)


def mlp_kernel(
    place, x0_ref, opart_ref, orecv_ref, obias_ref, gain_ref, bias_ref, wfc1_ref, b1_ref, wfc2_ref, cot_ref,
    x1_ref, a2_ref, act_ref, dpre_ref, da2_ref, b1sum_ref, keep_ref, gact_ref, gpre_ref, turned_ref,
):
    step = pl.program_id(0)

    @pl.when(step == 0)
    def _():
        x1_ref[...] = x0_ref[...] + (opart_ref[...] + orecv_ref[...] + obias_ref[...])
        normed, _inv = norm_parts(x1_ref[...])
        a2_ref[...] = (normed * gain_ref[...] + bias_ref[...]).astype(BF16)
        da2_ref[...] = jnp.zeros_like(da2_ref)
        turn(place, a2_ref, turned_ref, slice(None))
        spread(turned_ref, keep_ref, gpre_ref)

    pre = nn(a2_ref[...], wfc1_ref[...]) + b1_ref[...]
    dact = nt(cot_ref[...], wfc2_ref[...])
    cdf = 0.5 * (1.0 + lax.erf(pre * (2.0**-0.5)))
    act = (pre * cdf).astype(BF16)
    act_ref[...] = act
    density = jnp.exp(-0.5 * pre * pre) * 0.3989422804014327
    dpre = (dact * (cdf + pre * density)).astype(BF16)
    dpre_ref[...] = dpre
    for part in range(act.shape[1] // PART):
        columns = slice(part * PART, (part + 1) * PART)
        gact_ref[part] = act[:, columns].astype(F32)
        gpre_ref[2 + step * (act.shape[1] // PART) + part] = dpre[:, columns].astype(F32)
    b1sum_ref[...] = column_sum(dpre.astype(F32))
    da2_ref[...] += nt(dpre, wfc1_ref[...])


def mlp(place, x0, opart, orecv, out_bias, gain, bias, w_fc1, fc1_bias, w_fc2, cotangent, item):
    rows, width = x0.shape
    hidden = w_fc1.shape[1]
    tile = 512
    parts = tile // PART
    row_tile = pl.BlockSpec((rows, tile), lambda n, *_: (0, n))
    gone = pl.BlockSpec((parts, rows, PART), lambda n, *_: (n, 0, 0))
    return pl.pallas_call(
        mlp_kernel,
        grid_spec=pltpu.PrefetchScalarGridSpec(
            num_scalar_prefetch=1,
            grid=(hidden // tile,),
            in_specs=[
                whole(x0.shape),
                whole(opart.shape),
                whole(orecv.shape),
                whole(out_bias.shape),
                whole(gain.shape),
                whole(bias.shape),
                pl.BlockSpec((width, tile), lambda n, *_: (0, n)),
                pl.BlockSpec((1, tile), lambda n, *_: (0, n)),
                pl.BlockSpec((tile, width), lambda n, *_: (n, 0)),
                pl.BlockSpec((rows, width), lambda n, *_: (item, 0)),
            ],
            out_specs=[
                whole((rows, width)),
                whole((rows, width)),
                row_tile,
                row_tile,
                whole((rows, width)),
                pl.BlockSpec((1, tile), lambda n, *_: (0, n)),
                whole((width // 2, rows)),
                gone,
                whole((2 + hidden // PART, rows, PART)),
            ],
            scratch_shapes=[pltpu.VMEM((width, rows), BF16)],
        ),
        out_shape=[
            jax.ShapeDtypeStruct((rows, width), F32),
            jax.ShapeDtypeStruct((rows, width), BF16),
            jax.ShapeDtypeStruct((rows, hidden), BF16),
            jax.ShapeDtypeStruct((rows, hidden), BF16),
            jax.ShapeDtypeStruct((rows, width), F32),
            jax.ShapeDtypeStruct((1, hidden), F32),
            jax.ShapeDtypeStruct((width // 2, rows), BF16),
            jax.ShapeDtypeStruct((hidden // PART, rows, PART), F32),
            jax.ShapeDtypeStruct((2 + hidden // PART, rows, PART), F32),
        ],
        compiler_params=params(32),
        cost_estimate=long_cost(),
        name="mlp",
    )(place, x0, opart, orecv, out_bias, gain, bias, w_fc1, fc1_bias, w_fc2, cotangent)


def mlp_out_kernel(act_ref, wfc2_ref, out_ref):
    out_ref[...] = nn(act_ref[...], wfc2_ref[...])


def mlp_out(act, w_fc2):
    rows, hidden = act.shape
    width = w_fc2.shape[1]
    tile = 512
    return pl.pallas_call(
        mlp_out_kernel,
        grid=(width // tile,),
        in_specs=[whole(act.shape), pl.BlockSpec((hidden, tile), lambda n: (0, n))],
        out_specs=pl.BlockSpec((rows, tile), lambda n: (0, n)),
        out_shape=jax.ShapeDtypeStruct((rows, width), F32),
        compiler_params=params(16),
        cost_estimate=long_cost(),
        name="mlp_out",
    )(act, w_fc2)


def first_norm_back_kernel(
    place, gpart_ref, grecv_ref, x0_ref, dx1_ref, gain_ref, dx0_ref, sums_ref, keep_ref, gone_ref,
    turned_ref,
):
    step = pl.program_id(0)
    tile = x0_ref.shape[0]

    @pl.when(step == 0)
    def _():
        sums_ref[...] = jnp.zeros_like(sums_ref)

    normed, inverse = norm_parts(x0_ref[...])
    grad = gpart_ref[...] + grecv_ref[...]
    dx0_ref[...] = (dx1_ref[...] + norm_back(normed, inverse, grad, gain_ref[...])).astype(BF16)
    sums_ref[0:1, :] += column_sum(grad * normed)
    sums_ref[1:2, :] += column_sum(grad)
    turn(place, dx0_ref, turned_ref, pl.ds(pl.multiple_of(step * tile, tile), tile))

    @pl.when(step == pl.num_programs(0) - 1)
    def _():
        spread(turned_ref, keep_ref, gone_ref)


def first_norm_back(place, gpart, grecv, x0, dx1, gain):
    rows, width = x0.shape
    tile = 128
    block = pl.BlockSpec((tile, width), lambda n, *_: (n, 0))
    return pl.pallas_call(
        first_norm_back_kernel,
        grid_spec=pltpu.PrefetchScalarGridSpec(
            num_scalar_prefetch=1,
            grid=(rows // tile,),
            in_specs=[block, block, block, block, whole(gain.shape)],
            out_specs=[
                block,
                whole((8, width)),
                whole((width // 2, rows)),
                whole((2, PART, rows)),
            ],
            scratch_shapes=[pltpu.VMEM((width, rows), BF16)],
        ),
        out_shape=[
            jax.ShapeDtypeStruct((rows, width), BF16),
            jax.ShapeDtypeStruct((8, width), F32),
            jax.ShapeDtypeStruct((width // 2, rows), BF16),
            jax.ShapeDtypeStruct((2, PART, rows), F32),
        ],
        compiler_params=params(14),
        cost_estimate=short_cost(),
        name="first_norm_back",
    )(place, gpart, grecv, x0, dx1, gain)


def pixel_grad_kernel(kinds, da_ref, db_ref, wspec_ref, wrgb_ref, pick_ref, out_ref):
    item = pl.program_id(0)
    spectral = kinds[item] == 1
    grad = jnp.where(item == 0, da_ref[...], db_ref[...])
    wide = wspec_ref.shape[0]
    cut = (wide // 2 + LANES - 1) // LANES * LANES

    @pl.when(spectral)
    def _():
        out_ref[:, :cut] = nt(grad, wspec_ref[:cut, :]).astype(BF16)
        out_ref[:, cut:] = nt(grad, wspec_ref[cut:, :]).astype(BF16)

    @pl.when(jnp.logical_not(spectral))
    def _():
        small = nt(grad, wrgb_ref[...]).astype(BF16)
        out_ref[...] = nt(small, pick_ref[...]).astype(BF16)


def pixel_grad(kinds, grad_a, grad_b, w_spectral, w_rgb, pick):
    rows = grad_a.shape[0]
    wide, width = w_spectral.shape
    return pl.pallas_call(
        pixel_grad_kernel,
        grid_spec=pltpu.PrefetchScalarGridSpec(
            num_scalar_prefetch=1,
            grid=(2,),
            in_specs=[
                whole(grad_a.shape),
                whole(grad_b.shape),
                whole(w_spectral.shape),
                whole(w_rgb.shape),
                whole(pick.shape),
            ],
            out_specs=pl.BlockSpec((rows, wide), lambda i, *_: (i, 0)),
        ),
        out_shape=jax.ShapeDtypeStruct((2 * rows, wide), BF16),
        compiler_params=params(20),
        cost_estimate=long_cost(),
        name="pixel_grad",
    )(kinds, grad_a, grad_b, w_spectral, w_rgb, pick)


def gather_left(keep_refs, gone_refs, first, left_ref):
    rows = keep_refs[0].shape[-1]
    for pos, keep_ref in enumerate(keep_refs):
        left_ref[:, pos * rows : (pos + 1) * rows] = keep_ref[...]
    base = len(keep_refs) * rows
    for pos, gone_ref in enumerate(gone_refs):
        columns = slice(base + pos * rows, base + (pos + 1) * rows)
        for part in range(2):
            left_ref[part * PART : (part + 1) * PART, columns] = gone_ref[first + part].astype(BF16)


def emit(left_ref, rights, send_ref, keep_ref, moves):
    right = jnp.concatenate([r.astype(BF16) for r in rights], 0)
    total = nn(left_ref[...], right)
    half = LANES // 2
    for pos, block in enumerate(moves):
        out_ref = send_ref if pos < 4 else keep_ref
        out_ref[pos % 4] = total[block * half : (block + 1) * half]


def plain_grad_kernel(
    ka_ref, kb_ref, la_ref, lb_ref, ra_ref, rb_ref, oa_ref, ob_ref, send_ref, keep_ref, left_ref,
    *, moves,
):
    @pl.when(pl.program_id(0) == 0)
    def _():
        gather_left((ka_ref, kb_ref), (la_ref, lb_ref), 0, left_ref)

    rights = (ra_ref[...], rb_ref[...], oa_ref[0], ob_ref[0])
    emit(left_ref, rights, send_ref, keep_ref, moves)


def plain_grad(keeps, lefts, rights, others, moves, name, skip=0, columns=None, lead=0):
    half_width, rows = keeps[0][0].shape[-2:]
    columns = columns or rights[0].shape[1]
    base = skip // PART
    half = LANES // 2

    def keep_spec(array, item):
        if array.ndim == 2:
            return whole(array.shape)
        return pl.BlockSpec((None,) + array.shape[1:], lambda n: (item, 0, 0))

    right = pl.BlockSpec((rows, PART), lambda n: (0, n + base))
    other = pl.BlockSpec((1, rows, PART), lambda n: (n + base + lead, 0, 0))
    out = pl.BlockSpec((4, half, PART), lambda n: (0, 0, n))
    shape = jax.ShapeDtypeStruct((4, half, columns), F32)
    return pl.pallas_call(
        functools.partial(plain_grad_kernel, moves=moves),
        grid=(columns // PART,),
        in_specs=[keep_spec(*k) for k in keeps]
        + [pl.BlockSpec((2, PART, rows), lambda n, q=i: (q, 0, 0)) for _, i in lefts]
        + [right, right, other, other],
        out_specs=[out, out],
        scratch_shapes=[pltpu.VMEM((half_width, 4 * rows), BF16)],
        out_shape=[shape, shape],
        compiler_params=params(16),
        cost_estimate=short_cost(),
        name=name,
    )(*[k for k, _ in keeps], *[v for v, _ in lefts], *rights, *others)


def attn_grad_kernel(
    aa_ref, ab_ref, ya_ref, yb_ref, fa_ref, fb_ref, ba_ref, bb_ref, da_ref, db_ref, ma_ref, mb_ref,
    send_ref, keep_ref, left_ref, *, moves,
):
    plane, step = pl.program_id(0), pl.program_id(1)
    steps = pl.num_programs(1)

    @pl.when((plane == 0) & (step == 0))
    def _():
        gather_left((aa_ref, ab_ref), (fa_ref, fb_ref), 0, left_ref)

    @pl.when((plane == 3) & (step == 0))
    def _():
        gather_left((ya_ref, yb_ref), (ba_ref, bb_ref), 0, left_ref)

    @pl.when(plane < 3)
    def _():
        spot = 2 + plane * steps + step
        emit(left_ref, (da_ref[...], db_ref[...], ba_ref[spot], bb_ref[spot]), send_ref, keep_ref, moves)

    @pl.when(plane == 3)
    def _():
        spot = 2 + step
        emit(left_ref, (ma_ref[...], mb_ref[...], fa_ref[spot], fb_ref[spot]), send_ref, keep_ref, moves)


def attn_grad(keep_a1, keep_dya, other_f, other_b, dqkv, mix, moves):
    half_width, rows = keep_a1[0].shape
    columns = mix[0].shape[1]
    half = LANES // 2
    side = whole((half_width, rows))
    plane = pl.BlockSpec((None, rows, PART), lambda p, n: (jnp.minimum(p, 2), 0, n))
    mixed = pl.BlockSpec((rows, PART), lambda p, n: (0, n))
    out = pl.BlockSpec((4, half, PART), lambda p, n: (0, p, n))
    shape = jax.ShapeDtypeStruct((4, 4 * half, columns), F32)
    return pl.pallas_call(
        functools.partial(attn_grad_kernel, moves=moves),
        grid=(4, columns // PART),
        in_specs=[side, side, side, side]
        + [whole(v.shape) for v in (*other_f, *other_b)]
        + [plane, plane, mixed, mixed],
        out_specs=[out, out],
        scratch_shapes=[pltpu.VMEM((half_width, 4 * rows), BF16)],
        out_shape=[shape, shape],
        compiler_params=params(24),
        cost_estimate=short_cost(),
        name="attn_grad",
    )(*keep_a1, *keep_dya, *other_f, *other_b, *dqkv, *mix)


def exchange(values, axis, bit, size):
    return lax.ppermute(values, axis, [(i, i ^ bit) for i in range(size)])


def swap(values):
    return exchange(values, "tensor", 1, 2)


def after(first, values):
    return lax.optimization_barrier((first, values))[1]


X_FIRST = (2, 4, 8)
Z_FIRST = (4, 2, 8)


def block_flips(bits):
    return [sum((1 - ((p >> (2 - n)) & 1)) * (bits[n] // 2) for n in range(3)) for p in range(8)]


def block_moves(bits):
    stands = block_flips(X_FIRST)
    return tuple(stands.index(f) for f in block_flips(bits))


def places():
    me = lax.axis_index("dp")
    flips = jnp.array(block_flips(X_FIRST), jnp.int32)
    return jnp.concatenate([(me // 2) ^ flips, (me % 2)[None]]).astype(jnp.int32)


class Halving:
    def __init__(self, send, keep, bits, size):
        self.keep, self.bits, self.size = keep, bits, size
        self.recvs = [exchange(send, "dp", bits[0], size)]
        self.left = keep.shape[0]
        self.sent = send

    def step(self, order):
        self.recvs[-1] = order.tie(self.recvs[-1])
        left = self.left
        count = max(left // 2, 1)
        total = self.keep.shape[0] - left
        value = self.keep[total : total + count]
        for recv in self.recvs:
            first = recv.shape[0] - left
            value = value + recv[first : first + count]
        order.mark(value)
        if left == 1:
            return value[0]
        self.recvs.append(exchange(value, "dp", self.bits[len(self.recvs)], self.size))
        self.left = left // 2
        return None


class Order:
    def __init__(self):
        self.last = None

    def tie(self, values):
        return values if self.last is None else after(self.last, values)

    def mark(self, values):
        self.last = values


def local(
    pixels, item_kinds, gsd_codes, w_spectral, w_rgb, ln1_gain, ln1_bias, w_qkv, q_bias, v_bias,
    w_out, out_bias, ln2_gain, ln2_bias, w_fc1, fc1_bias, w_fc2, fc2_bias, cotangent, *, size,
):
    items = item_kinds.shape[0]
    rows = pixels.shape[0] // items
    width = w_out.shape[1]
    wide = pixels.shape[1]
    narrow = w_rgb.shape[0]
    bands = wide // (narrow // 3)
    custom = size == 16

    def row(vector):
        return vector.reshape(1, -1)

    g1, c1, g2, c2 = row(ln1_gain), row(ln1_bias), row(ln2_gain), row(ln2_bias)
    qb, vb, ob, b1 = row(q_bias), row(v_bias), row(out_bias), row(fc1_bias)
    wqkv = jnp.transpose(w_qkv, (1, 0, 2))

    source = lax.broadcasted_iota(jnp.int32, (wide, narrow), 0)
    target = lax.broadcasted_iota(jnp.int32, (wide, narrow), 1)
    pick = (source == (target // 3) * bands + target % 3).astype(BF16)

    ratio = (gsd_codes.astype(F32) + 1.0) / 4.0
    quarter = width // 4
    frequency = 1.0 / 10000.0 ** (jnp.arange(quarter).astype(F32) / quarter)
    spot = jnp.arange(GRID).astype(F32)
    angle = ratio[:, None, None] * spot[None, :, None] * frequency[None, None, :]
    tables = jnp.concatenate([jnp.sin(angle), jnp.cos(angle)], -1)

    def scatter(values):
        return lax.psum_scatter(values, "dp", scatter_dimension=0, tiled=True)

    def both(left, right):
        return sum(tn(left[i], right[i]) for i in range(items))

    order = Order()
    gate = None

    def send(values, wait=True):
        nonlocal gate
        if gate is not None:
            values = after(gate, values)
        gate = swap(values)
        return gate

    place = places() if custom else jnp.arange(9, dtype=jnp.int32) % 8
    move_x, move_z = block_moves(X_FIRST), block_moves(Z_FIRST)

    def other(values):
        return exchange(values, "dp", 1, size) if custom else values

    def settle(values):
        values = order.tie(values)
        order.mark(jax.tree.leaves(values)[0])
        return values

    none = [None] * items
    part, mixed, erecv, fwd, orecv, ffn, grecv, bwd, arecv, last, ycot = (list(none) for _ in range(11))
    gmix, pk, gfwd, gact, gpre, gbwd, gdx0 = (list(none) for _ in range(7))

    for i in range(items):
        part[i], mixed[i] = embed(order.tie(item_kinds), pixels, w_spectral, w_rgb, pick, i, rows)
        order.mark(part[i])
        erecv[i] = send(part[i])
    keep_cot, gone_cot = turn_cot(order.tie(place), cotangent, rows)
    order.mark(gone_cot)
    gone_mix = []
    for i in range(items):
        gone_mix.append(pack(order.tie(mixed[i])))
        order.mark(gone_mix[i])
    gcot = other(gone_cot)
    gmix = [other(v) for v in gone_mix]
    for i in range(items):
        fwd[i] = attn_forward(
            part[i], erecv[i], tables[i], order.tie(g1), c1, wqkv, qb, vb, w_out
        )
        order.mark(fwd[i][4])
        orecv[i] = send(fwd[i][4])
        if i == 0:
            gcot = settle(gcot)
        else:
            gmix = [settle(v) for v in gmix]
        pk[i] = pack_attn(order.tie(place), fwd[i][1], fwd[i][3])
        order.mark(pk[i][1])
        gfwd[i] = other(pk[i][1])
    x0, a1, qkv, mix, _ = zip(*fwd)
    for i in range(items):
        ffn[i] = mlp(
            place, x0[i], fwd[i][4], orecv[i], order.tie(ob), g2, c2, w_fc1, b1, w_fc2, cotangent, i
        )
        order.mark(ffn[i][4])
        if i == 0:
            grecv[i] = send(ffn[i][4])
        gact[i] = other(ffn[i][7])
        gpre[i] = other(ffn[i][8])
        if i == 0:
            gfwd = [settle(v) for v in gfwd]
        else:
            gact[0], gpre[0] = settle((gact[0], gpre[0]))
            ycot[1] = mlp_out(order.tie(ffn[1][2]), w_fc2)
            order.mark(ycot[1])
    x1, a2, act, dpre, _, b1sum, ka2 = list(zip(*ffn))[:7]
    if custom:
        gact[1] = order.tie(gact[1])
        fc2_h = Halving(
            *plain_grad(
                [(keep_cot, 0), (keep_cot, 1)], [(gcot, 0), (gcot, 1)], act, gact, move_x, "fc2_grad"
            ),
            X_FIRST, size,
        )
        order.mark(fc2_h.sent)
        gpre[1] = order.tie(gpre[1])
        fc1_h = Halving(
            *plain_grad(
                [(ka2[0], 0), (ka2[1], 0)], [(gpre[0], 0), (gpre[1], 0)], dpre, gpre, move_z, "fc1_grad", lead=2
            ),
            Z_FIRST, size,
        )
        order.mark(fc1_h.sent)
    grecv[1] = send(order.tie(ffn[1][4]))
    for i in range(items):
        bwd[i] = attn_backward(
            place, ffn[i][4], grecv[i], x1[i], cotangent, order.tie(g2), w_out, qkv[i], wqkv, i
        )
        order.mark(bwd[i][3])
        if i == 0:
            arecv[i] = send(bwd[i][3])
        if i == items - 1:
            gbwd = [other(order.tie(bwd[0][7])), other(bwd[1][7])]
            ycot[0] = mlp_out(order.tie(ffn[0][2]), w_fc2)
            order.mark(ycot[0])
    dx1, dya, dqkv, _, sums2, qvsum, kdya = list(zip(*bwd))[:7]
    if custom:
        gbwd = [order.tie(v) for v in gbwd]
        att_h = Halving(
            *attn_grad([v[0] for v in pk], kdya, gfwd, gbwd, dqkv, mix, move_x), X_FIRST, size
        )
        order.mark(att_h.sent)
    arecv[1] = send(order.tie(bwd[1][3]))
    for i in range(items):
        last[i] = first_norm_back(place, bwd[i][3], arecv[i], x0[i], dx1[i], order.tie(g1))
        order.mark(last[i][0])
        gdx0[i] = other(last[i][3])
        if custom and i == 0:
            fc2_h.step(order)
            fc1_h.step(order)
    dx0, sums1, kdx0, _ = zip(*last)
    pixels_grad = pixel_grad(order.tie(item_kinds), dx0[0], dx0[1], w_spectral, w_rgb, pick)
    order.mark(pixels_grad)
    if custom:
        mid = mixed[0].shape[1] // 2
        gdx0 = [order.tie(v) for v in gdx0]
        sides = ([(kdx0[0], 0), (kdx0[1], 0)], [(gdx0[0], 0), (gdx0[1], 0)], mixed, gmix)
        embx_h = Halving(*plain_grad(*sides, move_x, "embed_grad_a", 0, mid), X_FIRST, size)
        order.mark(embx_h.sent)
        sides[3][1] = order.tie(gmix[1])
        embz_h = Halving(*plain_grad(*sides, move_z, "embed_grad_b", mid, mid), Z_FIRST, size)
        order.mark(embz_h.sent)
        fc2_h.step(order)

    got = [send(order.tie(ycot[i])) for i in range(items)]
    sums2, sums1, qvsum, b1sum = order.tie((sums2, sums1, qvsum, b1sum))
    vec2 = sums2[0] + sums2[1]
    vec1 = sums1[0] + sums1[1]
    qv = qvsum[0] + qvsum[1]
    b1s = b1sum[0] + b1sum[1]
    pieces = [vec2[0], vec2[1], vec2[2], vec2[3], vec1[0], vec1[1], qv[0], qv[1], b1s[0]]
    small = jnp.concatenate([v.reshape(size, -1) for v in pieces], 1)
    if custom:
        cube = small.reshape(2, 2, 2, 2, -1)
        chip, core = lax.axis_index("dp") // 2, lax.axis_index("dp") % 2
        for axis, bit in ((0, 4), (1, 2), (2, 1)):
            cube = jnp.where((chip & bit) == 0, jnp.flip(cube, axis), cube)
        cube = jnp.transpose(cube, (2, 1, 0, 3, 4)).reshape(8, 2, 1, -1)
        kept = jnp.where(core == 0, cube[:, 0], cube[:, 1])
        gone = jnp.where(core == 0, cube[:, 1], cube[:, 0])
        gone = exchange(gone, "dp", 1, size)
        fc2_g = fc2_h.step(order)
        gone = order.tie(gone)
        small_h = Halving(kept[:4] + gone[:4], kept[4:] + gone[4:], X_FIRST, size)
        embz_h.step(order)
        fc1_h.step(order)
        small_h.step(order)
        att_h.step(order)
        small_h.step(order)
        embz_h.step(order)
        fc1_g = fc1_h.step(order)
        small = small_h.step(order)[0]
        att_h.step(order)
        embx_h.step(order)
        embz_g = embz_h.step(order)
        embx_h.step(order)
        att_g = att_h.step(order)
        embx_g = embx_h.step(order)
        emb_g = jnp.concatenate([embx_g, embz_g], 1)
        att_g = att_g.reshape(4, width // size, -1)
        qkv_grad = jnp.transpose(att_g[:3], (1, 0, 2))
        out_grad = att_g[3].T
    else:
        cot = [cotangent[i * rows : (i + 1) * rows] for i in range(items)]
        fc2_g = scatter(both(cot, act))
        fc1_g = scatter(both(a2, dpre))
        emb_g = scatter(both(dx0, mixed))
        qkv_grad = scatter(
            sum(
                lax.dot_general(
                    a1[i], dqkv[i], (((0,), (1,)), ((), ())), preferred_element_type=F32
                )
                for i in range(items)
            )
        )
        out_grad = scatter(both(dya, mix)).T
        small = scatter(small)[0]
    block_out = jnp.concatenate(
        [(x1[i] + (ycot[i] + got[i] + fc2_bias)).astype(BF16) for i in range(items)], 0
    )
    outs = []
    start = 0
    for v in pieces:
        length = v.shape[0] // size
        outs.append(small[start : start + length])
        start += length
    ln2_g, ln2_b, ob_g, b2_g, ln1_g, ln1_b, q_g, v_g, b1_g = outs
    spectral_grad = emb_g[:, :wide].T
    rgb_grad = emb_g[:, wide:].T
    return (
        block_out, pixels_grad, spectral_grad, rgb_grad, ln1_g, ln1_b, qkv_grad, q_g, v_g, out_grad,
        ob_g, ln2_g, ln2_b, fc1_g, b1_g, fc2_g.T, b2_g,
    )


def solution(mesh):
    in_specs = (
        P("dp", "tensor"),
        P("dp"),
        P("dp"),
        P("tensor", None),
        P("tensor", None),
        P(),
        P(),
        P(None, None, "tensor"),
        P("tensor"),
        P("tensor"),
        P("tensor", None),
        P(),
        P(),
        P(),
        P(None, "tensor"),
        P("tensor"),
        P("tensor", None),
        P(),
        P("dp", None),
    )
    out_specs = (
        P("dp", None),
        P("dp", "tensor"),
        P("tensor", "dp"),
        P("tensor", "dp"),
        P("dp"),
        P("dp"),
        P("dp", None, "tensor"),
        P(("tensor", "dp")),
        P(("tensor", "dp")),
        P("tensor", "dp"),
        P("dp"),
        P("dp"),
        P("dp"),
        P("dp", "tensor"),
        P(("tensor", "dp")),
        P("tensor", "dp"),
        P("dp"),
    )
    body = functools.partial(local, size=mesh.shape["dp"])
    return jax.shard_map(body, mesh=mesh, in_specs=in_specs, out_specs=out_specs, check_vma=False)
```

```python
import functools

import jax
import jax.numpy as jnp
import ml_dtypes
import numpy as np
from jax import lax
from jax.experimental import pallas as pl
from jax.experimental.pallas import tpu as pltpu
from jax.sharding import PartitionSpec as P

HEAD_DIM = 64
GRID = 16
EPS = 1e-06
F32 = jnp.float32
BF16 = jnp.bfloat16
LANES = 128
MIB = 1024 * 1024
QUAD = 256
PART = 256
WIDE = 2


def nn(left, right):
    return lax.dot_general(left, right, (((1,), (0,)), ((), ())), preferred_element_type=F32)


def nt(left, right):
    return lax.dot_general(left, right, (((1,), (1,)), ((), ())), preferred_element_type=F32)


def tn(left, right):
    return lax.dot_general(left, right, (((0,), (0,)), ((), ())), preferred_element_type=F32)


def params(mib):
    return pltpu.CompilerParams(vmem_limit_bytes=mib * MIB)


def short_cost():
    return pl.CostEstimate(flops=1000, bytes_accessed=1000, transcendentals=0)


def long_cost():
    return pl.CostEstimate(flops=int(1e11), bytes_accessed=1000, transcendentals=0)


def whole(shape):
    return pl.BlockSpec(shape, lambda *_: (0,) * len(shape), pipeline_mode=pl.Buffered(1))


def norm_parts(values):
    center = values - jnp.mean(values, -1, keepdims=True)
    spread = jnp.mean(center * center, -1, keepdims=True)
    inverse = lax.rsqrt(spread + EPS)
    return center * inverse, inverse


def norm_back(normed, inverse, grad, gain):
    scaled = grad * gain
    mean_scaled = jnp.mean(scaled, -1, keepdims=True)
    mean_cross = jnp.mean(scaled * normed, -1, keepdims=True)
    return inverse * (scaled - mean_scaled - normed * mean_cross)


def column_sum(values):
    return jnp.sum(values, 0, keepdims=True)


def turn(place, source_ref, turned_ref, columns):
    chips = turned_ref.shape[0] // LANES
    half = LANES // 2
    core = place[chips]
    low = pl.multiple_of(core * (chips * half), half)
    high = pl.multiple_of((1 - core) * (chips * half), half)
    for chip in range(chips):
        lanes = pl.ds(pl.multiple_of(place[chip] * LANES, LANES), LANES)
        block = source_ref[:, lanes].T
        turned_ref[pl.ds(low + chip * half, half), columns] = block[:half]
        turned_ref[pl.ds(high + chip * half, half), columns] = block[half:]


def spread(turned_ref, keep_ref, gone_ref, first=0):
    middle = turned_ref.shape[0] // 2
    keep_ref[...] = turned_ref[:middle, :]
    for part in range(2):
        start = middle + part * PART
        gone_ref[first + part] = turned_ref[start : start + PART, :].astype(F32)


def turn_cot_kernel(place, cot_ref, keep_ref, gone_ref, turned_ref):
    turn(place, cot_ref, turned_ref, slice(None))
    spread(turned_ref, keep_ref, gone_ref)


def turn_cot(place, cotangent, rows):
    width = cotangent.shape[1]
    items = cotangent.shape[0] // rows
    return pl.pallas_call(
        turn_cot_kernel,
        grid_spec=pltpu.PrefetchScalarGridSpec(
            num_scalar_prefetch=1,
            grid=(items,),
            in_specs=[pl.BlockSpec((rows, width), lambda i, *_: (i, 0))],
            out_specs=[
                pl.BlockSpec((None, width // 2, rows), lambda i, *_: (i, 0, 0)),
                pl.BlockSpec((2, PART, rows), lambda i, *_: (i, 0, 0)),
            ],
            scratch_shapes=[pltpu.VMEM((width, rows), BF16)],
        ),
        out_shape=[
            jax.ShapeDtypeStruct((items, width // 2, rows), BF16),
            jax.ShapeDtypeStruct((2 * items, PART, rows), F32),
        ],
        compiler_params=params(4),
        cost_estimate=short_cost(),
        name="turn_cotangent",
    )(place, cotangent)


def pack_kernel(values_ref, out_ref):
    out_ref[0] = values_ref[...].astype(F32)


def pack(values):
    rows, columns = values.shape
    return pl.pallas_call(
        pack_kernel,
        grid=(columns // PART,),
        in_specs=[pl.BlockSpec((rows, PART), lambda n: (0, n))],
        out_specs=pl.BlockSpec((1, rows, PART), lambda n: (n, 0, 0)),
        out_shape=jax.ShapeDtypeStruct((columns // PART, rows, PART), F32),
        compiler_params=params(4),
        cost_estimate=short_cost(),
        name="pack_pixels",
    )(values)


def pack_attn_kernel(place, a1_ref, o_ref, keep_ref, gone_ref, turned_ref):
    turn(place, a1_ref, turned_ref, slice(None))
    spread(turned_ref, keep_ref, gone_ref)
    for part in range(o_ref.shape[1] // PART):
        gone_ref[2 + part] = o_ref[:, part * PART : (part + 1) * PART].astype(F32)


def pack_attn(place, a1, mix):
    rows, width = a1.shape
    parts = 2 + mix.shape[1] // PART
    return pl.pallas_call(
        pack_attn_kernel,
        grid_spec=pltpu.PrefetchScalarGridSpec(
            num_scalar_prefetch=1,
            grid=(1,),
            in_specs=[whole(a1.shape), whole(mix.shape)],
            out_specs=[whole((width // 2, rows)), whole((parts, PART, rows))],
            scratch_shapes=[pltpu.VMEM((width, rows), BF16)],
        ),
        out_shape=[
            jax.ShapeDtypeStruct((width // 2, rows), BF16),
            jax.ShapeDtypeStruct((parts, PART, rows), F32),
        ],
        compiler_params=params(4),
        cost_estimate=short_cost(),
        name="pack_attn",
    )(place, a1, mix)


def pieces_of(length):
    third = length // 3 // LANES * LANES
    return [(0, third), (third, third), (2 * third, length - 2 * third)]


def embed_kernel(
    kinds, pix_ref, wspec_ref, wrgb_ref, pick_ref, part_ref, mixed_ref,
    pix_buf, wspec_buf, wrgb_buf, pick_buf, pix_sem, big_sem, small_sem, *, item,
):
    rows, wide = pix_buf.shape
    spectral = kinds[item] == 1
    pieces = pieces_of(wide)
    own_rows = pl.ds(item * rows, rows)

    @pl.when(spectral)
    def _():
        copies = []
        for n, (first, size) in enumerate(pieces):
            span = pl.ds(first, size)
            copies.append(
                (
                    pltpu.make_async_copy(
                        pix_ref.at[own_rows, span], mixed_ref.at[:, span], pix_sem.at[n]
                    ),
                    pltpu.make_async_copy(wspec_ref.at[span], wspec_buf.at[span], big_sem.at[n]),
                )
            )
        for pair in copies:
            for copy in pair:
                copy.start()
        mixed_ref[:, wide:] = jnp.zeros((rows, wrgb_buf.shape[0]), BF16)
        for n, (first, size) in enumerate(pieces):
            for copy in copies[n]:
                copy.wait()
            term = nn(mixed_ref[:, first : first + size], wspec_buf[first : first + size, :])
            if n == 0:
                part_ref[...] = term
            else:
                part_ref[...] += term

    @pl.when(jnp.logical_not(spectral))
    def _():
        copies = []
        for n, (first, size) in enumerate(pieces):
            span = pl.ds(first, size)
            copies.append(
                (
                    pltpu.make_async_copy(
                        pix_ref.at[own_rows, span], pix_buf.at[:, span], pix_sem.at[n]
                    ),
                    pltpu.make_async_copy(pick_ref.at[span], pick_buf.at[span], big_sem.at[n]),
                )
            )
        for pair in copies:
            for copy in pair:
                copy.start()
        weights = pltpu.make_async_copy(wrgb_ref, wrgb_buf, small_sem)
        weights.start()
        mixed_ref[:, :wide] = jnp.zeros((rows, wide), BF16)
        total = None
        for n, (first, size) in enumerate(pieces):
            for copy in copies[n]:
                copy.wait()
            term = nn(pix_buf[:, first : first + size], pick_buf[first : first + size, :])
            total = term if total is None else total + term
        mixed_ref[:, wide:] = total.astype(BF16)
        weights.wait()
        part_ref[...] = nn(mixed_ref[:, wide:], wrgb_buf[...])


def embed(kinds, pixels, w_spectral, w_rgb, pick, item, rows):
    wide, width = w_spectral.shape
    narrow = w_rgb.shape[0]
    far = pl.BlockSpec(memory_space=pltpu.HBM)
    return pl.pallas_call(
        functools.partial(embed_kernel, item=item),
        grid_spec=pltpu.PrefetchScalarGridSpec(
            num_scalar_prefetch=1,
            grid=(1,),
            in_specs=[far, far, far, far],
            out_specs=[whole((rows, width)), whole((rows, wide + narrow))],
            scratch_shapes=[
                pltpu.VMEM((rows, wide), BF16),
                pltpu.VMEM((wide, width), BF16),
                pltpu.VMEM((narrow, width), BF16),
                pltpu.VMEM((wide, narrow), BF16),
                pltpu.SemaphoreType.DMA((3,)),
                pltpu.SemaphoreType.DMA((3,)),
                pltpu.SemaphoreType.DMA(()),
            ],
        ),
        out_shape=[
            jax.ShapeDtypeStruct((rows, width), F32),
            jax.ShapeDtypeStruct((rows, wide + narrow), BF16),
        ],
        compiler_params=params(58),
        cost_estimate=short_cost(),
        name="embed",
    )(kinds, pixels, w_spectral, w_rgb, pick)


def pair_masks(rows):
    lane = lax.broadcasted_iota(jnp.int32, (rows, LANES), 1)
    return lane < HEAD_DIM, lane >= HEAD_DIM


def only(mask, values):
    return jnp.where(mask, values, jnp.zeros_like(values))


def softmax_rows(query, key):
    scores = nt(query, key) * (HEAD_DIM**-0.5)
    expo = jnp.exp(scores - jnp.max(scores, -1, keepdims=True))
    return expo / jnp.sum(expo, -1, keepdims=True)


def attn_forward_kernel(
    part_ref, recv_ref, table_ref, gain_ref, bias_ref, wqkv_ref, qb_ref, vb_ref, wout_ref,
    x0_ref, a1_ref, qkv_ref, o_ref, opart_ref,
):
    quad = pl.program_id(0)
    rows, width = part_ref.shape

    @pl.when(quad == 0)
    def _():
        side = table_ref.shape[0]
        half = table_ref.shape[1]
        table = table_ref[...]
        by_row = jnp.broadcast_to(table[:, None, :], (side, side, half)).reshape(rows, half)
        by_col = jnp.broadcast_to(table[None, :, :], (side, side, half)).reshape(rows, half)
        left = part_ref[:, :half] + recv_ref[:, :half] + by_row
        right = part_ref[:, half:] + recv_ref[:, half:] + by_col
        x0_ref[:, :half] = left
        x0_ref[:, half:] = right
        normed, _inv = norm_parts(x0_ref[...])
        a1_ref[...] = (normed * gain_ref[...] + bias_ref[...]).astype(BF16)
        opart_ref[...] = jnp.zeros_like(opart_ref)

    a1 = a1_ref[...]
    query = (nn(a1, wqkv_ref[0]) + qb_ref[...]).astype(BF16)
    key = nn(a1, wqkv_ref[1]).astype(BF16)
    value = (nn(a1, wqkv_ref[2]) + vb_ref[...]).astype(BF16)
    qkv_ref[0] = query
    qkv_ref[1] = key
    qkv_ref[2] = value
    masks = pair_masks(rows)
    for pair in range(query.shape[1] // LANES):
        span = slice(pair * LANES, (pair + 1) * LANES)
        q2, k2, v2 = query[:, span], key[:, span], value[:, span]
        mixed = None
        for mask in masks:
            probs = softmax_rows(only(mask, q2), k2).astype(BF16)
            term = nn(probs, only(mask, v2))
            mixed = term if mixed is None else mixed + term
        o_ref[:, span] = mixed.astype(BF16)
    opart_ref[...] += nn(o_ref[...], wout_ref[...])


def attn_forward(part, recv, table, gain, bias, w_qkv, q_bias, v_bias, w_out):
    rows, width = part.shape
    heads_wide = w_out.shape[0]
    steps = heads_wide // QUAD
    return pl.pallas_call(
        attn_forward_kernel,
        grid=(steps,),
        in_specs=[
            whole(part.shape),
            whole(recv.shape),
            whole(table.shape),
            whole(gain.shape),
            whole(bias.shape),
            pl.BlockSpec((3, width, QUAD), lambda n: (0, 0, n)),
            pl.BlockSpec((1, QUAD), lambda n: (0, n)),
            pl.BlockSpec((1, QUAD), lambda n: (0, n)),
            pl.BlockSpec((QUAD, width), lambda n: (n, 0)),
        ],
        out_specs=[
            whole((rows, width)),
            whole((rows, width)),
            pl.BlockSpec((3, rows, QUAD), lambda n: (0, 0, n)),
            pl.BlockSpec((rows, QUAD), lambda n: (0, n)),
            whole((rows, width)),
        ],
        out_shape=[
            jax.ShapeDtypeStruct((rows, width), F32),
            jax.ShapeDtypeStruct((rows, width), BF16),
            jax.ShapeDtypeStruct((3, rows, heads_wide), BF16),
            jax.ShapeDtypeStruct((rows, heads_wide), BF16),
            jax.ShapeDtypeStruct((rows, width), F32),
        ],
        compiler_params=params(10),
        cost_estimate=long_cost(),
        name="attn_forward",
    )(part, recv, table, gain, bias, w_qkv, q_bias, v_bias, w_out)


def put_rows(refs, values, add):
    first = 0
    for ref in refs:
        rows = ref.shape[0]
        if add:
            ref[...] += values[first : first + rows]
        else:
            ref[...] = values[first : first + rows]
        first += rows


def joined(refs):
    values = [ref[...] for ref in refs]
    return values[0] if len(values) == 1 else jnp.concatenate(values, 0)


def attn_backward_kernel(place, *refs, parts):
    gpart_refs, refs = refs[: parts[0]], refs[parts[0] :]
    grecv_refs, refs = refs[: parts[1]], refs[parts[1] :]
    x1_ref, cot_ref, gain_ref, wout_ref, qkv_ref, wqkv_ref, *refs = refs
    dx1_ref, dya_ref, dqkv_ref, sums_ref, qvsum_ref, keep_ref, gone_ref, *da1_refs = refs[:-1]
    turned_ref = refs[-1]
    quad = pl.program_id(0)
    rows = x1_ref.shape[0]

    @pl.when(quad == 0)
    def _():
        normed, inverse = norm_parts(x1_ref[...])
        grad = joined(gpart_refs) + joined(grecv_refs)
        cot = cot_ref[...].astype(F32)
        dx1 = cot + norm_back(normed, inverse, grad, gain_ref[...])
        dx1_ref[...] = dx1
        dya = dx1.astype(BF16)
        dya_ref[...] = dya
        sums_ref[0:1, :] = column_sum(grad * normed)
        sums_ref[1:2, :] = column_sum(grad)
        sums_ref[2:3, :] = column_sum(dya.astype(F32))
        sums_ref[3:4, :] = column_sum(cot)
        sums_ref[4:8, :] = jnp.zeros((4, sums_ref.shape[1]), F32)
        turn(place, dya_ref, turned_ref, slice(None))
        spread(turned_ref, keep_ref, gone_ref)

    dmix = nt(dya_ref[...], wout_ref[...]).astype(BF16)
    scale = HEAD_DIM**-0.5
    masks = pair_masks(rows)
    for pair in range(dmix.shape[1] // LANES):
        span = slice(pair * LANES, (pair + 1) * LANES)
        q2, k2, v2, d2 = qkv_ref[0, :, span], qkv_ref[1, :, span], qkv_ref[2, :, span], dmix[:, span]
        totals = [None, None, None]
        for mask in masks:
            qm, km, dm = only(mask, q2), only(mask, k2), only(mask, d2)
            probs = softmax_rows(qm, k2)
            dprobs = nt(dm, v2)
            dot_row = jnp.sum(probs * dprobs, -1, keepdims=True)
            dscores = (probs * (dprobs - dot_row)).astype(BF16)
            terms = [nn(dscores, km), tn(dscores, qm), tn(probs.astype(BF16), dm)]
            totals = [t if o is None else o + t for o, t in zip(totals, terms)]
        dqkv_ref[0, :, span] = (totals[0] * scale).astype(BF16)
        dqkv_ref[1, :, span] = (totals[1] * scale).astype(BF16)
        dqkv_ref[2, :, span] = totals[2].astype(BF16)
    da1 = nt(dqkv_ref[0], wqkv_ref[0]) + nt(dqkv_ref[1], wqkv_ref[1]) + nt(dqkv_ref[2], wqkv_ref[2])

    @pl.when(quad == 0)
    def _():
        put_rows(da1_refs, da1, False)

    @pl.when(quad != 0)
    def _():
        put_rows(da1_refs, da1, True)

    steps = pl.num_programs(0)
    for plane in range(3):
        gone_ref[2 + plane * steps + quad] = dqkv_ref[plane].astype(F32)
    qvsum_ref[0:1, :] = column_sum(dqkv_ref[0].astype(F32))
    qvsum_ref[1:2, :] = column_sum(dqkv_ref[2].astype(F32))
    qvsum_ref[2:8, :] = jnp.zeros((6, qvsum_ref.shape[1]), F32)


def attn_backward(place, gparts, grecvs, x1, cotangent, gain, w_out, qkv, w_qkv, item, cuts):
    rows, width = x1.shape
    heads_wide = w_out.shape[0]
    steps = heads_wide // QUAD
    return pl.pallas_call(
        functools.partial(attn_backward_kernel, parts=(len(gparts), len(grecvs))),
        grid_spec=pltpu.PrefetchScalarGridSpec(
            num_scalar_prefetch=1,
            grid=(steps,),
            in_specs=[
                *[whole(v.shape) for v in (*gparts, *grecvs)],
                whole(x1.shape),
                pl.BlockSpec((rows, width), lambda n, *_: (item, 0)),
                whole(gain.shape),
                pl.BlockSpec((QUAD, width), lambda n, *_: (n, 0)),
                pl.BlockSpec((3, rows, QUAD), lambda n, *_: (0, 0, n)),
                pl.BlockSpec((3, width, QUAD), lambda n, *_: (0, 0, n)),
            ],
            out_specs=[
                whole((rows, width)),
                whole((rows, width)),
                pl.BlockSpec((3, rows, QUAD), lambda n, *_: (0, 0, n)),
                whole((8, width)),
                pl.BlockSpec((8, QUAD), lambda n, *_: (0, n)),
                whole((width // 2, rows)),
                whole((2 + 3 * steps, PART, rows)),
                *[whole((cut, width)) for cut in cuts],
            ],
            scratch_shapes=[pltpu.VMEM((width, rows), BF16)],
        ),
        out_shape=[
            jax.ShapeDtypeStruct((rows, width), F32),
            jax.ShapeDtypeStruct((rows, width), BF16),
            jax.ShapeDtypeStruct((3, rows, heads_wide), BF16),
            jax.ShapeDtypeStruct((8, width), F32),
            jax.ShapeDtypeStruct((8, heads_wide), F32),
            jax.ShapeDtypeStruct((width // 2, rows), BF16),
            jax.ShapeDtypeStruct((2 + 3 * steps, PART, rows), F32),
            *[jax.ShapeDtypeStruct((cut, width), F32) for cut in cuts],
        ],
        compiler_params=params(16),
        cost_estimate=long_cost(),
        name="attn_backward",
    )(place, *gparts, *grecvs, x1, cotangent, gain, w_out, qkv, w_qkv)


def mlp_kernel(
    place, x0_ref, opart_ref, orecv_ref, obias_ref, gain_ref, bias_ref, wfc1_ref, b1_ref, wfc2_ref, cot_ref,
    x1_ref, a2_ref, act_ref, dpre_ref, b1sum_ref, keep_ref, gact_ref, gpre_ref, *refs,
):
    da2_refs, turned_ref = refs[:-1], refs[-1]
    step = pl.program_id(0)

    @pl.when(step == 0)
    def _():
        x1_ref[...] = x0_ref[...] + (opart_ref[...] + orecv_ref[...] + obias_ref[...])
        normed, _inv = norm_parts(x1_ref[...])
        a2_ref[...] = (normed * gain_ref[...] + bias_ref[...]).astype(BF16)
        turn(place, a2_ref, turned_ref, slice(None))
        spread(turned_ref, keep_ref, gpre_ref)

    pre = nn(a2_ref[...], wfc1_ref[...]) + b1_ref[...]
    dact = nt(cot_ref[...], wfc2_ref[...])
    cdf = 0.5 * (1.0 + lax.erf(pre * (2.0**-0.5)))
    act = (pre * cdf).astype(BF16)
    act_ref[...] = act
    density = jnp.exp(-0.5 * pre * pre) * 0.3989422804014327
    dpre = (dact * (cdf + pre * density)).astype(BF16)
    dpre_ref[...] = dpre
    for part in range(act.shape[1] // PART):
        columns = slice(part * PART, (part + 1) * PART)
        gact_ref[part] = act[:, columns].astype(F32)
        gpre_ref[2 + step * (act.shape[1] // PART) + part] = dpre[:, columns].astype(F32)
    b1sum_ref[...] = column_sum(dpre.astype(F32))
    da2 = nt(dpre, wfc1_ref[...])

    @pl.when(step == 0)
    def _():
        put_rows(da2_refs, da2, False)

    @pl.when(step != 0)
    def _():
        put_rows(da2_refs, da2, True)


def mlp(
    place, x0, opart, orecv, out_bias, gain, bias, w_fc1, fc1_bias, w_fc2, cotangent, item, cuts
):
    rows, width = x0.shape
    hidden = w_fc1.shape[1]
    tile = 512
    parts = tile // PART
    row_tile = pl.BlockSpec((rows, tile), lambda n, *_: (0, n))
    gone = pl.BlockSpec((parts, rows, PART), lambda n, *_: (n, 0, 0))
    return pl.pallas_call(
        mlp_kernel,
        grid_spec=pltpu.PrefetchScalarGridSpec(
            num_scalar_prefetch=1,
            grid=(hidden // tile,),
            in_specs=[
                whole(x0.shape),
                whole(opart.shape),
                whole(orecv.shape),
                whole(out_bias.shape),
                whole(gain.shape),
                whole(bias.shape),
                pl.BlockSpec((width, tile), lambda n, *_: (0, n)),
                pl.BlockSpec((1, tile), lambda n, *_: (0, n)),
                pl.BlockSpec((tile, width), lambda n, *_: (n, 0)),
                pl.BlockSpec((rows, width), lambda n, *_: (item, 0)),
            ],
            out_specs=[
                whole((rows, width)),
                whole((rows, width)),
                row_tile,
                row_tile,
                pl.BlockSpec((1, tile), lambda n, *_: (0, n)),
                whole((width // 2, rows)),
                gone,
                whole((2 + hidden // PART, rows, PART)),
                *[whole((cut, width)) for cut in cuts],
            ],
            scratch_shapes=[pltpu.VMEM((width, rows), BF16)],
        ),
        out_shape=[
            jax.ShapeDtypeStruct((rows, width), F32),
            jax.ShapeDtypeStruct((rows, width), BF16),
            jax.ShapeDtypeStruct((rows, hidden), BF16),
            jax.ShapeDtypeStruct((rows, hidden), BF16),
            jax.ShapeDtypeStruct((1, hidden), F32),
            jax.ShapeDtypeStruct((width // 2, rows), BF16),
            jax.ShapeDtypeStruct((hidden // PART, rows, PART), F32),
            jax.ShapeDtypeStruct((2 + hidden // PART, rows, PART), F32),
            *[jax.ShapeDtypeStruct((cut, width), F32) for cut in cuts],
        ],
        compiler_params=params(14),
        cost_estimate=long_cost(),
        name="mlp",
    )(place, x0, opart, orecv, out_bias, gain, bias, w_fc1, fc1_bias, w_fc2, cotangent)


def mlp_out_kernel(act_ref, wfc2_ref, out_ref):
    out_ref[...] = nn(act_ref[...], wfc2_ref[...])


def mlp_out(act, w_fc2):
    rows, hidden = act.shape
    width = w_fc2.shape[1]
    tile = 512
    return pl.pallas_call(
        mlp_out_kernel,
        grid=(width // tile,),
        in_specs=[whole(act.shape), pl.BlockSpec((hidden, tile), lambda n: (0, n))],
        out_specs=pl.BlockSpec((rows, tile), lambda n: (0, n)),
        out_shape=jax.ShapeDtypeStruct((rows, width), F32),
        compiler_params=params(6),
        cost_estimate=long_cost(),
        name="mlp_out",
    )(act, w_fc2)


def first_norm_back_kernel(place, *refs, parts):
    gpart_refs, refs = refs[: parts[0]], refs[parts[0] :]
    grecv_refs, refs = refs[: parts[1]], refs[parts[1] :]
    x0_ref, dx1_ref, gain_ref, dx0_ref, sums_ref, keep_ref, gone_ref, turned_ref = refs
    normed, inverse = norm_parts(x0_ref[...])
    grad = joined(gpart_refs) + joined(grecv_refs)
    dx0_ref[...] = (dx1_ref[...] + norm_back(normed, inverse, grad, gain_ref[...])).astype(BF16)
    sums_ref[0:1, :] = column_sum(grad * normed)
    sums_ref[1:2, :] = column_sum(grad)
    sums_ref[2:8, :] = jnp.zeros((6, sums_ref.shape[1]), F32)
    turn(place, dx0_ref, turned_ref, slice(None))
    spread(turned_ref, keep_ref, gone_ref)


def first_norm_back(place, gparts, grecvs, x0, dx1, gain, estimate):
    rows, width = x0.shape
    operands = (*gparts, *grecvs, x0, dx1, gain)
    shapes = [
        jax.ShapeDtypeStruct((rows, width), BF16),
        jax.ShapeDtypeStruct((8, width), F32),
        jax.ShapeDtypeStruct((width // 2, rows), BF16),
        jax.ShapeDtypeStruct((2, PART, rows), F32),
    ]
    return pl.pallas_call(
        functools.partial(first_norm_back_kernel, parts=(len(gparts), len(grecvs))),
        grid_spec=pltpu.PrefetchScalarGridSpec(
            num_scalar_prefetch=1,
            grid=(1,),
            in_specs=[whole(v.shape) for v in operands],
            out_specs=[whole(v.shape) for v in shapes],
            scratch_shapes=[pltpu.VMEM((width, rows), BF16)],
        ),
        out_shape=shapes,
        compiler_params=params(10),
        cost_estimate=estimate,
        name="first_norm_back",
    )(place, *operands)


def pixel_grad_kernel(kinds, da_ref, db_ref, wspec_ref, wrgb_ref, pick_ref, out_ref):
    item = pl.program_id(0)
    spectral = kinds[item] == 1
    grad = jnp.where(item == 0, da_ref[...], db_ref[...])
    wide = wspec_ref.shape[0]
    cut = (wide // 2 + LANES - 1) // LANES * LANES

    @pl.when(spectral)
    def _():
        out_ref[:, :cut] = nt(grad, wspec_ref[:cut, :]).astype(BF16)
        out_ref[:, cut:] = nt(grad, wspec_ref[cut:, :]).astype(BF16)

    @pl.when(jnp.logical_not(spectral))
    def _():
        small = nt(grad, wrgb_ref[...]).astype(BF16)
        out_ref[...] = nt(small, pick_ref[...]).astype(BF16)


def pixel_grad(kinds, grad_a, grad_b, w_spectral, w_rgb, pick):
    rows = grad_a.shape[0]
    wide, width = w_spectral.shape
    return pl.pallas_call(
        pixel_grad_kernel,
        grid_spec=pltpu.PrefetchScalarGridSpec(
            num_scalar_prefetch=1,
            grid=(2,),
            in_specs=[
                whole(grad_a.shape),
                whole(grad_b.shape),
                whole(w_spectral.shape),
                whole(w_rgb.shape),
                whole(pick.shape),
            ],
            out_specs=pl.BlockSpec((rows, wide), lambda i, *_: (i, 0)),
        ),
        out_shape=jax.ShapeDtypeStruct((2 * rows, wide), BF16),
        compiler_params=params(8),
        cost_estimate=long_cost(),
        name="pixel_grad",
    )(kinds, grad_a, grad_b, w_spectral, w_rgb, pick)


def gather_left(keep_refs, gone_refs, first, left_ref):
    rows = keep_refs[0].shape[-1]
    for pos, keep_ref in enumerate(keep_refs):
        left_ref[:, pos * rows : (pos + 1) * rows] = keep_ref[...]
    base = len(keep_refs) * rows
    for pos, gone_ref in enumerate(gone_refs):
        columns = slice(base + pos * rows, base + (pos + 1) * rows)
        for part in range(2):
            left_ref[part * PART : (part + 1) * PART, columns] = gone_ref[first + part].astype(BF16)


def emit(left_ref, rights, send_ref, keep_ref, moves, columns=slice(None)):
    right = jnp.concatenate([r.astype(BF16) for r in rights], 0)
    total = nn(left_ref[...], right)
    half = LANES // 2
    for pos, block in enumerate(moves):
        out_ref = send_ref if pos < 4 else keep_ref
        out_ref[pos % 4, :, columns] = total[block * half : (block + 1) * half]


def plain_grad_kernel(
    ka_ref, kb_ref, la_ref, lb_ref, ra_ref, rb_ref, oa_ref, ob_ref, send_ref, keep_ref, left_ref,
    *, moves,
):
    @pl.when(pl.program_id(0) == 0)
    def _():
        gather_left((ka_ref, kb_ref), (la_ref, lb_ref), 0, left_ref)

    for part in range(oa_ref.shape[0]):
        columns = slice(part * PART, (part + 1) * PART)
        rights = (ra_ref[:, columns], rb_ref[:, columns], oa_ref[part], ob_ref[part])
        emit(left_ref, rights, send_ref, keep_ref, moves, columns)


def plain_grad(keeps, lefts, rights, others, moves, name, skip=0, columns=None, lead=0):
    half_width, rows = keeps[0][0].shape[-2:]
    columns = columns or rights[0].shape[1]
    wide = WIDE
    base = skip // (wide * PART)
    half = LANES // 2

    def keep_spec(array, item):
        if array.ndim == 2:
            return whole(array.shape)
        return pl.BlockSpec((None,) + array.shape[1:], lambda n: (item, 0, 0))

    right = pl.BlockSpec((rows, wide * PART), lambda n: (0, n + base))
    other = pl.BlockSpec((wide, rows, PART), lambda n: (n + base + lead // wide, 0, 0))
    out = pl.BlockSpec((4, half, wide * PART), lambda n: (0, 0, n))
    shape = jax.ShapeDtypeStruct((4, half, columns), F32)
    return pl.pallas_call(
        functools.partial(plain_grad_kernel, moves=moves),
        grid=(columns // (wide * PART),),
        in_specs=[keep_spec(*k) for k in keeps]
        + [pl.BlockSpec((2, PART, rows), lambda n, q=i: (q, 0, 0)) for _, i in lefts]
        + [right, right, other, other],
        out_specs=[out, out],
        scratch_shapes=[pltpu.VMEM((half_width, 4 * rows), BF16)],
        out_shape=[shape, shape],
        compiler_params=params(14),
        cost_estimate=short_cost(),
        name=name,
    )(*[k for k, _ in keeps], *[v for v, _ in lefts], *rights, *others)


def attn_grad_kernel(
    aa_ref, ab_ref, ya_ref, yb_ref, fa_ref, fb_ref, ba_ref, bb_ref, da_ref, db_ref, ma_ref, mb_ref,
    send_ref, keep_ref, left_ref, *, moves,
):
    plane, step = pl.program_id(0), pl.program_id(1)
    steps = pl.num_programs(1)

    @pl.when((plane == 0) & (step == 0))
    def _():
        gather_left((aa_ref, ab_ref), (fa_ref, fb_ref), 0, left_ref)

    @pl.when((plane == 3) & (step == 0))
    def _():
        gather_left((ya_ref, yb_ref), (ba_ref, bb_ref), 0, left_ref)

    @pl.when(plane < 3)
    def _():
        spot = 2 + plane * steps + step
        emit(left_ref, (da_ref[...], db_ref[...], ba_ref[spot], bb_ref[spot]), send_ref, keep_ref, moves)

    @pl.when(plane == 3)
    def _():
        spot = 2 + step
        emit(left_ref, (ma_ref[...], mb_ref[...], fa_ref[spot], fb_ref[spot]), send_ref, keep_ref, moves)


def attn_grad(keep_a1, keep_dya, other_f, other_b, dqkv, mix, moves):
    half_width, rows = keep_a1[0].shape
    columns = mix[0].shape[1]
    half = LANES // 2
    side = whole((half_width, rows))
    plane = pl.BlockSpec((None, rows, PART), lambda p, n: (jnp.minimum(p, 2), 0, n))
    mixed = pl.BlockSpec((rows, PART), lambda p, n: (0, n))
    out = pl.BlockSpec((4, half, PART), lambda p, n: (0, p, n))
    shape = jax.ShapeDtypeStruct((4, 4 * half, columns), F32)
    return pl.pallas_call(
        functools.partial(attn_grad_kernel, moves=moves),
        grid=(4, columns // PART),
        in_specs=[side, side, side, side]
        + [whole(v.shape) for v in (*other_f, *other_b)]
        + [plane, plane, mixed, mixed],
        out_specs=[out, out],
        scratch_shapes=[pltpu.VMEM((half_width, 4 * rows), BF16)],
        out_shape=[shape, shape],
        compiler_params=params(8),
        cost_estimate=short_cost(),
        name="attn_grad",
    )(*keep_a1, *keep_dya, *other_f, *other_b, *dqkv, *mix)


def exchange(values, axis, bit, size):
    return lax.ppermute(values, axis, [(i, i ^ bit) for i in range(size)])


def swap(values):
    return exchange(values, "tensor", 1, 2)


def after(first, values):
    return lax.optimization_barrier((first, values))[1]


X_FIRST = (2, 4, 8)
Z_FIRST = (4, 2, 8)


def block_flips(bits):
    return [sum((1 - ((p >> (2 - n)) & 1)) * (bits[n] // 2) for n in range(3)) for p in range(8)]


def block_moves(bits):
    stands = block_flips(X_FIRST)
    return tuple(stands.index(f) for f in block_flips(bits))


def places():
    me = lax.axis_index("dp")
    flips = jnp.array(block_flips(X_FIRST), jnp.int32)
    return jnp.concatenate([(me // 2) ^ flips, (me % 2)[None]]).astype(jnp.int32)


class Halving:
    def __init__(self, send, keep, bits, size):
        self.keep, self.bits, self.size = keep, bits, size
        self.recvs = [exchange(send, "dp", bits[0], size)]
        self.left = keep.shape[0]
        self.sent = send

    def step(self, order):
        self.recvs[-1] = order.tie(self.recvs[-1])
        left = self.left
        count = max(left // 2, 1)
        total = self.keep.shape[0] - left
        value = self.keep[total : total + count]
        for recv in self.recvs:
            first = recv.shape[0] - left
            value = value + recv[first : first + count]
        order.mark(value)
        if left == 1:
            return value[0]
        self.recvs.append(exchange(value, "dp", self.bits[len(self.recvs)], self.size))
        self.left = left // 2
        return None


class Order:
    def __init__(self):
        self.last = None

    def tie(self, values):
        return values if self.last is None else after(self.last, values)

    def mark(self, values):
        self.last = values


def local(
    pixels, item_kinds, gsd_codes, w_spectral, w_rgb, ln1_gain, ln1_bias, w_qkv, q_bias, v_bias,
    w_out, out_bias, ln2_gain, ln2_bias, w_fc1, fc1_bias, w_fc2, fc2_bias, cotangent, *, size,
):
    items = item_kinds.shape[0]
    rows = pixels.shape[0] // items
    width = w_out.shape[1]
    wide = pixels.shape[1]
    narrow = w_rgb.shape[0]
    bands = wide // (narrow // 3)
    custom = size == 16

    def row(vector):
        return vector.reshape(1, -1)

    g1, c1, g2, c2 = row(ln1_gain), row(ln1_bias), row(ln2_gain), row(ln2_bias)
    qb, vb, ob, b1 = row(q_bias), row(v_bias), row(out_bias), row(fc1_bias)
    wqkv = jnp.transpose(w_qkv, (1, 0, 2))

    source = np.arange(wide)[:, None]
    target = np.arange(narrow)[None, :]
    pick = jnp.asarray((source == (target // 3) * bands + target % 3).astype(ml_dtypes.bfloat16))

    ratio = (gsd_codes.astype(F32) + 1.0) / 4.0
    quarter = width // 4
    frequency = 1.0 / 10000.0 ** (jnp.arange(quarter).astype(F32) / quarter)
    spot = jnp.arange(GRID).astype(F32)
    angle = ratio[:, None, None] * spot[None, :, None] * frequency[None, None, :]
    tables = jnp.concatenate([jnp.sin(angle), jnp.cos(angle)], -1)

    def scatter(values):
        return lax.psum_scatter(values, "dp", scatter_dimension=0, tiled=True)

    def both(left, right):
        return sum(tn(left[i], right[i]) for i in range(items))

    order = Order()
    gate = None

    def send(values, wait=True):
        nonlocal gate
        if gate is not None:
            values = after(gate, values)
        gate = swap(values)
        return gate

    place = places() if custom else jnp.arange(9, dtype=jnp.int32) % 8
    move_x, move_z = block_moves(X_FIRST), block_moves(Z_FIRST)

    def other(values):
        return exchange(values, "dp", 1, size) if custom else values

    cut = rows * 3 // 8 // 8 * 8
    cuts = [(cut, rows - cut)] + [(rows,)] * (items - 1)

    def settle(values):
        values = order.tie(values)
        order.mark(jax.tree.leaves(values)[0])
        return values

    none = [None] * items
    part, mixed, erecv, fwd, orecv, ffn, grecv, bwd, arecv, last, ycot = (list(none) for _ in range(11))
    gmix, pk, gfwd, gact, gpre, gbwd, gdx0, da1, da2 = (list(none) for _ in range(9))

    for i in range(items):
        part[i], mixed[i] = embed(order.tie(item_kinds), pixels, w_spectral, w_rgb, pick, i, rows)
        order.mark(part[i])
        erecv[i] = send(part[i])
    keep_cot, gone_cot = turn_cot(order.tie(place), cotangent, rows)
    order.mark(gone_cot)
    gone_mix = []
    for i in range(items):
        gone_mix.append(pack(order.tie(mixed[i])))
        order.mark(gone_mix[i])
    gcot = other(gone_cot)
    gmix = [other(v) for v in gone_mix]
    for i in range(items):
        fwd[i] = attn_forward(
            part[i], erecv[i], tables[i], order.tie(g1), c1, wqkv, qb, vb, w_out
        )
        order.mark(fwd[i][4])
        orecv[i] = send(fwd[i][4])
        if i == 0:
            gcot = settle(gcot)
        else:
            gmix = [settle(v) for v in gmix]
        pk[i] = pack_attn(order.tie(place), fwd[i][1], fwd[i][3])
        order.mark(pk[i][1])
        gfwd[i] = other(pk[i][1])
    x0, a1, qkv, mix, _ = zip(*fwd)
    for i in range(items):
        ffn[i] = mlp(
            place, x0[i], fwd[i][4], orecv[i], order.tie(ob), g2, c2, w_fc1, b1, w_fc2, cotangent, i,
            cuts[i],
        )
        da2[i] = ffn[i][8:]
        order.mark(da2[i][0])
        if i == 0:
            grecv[i] = [send(v) for v in da2[i]]
        gact[i] = other(ffn[i][6])
        gpre[i] = other(ffn[i][7])
        if i == 0:
            gfwd = [settle(v) for v in gfwd]
        else:
            grecv[0][0] = settle(grecv[0][0])
            gact[0], gpre[0] = settle((gact[0], gpre[0]))
            ycot[1] = mlp_out(order.tie(ffn[1][2]), w_fc2)
            order.mark(ycot[1])
    x1, a2, act, dpre, b1sum, ka2 = list(zip(*[v[:6] for v in ffn]))
    if custom:
        gact[1] = order.tie(gact[1])
        fc2_h = Halving(
            *plain_grad(
                [(keep_cot, 0), (keep_cot, 1)], [(gcot, 0), (gcot, 1)], act, gact, move_x, "fc2_grad"
            ),
            X_FIRST, size,
        )
        order.mark(fc2_h.sent)
        gpre[1] = order.tie(gpre[1])
        fc1_h = Halving(
            *plain_grad(
                [(ka2[0], 0), (ka2[1], 0)], [(gpre[0], 0), (gpre[1], 0)], dpre, gpre, move_z, "fc1_grad", lead=2
            ),
            Z_FIRST, size,
        )
        order.mark(fc1_h.sent)
    grecv[1] = [send(order.tie(da2[1][0]))]
    for i in range(items):
        bwd[i] = attn_backward(
            place, da2[i], grecv[i], x1[i], cotangent, order.tie(g2), w_out, qkv[i], wqkv, i, cuts[i]
        )
        da1[i] = bwd[i][7:]
        order.mark(da1[i][0])
        if i == 0:
            arecv[i] = [send(v) for v in da1[i]]
        else:
            arecv[0][0] = settle(arecv[0][0])
            gbwd = [other(order.tie(bwd[0][6])), other(bwd[1][6])]
            ycot[0] = mlp_out(order.tie(ffn[0][2]), w_fc2)
            order.mark(ycot[0])
    dx1, dya, dqkv, sums2, qvsum, kdya = list(zip(*[v[:6] for v in bwd]))
    if custom:
        fc2_h.step(order)
        gbwd = [order.tie(v) for v in gbwd]
        att_h = Halving(
            *attn_grad([v[0] for v in pk], kdya, gfwd, gbwd, dqkv, mix, move_x), X_FIRST, size
        )
        order.mark(att_h.sent)
        fc1_h.step(order)
    arecv[1] = [send(order.tie(da1[1][0]))]
    for i in range(items):
        estimate = long_cost() if i == 0 else short_cost()
        last[i] = first_norm_back(place, da1[i], arecv[i], x0[i], dx1[i], order.tie(g1), estimate)
        order.mark(last[i][0])
    summed = list(none)
    gdx0 = [other(order.tie(last[0][3])), other(last[1][3])]
    dx0, sums1, kdx0, _ = zip(*last)
    pixels_grad = pixel_grad(order.tie(item_kinds), dx0[0], dx0[1], w_spectral, w_rgb, pick)
    order.mark(pixels_grad)
    if custom:
        mid = mixed[0].shape[1] // 2
        gdx0 = [order.tie(v) for v in gdx0]
        sides = ([(kdx0[0], 0), (kdx0[1], 0)], [(gdx0[0], 0), (gdx0[1], 0)], mixed, gmix)
        embx_h = Halving(*plain_grad(*sides, move_x, "embed_grad_a", 0, mid), X_FIRST, size)
        order.mark(embx_h.sent)
        sides[3][1] = order.tie(gmix[1])
        embz_h = Halving(*plain_grad(*sides, move_z, "embed_grad_b", mid, mid), Z_FIRST, size)
        order.mark(embz_h.sent)
        fc2_h.step(order)
    summed[0] = send(order.tie(ycot[0]))
    if custom:
        fc1_h.step(order)

    sums2, sums1, qvsum, b1sum = order.tie((sums2, sums1, qvsum, b1sum))
    vec2 = sums2[0] + sums2[1]
    vec1 = sums1[0] + sums1[1]
    qv = qvsum[0] + qvsum[1]
    b1s = b1sum[0] + b1sum[1]
    pieces = [vec2[0], vec2[1], vec2[2], vec2[3], vec1[0], vec1[1], qv[0], qv[1], b1s[0]]
    small = jnp.concatenate([v.reshape(size, -1) for v in pieces], 1)
    if custom:
        cube = small.reshape(2, 2, 2, 2, -1)
        chip, core = lax.axis_index("dp") // 2, lax.axis_index("dp") % 2
        for axis, bit in ((0, 4), (1, 2), (2, 1)):
            cube = jnp.where((chip & bit) == 0, jnp.flip(cube, axis), cube)
        cube = jnp.transpose(cube, (2, 1, 0, 3, 4)).reshape(8, 2, 1, -1)
        kept = jnp.where(core == 0, cube[:, 0], cube[:, 1])
        gone = jnp.where(core == 0, cube[:, 1], cube[:, 0])
        order.mark(gone)
        fc2_g = fc2_h.step(order)
        embz_h.step(order)
    summed[0] = settle(summed[0])
    summed[1] = send(order.tie(ycot[1]))
    if custom:
        gone = exchange(order.tie(gone), "dp", 1, size)
        fc1_g = fc1_h.step(order)
        gone = order.tie(gone)
        small_h = Halving(kept[:4] + gone[:4], kept[4:] + gone[4:], X_FIRST, size)
        order.mark(small_h.sent)
        att_h.step(order)
        small_h.step(order)
        embx_h.step(order)
        summed[1] = settle(summed[1])
        small_h.step(order)
        embz_h.step(order)
        small = small_h.step(order)[0]
        att_h.step(order)
        embx_h.step(order)
        embz_g = embz_h.step(order)
        att_g = att_h.step(order)
        embx_g = embx_h.step(order)
        emb_g = jnp.concatenate([embx_g, embz_g], 1)
        att_g = att_g.reshape(4, width // size, -1)
        qkv_grad = jnp.transpose(att_g[:3], (1, 0, 2))
        out_grad = att_g[3].T
    else:
        cot = [cotangent[i * rows : (i + 1) * rows] for i in range(items)]
        fc2_g = scatter(both(cot, act))
        fc1_g = scatter(both(a2, dpre))
        emb_g = scatter(both(dx0, mixed))
        qkv_grad = scatter(
            sum(
                lax.dot_general(
                    a1[i], dqkv[i], (((0,), (1,)), ((), ())), preferred_element_type=F32
                )
                for i in range(items)
            )
        )
        out_grad = scatter(both(dya, mix)).T
        small = scatter(small)[0]
    block_out = jnp.concatenate(
        [(x1[i] + (ycot[i] + summed[i] + fc2_bias)).astype(BF16) for i in range(items)], 0
    )
    outs = []
    start = 0
    for v in pieces:
        length = v.shape[0] // size
        outs.append(small[start : start + length])
        start += length
    ln2_g, ln2_b, ob_g, b2_g, ln1_g, ln1_b, q_g, v_g, b1_g = outs
    spectral_grad = emb_g[:, :wide].T
    rgb_grad = emb_g[:, wide:].T
    return (
        block_out, pixels_grad, spectral_grad, rgb_grad, ln1_g, ln1_b, qkv_grad, q_g, v_g, out_grad,
        ob_g, ln2_g, ln2_b, fc1_g, b1_g, fc2_g.T, b2_g,
    )


def solution(mesh):
    in_specs = (
        P("dp", "tensor"),
        P("dp"),
        P("dp"),
        P("tensor", None),
        P("tensor", None),
        P(),
        P(),
        P(None, None, "tensor"),
        P("tensor"),
        P("tensor"),
        P("tensor", None),
        P(),
        P(),
        P(),
        P(None, "tensor"),
        P("tensor"),
        P("tensor", None),
        P(),
        P("dp", None),
    )
    out_specs = (
        P("dp", None),
        P("dp", "tensor"),
        P("tensor", "dp"),
        P("tensor", "dp"),
        P("dp"),
        P("dp"),
        P("dp", None, "tensor"),
        P(("tensor", "dp")),
        P(("tensor", "dp")),
        P("tensor", "dp"),
        P("dp"),
        P("dp"),
        P("dp"),
        P("dp", "tensor"),
        P(("tensor", "dp")),
        P("tensor", "dp"),
        P("dp"),
    )
    body = functools.partial(local, size=mesh.shape["dp"])
    return jax.shard_map(body, mesh=mesh, in_specs=in_specs, out_specs=out_specs, check_vma=False)
```

```python
import functools

import jax
import jax.numpy as jnp
import ml_dtypes
import numpy as np
from jax import lax
from jax.experimental import pallas as pl
from jax.experimental.pallas import tpu as pltpu
from jax.sharding import PartitionSpec as P

HEAD_DIM = 64
GRID = 16
EPS = 1e-06
F32 = jnp.float32
BF16 = jnp.bfloat16
LANES = 128
MIB = 1024 * 1024
QUAD = 256
PART = 256
WIDE = 2


def nn(left, right):
    return lax.dot_general(left, right, (((1,), (0,)), ((), ())), preferred_element_type=F32)


def nt(left, right):
    return lax.dot_general(left, right, (((1,), (1,)), ((), ())), preferred_element_type=F32)


def tn(left, right):
    return lax.dot_general(left, right, (((0,), (0,)), ((), ())), preferred_element_type=F32)


def params(mib):
    return pltpu.CompilerParams(vmem_limit_bytes=mib * MIB)


def short_cost():
    return pl.CostEstimate(flops=1000, bytes_accessed=1000, transcendentals=0)


def long_cost():
    return pl.CostEstimate(flops=int(1e11), bytes_accessed=1000, transcendentals=0)


def whole(shape):
    return pl.BlockSpec(shape, lambda *_: (0,) * len(shape), pipeline_mode=pl.Buffered(1))


def norm_parts(values):
    center = values - jnp.mean(values, -1, keepdims=True)
    spread = jnp.mean(center * center, -1, keepdims=True)
    inverse = lax.rsqrt(spread + EPS)
    return center * inverse, inverse


def norm_back(normed, inverse, grad, gain):
    scaled = grad * gain
    mean_scaled = jnp.mean(scaled, -1, keepdims=True)
    mean_cross = jnp.mean(scaled * normed, -1, keepdims=True)
    return inverse * (scaled - mean_scaled - normed * mean_cross)


def column_sum(values):
    return jnp.sum(values, 0, keepdims=True)


def turn(place, source_ref, turned_ref, columns):
    chips = turned_ref.shape[0] // LANES
    half = LANES // 2
    core = place[chips]
    low = pl.multiple_of(core * (chips * half), half)
    high = pl.multiple_of((1 - core) * (chips * half), half)
    for chip in range(chips):
        lanes = pl.ds(pl.multiple_of(place[chip] * LANES, LANES), LANES)
        block = source_ref[:, lanes].T
        turned_ref[pl.ds(low + chip * half, half), columns] = block[:half]
        turned_ref[pl.ds(high + chip * half, half), columns] = block[half:]


def spread(turned_ref, keep_ref, gone_ref, first=0):
    middle = turned_ref.shape[0] // 2
    keep_ref[...] = turned_ref[:middle, :]
    for part in range(2):
        start = middle + part * PART
        gone_ref[first + part] = turned_ref[start : start + PART, :].astype(F32)


def turn_cot_kernel(place, cot_ref, keep_ref, gone_ref, turned_ref):
    turn(place, cot_ref, turned_ref, slice(None))
    spread(turned_ref, keep_ref, gone_ref)


def turn_cot(place, cotangent, rows):
    width = cotangent.shape[1]
    items = cotangent.shape[0] // rows
    return pl.pallas_call(
        turn_cot_kernel,
        grid_spec=pltpu.PrefetchScalarGridSpec(
            num_scalar_prefetch=1,
            grid=(items,),
            in_specs=[pl.BlockSpec((rows, width), lambda i, *_: (i, 0))],
            out_specs=[
                pl.BlockSpec((None, width // 2, rows), lambda i, *_: (i, 0, 0)),
                pl.BlockSpec((2, PART, rows), lambda i, *_: (i, 0, 0)),
            ],
            scratch_shapes=[pltpu.VMEM((width, rows), BF16)],
        ),
        out_shape=[
            jax.ShapeDtypeStruct((items, width // 2, rows), BF16),
            jax.ShapeDtypeStruct((2 * items, PART, rows), F32),
        ],
        compiler_params=params(4),
        cost_estimate=short_cost(),
        name="turn_cotangent",
    )(place, cotangent)


def pack_kernel(values_ref, out_ref):
    out_ref[0] = values_ref[...].astype(F32)


def pack(values):
    rows, columns = values.shape
    return pl.pallas_call(
        pack_kernel,
        grid=(columns // PART,),
        in_specs=[pl.BlockSpec((rows, PART), lambda n: (0, n))],
        out_specs=pl.BlockSpec((1, rows, PART), lambda n: (n, 0, 0)),
        out_shape=jax.ShapeDtypeStruct((columns // PART, rows, PART), F32),
        compiler_params=params(4),
        cost_estimate=short_cost(),
        name="pack_pixels",
    )(values)


def pack_attn_kernel(place, a1_ref, o_ref, keep_ref, gone_ref, turned_ref):
    turn(place, a1_ref, turned_ref, slice(None))
    spread(turned_ref, keep_ref, gone_ref)
    for part in range(o_ref.shape[1] // PART):
        gone_ref[2 + part] = o_ref[:, part * PART : (part + 1) * PART].astype(F32)


def pack_attn(place, a1, mix):
    rows, width = a1.shape
    parts = 2 + mix.shape[1] // PART
    return pl.pallas_call(
        pack_attn_kernel,
        grid_spec=pltpu.PrefetchScalarGridSpec(
            num_scalar_prefetch=1,
            grid=(1,),
            in_specs=[whole(a1.shape), whole(mix.shape)],
            out_specs=[whole((width // 2, rows)), whole((parts, PART, rows))],
            scratch_shapes=[pltpu.VMEM((width, rows), BF16)],
        ),
        out_shape=[
            jax.ShapeDtypeStruct((width // 2, rows), BF16),
            jax.ShapeDtypeStruct((parts, PART, rows), F32),
        ],
        compiler_params=params(4),
        cost_estimate=short_cost(),
        name="pack_attn",
    )(place, a1, mix)


def pieces_of(length):
    third = length // 3 // LANES * LANES
    return [(0, third), (third, third), (2 * third, length - 2 * third)]


def embed_kernel(
    kinds, pix_ref, wspec_ref, wrgb_ref, pick_ref, part_ref, mixed_ref,
    pix_buf, wspec_buf, wrgb_buf, pick_buf, pix_sem, big_sem, small_sem, *, item,
):
    rows, wide = pix_buf.shape
    spectral = kinds[item] == 1
    pieces = pieces_of(wide)
    own_rows = pl.ds(item * rows, rows)

    @pl.when(spectral)
    def _():
        copies = []
        for n, (first, size) in enumerate(pieces):
            span = pl.ds(first, size)
            copies.append(
                (
                    pltpu.make_async_copy(
                        pix_ref.at[own_rows, span], mixed_ref.at[:, span], pix_sem.at[n]
                    ),
                    pltpu.make_async_copy(wspec_ref.at[span], wspec_buf.at[span], big_sem.at[n]),
                )
            )
        for pair in copies:
            for copy in pair:
                copy.start()
        mixed_ref[:, wide:] = jnp.zeros((rows, wrgb_buf.shape[0]), BF16)
        for n, (first, size) in enumerate(pieces):
            for copy in copies[n]:
                copy.wait()
            term = nn(mixed_ref[:, first : first + size], wspec_buf[first : first + size, :])
            if n == 0:
                part_ref[...] = term
            else:
                part_ref[...] += term

    @pl.when(jnp.logical_not(spectral))
    def _():
        copies = []
        for n, (first, size) in enumerate(pieces):
            span = pl.ds(first, size)
            copies.append(
                (
                    pltpu.make_async_copy(
                        pix_ref.at[own_rows, span], pix_buf.at[:, span], pix_sem.at[n]
                    ),
                    pltpu.make_async_copy(pick_ref.at[span], pick_buf.at[span], big_sem.at[n]),
                )
            )
        for pair in copies:
            for copy in pair:
                copy.start()
        weights = pltpu.make_async_copy(wrgb_ref, wrgb_buf, small_sem)
        weights.start()
        mixed_ref[:, :wide] = jnp.zeros((rows, wide), BF16)
        total = None
        for n, (first, size) in enumerate(pieces):
            for copy in copies[n]:
                copy.wait()
            term = nn(pix_buf[:, first : first + size], pick_buf[first : first + size, :])
            total = term if total is None else total + term
        mixed_ref[:, wide:] = total.astype(BF16)
        weights.wait()
        part_ref[...] = nn(mixed_ref[:, wide:], wrgb_buf[...])


def embed(kinds, pixels, w_spectral, w_rgb, pick, item, rows):
    wide, width = w_spectral.shape
    narrow = w_rgb.shape[0]
    far = pl.BlockSpec(memory_space=pltpu.HBM)
    return pl.pallas_call(
        functools.partial(embed_kernel, item=item),
        grid_spec=pltpu.PrefetchScalarGridSpec(
            num_scalar_prefetch=1,
            grid=(1,),
            in_specs=[far, far, far, far],
            out_specs=[whole((rows, width)), whole((rows, wide + narrow))],
            scratch_shapes=[
                pltpu.VMEM((rows, wide), BF16),
                pltpu.VMEM((wide, width), BF16),
                pltpu.VMEM((narrow, width), BF16),
                pltpu.VMEM((wide, narrow), BF16),
                pltpu.SemaphoreType.DMA((3,)),
                pltpu.SemaphoreType.DMA((3,)),
                pltpu.SemaphoreType.DMA(()),
            ],
        ),
        out_shape=[
            jax.ShapeDtypeStruct((rows, width), F32),
            jax.ShapeDtypeStruct((rows, wide + narrow), BF16),
        ],
        compiler_params=params(58),
        cost_estimate=short_cost(),
        name="embed",
    )(kinds, pixels, w_spectral, w_rgb, pick)


def pair_masks(rows):
    lane = lax.broadcasted_iota(jnp.int32, (rows, LANES), 1)
    return lane < HEAD_DIM, lane >= HEAD_DIM


def only(mask, values):
    return jnp.where(mask, values, jnp.zeros_like(values))


def softmax_rows(query, key):
    scores = nt(query, key) * (HEAD_DIM**-0.5)
    expo = jnp.exp(scores - jnp.max(scores, -1, keepdims=True))
    return expo / jnp.sum(expo, -1, keepdims=True)


def attn_forward_kernel(
    part_ref, recv_ref, table_ref, gain_ref, bias_ref, wqkv_ref, qb_ref, vb_ref, wout_ref,
    x0_ref, a1_ref, qkv_ref, o_ref, opart_ref,
):
    quad = pl.program_id(0)
    rows, width = part_ref.shape

    @pl.when(quad == 0)
    def _():
        side = table_ref.shape[0]
        half = table_ref.shape[1]
        table = table_ref[...]
        by_row = jnp.broadcast_to(table[:, None, :], (side, side, half)).reshape(rows, half)
        by_col = jnp.broadcast_to(table[None, :, :], (side, side, half)).reshape(rows, half)
        left = part_ref[:, :half] + recv_ref[:, :half] + by_row
        right = part_ref[:, half:] + recv_ref[:, half:] + by_col
        x0_ref[:, :half] = left
        x0_ref[:, half:] = right
        normed, _inv = norm_parts(x0_ref[...])
        a1_ref[...] = (normed * gain_ref[...] + bias_ref[...]).astype(BF16)
        opart_ref[...] = jnp.zeros_like(opart_ref)

    a1 = a1_ref[...]
    query = (nn(a1, wqkv_ref[0]) + qb_ref[...]).astype(BF16)
    key = nn(a1, wqkv_ref[1]).astype(BF16)
    value = (nn(a1, wqkv_ref[2]) + vb_ref[...]).astype(BF16)
    qkv_ref[0] = query
    qkv_ref[1] = key
    qkv_ref[2] = value
    masks = pair_masks(rows)
    for pair in range(query.shape[1] // LANES):
        span = slice(pair * LANES, (pair + 1) * LANES)
        q2, k2, v2 = query[:, span], key[:, span], value[:, span]
        mixed = None
        for mask in masks:
            probs = softmax_rows(only(mask, q2), k2).astype(BF16)
            term = nn(probs, only(mask, v2))
            mixed = term if mixed is None else mixed + term
        o_ref[:, span] = mixed.astype(BF16)
    opart_ref[...] += nn(o_ref[...], wout_ref[...])


def attn_forward(part, recv, table, gain, bias, w_qkv, q_bias, v_bias, w_out):
    rows, width = part.shape
    heads_wide = w_out.shape[0]
    steps = heads_wide // QUAD
    return pl.pallas_call(
        attn_forward_kernel,
        grid=(steps,),
        in_specs=[
            whole(part.shape),
            whole(recv.shape),
            whole(table.shape),
            whole(gain.shape),
            whole(bias.shape),
            pl.BlockSpec((3, width, QUAD), lambda n: (0, 0, n)),
            pl.BlockSpec((1, QUAD), lambda n: (0, n)),
            pl.BlockSpec((1, QUAD), lambda n: (0, n)),
            pl.BlockSpec((QUAD, width), lambda n: (n, 0)),
        ],
        out_specs=[
            whole((rows, width)),
            whole((rows, width)),
            pl.BlockSpec((3, rows, QUAD), lambda n: (0, 0, n)),
            pl.BlockSpec((rows, QUAD), lambda n: (0, n)),
            whole((rows, width)),
        ],
        out_shape=[
            jax.ShapeDtypeStruct((rows, width), F32),
            jax.ShapeDtypeStruct((rows, width), BF16),
            jax.ShapeDtypeStruct((3, rows, heads_wide), BF16),
            jax.ShapeDtypeStruct((rows, heads_wide), BF16),
            jax.ShapeDtypeStruct((rows, width), F32),
        ],
        compiler_params=params(10),
        cost_estimate=long_cost(),
        name="attn_forward",
    )(part, recv, table, gain, bias, w_qkv, q_bias, v_bias, w_out)


def put_rows(refs, values, add):
    first = 0
    for ref in refs:
        rows = ref.shape[0]
        if add:
            ref[...] += values[first : first + rows]
        else:
            ref[...] = values[first : first + rows]
        first += rows


def joined(refs):
    values = [ref[...] for ref in refs]
    return values[0] if len(values) == 1 else jnp.concatenate(values, 0)


def attn_backward_kernel(place, *refs, parts):
    gpart_refs, refs = refs[: parts[0]], refs[parts[0] :]
    grecv_refs, refs = refs[: parts[1]], refs[parts[1] :]
    x1_ref, cot_ref, gain_ref, wout_ref, qkv_ref, wqkv_ref, *refs = refs
    dx1_ref, dya_ref, dqkv_ref, sums_ref, qvsum_ref, keep_ref, gone_ref, *da1_refs = refs[:-1]
    turned_ref = refs[-1]
    quad = pl.program_id(0)
    rows = x1_ref.shape[0]

    @pl.when(quad == 0)
    def _():
        normed, inverse = norm_parts(x1_ref[...])
        grad = joined(gpart_refs) + joined(grecv_refs)
        cot = cot_ref[...].astype(F32)
        dx1 = cot + norm_back(normed, inverse, grad, gain_ref[...])
        dx1_ref[...] = dx1
        dya = dx1.astype(BF16)
        dya_ref[...] = dya
        sums_ref[0:1, :] = column_sum(grad * normed)
        sums_ref[1:2, :] = column_sum(grad)
        sums_ref[2:3, :] = column_sum(dya.astype(F32))
        sums_ref[3:4, :] = column_sum(cot)
        sums_ref[4:8, :] = jnp.zeros((4, sums_ref.shape[1]), F32)
        turn(place, dya_ref, turned_ref, slice(None))
        spread(turned_ref, keep_ref, gone_ref)

    dmix = nt(dya_ref[...], wout_ref[...]).astype(BF16)
    scale = HEAD_DIM**-0.5
    masks = pair_masks(rows)
    for pair in range(dmix.shape[1] // LANES):
        span = slice(pair * LANES, (pair + 1) * LANES)
        q2, k2, v2, d2 = qkv_ref[0, :, span], qkv_ref[1, :, span], qkv_ref[2, :, span], dmix[:, span]
        totals = [None, None, None]
        for mask in masks:
            qm, km, dm = only(mask, q2), only(mask, k2), only(mask, d2)
            probs = softmax_rows(qm, k2)
            dprobs = nt(dm, v2)
            dot_row = jnp.sum(probs * dprobs, -1, keepdims=True)
            dscores = (probs * (dprobs - dot_row)).astype(BF16)
            terms = [nn(dscores, km), tn(dscores, qm), tn(probs.astype(BF16), dm)]
            totals = [t if o is None else o + t for o, t in zip(totals, terms)]
        dqkv_ref[0, :, span] = (totals[0] * scale).astype(BF16)
        dqkv_ref[1, :, span] = (totals[1] * scale).astype(BF16)
        dqkv_ref[2, :, span] = totals[2].astype(BF16)
    da1 = nt(dqkv_ref[0], wqkv_ref[0]) + nt(dqkv_ref[1], wqkv_ref[1]) + nt(dqkv_ref[2], wqkv_ref[2])

    @pl.when(quad == 0)
    def _():
        put_rows(da1_refs, da1, False)

    @pl.when(quad != 0)
    def _():
        put_rows(da1_refs, da1, True)

    steps = pl.num_programs(0)
    for plane in range(3):
        gone_ref[2 + plane * steps + quad] = dqkv_ref[plane].astype(F32)
    qvsum_ref[0:1, :] = column_sum(dqkv_ref[0].astype(F32))
    qvsum_ref[1:2, :] = column_sum(dqkv_ref[2].astype(F32))
    qvsum_ref[2:8, :] = jnp.zeros((6, qvsum_ref.shape[1]), F32)


def attn_backward(place, gparts, grecvs, x1, cotangent, gain, w_out, qkv, w_qkv, item, cuts):
    rows, width = x1.shape
    heads_wide = w_out.shape[0]
    steps = heads_wide // QUAD
    return pl.pallas_call(
        functools.partial(attn_backward_kernel, parts=(len(gparts), len(grecvs))),
        grid_spec=pltpu.PrefetchScalarGridSpec(
            num_scalar_prefetch=1,
            grid=(steps,),
            in_specs=[
                *[whole(v.shape) for v in (*gparts, *grecvs)],
                whole(x1.shape),
                pl.BlockSpec((rows, width), lambda n, *_: (item, 0)),
                whole(gain.shape),
                pl.BlockSpec((QUAD, width), lambda n, *_: (n, 0)),
                pl.BlockSpec((3, rows, QUAD), lambda n, *_: (0, 0, n)),
                pl.BlockSpec((3, width, QUAD), lambda n, *_: (0, 0, n)),
            ],
            out_specs=[
                whole((rows, width)),
                whole((rows, width)),
                pl.BlockSpec((3, rows, QUAD), lambda n, *_: (0, 0, n)),
                whole((8, width)),
                pl.BlockSpec((8, QUAD), lambda n, *_: (0, n)),
                whole((width // 2, rows)),
                whole((2 + 3 * steps, PART, rows)),
                *[whole((cut, width)) for cut in cuts],
            ],
            scratch_shapes=[pltpu.VMEM((width, rows), BF16)],
        ),
        out_shape=[
            jax.ShapeDtypeStruct((rows, width), F32),
            jax.ShapeDtypeStruct((rows, width), BF16),
            jax.ShapeDtypeStruct((3, rows, heads_wide), BF16),
            jax.ShapeDtypeStruct((8, width), F32),
            jax.ShapeDtypeStruct((8, heads_wide), F32),
            jax.ShapeDtypeStruct((width // 2, rows), BF16),
            jax.ShapeDtypeStruct((2 + 3 * steps, PART, rows), F32),
            *[jax.ShapeDtypeStruct((cut, width), F32) for cut in cuts],
        ],
        compiler_params=params(16),
        cost_estimate=long_cost(),
        name="attn_backward",
    )(place, *gparts, *grecvs, x1, cotangent, gain, w_out, qkv, w_qkv)


def mlp_kernel(
    place, x0_ref, opart_ref, orecv_ref, obias_ref, gain_ref, bias_ref, wfc1_ref, b1_ref, wfc2_ref, cot_ref,
    x1_ref, a2_ref, act_ref, dpre_ref, b1sum_ref, keep_ref, gact_ref, gpre_ref, *refs,
):
    da2_refs, turned_ref = refs[:-1], refs[-1]
    step = pl.program_id(0)

    @pl.when(step == 0)
    def _():
        x1_ref[...] = x0_ref[...] + (opart_ref[...] + orecv_ref[...] + obias_ref[...])
        normed, _inv = norm_parts(x1_ref[...])
        a2_ref[...] = (normed * gain_ref[...] + bias_ref[...]).astype(BF16)
        turn(place, a2_ref, turned_ref, slice(None))
        spread(turned_ref, keep_ref, gpre_ref)

    pre = nn(a2_ref[...], wfc1_ref[...]) + b1_ref[...]
    dact = nt(cot_ref[...], wfc2_ref[...])
    cdf = 0.5 * (1.0 + lax.erf(pre * (2.0**-0.5)))
    act = (pre * cdf).astype(BF16)
    act_ref[...] = act
    density = jnp.exp(-0.5 * pre * pre) * 0.3989422804014327
    dpre = (dact * (cdf + pre * density)).astype(BF16)
    dpre_ref[...] = dpre
    for part in range(act.shape[1] // PART):
        columns = slice(part * PART, (part + 1) * PART)
        gact_ref[part] = act[:, columns].astype(F32)
        gpre_ref[2 + step * (act.shape[1] // PART) + part] = dpre[:, columns].astype(F32)
    b1sum_ref[...] = column_sum(dpre.astype(F32))
    da2 = nt(dpre, wfc1_ref[...])

    @pl.when(step == 0)
    def _():
        put_rows(da2_refs, da2, False)

    @pl.when(step != 0)
    def _():
        put_rows(da2_refs, da2, True)


def mlp(
    place, x0, opart, orecv, out_bias, gain, bias, w_fc1, fc1_bias, w_fc2, cotangent, item, cuts
):
    rows, width = x0.shape
    hidden = w_fc1.shape[1]
    tile = 512
    parts = tile // PART
    row_tile = pl.BlockSpec((rows, tile), lambda n, *_: (0, n))
    gone = pl.BlockSpec((parts, rows, PART), lambda n, *_: (n, 0, 0))
    return pl.pallas_call(
        mlp_kernel,
        grid_spec=pltpu.PrefetchScalarGridSpec(
            num_scalar_prefetch=1,
            grid=(hidden // tile,),
            in_specs=[
                whole(x0.shape),
                whole(opart.shape),
                whole(orecv.shape),
                whole(out_bias.shape),
                whole(gain.shape),
                whole(bias.shape),
                pl.BlockSpec((width, tile), lambda n, *_: (0, n)),
                pl.BlockSpec((1, tile), lambda n, *_: (0, n)),
                pl.BlockSpec((tile, width), lambda n, *_: (n, 0)),
                pl.BlockSpec((rows, width), lambda n, *_: (item, 0)),
            ],
            out_specs=[
                whole((rows, width)),
                whole((rows, width)),
                row_tile,
                row_tile,
                pl.BlockSpec((1, tile), lambda n, *_: (0, n)),
                whole((width // 2, rows)),
                gone,
                whole((2 + hidden // PART, rows, PART)),
                *[whole((cut, width)) for cut in cuts],
            ],
            scratch_shapes=[pltpu.VMEM((width, rows), BF16)],
        ),
        out_shape=[
            jax.ShapeDtypeStruct((rows, width), F32),
            jax.ShapeDtypeStruct((rows, width), BF16),
            jax.ShapeDtypeStruct((rows, hidden), BF16),
            jax.ShapeDtypeStruct((rows, hidden), BF16),
            jax.ShapeDtypeStruct((1, hidden), F32),
            jax.ShapeDtypeStruct((width // 2, rows), BF16),
            jax.ShapeDtypeStruct((hidden // PART, rows, PART), F32),
            jax.ShapeDtypeStruct((2 + hidden // PART, rows, PART), F32),
            *[jax.ShapeDtypeStruct((cut, width), F32) for cut in cuts],
        ],
        compiler_params=params(14),
        cost_estimate=long_cost(),
        name="mlp",
    )(place, x0, opart, orecv, out_bias, gain, bias, w_fc1, fc1_bias, w_fc2, cotangent)


def mlp_out_kernel(act_ref, wfc2_ref, out_ref):
    out_ref[...] = nn(act_ref[...], wfc2_ref[...])


def mlp_out(act, w_fc2):
    rows, hidden = act.shape
    width = w_fc2.shape[1]
    tile = 512
    return pl.pallas_call(
        mlp_out_kernel,
        grid=(width // tile,),
        in_specs=[whole(act.shape), pl.BlockSpec((hidden, tile), lambda n: (0, n))],
        out_specs=pl.BlockSpec((rows, tile), lambda n: (0, n)),
        out_shape=jax.ShapeDtypeStruct((rows, width), F32),
        compiler_params=params(6),
        cost_estimate=long_cost(),
        name="mlp_out",
    )(act, w_fc2)


def first_norm_back_kernel(place, *refs, parts):
    gpart_refs, refs = refs[: parts[0]], refs[parts[0] :]
    grecv_refs, refs = refs[: parts[1]], refs[parts[1] :]
    x0_ref, dx1_ref, gain_ref, dx0_ref, sums_ref, keep_ref, gone_ref, turned_ref = refs
    normed, inverse = norm_parts(x0_ref[...])
    grad = joined(gpart_refs) + joined(grecv_refs)
    dx0_ref[...] = (dx1_ref[...] + norm_back(normed, inverse, grad, gain_ref[...])).astype(BF16)
    sums_ref[0:1, :] = column_sum(grad * normed)
    sums_ref[1:2, :] = column_sum(grad)
    sums_ref[2:8, :] = jnp.zeros((6, sums_ref.shape[1]), F32)
    turn(place, dx0_ref, turned_ref, slice(None))
    spread(turned_ref, keep_ref, gone_ref)


def first_norm_back(place, gparts, grecvs, x0, dx1, gain, estimate):
    rows, width = x0.shape
    operands = (*gparts, *grecvs, x0, dx1, gain)
    shapes = [
        jax.ShapeDtypeStruct((rows, width), BF16),
        jax.ShapeDtypeStruct((8, width), F32),
        jax.ShapeDtypeStruct((width // 2, rows), BF16),
        jax.ShapeDtypeStruct((2, PART, rows), F32),
    ]
    return pl.pallas_call(
        functools.partial(first_norm_back_kernel, parts=(len(gparts), len(grecvs))),
        grid_spec=pltpu.PrefetchScalarGridSpec(
            num_scalar_prefetch=1,
            grid=(1,),
            in_specs=[whole(v.shape) for v in operands],
            out_specs=[whole(v.shape) for v in shapes],
            scratch_shapes=[pltpu.VMEM((width, rows), BF16)],
        ),
        out_shape=shapes,
        compiler_params=params(10),
        cost_estimate=estimate,
        name="first_norm_back",
    )(place, *operands)


def pixel_grad_kernel(kinds, da_ref, db_ref, wspec_ref, wrgb_ref, pick_ref, out_ref):
    item = pl.program_id(0)
    spectral = kinds[item] == 1
    grad = jnp.where(item == 0, da_ref[...], db_ref[...])
    wide = wspec_ref.shape[0]
    cut = (wide // 2 + LANES - 1) // LANES * LANES

    @pl.when(spectral)
    def _():
        out_ref[:, :cut] = nt(grad, wspec_ref[:cut, :]).astype(BF16)
        out_ref[:, cut:] = nt(grad, wspec_ref[cut:, :]).astype(BF16)

    @pl.when(jnp.logical_not(spectral))
    def _():
        small = nt(grad, wrgb_ref[...]).astype(BF16)
        out_ref[...] = nt(small, pick_ref[...]).astype(BF16)


def pixel_grad(kinds, grad_a, grad_b, w_spectral, w_rgb, pick):
    rows = grad_a.shape[0]
    wide, width = w_spectral.shape
    return pl.pallas_call(
        pixel_grad_kernel,
        grid_spec=pltpu.PrefetchScalarGridSpec(
            num_scalar_prefetch=1,
            grid=(2,),
            in_specs=[
                whole(grad_a.shape),
                whole(grad_b.shape),
                whole(w_spectral.shape),
                whole(w_rgb.shape),
                whole(pick.shape),
            ],
            out_specs=pl.BlockSpec((rows, wide), lambda i, *_: (i, 0)),
        ),
        out_shape=jax.ShapeDtypeStruct((2 * rows, wide), BF16),
        compiler_params=params(8),
        cost_estimate=long_cost(),
        name="pixel_grad",
    )(kinds, grad_a, grad_b, w_spectral, w_rgb, pick)


def gather_left(keep_refs, gone_refs, first, left_ref):
    rows = keep_refs[0].shape[-1]
    for pos, keep_ref in enumerate(keep_refs):
        left_ref[:, pos * rows : (pos + 1) * rows] = keep_ref[...]
    base = len(keep_refs) * rows
    for pos, gone_ref in enumerate(gone_refs):
        columns = slice(base + pos * rows, base + (pos + 1) * rows)
        for part in range(2):
            left_ref[part * PART : (part + 1) * PART, columns] = gone_ref[first + part].astype(BF16)


def emit(left_ref, rights, send_ref, keep_ref, moves, columns=slice(None)):
    right = jnp.concatenate([r.astype(BF16) for r in rights], 0)
    total = nn(left_ref[...], right)
    half = LANES // 2
    for pos, block in enumerate(moves):
        out_ref = send_ref if pos < 4 else keep_ref
        out_ref[pos % 4, :, columns] = total[block * half : (block + 1) * half]


def plain_grad_kernel(
    ka_ref, kb_ref, la_ref, lb_ref, ra_ref, rb_ref, oa_ref, ob_ref, send_ref, keep_ref, left_ref,
    *, moves,
):
    @pl.when(pl.program_id(0) == 0)
    def _():
        gather_left((ka_ref, kb_ref), (la_ref, lb_ref), 0, left_ref)

    for part in range(oa_ref.shape[0]):
        columns = slice(part * PART, (part + 1) * PART)
        rights = (ra_ref[:, columns], rb_ref[:, columns], oa_ref[part], ob_ref[part])
        emit(left_ref, rights, send_ref, keep_ref, moves, columns)


def plain_grad(keeps, lefts, rights, others, moves, name, skip=0, columns=None, lead=0):
    half_width, rows = keeps[0][0].shape[-2:]
    columns = columns or rights[0].shape[1]
    wide = WIDE
    base = skip // (wide * PART)
    half = LANES // 2

    def keep_spec(array, item):
        if array.ndim == 2:
            return whole(array.shape)
        return pl.BlockSpec((None,) + array.shape[1:], lambda n: (item, 0, 0))

    right = pl.BlockSpec((rows, wide * PART), lambda n: (0, n + base))
    other = pl.BlockSpec((wide, rows, PART), lambda n: (n + base + lead // wide, 0, 0))
    out = pl.BlockSpec((4, half, wide * PART), lambda n: (0, 0, n))
    shape = jax.ShapeDtypeStruct((4, half, columns), F32)
    return pl.pallas_call(
        functools.partial(plain_grad_kernel, moves=moves),
        grid=(columns // (wide * PART),),
        in_specs=[keep_spec(*k) for k in keeps]
        + [pl.BlockSpec((2, PART, rows), lambda n, q=i: (q, 0, 0)) for _, i in lefts]
        + [right, right, other, other],
        out_specs=[out, out],
        scratch_shapes=[pltpu.VMEM((half_width, 4 * rows), BF16)],
        out_shape=[shape, shape],
        compiler_params=params(14),
        cost_estimate=short_cost(),
        name=name,
    )(*[k for k, _ in keeps], *[v for v, _ in lefts], *rights, *others)


def attn_grad_kernel(
    aa_ref, ab_ref, ya_ref, yb_ref, fa_ref, fb_ref, ba_ref, bb_ref, da_ref, db_ref, ma_ref, mb_ref,
    send_ref, keep_ref, left_ref, *, moves,
):
    plane, step = pl.program_id(0), pl.program_id(1)
    steps = pl.num_programs(1)

    @pl.when((plane == 0) & (step == 0))
    def _():
        gather_left((aa_ref, ab_ref), (fa_ref, fb_ref), 0, left_ref)

    @pl.when((plane == 3) & (step == 0))
    def _():
        gather_left((ya_ref, yb_ref), (ba_ref, bb_ref), 0, left_ref)

    @pl.when(plane < 3)
    def _():
        spot = 2 + plane * steps + step
        emit(left_ref, (da_ref[...], db_ref[...], ba_ref[spot], bb_ref[spot]), send_ref, keep_ref, moves)

    @pl.when(plane == 3)
    def _():
        spot = 2 + step
        emit(left_ref, (ma_ref[...], mb_ref[...], fa_ref[spot], fb_ref[spot]), send_ref, keep_ref, moves)


def attn_grad(keep_a1, keep_dya, other_f, other_b, dqkv, mix, moves):
    half_width, rows = keep_a1[0].shape
    columns = mix[0].shape[1]
    half = LANES // 2
    side = whole((half_width, rows))
    plane = pl.BlockSpec((None, rows, PART), lambda p, n: (jnp.minimum(p, 2), 0, n))
    mixed = pl.BlockSpec((rows, PART), lambda p, n: (0, n))
    out = pl.BlockSpec((4, half, PART), lambda p, n: (0, p, n))
    shape = jax.ShapeDtypeStruct((4, 4 * half, columns), F32)
    return pl.pallas_call(
        functools.partial(attn_grad_kernel, moves=moves),
        grid=(4, columns // PART),
        in_specs=[side, side, side, side]
        + [whole(v.shape) for v in (*other_f, *other_b)]
        + [plane, plane, mixed, mixed],
        out_specs=[out, out],
        scratch_shapes=[pltpu.VMEM((half_width, 4 * rows), BF16)],
        out_shape=[shape, shape],
        compiler_params=params(8),
        cost_estimate=short_cost(),
        name="attn_grad",
    )(*keep_a1, *keep_dya, *other_f, *other_b, *dqkv, *mix)


def exchange(values, axis, bit, size):
    return lax.ppermute(values, axis, [(i, i ^ bit) for i in range(size)])


def swap(values):
    return exchange(values, "tensor", 1, 2)


def after(first, values):
    return lax.optimization_barrier((first, values))[1]


X_FIRST = (2, 4, 8)
Z_FIRST = (4, 2, 8)


def block_flips(bits):
    return [sum((1 - ((p >> (2 - n)) & 1)) * (bits[n] // 2) for n in range(3)) for p in range(8)]


def block_moves(bits):
    stands = block_flips(X_FIRST)
    return tuple(stands.index(f) for f in block_flips(bits))


def places():
    me = lax.axis_index("dp")
    flips = jnp.array(block_flips(X_FIRST), jnp.int32)
    return jnp.concatenate([(me // 2) ^ flips, (me % 2)[None]]).astype(jnp.int32)


class Halving:
    def __init__(self, send, keep, bits, size):
        self.keep, self.bits, self.size = keep, bits, size
        self.recvs = [exchange(send, "dp", bits[0], size)]
        self.left = keep.shape[0]
        self.sent = send

    def step(self, order):
        self.recvs[-1] = order.tie(self.recvs[-1])
        left = self.left
        count = max(left // 2, 1)
        total = self.keep.shape[0] - left
        value = self.keep[total : total + count]
        for recv in self.recvs:
            first = recv.shape[0] - left
            value = value + recv[first : first + count]
        order.mark(value)
        if left == 1:
            return value[0]
        self.recvs.append(exchange(value, "dp", self.bits[len(self.recvs)], self.size))
        self.left = left // 2
        return None


class Order:
    def __init__(self):
        self.last = None

    def tie(self, values):
        return values if self.last is None else after(self.last, values)

    def mark(self, values):
        self.last = values


def local(
    pixels, item_kinds, gsd_codes, w_spectral, w_rgb, ln1_gain, ln1_bias, w_qkv, q_bias, v_bias,
    w_out, out_bias, ln2_gain, ln2_bias, w_fc1, fc1_bias, w_fc2, fc2_bias, cotangent, *, size,
):
    items = item_kinds.shape[0]
    rows = pixels.shape[0] // items
    width = w_out.shape[1]
    wide = pixels.shape[1]
    narrow = w_rgb.shape[0]
    bands = wide // (narrow // 3)
    custom = size == 16

    def row(vector):
        return vector.reshape(1, -1)

    g1, c1, g2, c2 = row(ln1_gain), row(ln1_bias), row(ln2_gain), row(ln2_bias)
    qb, vb, ob, b1 = row(q_bias), row(v_bias), row(out_bias), row(fc1_bias)
    wqkv = jnp.transpose(w_qkv, (1, 0, 2))

    source = np.arange(wide)[:, None]
    target = np.arange(narrow)[None, :]
    pick = jnp.asarray((source == (target // 3) * bands + target % 3).astype(ml_dtypes.bfloat16))

    ratio = (gsd_codes.astype(F32) + 1.0) / 4.0
    quarter = width // 4
    frequency = 1.0 / 10000.0 ** (jnp.arange(quarter).astype(F32) / quarter)
    spot = jnp.arange(GRID).astype(F32)
    angle = ratio[:, None, None] * spot[None, :, None] * frequency[None, None, :]
    tables = jnp.concatenate([jnp.sin(angle), jnp.cos(angle)], -1)

    def scatter(values):
        return lax.psum_scatter(values, "dp", scatter_dimension=0, tiled=True)

    def both(left, right):
        return sum(tn(left[i], right[i]) for i in range(items))

    order = Order()
    gate = None

    def send(values, wait=True):
        nonlocal gate
        if gate is not None:
            values = after(gate, values)
        gate = swap(values)
        return gate

    place = places() if custom else jnp.arange(9, dtype=jnp.int32) % 8
    move_x, move_z = block_moves(X_FIRST), block_moves(Z_FIRST)

    def other(values):
        return exchange(values, "dp", 1, size) if custom else values

    cut = rows * 3 // 8 // 8 * 8
    cuts = [(cut, rows - cut)] + [(rows,)] * (items - 1)

    def settle(values):
        values = order.tie(values)
        order.mark(jax.tree.leaves(values)[0])
        return values

    none = [None] * items
    part, mixed, erecv, fwd, orecv, ffn, grecv, bwd, arecv, last, ycot = (list(none) for _ in range(11))
    gmix, pk, gfwd, gact, gpre, gbwd, gdx0, da1, da2 = (list(none) for _ in range(9))

    for i in range(items):
        part[i], mixed[i] = embed(order.tie(item_kinds), pixels, w_spectral, w_rgb, pick, i, rows)
        order.mark(part[i])
        erecv[i] = send(part[i])
    keep_cot, gone_cot = turn_cot(order.tie(place), cotangent, rows)
    order.mark(gone_cot)
    gone_mix = []
    for i in range(items):
        gone_mix.append(pack(order.tie(mixed[i])))
        order.mark(gone_mix[i])
    gcot = other(gone_cot)
    gmix = [other(v) for v in gone_mix]
    for i in range(items):
        fwd[i] = attn_forward(
            part[i], erecv[i], tables[i], order.tie(g1), c1, wqkv, qb, vb, w_out
        )
        order.mark(fwd[i][4])
        orecv[i] = send(fwd[i][4])
        if i == 0:
            gcot = settle(gcot)
        else:
            gmix = [settle(v) for v in gmix]
        pk[i] = pack_attn(order.tie(place), fwd[i][1], fwd[i][3])
        order.mark(pk[i][1])
        gfwd[i] = other(pk[i][1])
    x0, a1, qkv, mix, _ = zip(*fwd)
    for i in range(items):
        ffn[i] = mlp(
            place, x0[i], fwd[i][4], orecv[i], order.tie(ob), g2, c2, w_fc1, b1, w_fc2, cotangent, i,
            cuts[i],
        )
        da2[i] = ffn[i][8:]
        order.mark(da2[i][0])
        if i == 0:
            grecv[i] = [send(v) for v in da2[i]]
        gact[i] = other(ffn[i][6])
        gpre[i] = other(ffn[i][7])
        if i == 0:
            gfwd = [settle(v) for v in gfwd]
        else:
            grecv[0][0] = settle(grecv[0][0])
            gact[0], gpre[0] = settle((gact[0], gpre[0]))
            ycot[1] = mlp_out(order.tie(ffn[1][2]), w_fc2)
            order.mark(ycot[1])
    x1, a2, act, dpre, b1sum, ka2 = list(zip(*[v[:6] for v in ffn]))
    if custom:
        gact[1] = order.tie(gact[1])
        fc2_h = Halving(
            *plain_grad(
                [(keep_cot, 0), (keep_cot, 1)], [(gcot, 0), (gcot, 1)], act, gact, move_x, "fc2_grad"
            ),
            X_FIRST, size,
        )
        order.mark(fc2_h.sent)
        gpre[1] = order.tie(gpre[1])
        fc1_h = Halving(
            *plain_grad(
                [(ka2[0], 0), (ka2[1], 0)], [(gpre[0], 0), (gpre[1], 0)], dpre, gpre, move_z, "fc1_grad", lead=2
            ),
            Z_FIRST, size,
        )
        order.mark(fc1_h.sent)
    grecv[1] = [send(order.tie(da2[1][0]))]
    for i in range(items):
        bwd[i] = attn_backward(
            place, da2[i], grecv[i], x1[i], cotangent, order.tie(g2), w_out, qkv[i], wqkv, i, cuts[i]
        )
        da1[i] = bwd[i][7:]
        order.mark(da1[i][0])
        if i == 0:
            arecv[i] = [send(v) for v in da1[i]]
        else:
            arecv[0][0] = settle(arecv[0][0])
            gbwd = [other(order.tie(bwd[0][6])), other(bwd[1][6])]
            ycot[0] = mlp_out(order.tie(ffn[0][2]), w_fc2)
            order.mark(ycot[0])
    dx1, dya, dqkv, sums2, qvsum, kdya = list(zip(*[v[:6] for v in bwd]))
    if custom:
        fc2_h.step(order)
        gbwd = [order.tie(v) for v in gbwd]
        att_h = Halving(
            *attn_grad([v[0] for v in pk], kdya, gfwd, gbwd, dqkv, mix, move_x), X_FIRST, size
        )
        order.mark(att_h.sent)
        fc1_h.step(order)
    arecv[1] = [send(order.tie(da1[1][0]))]
    for i in range(items):
        estimate = long_cost() if i == 0 else short_cost()
        last[i] = first_norm_back(place, da1[i], arecv[i], x0[i], dx1[i], order.tie(g1), estimate)
        order.mark(last[i][0])
        if custom and i == 0:
            fc2_h.step(order)
    summed = list(none)
    gdx0 = [other(order.tie(last[0][3])), other(last[1][3])]
    dx0, sums1, kdx0, _ = zip(*last)
    pixels_grad = pixel_grad(order.tie(item_kinds), dx0[0], dx0[1], w_spectral, w_rgb, pick)
    order.mark(pixels_grad)
    if custom:
        mid = mixed[0].shape[1] // 2
        gdx0 = [order.tie(v) for v in gdx0]
        sides = ([(kdx0[0], 0), (kdx0[1], 0)], [(gdx0[0], 0), (gdx0[1], 0)], mixed, gmix)
        embx_h = Halving(*plain_grad(*sides, move_x, "embed_grad_a", 0, mid), X_FIRST, size)
        order.mark(embx_h.sent)
        sides[3][1] = order.tie(gmix[1])
        embz_h = Halving(*plain_grad(*sides, move_z, "embed_grad_b", mid, mid), Z_FIRST, size)
        order.mark(embz_h.sent)
        fc1_h.step(order)

    sums2, sums1, qvsum, b1sum = order.tie((sums2, sums1, qvsum, b1sum))
    vec2 = sums2[0] + sums2[1]
    vec1 = sums1[0] + sums1[1]
    qv = qvsum[0] + qvsum[1]
    b1s = b1sum[0] + b1sum[1]
    pieces = [vec2[0], vec2[1], vec2[2], vec2[3], vec1[0], vec1[1], qv[0], qv[1], b1s[0]]
    small = jnp.concatenate([v.reshape(size, -1) for v in pieces], 1)
    if custom:
        cube = small.reshape(2, 2, 2, 2, -1)
        chip, core = lax.axis_index("dp") // 2, lax.axis_index("dp") % 2
        for axis, bit in ((0, 4), (1, 2), (2, 1)):
            cube = jnp.where((chip & bit) == 0, jnp.flip(cube, axis), cube)
        cube = jnp.transpose(cube, (2, 1, 0, 3, 4)).reshape(8, 2, 1, -1)
        kept = jnp.where(core == 0, cube[:, 0], cube[:, 1])
        gone = jnp.where(core == 0, cube[:, 1], cube[:, 0])
        order.mark(gone)
        embz_h.step(order)
        att_h.step(order)
        fc2_g = fc2_h.step(order)
        fc1_g = fc1_h.step(order)
    summed[0] = send(order.tie(ycot[0]))
    if custom:
        gone = exchange(order.tie(gone), "dp", 1, size)
        embx_h.step(order)
        gone = order.tie(gone)
        small_h = Halving(kept[:4] + gone[:4], kept[4:] + gone[4:], X_FIRST, size)
        order.mark(small_h.sent)
    summed[0] = settle(summed[0])
    summed[1] = send(order.tie(ycot[1]))
    if custom:
        att_h.step(order)
        small_h.step(order)
        embz_h.step(order)
        small_h.step(order)
        embx_h.step(order)
        small = small_h.step(order)[0]
        summed[1] = settle(summed[1])
        att_g = att_h.step(order)
        embz_g = embz_h.step(order)
        embx_g = embx_h.step(order)
        emb_g = jnp.concatenate([embx_g, embz_g], 1)
        att_g = att_g.reshape(4, width // size, -1)
        qkv_grad = jnp.transpose(att_g[:3], (1, 0, 2))
        out_grad = att_g[3].T
    else:
        cot = [cotangent[i * rows : (i + 1) * rows] for i in range(items)]
        fc2_g = scatter(both(cot, act))
        fc1_g = scatter(both(a2, dpre))
        emb_g = scatter(both(dx0, mixed))
        qkv_grad = scatter(
            sum(
                lax.dot_general(
                    a1[i], dqkv[i], (((0,), (1,)), ((), ())), preferred_element_type=F32
                )
                for i in range(items)
            )
        )
        out_grad = scatter(both(dya, mix)).T
        small = scatter(small)[0]
    block_out = jnp.concatenate(
        [(x1[i] + (ycot[i] + summed[i] + fc2_bias)).astype(BF16) for i in range(items)], 0
    )
    outs = []
    start = 0
    for v in pieces:
        length = v.shape[0] // size
        outs.append(small[start : start + length])
        start += length
    ln2_g, ln2_b, ob_g, b2_g, ln1_g, ln1_b, q_g, v_g, b1_g = outs
    spectral_grad = emb_g[:, :wide].T
    rgb_grad = emb_g[:, wide:].T
    return (
        block_out, pixels_grad, spectral_grad, rgb_grad, ln1_g, ln1_b, qkv_grad, q_g, v_g, out_grad,
        ob_g, ln2_g, ln2_b, fc1_g, b1_g, fc2_g.T, b2_g,
    )


def solution(mesh):
    in_specs = (
        P("dp", "tensor"),
        P("dp"),
        P("dp"),
        P("tensor", None),
        P("tensor", None),
        P(),
        P(),
        P(None, None, "tensor"),
        P("tensor"),
        P("tensor"),
        P("tensor", None),
        P(),
        P(),
        P(),
        P(None, "tensor"),
        P("tensor"),
        P("tensor", None),
        P(),
        P("dp", None),
    )
    out_specs = (
        P("dp", None),
        P("dp", "tensor"),
        P("tensor", "dp"),
        P("tensor", "dp"),
        P("dp"),
        P("dp"),
        P("dp", None, "tensor"),
        P(("tensor", "dp")),
        P(("tensor", "dp")),
        P("tensor", "dp"),
        P("dp"),
        P("dp"),
        P("dp"),
        P("dp", "tensor"),
        P(("tensor", "dp")),
        P("tensor", "dp"),
        P("dp"),
    )
    body = functools.partial(local, size=mesh.shape["dp"])
    return jax.shard_map(body, mesh=mesh, in_specs=in_specs, out_specs=out_specs, check_vma=False)
```

```python
import functools

import jax
import jax.numpy as jnp
import ml_dtypes
import numpy as np
from jax import lax
from jax.experimental import pallas as pl
from jax.experimental.pallas import tpu as pltpu
from jax.sharding import PartitionSpec as P

HEAD_DIM = 64
GRID = 16
EPS = 1e-06
F32 = jnp.float32
BF16 = jnp.bfloat16
LANES = 128
MIB = 1024 * 1024
QUAD = 256
PART = 256
WIDE = 2


def nn(left, right):
    return lax.dot_general(left, right, (((1,), (0,)), ((), ())), preferred_element_type=F32)


def nt(left, right):
    return lax.dot_general(left, right, (((1,), (1,)), ((), ())), preferred_element_type=F32)


def tn(left, right):
    return lax.dot_general(left, right, (((0,), (0,)), ((), ())), preferred_element_type=F32)


def params(mib):
    return pltpu.CompilerParams(vmem_limit_bytes=mib * MIB)


def short_cost():
    return pl.CostEstimate(flops=1000, bytes_accessed=1000, transcendentals=0)


def long_cost():
    return pl.CostEstimate(flops=int(1e11), bytes_accessed=1000, transcendentals=0)


def whole(shape):
    return pl.BlockSpec(shape, lambda *_: (0,) * len(shape), pipeline_mode=pl.Buffered(1))


def norm_parts(values):
    center = values - jnp.mean(values, -1, keepdims=True)
    spread = jnp.mean(center * center, -1, keepdims=True)
    inverse = lax.rsqrt(spread + EPS)
    return center * inverse, inverse


def norm_back(normed, inverse, grad, gain):
    scaled = grad * gain
    mean_scaled = jnp.mean(scaled, -1, keepdims=True)
    mean_cross = jnp.mean(scaled * normed, -1, keepdims=True)
    return inverse * (scaled - mean_scaled - normed * mean_cross)


def column_sum(values):
    return jnp.sum(values, 0, keepdims=True)


def turn(place, source_ref, turned_ref, columns):
    chips = turned_ref.shape[0] // LANES
    half = LANES // 2
    core = place[chips]
    low = pl.multiple_of(core * (chips * half), half)
    high = pl.multiple_of((1 - core) * (chips * half), half)
    for chip in range(chips):
        lanes = pl.ds(pl.multiple_of(place[chip] * LANES, LANES), LANES)
        block = source_ref[:, lanes].T
        turned_ref[pl.ds(low + chip * half, half), columns] = block[:half]
        turned_ref[pl.ds(high + chip * half, half), columns] = block[half:]


def spread(turned_ref, keep_ref, gone_ref, first=0):
    middle = turned_ref.shape[0] // 2
    keep_ref[...] = turned_ref[:middle, :]
    for part in range(2):
        start = middle + part * PART
        gone_ref[first + part] = turned_ref[start : start + PART, :].astype(F32)


def turn_cot_kernel(place, cot_ref, keep_ref, gone_ref, turned_ref):
    turn(place, cot_ref, turned_ref, slice(None))
    spread(turned_ref, keep_ref, gone_ref)


def turn_cot(place, cotangent, rows):
    width = cotangent.shape[1]
    items = cotangent.shape[0] // rows
    return pl.pallas_call(
        turn_cot_kernel,
        grid_spec=pltpu.PrefetchScalarGridSpec(
            num_scalar_prefetch=1,
            grid=(items,),
            in_specs=[pl.BlockSpec((rows, width), lambda i, *_: (i, 0))],
            out_specs=[
                pl.BlockSpec((None, width // 2, rows), lambda i, *_: (i, 0, 0)),
                pl.BlockSpec((2, PART, rows), lambda i, *_: (i, 0, 0)),
            ],
            scratch_shapes=[pltpu.VMEM((width, rows), BF16)],
        ),
        out_shape=[
            jax.ShapeDtypeStruct((items, width // 2, rows), BF16),
            jax.ShapeDtypeStruct((2 * items, PART, rows), F32),
        ],
        compiler_params=params(4),
        cost_estimate=short_cost(),
        name="turn_cotangent",
    )(place, cotangent)


def pack_kernel(values_ref, out_ref):
    out_ref[0] = values_ref[...].astype(F32)


def pack(values):
    rows, columns = values.shape
    return pl.pallas_call(
        pack_kernel,
        grid=(columns // PART,),
        in_specs=[pl.BlockSpec((rows, PART), lambda n: (0, n))],
        out_specs=pl.BlockSpec((1, rows, PART), lambda n: (n, 0, 0)),
        out_shape=jax.ShapeDtypeStruct((columns // PART, rows, PART), F32),
        compiler_params=params(4),
        cost_estimate=short_cost(),
        name="pack_pixels",
    )(values)


def pack_attn_kernel(place, a1_ref, o_ref, keep_ref, gone_ref, turned_ref):
    turn(place, a1_ref, turned_ref, slice(None))
    spread(turned_ref, keep_ref, gone_ref)
    for part in range(o_ref.shape[1] // PART):
        gone_ref[2 + part] = o_ref[:, part * PART : (part + 1) * PART].astype(F32)


def pack_attn(place, a1, mix):
    rows, width = a1.shape
    parts = 2 + mix.shape[1] // PART
    return pl.pallas_call(
        pack_attn_kernel,
        grid_spec=pltpu.PrefetchScalarGridSpec(
            num_scalar_prefetch=1,
            grid=(1,),
            in_specs=[whole(a1.shape), whole(mix.shape)],
            out_specs=[whole((width // 2, rows)), whole((parts, PART, rows))],
            scratch_shapes=[pltpu.VMEM((width, rows), BF16)],
        ),
        out_shape=[
            jax.ShapeDtypeStruct((width // 2, rows), BF16),
            jax.ShapeDtypeStruct((parts, PART, rows), F32),
        ],
        compiler_params=params(4),
        cost_estimate=short_cost(),
        name="pack_attn",
    )(place, a1, mix)


def pieces_of(length):
    third = length // 3 // LANES * LANES
    return [(0, third), (third, third), (2 * third, length - 2 * third)]


def embed_kernel(
    kinds, pix_ref, wspec_ref, wrgb_ref, pick_ref, part_ref, mixed_ref,
    pix_buf, wspec_buf, wrgb_buf, pick_buf, pix_sem, big_sem, small_sem, *, item,
):
    rows, wide = pix_buf.shape
    spectral = kinds[item] == 1
    pieces = pieces_of(wide)
    own_rows = pl.ds(item * rows, rows)

    @pl.when(spectral)
    def _():
        copies = []
        for n, (first, size) in enumerate(pieces):
            span = pl.ds(first, size)
            copies.append(
                (
                    pltpu.make_async_copy(
                        pix_ref.at[own_rows, span], mixed_ref.at[:, span], pix_sem.at[n]
                    ),
                    pltpu.make_async_copy(wspec_ref.at[span], wspec_buf.at[span], big_sem.at[n]),
                )
            )
        for pair in copies:
            for copy in pair:
                copy.start()
        mixed_ref[:, wide:] = jnp.zeros((rows, wrgb_buf.shape[0]), BF16)
        for n, (first, size) in enumerate(pieces):
            for copy in copies[n]:
                copy.wait()
            term = nn(mixed_ref[:, first : first + size], wspec_buf[first : first + size, :])
            if n == 0:
                part_ref[...] = term
            else:
                part_ref[...] += term

    @pl.when(jnp.logical_not(spectral))
    def _():
        copies = []
        for n, (first, size) in enumerate(pieces):
            span = pl.ds(first, size)
            copies.append(
                (
                    pltpu.make_async_copy(
                        pix_ref.at[own_rows, span], pix_buf.at[:, span], pix_sem.at[n]
                    ),
                    pltpu.make_async_copy(pick_ref.at[span], pick_buf.at[span], big_sem.at[n]),
                )
            )
        for pair in copies:
            for copy in pair:
                copy.start()
        weights = pltpu.make_async_copy(wrgb_ref, wrgb_buf, small_sem)
        weights.start()
        mixed_ref[:, :wide] = jnp.zeros((rows, wide), BF16)
        total = None
        for n, (first, size) in enumerate(pieces):
            for copy in copies[n]:
                copy.wait()
            term = nn(pix_buf[:, first : first + size], pick_buf[first : first + size, :])
            total = term if total is None else total + term
        mixed_ref[:, wide:] = total.astype(BF16)
        weights.wait()
        part_ref[...] = nn(mixed_ref[:, wide:], wrgb_buf[...])


def embed(kinds, pixels, w_spectral, w_rgb, pick, item, rows):
    wide, width = w_spectral.shape
    narrow = w_rgb.shape[0]
    far = pl.BlockSpec(memory_space=pltpu.HBM)
    return pl.pallas_call(
        functools.partial(embed_kernel, item=item),
        grid_spec=pltpu.PrefetchScalarGridSpec(
            num_scalar_prefetch=1,
            grid=(1,),
            in_specs=[far, far, far, far],
            out_specs=[whole((rows, width)), whole((rows, wide + narrow))],
            scratch_shapes=[
                pltpu.VMEM((rows, wide), BF16),
                pltpu.VMEM((wide, width), BF16),
                pltpu.VMEM((narrow, width), BF16),
                pltpu.VMEM((wide, narrow), BF16),
                pltpu.SemaphoreType.DMA((3,)),
                pltpu.SemaphoreType.DMA((3,)),
                pltpu.SemaphoreType.DMA(()),
            ],
        ),
        out_shape=[
            jax.ShapeDtypeStruct((rows, width), F32),
            jax.ShapeDtypeStruct((rows, wide + narrow), BF16),
        ],
        compiler_params=params(58),
        cost_estimate=short_cost(),
        name="embed",
    )(kinds, pixels, w_spectral, w_rgb, pick)


def pair_masks(rows):
    lane = lax.broadcasted_iota(jnp.int32, (rows, LANES), 1)
    return lane < HEAD_DIM, lane >= HEAD_DIM


def only(mask, values):
    return jnp.where(mask, values, jnp.zeros_like(values))


def softmax_rows(query, key):
    scores = nt(query, key) * (HEAD_DIM**-0.5)
    expo = jnp.exp(scores - jnp.max(scores, -1, keepdims=True))
    return expo / jnp.sum(expo, -1, keepdims=True)


def attn_forward_kernel(
    part_ref, recv_ref, table_ref, gain_ref, bias_ref, wqkv_ref, qb_ref, vb_ref, wout_ref,
    x0_ref, a1_ref, qkv_ref, o_ref, opart_ref,
):
    quad = pl.program_id(0)
    rows, width = part_ref.shape

    @pl.when(quad == 0)
    def _():
        side = table_ref.shape[0]
        half = table_ref.shape[1]
        table = table_ref[...]
        by_row = jnp.broadcast_to(table[:, None, :], (side, side, half)).reshape(rows, half)
        by_col = jnp.broadcast_to(table[None, :, :], (side, side, half)).reshape(rows, half)
        left = part_ref[:, :half] + recv_ref[:, :half] + by_row
        right = part_ref[:, half:] + recv_ref[:, half:] + by_col
        x0_ref[:, :half] = left
        x0_ref[:, half:] = right
        normed, _inv = norm_parts(x0_ref[...])
        a1_ref[...] = (normed * gain_ref[...] + bias_ref[...]).astype(BF16)
        opart_ref[...] = jnp.zeros_like(opart_ref)

    a1 = a1_ref[...]
    query = (nn(a1, wqkv_ref[0]) + qb_ref[...]).astype(BF16)
    key = nn(a1, wqkv_ref[1]).astype(BF16)
    value = (nn(a1, wqkv_ref[2]) + vb_ref[...]).astype(BF16)
    qkv_ref[0] = query
    qkv_ref[1] = key
    qkv_ref[2] = value
    masks = pair_masks(rows)
    for pair in range(query.shape[1] // LANES):
        span = slice(pair * LANES, (pair + 1) * LANES)
        q2, k2, v2 = query[:, span], key[:, span], value[:, span]
        mixed = None
        for mask in masks:
            probs = softmax_rows(only(mask, q2), k2).astype(BF16)
            term = nn(probs, only(mask, v2))
            mixed = term if mixed is None else mixed + term
        o_ref[:, span] = mixed.astype(BF16)
    opart_ref[...] += nn(o_ref[...], wout_ref[...])


def attn_forward(part, recv, table, gain, bias, w_qkv, q_bias, v_bias, w_out):
    rows, width = part.shape
    heads_wide = w_out.shape[0]
    steps = heads_wide // QUAD
    return pl.pallas_call(
        attn_forward_kernel,
        grid=(steps,),
        in_specs=[
            whole(part.shape),
            whole(recv.shape),
            whole(table.shape),
            whole(gain.shape),
            whole(bias.shape),
            pl.BlockSpec((3, width, QUAD), lambda n: (0, 0, n)),
            pl.BlockSpec((1, QUAD), lambda n: (0, n)),
            pl.BlockSpec((1, QUAD), lambda n: (0, n)),
            pl.BlockSpec((QUAD, width), lambda n: (n, 0)),
        ],
        out_specs=[
            whole((rows, width)),
            whole((rows, width)),
            pl.BlockSpec((3, rows, QUAD), lambda n: (0, 0, n)),
            pl.BlockSpec((rows, QUAD), lambda n: (0, n)),
            whole((rows, width)),
        ],
        out_shape=[
            jax.ShapeDtypeStruct((rows, width), F32),
            jax.ShapeDtypeStruct((rows, width), BF16),
            jax.ShapeDtypeStruct((3, rows, heads_wide), BF16),
            jax.ShapeDtypeStruct((rows, heads_wide), BF16),
            jax.ShapeDtypeStruct((rows, width), F32),
        ],
        compiler_params=params(10),
        cost_estimate=long_cost(),
        name="attn_forward",
    )(part, recv, table, gain, bias, w_qkv, q_bias, v_bias, w_out)


def put_rows(refs, values, add):
    first = 0
    for ref in refs:
        rows = ref.shape[0]
        if add:
            ref[...] += values[first : first + rows]
        else:
            ref[...] = values[first : first + rows]
        first += rows


def joined(refs):
    values = [ref[...] for ref in refs]
    return values[0] if len(values) == 1 else jnp.concatenate(values, 0)


def attn_backward_kernel(place, *refs, parts):
    gpart_refs, refs = refs[: parts[0]], refs[parts[0] :]
    grecv_refs, refs = refs[: parts[1]], refs[parts[1] :]
    x1_ref, cot_ref, gain_ref, wout_ref, qkv_ref, wqkv_ref, *refs = refs
    dx1_ref, dya_ref, dqkv_ref, sums_ref, qvsum_ref, keep_ref, gone_ref, *da1_refs = refs[:-1]
    turned_ref = refs[-1]
    quad = pl.program_id(0)
    rows = x1_ref.shape[0]

    @pl.when(quad == 0)
    def _():
        normed, inverse = norm_parts(x1_ref[...])
        grad = joined(gpart_refs) + joined(grecv_refs)
        cot = cot_ref[...].astype(F32)
        dx1 = cot + norm_back(normed, inverse, grad, gain_ref[...])
        dx1_ref[...] = dx1
        dya = dx1.astype(BF16)
        dya_ref[...] = dya
        sums_ref[0:1, :] = column_sum(grad * normed)
        sums_ref[1:2, :] = column_sum(grad)
        sums_ref[2:3, :] = column_sum(dya.astype(F32))
        sums_ref[3:4, :] = column_sum(cot)
        sums_ref[4:8, :] = jnp.zeros((4, sums_ref.shape[1]), F32)
        turn(place, dya_ref, turned_ref, slice(None))
        spread(turned_ref, keep_ref, gone_ref)

    dmix = nt(dya_ref[...], wout_ref[...]).astype(BF16)
    scale = HEAD_DIM**-0.5
    masks = pair_masks(rows)
    for pair in range(dmix.shape[1] // LANES):
        span = slice(pair * LANES, (pair + 1) * LANES)
        q2, k2, v2, d2 = qkv_ref[0, :, span], qkv_ref[1, :, span], qkv_ref[2, :, span], dmix[:, span]
        totals = [None, None, None]
        for mask in masks:
            qm, km, dm = only(mask, q2), only(mask, k2), only(mask, d2)
            probs = softmax_rows(qm, k2)
            dprobs = nt(dm, v2)
            dot_row = jnp.sum(probs * dprobs, -1, keepdims=True)
            dscores = (probs * (dprobs - dot_row)).astype(BF16)
            terms = [nn(dscores, km), tn(dscores, qm), tn(probs.astype(BF16), dm)]
            totals = [t if o is None else o + t for o, t in zip(totals, terms)]
        dqkv_ref[0, :, span] = (totals[0] * scale).astype(BF16)
        dqkv_ref[1, :, span] = (totals[1] * scale).astype(BF16)
        dqkv_ref[2, :, span] = totals[2].astype(BF16)
    da1 = nt(dqkv_ref[0], wqkv_ref[0]) + nt(dqkv_ref[1], wqkv_ref[1]) + nt(dqkv_ref[2], wqkv_ref[2])

    @pl.when(quad == 0)
    def _():
        put_rows(da1_refs, da1, False)

    @pl.when(quad != 0)
    def _():
        put_rows(da1_refs, da1, True)

    steps = pl.num_programs(0)
    for plane in range(3):
        gone_ref[2 + plane * steps + quad] = dqkv_ref[plane].astype(F32)
    qvsum_ref[0:1, :] = column_sum(dqkv_ref[0].astype(F32))
    qvsum_ref[1:2, :] = column_sum(dqkv_ref[2].astype(F32))
    qvsum_ref[2:8, :] = jnp.zeros((6, qvsum_ref.shape[1]), F32)


def attn_backward(place, gparts, grecvs, x1, cotangent, gain, w_out, qkv, w_qkv, item, cuts):
    rows, width = x1.shape
    heads_wide = w_out.shape[0]
    steps = heads_wide // QUAD
    return pl.pallas_call(
        functools.partial(attn_backward_kernel, parts=(len(gparts), len(grecvs))),
        grid_spec=pltpu.PrefetchScalarGridSpec(
            num_scalar_prefetch=1,
            grid=(steps,),
            in_specs=[
                *[whole(v.shape) for v in (*gparts, *grecvs)],
                whole(x1.shape),
                pl.BlockSpec((rows, width), lambda n, *_: (item, 0)),
                whole(gain.shape),
                pl.BlockSpec((QUAD, width), lambda n, *_: (n, 0)),
                pl.BlockSpec((3, rows, QUAD), lambda n, *_: (0, 0, n)),
                pl.BlockSpec((3, width, QUAD), lambda n, *_: (0, 0, n)),
            ],
            out_specs=[
                whole((rows, width)),
                whole((rows, width)),
                pl.BlockSpec((3, rows, QUAD), lambda n, *_: (0, 0, n)),
                whole((8, width)),
                pl.BlockSpec((8, QUAD), lambda n, *_: (0, n)),
                whole((width // 2, rows)),
                whole((2 + 3 * steps, PART, rows)),
                *[whole((cut, width)) for cut in cuts],
            ],
            scratch_shapes=[pltpu.VMEM((width, rows), BF16)],
        ),
        out_shape=[
            jax.ShapeDtypeStruct((rows, width), F32),
            jax.ShapeDtypeStruct((rows, width), BF16),
            jax.ShapeDtypeStruct((3, rows, heads_wide), BF16),
            jax.ShapeDtypeStruct((8, width), F32),
            jax.ShapeDtypeStruct((8, heads_wide), F32),
            jax.ShapeDtypeStruct((width // 2, rows), BF16),
            jax.ShapeDtypeStruct((2 + 3 * steps, PART, rows), F32),
            *[jax.ShapeDtypeStruct((cut, width), F32) for cut in cuts],
        ],
        compiler_params=params(16),
        cost_estimate=long_cost(),
        name="attn_backward",
    )(place, *gparts, *grecvs, x1, cotangent, gain, w_out, qkv, w_qkv)


def mlp_kernel(
    place, x0_ref, opart_ref, orecv_ref, obias_ref, gain_ref, bias_ref, wfc1_ref, b1_ref, wfc2_ref, cot_ref,
    x1_ref, a2_ref, act_ref, dpre_ref, b1sum_ref, keep_ref, gact_ref, gpre_ref, *refs,
):
    da2_refs, turned_ref = refs[:-1], refs[-1]
    step = pl.program_id(0)

    @pl.when(step == 0)
    def _():
        x1_ref[...] = x0_ref[...] + (opart_ref[...] + orecv_ref[...] + obias_ref[...])
        normed, _inv = norm_parts(x1_ref[...])
        a2_ref[...] = (normed * gain_ref[...] + bias_ref[...]).astype(BF16)
        turn(place, a2_ref, turned_ref, slice(None))
        spread(turned_ref, keep_ref, gpre_ref)

    pre = nn(a2_ref[...], wfc1_ref[...]) + b1_ref[...]
    dact = nt(cot_ref[...], wfc2_ref[...])
    cdf = 0.5 * (1.0 + lax.erf(pre * (2.0**-0.5)))
    act = (pre * cdf).astype(BF16)
    act_ref[...] = act
    density = jnp.exp(-0.5 * pre * pre) * 0.3989422804014327
    dpre = (dact * (cdf + pre * density)).astype(BF16)
    dpre_ref[...] = dpre
    for part in range(act.shape[1] // PART):
        columns = slice(part * PART, (part + 1) * PART)
        gact_ref[part] = act[:, columns].astype(F32)
        gpre_ref[2 + step * (act.shape[1] // PART) + part] = dpre[:, columns].astype(F32)
    b1sum_ref[...] = column_sum(dpre.astype(F32))
    da2 = nt(dpre, wfc1_ref[...])

    @pl.when(step == 0)
    def _():
        put_rows(da2_refs, da2, False)

    @pl.when(step != 0)
    def _():
        put_rows(da2_refs, da2, True)


def mlp(
    place, x0, opart, orecv, out_bias, gain, bias, w_fc1, fc1_bias, w_fc2, cotangent, item, cuts
):
    rows, width = x0.shape
    hidden = w_fc1.shape[1]
    tile = 512
    parts = tile // PART
    row_tile = pl.BlockSpec((rows, tile), lambda n, *_: (0, n))
    gone = pl.BlockSpec((parts, rows, PART), lambda n, *_: (n, 0, 0))
    return pl.pallas_call(
        mlp_kernel,
        grid_spec=pltpu.PrefetchScalarGridSpec(
            num_scalar_prefetch=1,
            grid=(hidden // tile,),
            in_specs=[
                whole(x0.shape),
                whole(opart.shape),
                whole(orecv.shape),
                whole(out_bias.shape),
                whole(gain.shape),
                whole(bias.shape),
                pl.BlockSpec((width, tile), lambda n, *_: (0, n)),
                pl.BlockSpec((1, tile), lambda n, *_: (0, n)),
                pl.BlockSpec((tile, width), lambda n, *_: (n, 0)),
                pl.BlockSpec((rows, width), lambda n, *_: (item, 0)),
            ],
            out_specs=[
                whole((rows, width)),
                whole((rows, width)),
                row_tile,
                row_tile,
                pl.BlockSpec((1, tile), lambda n, *_: (0, n)),
                whole((width // 2, rows)),
                gone,
                whole((2 + hidden // PART, rows, PART)),
                *[whole((cut, width)) for cut in cuts],
            ],
            scratch_shapes=[pltpu.VMEM((width, rows), BF16)],
        ),
        out_shape=[
            jax.ShapeDtypeStruct((rows, width), F32),
            jax.ShapeDtypeStruct((rows, width), BF16),
            jax.ShapeDtypeStruct((rows, hidden), BF16),
            jax.ShapeDtypeStruct((rows, hidden), BF16),
            jax.ShapeDtypeStruct((1, hidden), F32),
            jax.ShapeDtypeStruct((width // 2, rows), BF16),
            jax.ShapeDtypeStruct((hidden // PART, rows, PART), F32),
            jax.ShapeDtypeStruct((2 + hidden // PART, rows, PART), F32),
            *[jax.ShapeDtypeStruct((cut, width), F32) for cut in cuts],
        ],
        compiler_params=params(14),
        cost_estimate=long_cost(),
        name="mlp",
    )(place, x0, opart, orecv, out_bias, gain, bias, w_fc1, fc1_bias, w_fc2, cotangent)


def mlp_out_kernel(act_ref, wfc2_ref, out_ref):
    out_ref[...] = nn(act_ref[...], wfc2_ref[...])


def mlp_out(act, w_fc2):
    rows, hidden = act.shape
    width = w_fc2.shape[1]
    tile = 512
    return pl.pallas_call(
        mlp_out_kernel,
        grid=(width // tile,),
        in_specs=[whole(act.shape), pl.BlockSpec((hidden, tile), lambda n: (0, n))],
        out_specs=pl.BlockSpec((rows, tile), lambda n: (0, n)),
        out_shape=jax.ShapeDtypeStruct((rows, width), F32),
        compiler_params=params(6),
        cost_estimate=long_cost(),
        name="mlp_out",
    )(act, w_fc2)


def first_norm_back_kernel(place, *refs, parts, riders):
    gpart_refs, refs = refs[: parts[0]], refs[parts[0] :]
    grecv_refs, refs = refs[: parts[1]], refs[parts[1] :]
    rider_refs, refs = refs[:riders], refs[riders:]
    x0_ref, dx1_ref, gain_ref, dx0_ref, sums_ref, keep_ref, gone_ref, block_ref, turned_ref = refs
    normed, inverse = norm_parts(x0_ref[...])
    grad = joined(gpart_refs) + joined(grecv_refs)
    dx0_ref[...] = (dx1_ref[...] + norm_back(normed, inverse, grad, gain_ref[...])).astype(BF16)
    sums_ref[0:1, :] = column_sum(grad * normed)
    sums_ref[1:2, :] = column_sum(grad)
    sums_ref[2:8, :] = jnp.zeros((6, sums_ref.shape[1]), F32)
    turn(place, dx0_ref, turned_ref, slice(None))
    middle = turned_ref.shape[0] // 2
    keep_ref[...] = turned_ref[:middle, :]
    gone_ref[:middle, :] = turned_ref[middle:, :].astype(F32)
    for chip in range(8):
        lanes = pl.ds(pl.multiple_of(place[chip] * LANES, LANES), LANES)
        for row in range(2):
            block_ref[chip : chip + 1, row * LANES : (row + 1) * LANES] = sums_ref[row : row + 1, lanes]
    gone_ref[middle : middle + 8, :] = block_ref[...]
    first = middle + 8
    for rider_ref in rider_refs:
        gone_ref[first : first + rider_ref.shape[0], :] = rider_ref[...]
        first += rider_ref.shape[0]


def first_norm_back(place, gparts, grecvs, x0, dx1, gain, estimate, riders=()):
    rows, width = x0.shape
    operands = (*gparts, *grecvs, *riders, x0, dx1, gain)
    extra = sum(v.shape[0] for v in riders)
    shapes = [
        jax.ShapeDtypeStruct((rows, width), BF16),
        jax.ShapeDtypeStruct((8, width), F32),
        jax.ShapeDtypeStruct((width // 2, rows), BF16),
        jax.ShapeDtypeStruct((width // 2 + 8 + extra, rows), F32),
        jax.ShapeDtypeStruct((8, 2 * LANES), F32),
    ]
    return pl.pallas_call(
        functools.partial(
            first_norm_back_kernel, parts=(len(gparts), len(grecvs)), riders=len(riders)
        ),
        grid_spec=pltpu.PrefetchScalarGridSpec(
            num_scalar_prefetch=1,
            grid=(1,),
            in_specs=[whole(v.shape) for v in operands],
            out_specs=[whole(v.shape) for v in shapes],
            scratch_shapes=[pltpu.VMEM((width, rows), BF16)],
        ),
        out_shape=shapes,
        compiler_params=params(10),
        cost_estimate=estimate,
        name="first_norm_back",
    )(place, *operands)


def pack_vectors_kernel(place, sa_ref, sb_ref, qa_ref, qb_ref, ba_ref, bb_ref, out_ref, *refs):
    sums_ref, qv_ref, hidden_ref = refs
    sums_ref[...] = sa_ref[...] + sb_ref[...]
    qv_ref[...] = qa_ref[...] + qb_ref[...]
    hidden_ref[...] = ba_ref[...] + bb_ref[...]
    out_ref[...] = jnp.zeros_like(out_ref)
    half = LANES // 2
    for pos in range(8):
        chip = place[pos]
        lanes = pl.ds(pl.multiple_of(chip * LANES, LANES), LANES)
        for row in range(4):
            first = row % 2 * LANES
            spot = 4 * pos + row // 2
            out_ref[spot : spot + 1, first : first + LANES] = sums_ref[row : row + 1, lanes]
        both = pl.ds(pl.multiple_of(chip // 2 * LANES, LANES), LANES)
        spot = 4 * pos + 2
        for row in range(2):
            pair = qv_ref[row : row + 1, both]
            own = jnp.where(chip % 2 == 0, pair[:, :half], pair[:, half:])
            out_ref[spot : spot + 1, row * half : (row + 1) * half] = own
        wide = pl.ds(pl.multiple_of(chip * 2 * LANES, 2 * LANES), 2 * LANES)
        out_ref[spot + 1 : spot + 2, :] = hidden_ref[0:1, wide]


def pack_vectors(place, sums, qv, hidden):
    operands = (*sums, *qv, *hidden)
    return pl.pallas_call(
        pack_vectors_kernel,
        grid_spec=pltpu.PrefetchScalarGridSpec(
            num_scalar_prefetch=1,
            grid=(1,),
            in_specs=[whole(v.shape) for v in operands],
            out_specs=whole((32, 2 * LANES)),
            scratch_shapes=[pltpu.VMEM(v[0].shape, F32) for v in (sums, qv, hidden)],
        ),
        out_shape=jax.ShapeDtypeStruct((32, 2 * LANES), F32),
        compiler_params=params(4),
        cost_estimate=short_cost(),
        name="pack_vectors",
    )(place, *operands)


def pixel_grad_kernel(kinds, grad_ref, wspec_ref, wrgb_ref, pick_ref, *refs, item):
    out_ref = refs[-1]
    spectral = kinds[item] == 1
    grad = grad_ref[...]
    wide = wspec_ref.shape[0]
    cut = (wide // 2 + LANES - 1) // LANES * LANES

    @pl.when(spectral)
    def _():
        out_ref[:, :cut] = nt(grad, wspec_ref[:cut, :]).astype(BF16)
        out_ref[:, cut:] = nt(grad, wspec_ref[cut:, :]).astype(BF16)

    @pl.when(jnp.logical_not(spectral))
    def _():
        small = nt(grad, wrgb_ref[...]).astype(BF16)
        out_ref[...] = nt(small, pick_ref[...]).astype(BF16)


def pixel_grad(kinds, grad, w_spectral, w_rgb, pick, item, items, filled=None):
    rows = grad.shape[0]
    wide, width = w_spectral.shape
    more = [] if filled is None else [filled]
    return pl.pallas_call(
        functools.partial(pixel_grad_kernel, item=item),
        grid_spec=pltpu.PrefetchScalarGridSpec(
            num_scalar_prefetch=1,
            grid=(1,),
            in_specs=[
                whole(grad.shape),
                whole(w_spectral.shape),
                whole(w_rgb.shape),
                whole(pick.shape),
            ]
            + [pl.BlockSpec(memory_space=pl.ANY)] * len(more),
            out_specs=pl.BlockSpec((rows, wide), lambda i, *_: (item, 0)),
        ),
        out_shape=jax.ShapeDtypeStruct((items * rows, wide), BF16),
        input_output_aliases={5: 0} if more else {},
        compiler_params=params(12),
        cost_estimate=long_cost(),
        name="pixel_grad",
    )(kinds, grad, w_spectral, w_rgb, pick, *more)


def gather_left(keep_refs, gone_refs, first, left_ref):
    rows = keep_refs[0].shape[-1]
    for pos, keep_ref in enumerate(keep_refs):
        left_ref[:, pos * rows : (pos + 1) * rows] = keep_ref[...]
    base = len(keep_refs) * rows
    for pos, gone_ref in enumerate(gone_refs):
        columns = slice(base + pos * rows, base + (pos + 1) * rows)
        if len(gone_ref.shape) == 2:
            left_ref[:, columns] = gone_ref[: left_ref.shape[0], :].astype(BF16)
            continue
        for part in range(2):
            left_ref[part * PART : (part + 1) * PART, columns] = gone_ref[first + part].astype(BF16)


def emit(left_ref, rights, send_ref, keep_ref, moves, columns=slice(None)):
    right = jnp.concatenate([r.astype(BF16) for r in rights], 0)
    total = nn(left_ref[...], right)
    half = LANES // 2
    for pos, block in enumerate(moves):
        out_ref = send_ref if pos < 4 else keep_ref
        out_ref[pos % 4, :half, columns] = total[block * half : (block + 1) * half]


def plain_grad_kernel(
    ka_ref, kb_ref, la_ref, lb_ref, ra_ref, rb_ref, oa_ref, ob_ref, *refs, moves, vectors
):
    send_ref, keep_ref, left_ref = refs[-3:]

    @pl.when(pl.program_id(0) == 0)
    def _():
        gather_left((ka_ref, kb_ref), (la_ref, lb_ref), 0, left_ref)

    for part in range(oa_ref.shape[0]):
        columns = slice(part * PART, (part + 1) * PART)
        rights = (ra_ref[:, columns], rb_ref[:, columns], oa_ref[part], ob_ref[part])
        emit(left_ref, rights, send_ref, keep_ref, moves, columns)
    if vectors:
        early_ref, sa_ref, sb_ref = refs[:3]
        half = LANES // 2
        middle = left_ref.shape[0]
        late = sa_ref[...] + sb_ref[...] + (la_ref[middle:, :] + lb_ref[middle:, :])
        for pos, block in enumerate(moves):
            out_ref = send_ref if pos < 4 else keep_ref
            out_ref[pos % 4, half:, :] = early_ref[block]

            @pl.when(pl.program_id(0) == 0)
            def _(out_ref=out_ref, pos=pos, block=block):
                out_ref[pos % 4, half + 1 : half + 2, : late.shape[1]] = late[block : block + 1]


def plain_grad(keeps, lefts, rights, others, moves, name, skip=0, columns=None, lead=0, vectors=()):
    half_width, rows = keeps[0][0].shape[-2:]
    columns = columns or rights[0].shape[1]
    wide = WIDE
    base = skip // (wide * PART)
    half = LANES // 2

    def keep_spec(array, item):
        if array.ndim == 2:
            return whole(array.shape)
        return pl.BlockSpec((None,) + array.shape[1:], lambda n: (item, 0, 0))

    right = pl.BlockSpec((rows, wide * PART), lambda n: (0, n + base))
    other = pl.BlockSpec((wide, rows, PART), lambda n: (n + base + lead // wide, 0, 0))
    height = half + 8 if vectors else half
    out = pl.BlockSpec((4, height, wide * PART), lambda n: (0, 0, n))
    shape = jax.ShapeDtypeStruct((4, height, columns), F32)

    def left_spec(array, item):
        if array.ndim == 2:
            return pl.BlockSpec((half_width + 8, rows), lambda n: (item, 0))
        return pl.BlockSpec((2, PART, rows), lambda n: (item, 0, 0))

    vector_specs = []
    if vectors:
        vector_specs = [pl.BlockSpec((8, 8, wide * PART), lambda n: (0, 0, n))]
        vector_specs += [whole(v.shape) for v in vectors[1:]]
    return pl.pallas_call(
        functools.partial(plain_grad_kernel, moves=moves, vectors=bool(vectors)),
        grid=(columns // (wide * PART),),
        in_specs=[keep_spec(*k) for k in keeps]
        + [left_spec(*v) for v in lefts]
        + [right, right, other, other]
        + vector_specs,
        out_specs=[out, out],
        scratch_shapes=[pltpu.VMEM((half_width, 4 * rows), BF16)],
        out_shape=[shape, shape],
        compiler_params=params(14),
        cost_estimate=short_cost(),
        name=name,
    )(*[k for k, _ in keeps], *[v for v, _ in lefts], *rights, *others, *vectors)


def attn_grad_kernel(
    aa_ref, ab_ref, ya_ref, yb_ref, fa_ref, fb_ref, ba_ref, bb_ref, da_ref, db_ref, ma_ref, mb_ref,
    send_ref, keep_ref, left_ref, *, moves,
):
    plane, step = pl.program_id(0), pl.program_id(1)
    steps = pl.num_programs(1)

    @pl.when((plane == 0) & (step == 0))
    def _():
        gather_left((aa_ref, ab_ref), (fa_ref, fb_ref), 0, left_ref)

    @pl.when((plane == 3) & (step == 0))
    def _():
        gather_left((ya_ref, yb_ref), (ba_ref, bb_ref), 0, left_ref)

    @pl.when(plane < 3)
    def _():
        spot = 2 + plane * steps + step
        emit(left_ref, (da_ref[...], db_ref[...], ba_ref[spot], bb_ref[spot]), send_ref, keep_ref, moves)

    @pl.when(plane == 3)
    def _():
        spot = 2 + step
        emit(left_ref, (ma_ref[...], mb_ref[...], fa_ref[spot], fb_ref[spot]), send_ref, keep_ref, moves)


def attn_grad(keep_a1, keep_dya, other_f, other_b, dqkv, mix, moves):
    half_width, rows = keep_a1[0].shape
    columns = mix[0].shape[1]
    half = LANES // 2
    side = whole((half_width, rows))
    plane = pl.BlockSpec((None, rows, PART), lambda p, n: (jnp.minimum(p, 2), 0, n))
    mixed = pl.BlockSpec((rows, PART), lambda p, n: (0, n))
    out = pl.BlockSpec((4, half, PART), lambda p, n: (0, p, n))
    shape = jax.ShapeDtypeStruct((4, 4 * half, columns), F32)
    return pl.pallas_call(
        functools.partial(attn_grad_kernel, moves=moves),
        grid=(4, columns // PART),
        in_specs=[side, side, side, side]
        + [whole(v.shape) for v in (*other_f, *other_b)]
        + [plane, plane, mixed, mixed],
        out_specs=[out, out],
        scratch_shapes=[pltpu.VMEM((half_width, 4 * rows), BF16)],
        out_shape=[shape, shape],
        compiler_params=params(8),
        cost_estimate=short_cost(),
        name="attn_grad",
    )(*keep_a1, *keep_dya, *other_f, *other_b, *dqkv, *mix)


def exchange(values, axis, bit, size):
    return lax.ppermute(values, axis, [(i, i ^ bit) for i in range(size)])


def swap(values):
    return exchange(values, "tensor", 1, 2)


def after(first, values):
    return lax.optimization_barrier((first, values))[1]


X_FIRST = (2, 4, 8)
Z_FIRST = (4, 2, 8)


def block_flips(bits):
    return [sum((1 - ((p >> (2 - n)) & 1)) * (bits[n] // 2) for n in range(3)) for p in range(8)]


def block_moves(bits):
    stands = block_flips(X_FIRST)
    return tuple(stands.index(f) for f in block_flips(bits))


def places():
    me = lax.axis_index("dp")
    flips = jnp.array(block_flips(X_FIRST), jnp.int32)
    return jnp.concatenate([(me // 2) ^ flips, (me % 2)[None]]).astype(jnp.int32)


class Halving:
    def __init__(self, send, keep, bits, size):
        self.keep, self.bits, self.size = keep, bits, size
        self.recvs = [exchange(send, "dp", bits[0], size)]
        self.left = keep.shape[0]
        self.sent = send

    def step(self, order):
        self.recvs[-1] = order.tie(self.recvs[-1])
        left = self.left
        count = max(left // 2, 1)
        total = self.keep.shape[0] - left
        value = self.keep[total : total + count]
        for recv in self.recvs:
            first = recv.shape[0] - left
            value = value + recv[first : first + count]
        order.mark(value)
        if left == 1:
            return value[0]
        self.recvs.append(exchange(value, "dp", self.bits[len(self.recvs)], self.size))
        self.left = left // 2
        return None


class Order:
    def __init__(self):
        self.last = None

    def tie(self, values):
        return values if self.last is None else after(self.last, values)

    def mark(self, values):
        self.last = values


def local(
    pixels, item_kinds, gsd_codes, w_spectral, w_rgb, ln1_gain, ln1_bias, w_qkv, q_bias, v_bias,
    w_out, out_bias, ln2_gain, ln2_bias, w_fc1, fc1_bias, w_fc2, fc2_bias, cotangent, *, size,
):
    items = item_kinds.shape[0]
    rows = pixels.shape[0] // items
    width = w_out.shape[1]
    wide = pixels.shape[1]
    narrow = w_rgb.shape[0]
    bands = wide // (narrow // 3)
    custom = size == 16

    def row(vector):
        return vector.reshape(1, -1)

    g1, c1, g2, c2 = row(ln1_gain), row(ln1_bias), row(ln2_gain), row(ln2_bias)
    qb, vb, ob, b1 = row(q_bias), row(v_bias), row(out_bias), row(fc1_bias)
    wqkv = jnp.transpose(w_qkv, (1, 0, 2))

    source = np.arange(wide)[:, None]
    target = np.arange(narrow)[None, :]
    pick = jnp.asarray((source == (target // 3) * bands + target % 3).astype(ml_dtypes.bfloat16))

    ratio = (gsd_codes.astype(F32) + 1.0) / 4.0
    quarter = width // 4
    frequency = 1.0 / 10000.0 ** (jnp.arange(quarter).astype(F32) / quarter)
    spot = jnp.arange(GRID).astype(F32)
    angle = ratio[:, None, None] * spot[None, :, None] * frequency[None, None, :]
    tables = jnp.concatenate([jnp.sin(angle), jnp.cos(angle)], -1)

    def scatter(values):
        return lax.psum_scatter(values, "dp", scatter_dimension=0, tiled=True)

    def both(left, right):
        return sum(tn(left[i], right[i]) for i in range(items))

    order = Order()
    gate = None

    def send(values, wait=True):
        nonlocal gate
        if gate is not None:
            values = after(gate, values)
        gate = swap(values)
        return gate

    place = places() if custom else jnp.arange(9, dtype=jnp.int32) % 8
    move_x, move_z = block_moves(X_FIRST), block_moves(Z_FIRST)

    def other(values):
        return exchange(values, "dp", 1, size) if custom else values

    cut = rows * 3 // 8 // 8 * 8
    cuts = [(cut, rows - cut)] + [(rows,)] * (items - 1)

    def settle(values):
        values = order.tie(values)
        order.mark(jax.tree.leaves(values)[0])
        return values

    none = [None] * items
    part, mixed, erecv, fwd, orecv, ffn, grecv, bwd, arecv, last, ycot = (list(none) for _ in range(11))
    gmix, pk, gfwd, gact, gpre, gbwd, gdx0, da1, da2 = (list(none) for _ in range(9))

    for i in range(items):
        part[i], mixed[i] = embed(order.tie(item_kinds), pixels, w_spectral, w_rgb, pick, i, rows)
        order.mark(part[i])
        erecv[i] = send(part[i])
    keep_cot, gone_cot = turn_cot(order.tie(place), cotangent, rows)
    order.mark(gone_cot)
    gone_mix = []
    for i in range(items):
        gone_mix.append(pack(order.tie(mixed[i])))
        order.mark(gone_mix[i])
    gcot = other(gone_cot)
    gmix = [other(v) for v in gone_mix]
    for i in range(items):
        fwd[i] = attn_forward(
            part[i], erecv[i], tables[i], order.tie(g1), c1, wqkv, qb, vb, w_out
        )
        order.mark(fwd[i][4])
        orecv[i] = send(fwd[i][4])
        if i == 0:
            gcot = settle(gcot)
        else:
            gmix = [settle(v) for v in gmix]
        pk[i] = pack_attn(order.tie(place), fwd[i][1], fwd[i][3])
        order.mark(pk[i][1])
        gfwd[i] = other(pk[i][1])
    x0, a1, qkv, mix, _ = zip(*fwd)
    for i in range(items):
        ffn[i] = mlp(
            place, x0[i], fwd[i][4], orecv[i], order.tie(ob), g2, c2, w_fc1, b1, w_fc2, cotangent, i,
            cuts[i],
        )
        da2[i] = ffn[i][8:]
        order.mark(da2[i][0])
        if i == 0:
            grecv[i] = [send(v) for v in da2[i]]
        gact[i] = other(ffn[i][6])
        gpre[i] = other(ffn[i][7])
        if i == 0:
            gfwd = [settle(v) for v in gfwd]
        else:
            grecv[0][0] = settle(grecv[0][0])
            gact[0], gpre[0] = settle((gact[0], gpre[0]))
            ycot[1] = mlp_out(order.tie(ffn[1][2]), w_fc2)
            order.mark(ycot[1])
    x1, a2, act, dpre, b1sum, ka2 = list(zip(*[v[:6] for v in ffn]))
    if custom:
        gact[1] = order.tie(gact[1])
        fc2_h = Halving(
            *plain_grad(
                [(keep_cot, 0), (keep_cot, 1)], [(gcot, 0), (gcot, 1)], act, gact, move_x, "fc2_grad"
            ),
            X_FIRST, size,
        )
        order.mark(fc2_h.sent)
        gpre[1] = order.tie(gpre[1])
        fc1_h = Halving(
            *plain_grad(
                [(ka2[0], 0), (ka2[1], 0)], [(gpre[0], 0), (gpre[1], 0)], dpre, gpre, move_z, "fc1_grad", lead=2
            ),
            Z_FIRST, size,
        )
        order.mark(fc1_h.sent)
    grecv[1] = [send(order.tie(da2[1][0]))]
    for i in range(items):
        bwd[i] = attn_backward(
            place, da2[i], grecv[i], x1[i], cotangent, order.tie(g2), w_out, qkv[i], wqkv, i, cuts[i]
        )
        da1[i] = bwd[i][7:]
        order.mark(da1[i][0])
        if i == 0:
            arecv[i] = [send(v) for v in da1[i]]
        else:
            arecv[0][0] = settle(arecv[0][0])
            gbwd = [other(order.tie(bwd[0][6])), other(bwd[1][6])]
            ycot[0] = mlp_out(order.tie(ffn[0][2]), w_fc2)
            order.mark(ycot[0])
    dx1, dya, dqkv, sums2, qvsum, kdya = list(zip(*[v[:6] for v in bwd]))
    if custom:
        fc2_h.step(order)
        gbwd = [order.tie(v) for v in gbwd]
        att_h = Halving(
            *attn_grad([v[0] for v in pk], kdya, gfwd, gbwd, dqkv, mix, move_x), X_FIRST, size
        )
        order.mark(att_h.sent)
        fc1_h.step(order)
    arecv[1] = [send(order.tie(da1[1][0]))]
    riders = ()
    for i in range(items):
        estimate = long_cost() if i == 0 else short_cost()
        last[i] = first_norm_back(
            place, da1[i], arecv[i], x0[i], dx1[i], order.tie(g1), estimate, riders
        )
        order.mark(last[i][0])
        if custom and i == 0:
            fc2_h.step(order)
        if custom and i == 0:
            cube = pack_vectors(order.tie(place), sums2, qvsum, b1sum)
            order.mark(cube)
            riders = (last[0][3], cube)
    summed = list(none)
    dx0, sums1, kdx0, gone, blocks = zip(*last)
    pixels_grad = pixel_grad(order.tie(item_kinds), dx0[0], w_spectral, w_rgb, pick, 0, items)
    order.mark(pixels_grad)
    if custom:
        mid = mixed[0].shape[1] // 2
        gdx0 = order.tie(other(gone[1]))
        sides = ([(kdx0[0], 0), (kdx0[1], 0)], [(gdx0, 1), (gdx0, 0)], mixed, gmix)
        embx_h = Halving(*plain_grad(*sides, move_x, "embed_grad_a", 0, mid), X_FIRST, size)
        order.mark(embx_h.sent)
        sides[3][1] = order.tie(gmix[1])
        cube = (cube + order.tie(gdx0)[-cube.shape[0] :]).reshape(8, 1, -1)
        cube = jnp.pad(cube, ((0, 0), (0, 7), (0, 0)))
        embz_h = Halving(
            *plain_grad(*sides, move_z, "embed_grad_b", mid, mid, vectors=(cube, *blocks)),
            Z_FIRST, size,
        )
        order.mark(embz_h.sent)
    pixels_grad = pixel_grad(
        order.tie(item_kinds), dx0[1], w_spectral, w_rgb, pick, 1, items, pixels_grad
    )
    order.mark(pixels_grad)
    if custom:
        fc1_h.step(order)
        att_h.step(order)
        embz_h.step(order)
        embx_h.step(order)
        fc2_g = fc2_h.step(order)
        fc1_g = fc1_h.step(order)
    summed[0] = send(order.tie(ycot[0]))
    if custom:
        embz_h.step(order)
        att_h.step(order)
    summed[0] = settle(summed[0])
    summed[1] = send(order.tie(ycot[1]))
    if custom:
        embx_h.step(order)
        embz_g = embz_h.step(order)
    summed[1] = settle(summed[1])
    block_out = jnp.concatenate(
        [(x1[i] + (ycot[i] + summed[i] + fc2_bias)).astype(BF16) for i in range(items)], 0
    )
    order.mark(block_out)
    if custom:
        att_g = att_h.step(order)
        embx_g = embx_h.step(order)
        shard = width // size
        core = lax.axis_index("dp") % 2
        spans = [(shard, row * LANES, LANES) for row in range(4)]
        spans += [(shard, 4 * LANES + row * LANES // 2, LANES // 2) for row in range(2)]
        spans += [(shard, 6 * LANES, 2 * LANES)]
        spans += [(shard + 1, row * LANES, LANES) for row in range(2)]
        outs = []
        for row, first, length in spans:
            low = embz_g[row, first : first + length // 2]
            high = embz_g[row, first + length // 2 : first + length]
            outs.append(jnp.where(core == 0, low, high))
        ln2_g, ln2_b, ob_g, b2_g, q_g, v_g, b1_g, ln1_g, ln1_b = outs
        embz_g = embz_g[:shard]
        emb_g = jnp.concatenate([embx_g, embz_g], 1)
        att_g = att_g.reshape(4, shard, -1)
        qkv_grad = jnp.transpose(att_g[:3], (1, 0, 2))
        out_grad = att_g[3].T
    else:
        cot = [cotangent[i * rows : (i + 1) * rows] for i in range(items)]
        fc2_g = scatter(both(cot, act))
        fc1_g = scatter(both(a2, dpre))
        emb_g = scatter(both(dx0, mixed))
        qkv_grad = scatter(
            sum(
                lax.dot_general(
                    a1[i], dqkv[i], (((0,), (1,)), ((), ())), preferred_element_type=F32
                )
                for i in range(items)
            )
        )
        out_grad = scatter(both(dya, mix)).T
        totals = [v[0] + v[1] for v in (sums2, qvsum, b1sum, sums1)]
        rows_of = [(0, 0), (0, 1), (0, 2), (0, 3), (1, 0), (1, 1), (2, 0), (3, 0), (3, 1)]
        outs = [scatter(totals[n][row]) for n, row in rows_of]
        ln2_g, ln2_b, ob_g, b2_g, q_g, v_g, b1_g, ln1_g, ln1_b = outs
    spectral_grad = emb_g[:, :wide].T
    rgb_grad = emb_g[:, wide:].T
    return (
        block_out, pixels_grad, spectral_grad, rgb_grad, ln1_g, ln1_b, qkv_grad, q_g, v_g, out_grad,
        ob_g, ln2_g, ln2_b, fc1_g, b1_g, fc2_g.T, b2_g,
    )


def solution(mesh):
    in_specs = (
        P("dp", "tensor"),
        P("dp"),
        P("dp"),
        P("tensor", None),
        P("tensor", None),
        P(),
        P(),
        P(None, None, "tensor"),
        P("tensor"),
        P("tensor"),
        P("tensor", None),
        P(),
        P(),
        P(),
        P(None, "tensor"),
        P("tensor"),
        P("tensor", None),
        P(),
        P("dp", None),
    )
    out_specs = (
        P("dp", None),
        P("dp", "tensor"),
        P("tensor", "dp"),
        P("tensor", "dp"),
        P("dp"),
        P("dp"),
        P("dp", None, "tensor"),
        P(("tensor", "dp")),
        P(("tensor", "dp")),
        P("tensor", "dp"),
        P("dp"),
        P("dp"),
        P("dp"),
        P("dp", "tensor"),
        P(("tensor", "dp")),
        P("tensor", "dp"),
        P("dp"),
    )
    body = functools.partial(local, size=mesh.shape["dp"])
    return jax.shard_map(body, mesh=mesh, in_specs=in_specs, out_specs=out_specs, check_vma=False)
```

```python
import functools

import jax
import jax.numpy as jnp
import ml_dtypes
import numpy as np
from jax import lax
from jax.experimental import pallas as pl
from jax.experimental.pallas import tpu as pltpu
from jax.sharding import PartitionSpec as P

HEAD_DIM = 64
GRID = 16
EPS = 1e-06
F32 = jnp.float32
BF16 = jnp.bfloat16
LANES = 128
MIB = 1024 * 1024
QUAD = 256
PART = 256
WIDE = 2


def nn(left, right):
    return lax.dot_general(left, right, (((1,), (0,)), ((), ())), preferred_element_type=F32)


def nt(left, right):
    return lax.dot_general(left, right, (((1,), (1,)), ((), ())), preferred_element_type=F32)


def tn(left, right):
    return lax.dot_general(left, right, (((0,), (0,)), ((), ())), preferred_element_type=F32)


def params(mib):
    return pltpu.CompilerParams(vmem_limit_bytes=mib * MIB)


def short_cost():
    return pl.CostEstimate(flops=1000, bytes_accessed=1000, transcendentals=0)


def long_cost():
    return pl.CostEstimate(flops=int(1e11), bytes_accessed=1000, transcendentals=0)


def whole(shape):
    return pl.BlockSpec(shape, lambda *_: (0,) * len(shape), pipeline_mode=pl.Buffered(1))


def norm_parts(values):
    center = values - jnp.mean(values, -1, keepdims=True)
    spread = jnp.mean(center * center, -1, keepdims=True)
    inverse = lax.rsqrt(spread + EPS)
    return center * inverse, inverse


def norm_back(normed, inverse, grad, gain):
    scaled = grad * gain
    mean_scaled = jnp.mean(scaled, -1, keepdims=True)
    mean_cross = jnp.mean(scaled * normed, -1, keepdims=True)
    return inverse * (scaled - mean_scaled - normed * mean_cross)


def column_sum(values):
    return jnp.sum(values, 0, keepdims=True)


def turn(place, source_ref, turned_ref, columns):
    chips = turned_ref.shape[0] // LANES
    half = LANES // 2
    core = place[chips]
    low = pl.multiple_of(core * (chips * half), half)
    high = pl.multiple_of((1 - core) * (chips * half), half)
    for chip in range(chips):
        lanes = pl.ds(pl.multiple_of(place[chip] * LANES, LANES), LANES)
        block = source_ref[:, lanes].T
        turned_ref[pl.ds(low + chip * half, half), columns] = block[:half]
        turned_ref[pl.ds(high + chip * half, half), columns] = block[half:]


def spread(turned_ref, keep_ref, gone_ref, first=0):
    middle = turned_ref.shape[0] // 2
    keep_ref[...] = turned_ref[:middle, :]
    for part in range(2):
        start = middle + part * PART
        gone_ref[first + part] = turned_ref[start : start + PART, :].astype(F32)


def turn_cot_kernel(place, cot_ref, keep_ref, gone_ref, turned_ref):
    turn(place, cot_ref, turned_ref, slice(None))
    spread(turned_ref, keep_ref, gone_ref)


def turn_cot(place, cotangent, rows):
    width = cotangent.shape[1]
    items = cotangent.shape[0] // rows
    return pl.pallas_call(
        turn_cot_kernel,
        grid_spec=pltpu.PrefetchScalarGridSpec(
            num_scalar_prefetch=1,
            grid=(items,),
            in_specs=[pl.BlockSpec((rows, width), lambda i, *_: (i, 0))],
            out_specs=[
                pl.BlockSpec((None, width // 2, rows), lambda i, *_: (i, 0, 0)),
                pl.BlockSpec((2, PART, rows), lambda i, *_: (i, 0, 0)),
            ],
            scratch_shapes=[pltpu.VMEM((width, rows), BF16)],
        ),
        out_shape=[
            jax.ShapeDtypeStruct((items, width // 2, rows), BF16),
            jax.ShapeDtypeStruct((2 * items, PART, rows), F32),
        ],
        compiler_params=params(4),
        cost_estimate=short_cost(),
        name="turn_cotangent",
    )(place, cotangent)


def pack_kernel(values_ref, out_ref):
    out_ref[0] = values_ref[...].astype(F32)


def pack(values):
    rows, columns = values.shape
    return pl.pallas_call(
        pack_kernel,
        grid=(columns // PART,),
        in_specs=[pl.BlockSpec((rows, PART), lambda n: (0, n))],
        out_specs=pl.BlockSpec((1, rows, PART), lambda n: (n, 0, 0)),
        out_shape=jax.ShapeDtypeStruct((columns // PART, rows, PART), F32),
        compiler_params=params(4),
        cost_estimate=short_cost(),
        name="pack_pixels",
    )(values)


def pack_attn_kernel(place, a1_ref, o_ref, keep_ref, gone_ref, turned_ref):
    turn(place, a1_ref, turned_ref, slice(None))
    spread(turned_ref, keep_ref, gone_ref)
    for part in range(o_ref.shape[1] // PART):
        gone_ref[2 + part] = o_ref[:, part * PART : (part + 1) * PART].astype(F32)


def pack_attn(place, a1, mix):
    rows, width = a1.shape
    parts = 2 + mix.shape[1] // PART
    return pl.pallas_call(
        pack_attn_kernel,
        grid_spec=pltpu.PrefetchScalarGridSpec(
            num_scalar_prefetch=1,
            grid=(1,),
            in_specs=[whole(a1.shape), whole(mix.shape)],
            out_specs=[whole((width // 2, rows)), whole((parts, PART, rows))],
            scratch_shapes=[pltpu.VMEM((width, rows), BF16)],
        ),
        out_shape=[
            jax.ShapeDtypeStruct((width // 2, rows), BF16),
            jax.ShapeDtypeStruct((parts, PART, rows), F32),
        ],
        compiler_params=params(4),
        cost_estimate=short_cost(),
        name="pack_attn",
    )(place, a1, mix)


def pieces_of(length):
    third = length // 3 // LANES * LANES
    return [(0, third), (third, third), (2 * third, length - 2 * third)]


def embed_kernel(
    kinds, pix_ref, wspec_ref, wrgb_ref, pick_ref, part_ref, mixed_ref,
    pix_buf, wspec_buf, wrgb_buf, pick_buf, pix_sem, big_sem, small_sem, *, item,
):
    rows, wide = pix_buf.shape
    spectral = kinds[item] == 1
    pieces = pieces_of(wide)
    own_rows = pl.ds(item * rows, rows)

    @pl.when(spectral)
    def _():
        copies = []
        for n, (first, size) in enumerate(pieces):
            span = pl.ds(first, size)
            copies.append(
                (
                    pltpu.make_async_copy(
                        pix_ref.at[own_rows, span], mixed_ref.at[:, span], pix_sem.at[n]
                    ),
                    pltpu.make_async_copy(wspec_ref.at[span], wspec_buf.at[span], big_sem.at[n]),
                )
            )
        for pair in copies:
            for copy in pair:
                copy.start()
        mixed_ref[:, wide:] = jnp.zeros((rows, wrgb_buf.shape[0]), BF16)
        for n, (first, size) in enumerate(pieces):
            for copy in copies[n]:
                copy.wait()
            term = nn(mixed_ref[:, first : first + size], wspec_buf[first : first + size, :])
            if n == 0:
                part_ref[...] = term
            else:
                part_ref[...] += term

    @pl.when(jnp.logical_not(spectral))
    def _():
        copies = []
        for n, (first, size) in enumerate(pieces):
            span = pl.ds(first, size)
            copies.append(
                (
                    pltpu.make_async_copy(
                        pix_ref.at[own_rows, span], pix_buf.at[:, span], pix_sem.at[n]
                    ),
                    pltpu.make_async_copy(pick_ref.at[span], pick_buf.at[span], big_sem.at[n]),
                )
            )
        for pair in copies:
            for copy in pair:
                copy.start()
        weights = pltpu.make_async_copy(wrgb_ref, wrgb_buf, small_sem)
        weights.start()
        mixed_ref[:, :wide] = jnp.zeros((rows, wide), BF16)
        total = None
        for n, (first, size) in enumerate(pieces):
            for copy in copies[n]:
                copy.wait()
            term = nn(pix_buf[:, first : first + size], pick_buf[first : first + size, :])
            total = term if total is None else total + term
        mixed_ref[:, wide:] = total.astype(BF16)
        weights.wait()
        part_ref[...] = nn(mixed_ref[:, wide:], wrgb_buf[...])


def embed(kinds, pixels, w_spectral, w_rgb, pick, item, rows):
    wide, width = w_spectral.shape
    narrow = w_rgb.shape[0]
    far = pl.BlockSpec(memory_space=pltpu.HBM)
    return pl.pallas_call(
        functools.partial(embed_kernel, item=item),
        grid_spec=pltpu.PrefetchScalarGridSpec(
            num_scalar_prefetch=1,
            grid=(1,),
            in_specs=[far, far, far, far],
            out_specs=[whole((rows, width)), whole((rows, wide + narrow))],
            scratch_shapes=[
                pltpu.VMEM((rows, wide), BF16),
                pltpu.VMEM((wide, width), BF16),
                pltpu.VMEM((narrow, width), BF16),
                pltpu.VMEM((wide, narrow), BF16),
                pltpu.SemaphoreType.DMA((3,)),
                pltpu.SemaphoreType.DMA((3,)),
                pltpu.SemaphoreType.DMA(()),
            ],
        ),
        out_shape=[
            jax.ShapeDtypeStruct((rows, width), F32),
            jax.ShapeDtypeStruct((rows, wide + narrow), BF16),
        ],
        compiler_params=params(58),
        cost_estimate=short_cost(),
        name="embed",
    )(kinds, pixels, w_spectral, w_rgb, pick)


def pair_masks(rows):
    lane = lax.broadcasted_iota(jnp.int32, (rows, LANES), 1)
    return lane < HEAD_DIM, lane >= HEAD_DIM


def only(mask, values):
    return jnp.where(mask, values, jnp.zeros_like(values))


def softmax_rows(query, key):
    scores = nt(query, key) * (HEAD_DIM**-0.5)
    expo = jnp.exp(scores - jnp.max(scores, -1, keepdims=True))
    return expo / jnp.sum(expo, -1, keepdims=True)


def attn_forward_kernel(
    part_ref, recv_ref, table_ref, gain_ref, bias_ref, wqkv_ref, qb_ref, vb_ref, wout_ref,
    x0_ref, a1_ref, qkv_ref, o_ref, opart_ref,
):
    quad = pl.program_id(0)
    rows, width = part_ref.shape

    @pl.when(quad == 0)
    def _():
        side = table_ref.shape[0]
        half = table_ref.shape[1]
        table = table_ref[...]
        by_row = jnp.broadcast_to(table[:, None, :], (side, side, half)).reshape(rows, half)
        by_col = jnp.broadcast_to(table[None, :, :], (side, side, half)).reshape(rows, half)
        left = part_ref[:, :half] + recv_ref[:, :half] + by_row
        right = part_ref[:, half:] + recv_ref[:, half:] + by_col
        x0_ref[:, :half] = left
        x0_ref[:, half:] = right
        normed, _inv = norm_parts(x0_ref[...])
        a1_ref[...] = (normed * gain_ref[...] + bias_ref[...]).astype(BF16)
        opart_ref[...] = jnp.zeros_like(opart_ref)

    a1 = a1_ref[...]
    query = (nn(a1, wqkv_ref[0]) + qb_ref[...]).astype(BF16)
    key = nn(a1, wqkv_ref[1]).astype(BF16)
    value = (nn(a1, wqkv_ref[2]) + vb_ref[...]).astype(BF16)
    qkv_ref[0] = query
    qkv_ref[1] = key
    qkv_ref[2] = value
    masks = pair_masks(rows)
    for pair in range(query.shape[1] // LANES):
        span = slice(pair * LANES, (pair + 1) * LANES)
        q2, k2, v2 = query[:, span], key[:, span], value[:, span]
        mixed = None
        for mask in masks:
            probs = softmax_rows(only(mask, q2), k2).astype(BF16)
            term = nn(probs, only(mask, v2))
            mixed = term if mixed is None else mixed + term
        o_ref[:, span] = mixed.astype(BF16)
    opart_ref[...] += nn(o_ref[...], wout_ref[...])


def attn_forward(part, recv, table, gain, bias, w_qkv, q_bias, v_bias, w_out):
    rows, width = part.shape
    heads_wide = w_out.shape[0]
    steps = heads_wide // QUAD
    return pl.pallas_call(
        attn_forward_kernel,
        grid=(steps,),
        in_specs=[
            whole(part.shape),
            whole(recv.shape),
            whole(table.shape),
            whole(gain.shape),
            whole(bias.shape),
            pl.BlockSpec((3, width, QUAD), lambda n: (0, 0, n)),
            pl.BlockSpec((1, QUAD), lambda n: (0, n)),
            pl.BlockSpec((1, QUAD), lambda n: (0, n)),
            pl.BlockSpec((QUAD, width), lambda n: (n, 0)),
        ],
        out_specs=[
            whole((rows, width)),
            whole((rows, width)),
            pl.BlockSpec((3, rows, QUAD), lambda n: (0, 0, n)),
            pl.BlockSpec((rows, QUAD), lambda n: (0, n)),
            whole((rows, width)),
        ],
        out_shape=[
            jax.ShapeDtypeStruct((rows, width), F32),
            jax.ShapeDtypeStruct((rows, width), BF16),
            jax.ShapeDtypeStruct((3, rows, heads_wide), BF16),
            jax.ShapeDtypeStruct((rows, heads_wide), BF16),
            jax.ShapeDtypeStruct((rows, width), F32),
        ],
        compiler_params=params(10),
        cost_estimate=long_cost(),
        name="attn_forward",
    )(part, recv, table, gain, bias, w_qkv, q_bias, v_bias, w_out)


def put_rows(refs, values, add):
    first = 0
    for ref in refs:
        rows = ref.shape[0]
        if add:
            ref[...] += values[first : first + rows]
        else:
            ref[...] = values[first : first + rows]
        first += rows


def joined(refs):
    values = [ref[...] for ref in refs]
    return values[0] if len(values) == 1 else jnp.concatenate(values, 0)


def attn_backward_kernel(place, *refs, parts):
    gpart_refs, refs = refs[: parts[0]], refs[parts[0] :]
    grecv_refs, refs = refs[: parts[1]], refs[parts[1] :]
    x1_ref, cot_ref, gain_ref, wout_ref, qkv_ref, wqkv_ref, *refs = refs
    dx1_ref, dya_ref, dqkv_ref, sums_ref, qvsum_ref, keep_ref, gone_ref, *da1_refs = refs[:-1]
    turned_ref = refs[-1]
    quad = pl.program_id(0)
    rows = x1_ref.shape[0]

    @pl.when(quad == 0)
    def _():
        normed, inverse = norm_parts(x1_ref[...])
        grad = joined(gpart_refs) + joined(grecv_refs)
        cot = cot_ref[...].astype(F32)
        dx1 = cot + norm_back(normed, inverse, grad, gain_ref[...])
        dx1_ref[...] = dx1
        dya = dx1.astype(BF16)
        dya_ref[...] = dya
        sums_ref[0:1, :] = column_sum(grad * normed)
        sums_ref[1:2, :] = column_sum(grad)
        sums_ref[2:3, :] = column_sum(dya.astype(F32))
        sums_ref[3:4, :] = column_sum(cot)
        sums_ref[4:8, :] = jnp.zeros((4, sums_ref.shape[1]), F32)
        turn(place, dya_ref, turned_ref, slice(None))
        spread(turned_ref, keep_ref, gone_ref)

    dmix = nt(dya_ref[...], wout_ref[...]).astype(BF16)
    scale = HEAD_DIM**-0.5
    masks = pair_masks(rows)
    for pair in range(dmix.shape[1] // LANES):
        span = slice(pair * LANES, (pair + 1) * LANES)
        q2, k2, v2, d2 = qkv_ref[0, :, span], qkv_ref[1, :, span], qkv_ref[2, :, span], dmix[:, span]
        totals = [None, None, None]
        for mask in masks:
            qm, km, dm = only(mask, q2), only(mask, k2), only(mask, d2)
            probs = softmax_rows(qm, k2)
            dprobs = nt(dm, v2)
            dot_row = jnp.sum(probs * dprobs, -1, keepdims=True)
            dscores = (probs * (dprobs - dot_row)).astype(BF16)
            terms = [nn(dscores, km), tn(dscores, qm), tn(probs.astype(BF16), dm)]
            totals = [t if o is None else o + t for o, t in zip(totals, terms)]
        dqkv_ref[0, :, span] = (totals[0] * scale).astype(BF16)
        dqkv_ref[1, :, span] = (totals[1] * scale).astype(BF16)
        dqkv_ref[2, :, span] = totals[2].astype(BF16)
    da1 = nt(dqkv_ref[0], wqkv_ref[0]) + nt(dqkv_ref[1], wqkv_ref[1]) + nt(dqkv_ref[2], wqkv_ref[2])

    @pl.when(quad == 0)
    def _():
        put_rows(da1_refs, da1, False)

    @pl.when(quad != 0)
    def _():
        put_rows(da1_refs, da1, True)

    steps = pl.num_programs(0)
    for plane in range(3):
        gone_ref[2 + plane * steps + quad] = dqkv_ref[plane].astype(F32)
    qvsum_ref[0:1, :] = column_sum(dqkv_ref[0].astype(F32))
    qvsum_ref[1:2, :] = column_sum(dqkv_ref[2].astype(F32))
    qvsum_ref[2:8, :] = jnp.zeros((6, qvsum_ref.shape[1]), F32)


def attn_backward(place, gparts, grecvs, x1, cotangent, gain, w_out, qkv, w_qkv, item, cuts):
    rows, width = x1.shape
    heads_wide = w_out.shape[0]
    steps = heads_wide // QUAD
    return pl.pallas_call(
        functools.partial(attn_backward_kernel, parts=(len(gparts), len(grecvs))),
        grid_spec=pltpu.PrefetchScalarGridSpec(
            num_scalar_prefetch=1,
            grid=(steps,),
            in_specs=[
                *[whole(v.shape) for v in (*gparts, *grecvs)],
                whole(x1.shape),
                pl.BlockSpec((rows, width), lambda n, *_: (item, 0)),
                whole(gain.shape),
                pl.BlockSpec((QUAD, width), lambda n, *_: (n, 0)),
                pl.BlockSpec((3, rows, QUAD), lambda n, *_: (0, 0, n)),
                pl.BlockSpec((3, width, QUAD), lambda n, *_: (0, 0, n)),
            ],
            out_specs=[
                whole((rows, width)),
                whole((rows, width)),
                pl.BlockSpec((3, rows, QUAD), lambda n, *_: (0, 0, n)),
                whole((8, width)),
                pl.BlockSpec((8, QUAD), lambda n, *_: (0, n)),
                whole((width // 2, rows)),
                whole((2 + 3 * steps, PART, rows)),
                *[whole((cut, width)) for cut in cuts],
            ],
            scratch_shapes=[pltpu.VMEM((width, rows), BF16)],
        ),
        out_shape=[
            jax.ShapeDtypeStruct((rows, width), F32),
            jax.ShapeDtypeStruct((rows, width), BF16),
            jax.ShapeDtypeStruct((3, rows, heads_wide), BF16),
            jax.ShapeDtypeStruct((8, width), F32),
            jax.ShapeDtypeStruct((8, heads_wide), F32),
            jax.ShapeDtypeStruct((width // 2, rows), BF16),
            jax.ShapeDtypeStruct((2 + 3 * steps, PART, rows), F32),
            *[jax.ShapeDtypeStruct((cut, width), F32) for cut in cuts],
        ],
        compiler_params=params(16),
        cost_estimate=long_cost(),
        name="attn_backward",
    )(place, *gparts, *grecvs, x1, cotangent, gain, w_out, qkv, w_qkv)


def mlp_kernel(
    place, x0_ref, opart_ref, orecv_ref, obias_ref, gain_ref, bias_ref, wfc1_ref, b1_ref, wfc2_ref, cot_ref,
    x1_ref, a2_ref, act_ref, dpre_ref, b1sum_ref, keep_ref, gact_ref, gpre_ref, *refs,
):
    da2_refs, turned_ref = refs[:-1], refs[-1]
    step = pl.program_id(0)

    @pl.when(step == 0)
    def _():
        x1_ref[...] = x0_ref[...] + (opart_ref[...] + orecv_ref[...] + obias_ref[...])
        normed, _inv = norm_parts(x1_ref[...])
        a2_ref[...] = (normed * gain_ref[...] + bias_ref[...]).astype(BF16)
        turn(place, a2_ref, turned_ref, slice(None))
        spread(turned_ref, keep_ref, gpre_ref)

    pre = nn(a2_ref[...], wfc1_ref[...]) + b1_ref[...]
    dact = nt(cot_ref[...], wfc2_ref[...])
    cdf = 0.5 * (1.0 + lax.erf(pre * (2.0**-0.5)))
    act = (pre * cdf).astype(BF16)
    act_ref[...] = act
    density = jnp.exp(-0.5 * pre * pre) * 0.3989422804014327
    dpre = (dact * (cdf + pre * density)).astype(BF16)
    dpre_ref[...] = dpre
    for part in range(act.shape[1] // PART):
        columns = slice(part * PART, (part + 1) * PART)
        gact_ref[part] = act[:, columns].astype(F32)
        gpre_ref[2 + step * (act.shape[1] // PART) + part] = dpre[:, columns].astype(F32)
    b1sum_ref[...] = column_sum(dpre.astype(F32))
    da2 = nt(dpre, wfc1_ref[...])

    @pl.when(step == 0)
    def _():
        put_rows(da2_refs, da2, False)

    @pl.when(step != 0)
    def _():
        put_rows(da2_refs, da2, True)


def mlp(
    place, x0, opart, orecv, out_bias, gain, bias, w_fc1, fc1_bias, w_fc2, cotangent, item, cuts
):
    rows, width = x0.shape
    hidden = w_fc1.shape[1]
    tile = 512
    parts = tile // PART
    row_tile = pl.BlockSpec((rows, tile), lambda n, *_: (0, n))
    gone = pl.BlockSpec((parts, rows, PART), lambda n, *_: (n, 0, 0))
    return pl.pallas_call(
        mlp_kernel,
        grid_spec=pltpu.PrefetchScalarGridSpec(
            num_scalar_prefetch=1,
            grid=(hidden // tile,),
            in_specs=[
                whole(x0.shape),
                whole(opart.shape),
                whole(orecv.shape),
                whole(out_bias.shape),
                whole(gain.shape),
                whole(bias.shape),
                pl.BlockSpec((width, tile), lambda n, *_: (0, n)),
                pl.BlockSpec((1, tile), lambda n, *_: (0, n)),
                pl.BlockSpec((tile, width), lambda n, *_: (n, 0)),
                pl.BlockSpec((rows, width), lambda n, *_: (item, 0)),
            ],
            out_specs=[
                whole((rows, width)),
                whole((rows, width)),
                row_tile,
                row_tile,
                pl.BlockSpec((1, tile), lambda n, *_: (0, n)),
                whole((width // 2, rows)),
                gone,
                whole((2 + hidden // PART, rows, PART)),
                *[whole((cut, width)) for cut in cuts],
            ],
            scratch_shapes=[pltpu.VMEM((width, rows), BF16)],
        ),
        out_shape=[
            jax.ShapeDtypeStruct((rows, width), F32),
            jax.ShapeDtypeStruct((rows, width), BF16),
            jax.ShapeDtypeStruct((rows, hidden), BF16),
            jax.ShapeDtypeStruct((rows, hidden), BF16),
            jax.ShapeDtypeStruct((1, hidden), F32),
            jax.ShapeDtypeStruct((width // 2, rows), BF16),
            jax.ShapeDtypeStruct((hidden // PART, rows, PART), F32),
            jax.ShapeDtypeStruct((2 + hidden // PART, rows, PART), F32),
            *[jax.ShapeDtypeStruct((cut, width), F32) for cut in cuts],
        ],
        compiler_params=params(14),
        cost_estimate=long_cost(),
        name="mlp",
    )(place, x0, opart, orecv, out_bias, gain, bias, w_fc1, fc1_bias, w_fc2, cotangent)


def mlp_out_kernel(act_ref, wfc2_ref, out_ref):
    out_ref[...] = nn(act_ref[...], wfc2_ref[...])


def mlp_out(act, w_fc2):
    rows, hidden = act.shape
    width = w_fc2.shape[1]
    tile = 512
    return pl.pallas_call(
        mlp_out_kernel,
        grid=(width // tile,),
        in_specs=[whole(act.shape), pl.BlockSpec((hidden, tile), lambda n: (0, n))],
        out_specs=pl.BlockSpec((rows, tile), lambda n: (0, n)),
        out_shape=jax.ShapeDtypeStruct((rows, width), F32),
        compiler_params=params(6),
        cost_estimate=long_cost(),
        name="mlp_out",
    )(act, w_fc2)


def first_norm_back_kernel(place, *refs, parts, riders):
    gpart_refs, refs = refs[: parts[0]], refs[parts[0] :]
    grecv_refs, refs = refs[: parts[1]], refs[parts[1] :]
    rider_refs, refs = refs[:riders], refs[riders:]
    x0_ref, dx1_ref, gain_ref, dx0_ref, sums_ref, keep_ref, gone_ref, block_ref, turned_ref = refs
    normed, inverse = norm_parts(x0_ref[...])
    grad = joined(gpart_refs) + joined(grecv_refs)
    dx0_ref[...] = (dx1_ref[...] + norm_back(normed, inverse, grad, gain_ref[...])).astype(BF16)
    sums_ref[0:1, :] = column_sum(grad * normed)
    sums_ref[1:2, :] = column_sum(grad)
    sums_ref[2:8, :] = jnp.zeros((6, sums_ref.shape[1]), F32)
    turn(place, dx0_ref, turned_ref, slice(None))
    middle = turned_ref.shape[0] // 2
    keep_ref[...] = turned_ref[:middle, :]
    gone_ref[:middle, :] = turned_ref[middle:, :].astype(F32)
    for chip in range(8):
        lanes = pl.ds(pl.multiple_of(place[chip] * LANES, LANES), LANES)
        for row in range(2):
            block_ref[chip : chip + 1, row * LANES : (row + 1) * LANES] = sums_ref[row : row + 1, lanes]
    gone_ref[middle : middle + 8, :] = block_ref[...]
    first = middle + 8
    for rider_ref in rider_refs:
        gone_ref[first : first + rider_ref.shape[0], :] = rider_ref[...]
        first += rider_ref.shape[0]


def first_norm_back(place, gparts, grecvs, x0, dx1, gain, estimate, riders=()):
    rows, width = x0.shape
    operands = (*gparts, *grecvs, *riders, x0, dx1, gain)
    extra = sum(v.shape[0] for v in riders)
    shapes = [
        jax.ShapeDtypeStruct((rows, width), BF16),
        jax.ShapeDtypeStruct((8, width), F32),
        jax.ShapeDtypeStruct((width // 2, rows), BF16),
        jax.ShapeDtypeStruct((width // 2 + 8 + extra, rows), F32),
        jax.ShapeDtypeStruct((8, 2 * LANES), F32),
    ]
    return pl.pallas_call(
        functools.partial(
            first_norm_back_kernel, parts=(len(gparts), len(grecvs)), riders=len(riders)
        ),
        grid_spec=pltpu.PrefetchScalarGridSpec(
            num_scalar_prefetch=1,
            grid=(1,),
            in_specs=[whole(v.shape) for v in operands],
            out_specs=[whole(v.shape) for v in shapes],
            scratch_shapes=[pltpu.VMEM((width, rows), BF16)],
        ),
        out_shape=shapes,
        compiler_params=params(10),
        cost_estimate=estimate,
        name="first_norm_back",
    )(place, *operands)


def pack_vectors_kernel(place, sa_ref, sb_ref, qa_ref, qb_ref, ba_ref, bb_ref, out_ref, *refs):
    sums_ref, qv_ref, hidden_ref = refs
    sums_ref[...] = sa_ref[...] + sb_ref[...]
    qv_ref[...] = qa_ref[...] + qb_ref[...]
    hidden_ref[...] = ba_ref[...] + bb_ref[...]
    out_ref[...] = jnp.zeros_like(out_ref)
    half = LANES // 2
    for pos in range(8):
        chip = place[pos]
        lanes = pl.ds(pl.multiple_of(chip * LANES, LANES), LANES)
        for row in range(4):
            first = row % 2 * LANES
            spot = 4 * pos + row // 2
            out_ref[spot : spot + 1, first : first + LANES] = sums_ref[row : row + 1, lanes]
        both = pl.ds(pl.multiple_of(chip // 2 * LANES, LANES), LANES)
        spot = 4 * pos + 2
        for row in range(2):
            pair = qv_ref[row : row + 1, both]
            own = jnp.where(chip % 2 == 0, pair[:, :half], pair[:, half:])
            out_ref[spot : spot + 1, row * half : (row + 1) * half] = own
        wide = pl.ds(pl.multiple_of(chip * 2 * LANES, 2 * LANES), 2 * LANES)
        out_ref[spot + 1 : spot + 2, :] = hidden_ref[0:1, wide]


def pack_vectors(place, sums, qv, hidden):
    operands = (*sums, *qv, *hidden)
    return pl.pallas_call(
        pack_vectors_kernel,
        grid_spec=pltpu.PrefetchScalarGridSpec(
            num_scalar_prefetch=1,
            grid=(1,),
            in_specs=[whole(v.shape) for v in operands],
            out_specs=whole((32, 2 * LANES)),
            scratch_shapes=[pltpu.VMEM(v[0].shape, F32) for v in (sums, qv, hidden)],
        ),
        out_shape=jax.ShapeDtypeStruct((32, 2 * LANES), F32),
        compiler_params=params(4),
        cost_estimate=short_cost(),
        name="pack_vectors",
    )(place, *operands)


def pixel_grad_kernel(kinds, grad_ref, wspec_ref, wrgb_ref, pick_ref, *refs, item):
    out_ref = refs[-1]
    spectral = kinds[item] == 1
    grad = grad_ref[...]
    wide = wspec_ref.shape[0]
    cut = (wide // 2 + LANES - 1) // LANES * LANES

    @pl.when(spectral)
    def _():
        out_ref[:, :cut] = nt(grad, wspec_ref[:cut, :]).astype(BF16)
        out_ref[:, cut:] = nt(grad, wspec_ref[cut:, :]).astype(BF16)

    @pl.when(jnp.logical_not(spectral))
    def _():
        small = nt(grad, wrgb_ref[...]).astype(BF16)
        out_ref[...] = nt(small, pick_ref[...]).astype(BF16)


def pixel_grad(kinds, grad, w_spectral, w_rgb, pick, item, items, filled=None):
    rows = grad.shape[0]
    wide, width = w_spectral.shape
    more = [] if filled is None else [filled]
    return pl.pallas_call(
        functools.partial(pixel_grad_kernel, item=item),
        grid_spec=pltpu.PrefetchScalarGridSpec(
            num_scalar_prefetch=1,
            grid=(1,),
            in_specs=[
                whole(grad.shape),
                whole(w_spectral.shape),
                whole(w_rgb.shape),
                whole(pick.shape),
            ]
            + [pl.BlockSpec(memory_space=pl.ANY)] * len(more),
            out_specs=pl.BlockSpec((rows, wide), lambda i, *_: (item, 0)),
        ),
        out_shape=jax.ShapeDtypeStruct((items * rows, wide), BF16),
        input_output_aliases={5: 0} if more else {},
        compiler_params=params(12),
        cost_estimate=long_cost(),
        name="pixel_grad",
    )(kinds, grad, w_spectral, w_rgb, pick, *more)


def gather_left(keep_refs, gone_refs, first, left_ref):
    rows = keep_refs[0].shape[-1]
    for pos, keep_ref in enumerate(keep_refs):
        left_ref[:, pos * rows : (pos + 1) * rows] = keep_ref[...]
    base = len(keep_refs) * rows
    for pos, gone_ref in enumerate(gone_refs):
        columns = slice(base + pos * rows, base + (pos + 1) * rows)
        if len(gone_ref.shape) == 2:
            left_ref[:, columns] = gone_ref[: left_ref.shape[0], :].astype(BF16)
            continue
        for part in range(2):
            left_ref[part * PART : (part + 1) * PART, columns] = gone_ref[first + part].astype(BF16)


def emit(left_ref, rights, send_ref, keep_ref, moves, columns=slice(None)):
    right = jnp.concatenate([r.astype(BF16) for r in rights], 0)
    total = nn(left_ref[...], right)
    half = LANES // 2
    for pos, block in enumerate(moves):
        out_ref = send_ref if pos < 4 else keep_ref
        value = total[block * half : (block + 1) * half]
        if len(out_ref.shape) == 4:
            out_ref[pos % 4, 0, :, columns] = value
        else:
            out_ref[pos % 4, :half, columns] = value


def plain_grad_kernel(
    ka_ref, kb_ref, la_ref, lb_ref, ra_ref, rb_ref, oa_ref, ob_ref, *refs, moves, vectors
):
    send_ref, keep_ref, left_ref = refs[-3:]

    @pl.when(pl.program_id(0) == 0)
    def _():
        gather_left((ka_ref, kb_ref), (la_ref, lb_ref), 0, left_ref)

    for part in range(oa_ref.shape[0]):
        columns = slice(part * PART, (part + 1) * PART)
        rights = (ra_ref[:, columns], rb_ref[:, columns], oa_ref[part], ob_ref[part])
        emit(left_ref, rights, send_ref, keep_ref, moves, columns)
    if vectors:
        early_ref, sa_ref, sb_ref = refs[:3]
        half = LANES // 2
        middle = left_ref.shape[0]
        late = sa_ref[...] + sb_ref[...] + (la_ref[middle:, :] + lb_ref[middle:, :])
        for pos, block in enumerate(moves):
            out_ref = send_ref if pos < 4 else keep_ref
            out_ref[pos % 4, half:, :] = early_ref[block]

            @pl.when(pl.program_id(0) == 0)
            def _(out_ref=out_ref, pos=pos, block=block):
                out_ref[pos % 4, half + 1 : half + 2, : late.shape[1]] = late[block : block + 1]


def plain_grad(keeps, lefts, rights, others, moves, name, skip=0, columns=None, lead=0, vectors=(), planes=1):
    half_width, rows = keeps[0][0].shape[-2:]
    columns = columns or rights[0].shape[1]
    wide = WIDE
    base = skip // (wide * PART)
    half = LANES // 2

    def keep_spec(array, item):
        if array.ndim == 2:
            return whole(array.shape)
        return pl.BlockSpec((None,) + array.shape[1:], lambda n: (item, 0, 0))

    right = pl.BlockSpec((rows, wide * PART), lambda n: (0, n + base))
    other = pl.BlockSpec((wide, rows, PART), lambda n: (n + base + lead // wide, 0, 0))
    height = half + 8 if vectors else half
    out = pl.BlockSpec((4, height, wide * PART), lambda n: (0, 0, n))
    shape = jax.ShapeDtypeStruct((4, height, columns), F32)
    if planes > 1:
        per = columns // planes // (wide * PART)
        out = pl.BlockSpec((4, 1, half, wide * PART), lambda n: (0, n // per, 0, n % per))
        shape = jax.ShapeDtypeStruct((4, planes, half, columns // planes), F32)

    def left_spec(array, item):
        if array.ndim == 2:
            return pl.BlockSpec((half_width + 8, rows), lambda n: (item, 0))
        return pl.BlockSpec((2, PART, rows), lambda n: (item, 0, 0))

    vector_specs = []
    if vectors:
        vector_specs = [pl.BlockSpec((8, 8, wide * PART), lambda n: (0, 0, n))]
        vector_specs += [whole(v.shape) for v in vectors[1:]]
    return pl.pallas_call(
        functools.partial(plain_grad_kernel, moves=moves, vectors=bool(vectors)),
        grid=(columns // (wide * PART),),
        in_specs=[keep_spec(*k) for k in keeps]
        + [left_spec(*v) for v in lefts]
        + [right, right, other, other]
        + vector_specs,
        out_specs=[out, out],
        scratch_shapes=[pltpu.VMEM((half_width, 4 * rows), BF16)],
        out_shape=[shape, shape],
        compiler_params=params(14),
        cost_estimate=short_cost(),
        name=name,
    )(*[k for k, _ in keeps], *[v for v, _ in lefts], *rights, *others, *vectors)


def query_key_kernel(
    aa_ref, ab_ref, fa_ref, fb_ref, ba_ref, bb_ref, da_ref, db_ref, send_ref, keep_ref, left_ref,
    *, moves,
):
    plane, step = pl.program_id(0), pl.program_id(1)

    @pl.when((plane == 0) & (step == 0))
    def _():
        gather_left((aa_ref, ab_ref), (fa_ref, fb_ref), 0, left_ref)

    spot = 2 + plane * pl.num_programs(1) + step
    emit(left_ref, (da_ref[...], db_ref[...], ba_ref[spot], bb_ref[spot]), send_ref, keep_ref, moves)


def value_out_kernel(
    aa_ref, ab_ref, fa_ref, fb_ref, ba_ref, bb_ref, da_ref, db_ref, ya_ref, yb_ref, ma_ref, mb_ref,
    send_ref, keep_ref, left_ref, *, moves,
):
    plane, step = pl.program_id(0), pl.program_id(1)

    @pl.when((plane == 0) & (step == 0))
    def _():
        gather_left((aa_ref, ab_ref), (fa_ref, fb_ref), 0, left_ref)

    @pl.when((plane == 1) & (step == 0))
    def _():
        gather_left((ya_ref, yb_ref), (ba_ref, bb_ref), 0, left_ref)

    @pl.when(plane == 0)
    def _():
        spot = 2 + 2 * pl.num_programs(1) + step
        emit(left_ref, (da_ref[...], db_ref[...], ba_ref[spot], bb_ref[spot]), send_ref, keep_ref, moves)

    @pl.when(plane == 1)
    def _():
        spot = 2 + step
        emit(left_ref, (ma_ref[...], mb_ref[...], fa_ref[spot], fb_ref[spot]), send_ref, keep_ref, moves)


def attn_grad(keep_a1, other_f, other_b, dqkv, moves, out_side=None):
    half_width, rows = keep_a1[0].shape
    columns = dqkv[0].shape[2]
    steps = columns // PART
    half = LANES // 2
    side = whole((half_width, rows))
    specs = [side, side] + [whole(v.shape) for v in (*other_f, *other_b)]
    if out_side is None:
        kernel, name, more = query_key_kernel, "query_key_grad", []
        plane = pl.BlockSpec((None, rows, PART), lambda p, n: (p, 0, n))
        specs += [plane, plane]
    else:
        kernel, name, more = value_out_kernel, "value_out_grad", [*out_side[0], *out_side[1]]
        plane = pl.BlockSpec((None, rows, PART), lambda p, n: (2, 0, n))
        mixed = pl.BlockSpec((rows, PART), lambda p, n: (0, n))
        specs += [plane, plane, side, side, mixed, mixed]
    out = pl.BlockSpec((4, half, PART), lambda p, n: (0, 0, p * steps + n))
    shape = jax.ShapeDtypeStruct((4, half, 2 * columns), F32)
    return pl.pallas_call(
        functools.partial(kernel, moves=moves),
        grid=(2, steps),
        in_specs=specs,
        out_specs=[out, out],
        scratch_shapes=[pltpu.VMEM((half_width, 4 * rows), BF16)],
        out_shape=[shape, shape],
        compiler_params=params(12),
        cost_estimate=short_cost(),
        name=name,
    )(*keep_a1, *other_f, *other_b, *dqkv, *more)


def exchange(values, axis, bit, size):
    return lax.ppermute(values, axis, [(i, i ^ bit) for i in range(size)])


def swap(values):
    return exchange(values, "tensor", 1, 2)


def after(first, values):
    return lax.optimization_barrier((first, values))[1]


X_FIRST = (2, 4, 8)
Z_FIRST = (4, 2, 8)


def block_flips(bits):
    return [sum((1 - ((p >> (2 - n)) & 1)) * (bits[n] // 2) for n in range(3)) for p in range(8)]


def block_moves(bits):
    stands = block_flips(X_FIRST)
    return tuple(stands.index(f) for f in block_flips(bits))


def places():
    me = lax.axis_index("dp")
    flips = jnp.array(block_flips(X_FIRST), jnp.int32)
    return jnp.concatenate([(me // 2) ^ flips, (me % 2)[None]]).astype(jnp.int32)


class Halving:
    def __init__(self, send, keep, bits, size, first=True):
        self.keep, self.bits, self.size = keep, bits, size
        self.unit = keep.shape[0] // 4
        self.recvs = [exchange(send, "dp", bits[0], size)] if first else []
        self.left = keep.shape[0]
        self.sent = send

    def value(self, order, tie=True):
        if tie:
            self.recvs[-1] = order.tie(self.recvs[-1])
        left = self.left
        count = max(left // 2, self.unit)
        total = self.keep.shape[0] - left
        value = self.keep[total : total + count]
        for recv in self.recvs:
            first = recv.shape[0] - left
            value = value + recv[first : first + count]
        order.mark(value)
        return value

    def came(self, recv):
        self.recvs.append(recv)
        self.left = self.left // 2

    def step(self, order):
        value = self.value(order)
        if self.left == self.unit:
            return value[0] if self.unit == 1 else value
        self.came(exchange(value, "dp", self.bits[len(self.recvs)], self.size))
        return None


class Order:
    def __init__(self):
        self.last = None

    def tie(self, values):
        return values if self.last is None else after(self.last, values)

    def mark(self, values):
        self.last = values


def local(
    pixels, item_kinds, gsd_codes, w_spectral, w_rgb, ln1_gain, ln1_bias, w_qkv, q_bias, v_bias,
    w_out, out_bias, ln2_gain, ln2_bias, w_fc1, fc1_bias, w_fc2, fc2_bias, cotangent, *, size,
):
    items = item_kinds.shape[0]
    rows = pixels.shape[0] // items
    width = w_out.shape[1]
    wide = pixels.shape[1]
    narrow = w_rgb.shape[0]
    bands = wide // (narrow // 3)
    custom = size == 16

    def row(vector):
        return vector.reshape(1, -1)

    g1, c1, g2, c2 = row(ln1_gain), row(ln1_bias), row(ln2_gain), row(ln2_bias)
    qb, vb, ob, b1 = row(q_bias), row(v_bias), row(out_bias), row(fc1_bias)
    wqkv = jnp.transpose(w_qkv, (1, 0, 2))

    source = np.arange(wide)[:, None]
    target = np.arange(narrow)[None, :]
    pick = jnp.asarray((source == (target // 3) * bands + target % 3).astype(ml_dtypes.bfloat16))

    ratio = (gsd_codes.astype(F32) + 1.0) / 4.0
    quarter = width // 4
    frequency = 1.0 / 10000.0 ** (jnp.arange(quarter).astype(F32) / quarter)
    spot = jnp.arange(GRID).astype(F32)
    angle = ratio[:, None, None] * spot[None, :, None] * frequency[None, None, :]
    tables = jnp.concatenate([jnp.sin(angle), jnp.cos(angle)], -1)

    def scatter(values):
        return lax.psum_scatter(values, "dp", scatter_dimension=0, tiled=True)

    def both(left, right):
        return sum(tn(left[i], right[i]) for i in range(items))

    order = Order()
    gate = None

    def send(values, wait=True):
        nonlocal gate
        if gate is not None:
            values = after(gate, values)
        gate = swap(values)
        return gate

    place = places() if custom else jnp.arange(9, dtype=jnp.int32) % 8
    move_x, move_z = block_moves(X_FIRST), block_moves(Z_FIRST)

    def other(values):
        return exchange(values, "dp", 1, size) if custom else values

    cut = rows * 3 // 8 // 8 * 8
    cuts = [(cut, rows - cut)] + [(rows,)] * (items - 1)

    def settle(values):
        values = order.tie(values)
        order.mark(jax.tree.leaves(values)[0])
        return values

    none = [None] * items
    part, mixed, erecv, fwd, orecv, ffn, grecv, bwd, arecv, last, ycot = (list(none) for _ in range(11))
    gmix, pk, gfwd, gact, gpre, gbwd, gdx0, da1, da2 = (list(none) for _ in range(9))

    for i in range(items):
        part[i], mixed[i] = embed(order.tie(item_kinds), pixels, w_spectral, w_rgb, pick, i, rows)
        order.mark(part[i])
        erecv[i] = send(part[i])
    keep_cot, gone_cot = turn_cot(order.tie(place), cotangent, rows)
    order.mark(gone_cot)
    gone_mix = []
    for i in range(items):
        gone_mix.append(pack(order.tie(mixed[i])))
        order.mark(gone_mix[i])
    gcot = other(gone_cot)
    gmix = [other(v) for v in gone_mix]
    for i in range(items):
        fwd[i] = attn_forward(
            part[i], erecv[i], tables[i], order.tie(g1), c1, wqkv, qb, vb, w_out
        )
        order.mark(fwd[i][4])
        orecv[i] = send(fwd[i][4])
        if i == 0:
            gcot = settle(gcot)
        else:
            gmix = [settle(v) for v in gmix]
        pk[i] = pack_attn(order.tie(place), fwd[i][1], fwd[i][3])
        order.mark(pk[i][1])
        gfwd[i] = other(pk[i][1])
    x0, a1, qkv, mix, _ = zip(*fwd)
    for i in range(items):
        ffn[i] = mlp(
            place, x0[i], fwd[i][4], orecv[i], order.tie(ob), g2, c2, w_fc1, b1, w_fc2, cotangent, i,
            cuts[i],
        )
        da2[i] = ffn[i][8:]
        order.mark(da2[i][0])
        if i == 0:
            grecv[i] = [send(v) for v in da2[i]]
        gact[i] = other(ffn[i][6])
        gpre[i] = other(ffn[i][7])
        if i == 0:
            gfwd = [settle(v) for v in gfwd]
        else:
            grecv[0][0] = settle(grecv[0][0])
            gact[0], gpre[0] = settle((gact[0], gpre[0]))
            ycot[1] = mlp_out(order.tie(ffn[1][2]), w_fc2)
            order.mark(ycot[1])
    x1, a2, act, dpre, b1sum, ka2 = list(zip(*[v[:6] for v in ffn]))
    if custom:
        gact[1] = order.tie(gact[1])
        fc2_h = Halving(
            *plain_grad(
                [(keep_cot, 0), (keep_cot, 1)], [(gcot, 0), (gcot, 1)], act, gact, move_x, "fc2_grad"
            ),
            X_FIRST, size,
        )
        order.mark(fc2_h.sent)
        gpre[1] = order.tie(gpre[1])
        fc1_s = plain_grad(
            [(ka2[0], 0), (ka2[1], 0)], [(gpre[0], 0), (gpre[1], 0)], dpre, gpre, move_z, "fc1_grad",
            lead=2, planes=2,
        )
        fc1_s = [v.reshape(8, *v.shape[2:]) for v in fc1_s]
        fc1_h = Halving(*fc1_s, Z_FIRST, size)
        order.mark(fc1_h.sent)
    grecv[1] = [send(order.tie(da2[1][0]))]
    for i in range(items):
        bwd[i] = attn_backward(
            place, da2[i], grecv[i], x1[i], cotangent, order.tie(g2), w_out, qkv[i], wqkv, i, cuts[i]
        )
        da1[i] = bwd[i][7:]
        order.mark(da1[i][0])
        if i == 0:
            arecv[i] = [send(v) for v in da1[i]]
        else:
            arecv[0][0] = settle(arecv[0][0])
            gbwd = [other(order.tie(bwd[0][6])), other(bwd[1][6])]
            ycot[0] = mlp_out(order.tie(ffn[0][2]), w_fc2)
            order.mark(ycot[0])
    dx1, dya, dqkv, sums2, qvsum, kdya = list(zip(*[v[:6] for v in bwd]))
    if custom:
        fc2_h.step(order)
        gbwd = [order.tie(v) for v in gbwd]
        keep_a1 = [v[0] for v in pk]
        attx_h = Halving(*attn_grad(keep_a1, gfwd, gbwd, dqkv, move_x), X_FIRST, size, first=False)
        order.mark(attx_h.sent)
        both_x = jnp.concatenate([fc1_h.value(order), attx_h.sent], 0)
        order.mark(both_x)
        gbwd[1] = order.tie(gbwd[1])
        both_x = exchange(both_x, "dp", 2, size)
        attz_h = Halving(
            *attn_grad(keep_a1, gfwd, gbwd, dqkv, move_z, (kdya, mix)), Z_FIRST, size
        )
        order.mark(attz_h.sent)
    arecv[1] = [send(order.tie(da1[1][0]))]
    riders = ()
    for i in range(items):
        estimate = long_cost() if i == 0 else short_cost()
        last[i] = first_norm_back(
            place, da1[i], arecv[i], x0[i], dx1[i], order.tie(g1), estimate, riders
        )
        order.mark(last[i][0])
        if custom and i == 0:
            fc2_h.step(order)
        if custom and i == 0:
            cube = pack_vectors(order.tie(place), sums2, qvsum, b1sum)
            order.mark(cube)
            riders = (last[0][3], cube)
    summed = list(none)
    summed[0] = send(order.tie(ycot[0]))
    dx0, sums1, kdx0, gone, blocks = zip(*last)
    pixels_grad = pixel_grad(order.tie(item_kinds), dx0[0], w_spectral, w_rgb, pick, 0, items)
    order.mark(pixels_grad)
    if custom:
        mid = mixed[0].shape[1] // 2
        gdx0 = order.tie(other(gone[1]))
        sides = ([(kdx0[0], 0), (kdx0[1], 0)], [(gdx0, 1), (gdx0, 0)], mixed, gmix)
        embx_h = Halving(*plain_grad(*sides, move_x, "embed_grad_a", 0, mid), X_FIRST, size)
        order.mark(embx_h.sent)
        sides[3][1] = order.tie(gmix[1])
        cube = (cube + order.tie(gdx0)[-cube.shape[0] :]).reshape(8, 1, -1)
        cube = jnp.pad(cube, ((0, 0), (0, 7), (0, 0)))
        embz_h = Halving(
            *plain_grad(*sides, move_z, "embed_grad_b", mid, mid, vectors=(cube, *blocks)),
            Z_FIRST, size,
        )
        order.mark(embz_h.sent)
    pixels_grad = pixel_grad(
        order.tie(item_kinds), dx0[1], w_spectral, w_rgb, pick, 1, items, pixels_grad
    )
    order.mark(pixels_grad)
    if custom:
        both_x = order.tie(both_x)
        fc1_h.came(both_x[:4])
        attx_h.recvs.append(both_x[4:])
        fc1_v = fc1_h.value(order, False)
        attx_v = attx_h.value(order, False)
    summed[0] = settle(summed[0])
    if custom:
        fc1_h.came(exchange(fc1_v, "dp", 8, size))
        attx_h.came(exchange(attx_v, "dp", 4, size))
        attz_h.step(order)
        fc2_g = fc2_h.step(order)
        attz_h.step(order)
        embz_h.step(order)
        fc1_g = fc1_h.step(order)
    summed[1] = send(order.tie(ycot[1]))
    if custom:
        embx_h.step(order)
        attx_h.step(order)
        embz_h.step(order)
        attz_g = attz_h.step(order)
    if custom:
        embx_h.step(order)
        attx_g = attx_h.step(order)
        embz_g = embz_h.step(order)
    summed[1] = settle(summed[1])
    block_out = jnp.concatenate(
        [(x1[i] + (ycot[i] + summed[i] + fc2_bias)).astype(BF16) for i in range(items)], 0
    )
    order.mark(block_out)
    if custom:
        embx_g = embx_h.step(order)
        shard = width // size
        core = lax.axis_index("dp") % 2
        spans = [(shard, row * LANES, LANES) for row in range(4)]
        spans += [(shard, 4 * LANES + row * LANES // 2, LANES // 2) for row in range(2)]
        spans += [(shard, 6 * LANES, 2 * LANES)]
        spans += [(shard + 1, row * LANES, LANES) for row in range(2)]
        outs = []
        for row, first, length in spans:
            low = embz_g[row, first : first + length // 2]
            high = embz_g[row, first + length // 2 : first + length]
            outs.append(jnp.where(core == 0, low, high))
        ln2_g, ln2_b, ob_g, b2_g, q_g, v_g, b1_g, ln1_g, ln1_b = outs
        embz_g = embz_g[:shard]
        emb_g = jnp.concatenate([embx_g, embz_g], 1)
        cut = attx_g.shape[1] // 2
        planes = [attx_g[:, :cut], attx_g[:, cut:], attz_g[:, :cut]]
        qkv_grad = jnp.transpose(jnp.stack(planes), (1, 0, 2))
        out_grad = attz_g[:, cut:].T
        fc1_g = jnp.concatenate([fc1_g[0], fc1_g[1]], 1)
    else:
        cot = [cotangent[i * rows : (i + 1) * rows] for i in range(items)]
        fc2_g = scatter(both(cot, act))
        fc1_g = scatter(both(a2, dpre))
        emb_g = scatter(both(dx0, mixed))
        qkv_grad = scatter(
            sum(
                lax.dot_general(
                    a1[i], dqkv[i], (((0,), (1,)), ((), ())), preferred_element_type=F32
                )
                for i in range(items)
            )
        )
        out_grad = scatter(both(dya, mix)).T
        totals = [v[0] + v[1] for v in (sums2, qvsum, b1sum, sums1)]
        rows_of = [(0, 0), (0, 1), (0, 2), (0, 3), (1, 0), (1, 1), (2, 0), (3, 0), (3, 1)]
        outs = [scatter(totals[n][row]) for n, row in rows_of]
        ln2_g, ln2_b, ob_g, b2_g, q_g, v_g, b1_g, ln1_g, ln1_b = outs
    spectral_grad = emb_g[:, :wide].T
    rgb_grad = emb_g[:, wide:].T
    return (
        block_out, pixels_grad, spectral_grad, rgb_grad, ln1_g, ln1_b, qkv_grad, q_g, v_g, out_grad,
        ob_g, ln2_g, ln2_b, fc1_g, b1_g, fc2_g.T, b2_g,
    )


def solution(mesh):
    in_specs = (
        P("dp", "tensor"),
        P("dp"),
        P("dp"),
        P("tensor", None),
        P("tensor", None),
        P(),
        P(),
        P(None, None, "tensor"),
        P("tensor"),
        P("tensor"),
        P("tensor", None),
        P(),
        P(),
        P(),
        P(None, "tensor"),
        P("tensor"),
        P("tensor", None),
        P(),
        P("dp", None),
    )
    out_specs = (
        P("dp", None),
        P("dp", "tensor"),
        P("tensor", "dp"),
        P("tensor", "dp"),
        P("dp"),
        P("dp"),
        P("dp", None, "tensor"),
        P(("tensor", "dp")),
        P(("tensor", "dp")),
        P("tensor", "dp"),
        P("dp"),
        P("dp"),
        P("dp"),
        P("dp", "tensor"),
        P(("tensor", "dp")),
        P("tensor", "dp"),
        P("dp"),
    )
    body = functools.partial(local, size=mesh.shape["dp"])
    return jax.shard_map(body, mesh=mesh, in_specs=in_specs, out_specs=out_specs, check_vma=False)
```

```python
import functools

import jax
import jax.numpy as jnp
import ml_dtypes
import numpy as np
from jax import lax
from jax.experimental import pallas as pl
from jax.experimental.pallas import tpu as pltpu
from jax.sharding import PartitionSpec as P

HEAD_DIM = 64
GRID = 16
EPS = 1e-06
F32 = jnp.float32
BF16 = jnp.bfloat16
LANES = 128
MIB = 1024 * 1024
QUAD = 256
PART = 256
WIDE = 2


def nn(left, right):
    return lax.dot_general(left, right, (((1,), (0,)), ((), ())), preferred_element_type=F32)


def nt(left, right):
    return lax.dot_general(left, right, (((1,), (1,)), ((), ())), preferred_element_type=F32)


def tn(left, right):
    return lax.dot_general(left, right, (((0,), (0,)), ((), ())), preferred_element_type=F32)


def params(mib):
    return pltpu.CompilerParams(vmem_limit_bytes=mib * MIB)


def short_cost():
    return pl.CostEstimate(flops=1000, bytes_accessed=1000, transcendentals=0)


def long_cost():
    return pl.CostEstimate(flops=int(1e11), bytes_accessed=1000, transcendentals=0)


def whole(shape):
    return pl.BlockSpec(shape, lambda *_: (0,) * len(shape), pipeline_mode=pl.Buffered(1))


def norm_parts(values):
    center = values - jnp.mean(values, -1, keepdims=True)
    spread = jnp.mean(center * center, -1, keepdims=True)
    inverse = lax.rsqrt(spread + EPS)
    return center * inverse, inverse


def norm_back(normed, inverse, grad, gain):
    scaled = grad * gain
    mean_scaled = jnp.mean(scaled, -1, keepdims=True)
    mean_cross = jnp.mean(scaled * normed, -1, keepdims=True)
    return inverse * (scaled - mean_scaled - normed * mean_cross)


def column_sum(values):
    return jnp.sum(values, 0, keepdims=True)


def turn(place, source_ref, turned_ref, columns):
    chips = turned_ref.shape[0] // LANES
    half = LANES // 2
    core = place[chips]
    low = pl.multiple_of(core * (chips * half), half)
    high = pl.multiple_of((1 - core) * (chips * half), half)
    for chip in range(chips):
        lanes = pl.ds(pl.multiple_of(place[chip] * LANES, LANES), LANES)
        block = source_ref[:, lanes].T
        turned_ref[pl.ds(low + chip * half, half), columns] = block[:half]
        turned_ref[pl.ds(high + chip * half, half), columns] = block[half:]


def spread(turned_ref, keep_ref, gone_ref, first=0):
    middle = turned_ref.shape[0] // 2
    keep_ref[...] = turned_ref[:middle, :]
    for part in range(2):
        start = middle + part * PART
        gone_ref[first + part] = turned_ref[start : start + PART, :].astype(F32)


def turn_cot_kernel(place, cot_ref, keep_ref, gone_ref, turned_ref):
    turn(place, cot_ref, turned_ref, slice(None))
    spread(turned_ref, keep_ref, gone_ref)


def turn_cot(place, cotangent, rows):
    width = cotangent.shape[1]
    items = cotangent.shape[0] // rows
    return pl.pallas_call(
        turn_cot_kernel,
        grid_spec=pltpu.PrefetchScalarGridSpec(
            num_scalar_prefetch=1,
            grid=(items,),
            in_specs=[pl.BlockSpec((rows, width), lambda i, *_: (i, 0))],
            out_specs=[
                pl.BlockSpec((None, width // 2, rows), lambda i, *_: (i, 0, 0)),
                pl.BlockSpec((2, PART, rows), lambda i, *_: (i, 0, 0)),
            ],
            scratch_shapes=[pltpu.VMEM((width, rows), BF16)],
        ),
        out_shape=[
            jax.ShapeDtypeStruct((items, width // 2, rows), BF16),
            jax.ShapeDtypeStruct((2 * items, PART, rows), F32),
        ],
        compiler_params=params(4),
        cost_estimate=short_cost(),
        name="turn_cotangent",
    )(place, cotangent)


def pack_kernel(values_ref, out_ref):
    out_ref[0] = values_ref[...].astype(F32)


def pack(values):
    rows, columns = values.shape
    return pl.pallas_call(
        pack_kernel,
        grid=(columns // PART,),
        in_specs=[pl.BlockSpec((rows, PART), lambda n: (0, n))],
        out_specs=pl.BlockSpec((1, rows, PART), lambda n: (n, 0, 0)),
        out_shape=jax.ShapeDtypeStruct((columns // PART, rows, PART), F32),
        compiler_params=params(4),
        cost_estimate=short_cost(),
        name="pack_pixels",
    )(values)


def pack_attn_kernel(place, a1_ref, o_ref, keep_ref, gone_ref, turned_ref):
    turn(place, a1_ref, turned_ref, slice(None))
    spread(turned_ref, keep_ref, gone_ref)
    for part in range(o_ref.shape[1] // PART):
        gone_ref[2 + part] = o_ref[:, part * PART : (part + 1) * PART].astype(F32)


def pack_attn(place, a1, mix):
    rows, width = a1.shape
    parts = 2 + mix.shape[1] // PART
    return pl.pallas_call(
        pack_attn_kernel,
        grid_spec=pltpu.PrefetchScalarGridSpec(
            num_scalar_prefetch=1,
            grid=(1,),
            in_specs=[whole(a1.shape), whole(mix.shape)],
            out_specs=[whole((width // 2, rows)), whole((parts, PART, rows))],
            scratch_shapes=[pltpu.VMEM((width, rows), BF16)],
        ),
        out_shape=[
            jax.ShapeDtypeStruct((width // 2, rows), BF16),
            jax.ShapeDtypeStruct((parts, PART, rows), F32),
        ],
        compiler_params=params(4),
        cost_estimate=short_cost(),
        name="pack_attn",
    )(place, a1, mix)


def pieces_of(length):
    third = length // 3 // LANES * LANES
    return [(0, third), (third, third), (2 * third, length - 2 * third)]


def embed_kernel(
    kinds, pix_ref, wspec_ref, wrgb_ref, pick_ref, part_ref, mixed_ref,
    pix_buf, wspec_buf, wrgb_buf, pick_buf, pix_sem, big_sem, small_sem, *, item,
):
    rows, wide = pix_buf.shape
    spectral = kinds[item] == 1
    pieces = pieces_of(wide)
    own_rows = pl.ds(item * rows, rows)

    @pl.when(spectral)
    def _():
        copies = []
        for n, (first, size) in enumerate(pieces):
            span = pl.ds(first, size)
            copies.append(
                (
                    pltpu.make_async_copy(
                        pix_ref.at[own_rows, span], mixed_ref.at[:, span], pix_sem.at[n]
                    ),
                    pltpu.make_async_copy(wspec_ref.at[span], wspec_buf.at[span], big_sem.at[n]),
                )
            )
        for pair in copies:
            for copy in pair:
                copy.start()
        mixed_ref[:, wide:] = jnp.zeros((rows, wrgb_buf.shape[0]), BF16)
        for n, (first, size) in enumerate(pieces):
            for copy in copies[n]:
                copy.wait()
            term = nn(mixed_ref[:, first : first + size], wspec_buf[first : first + size, :])
            if n == 0:
                part_ref[...] = term
            else:
                part_ref[...] += term

    @pl.when(jnp.logical_not(spectral))
    def _():
        copies = []
        for n, (first, size) in enumerate(pieces):
            span = pl.ds(first, size)
            copies.append(
                (
                    pltpu.make_async_copy(
                        pix_ref.at[own_rows, span], pix_buf.at[:, span], pix_sem.at[n]
                    ),
                    pltpu.make_async_copy(pick_ref.at[span], pick_buf.at[span], big_sem.at[n]),
                )
            )
        for pair in copies:
            for copy in pair:
                copy.start()
        weights = pltpu.make_async_copy(wrgb_ref, wrgb_buf, small_sem)
        weights.start()
        mixed_ref[:, :wide] = jnp.zeros((rows, wide), BF16)
        total = None
        for n, (first, size) in enumerate(pieces):
            for copy in copies[n]:
                copy.wait()
            term = nn(pix_buf[:, first : first + size], pick_buf[first : first + size, :])
            total = term if total is None else total + term
        mixed_ref[:, wide:] = total.astype(BF16)
        weights.wait()
        part_ref[...] = nn(mixed_ref[:, wide:], wrgb_buf[...])


def embed(kinds, pixels, w_spectral, w_rgb, pick, item, rows):
    wide, width = w_spectral.shape
    narrow = w_rgb.shape[0]
    far = pl.BlockSpec(memory_space=pltpu.HBM)
    return pl.pallas_call(
        functools.partial(embed_kernel, item=item),
        grid_spec=pltpu.PrefetchScalarGridSpec(
            num_scalar_prefetch=1,
            grid=(1,),
            in_specs=[far, far, far, far],
            out_specs=[whole((rows, width)), whole((rows, wide + narrow))],
            scratch_shapes=[
                pltpu.VMEM((rows, wide), BF16),
                pltpu.VMEM((wide, width), BF16),
                pltpu.VMEM((narrow, width), BF16),
                pltpu.VMEM((wide, narrow), BF16),
                pltpu.SemaphoreType.DMA((3,)),
                pltpu.SemaphoreType.DMA((3,)),
                pltpu.SemaphoreType.DMA(()),
            ],
        ),
        out_shape=[
            jax.ShapeDtypeStruct((rows, width), F32),
            jax.ShapeDtypeStruct((rows, wide + narrow), BF16),
        ],
        compiler_params=params(58),
        cost_estimate=short_cost(),
        name="embed",
    )(kinds, pixels, w_spectral, w_rgb, pick)


def pair_masks(rows):
    lane = lax.broadcasted_iota(jnp.int32, (rows, LANES), 1)
    return lane < HEAD_DIM, lane >= HEAD_DIM


def only(mask, values):
    return jnp.where(mask, values, jnp.zeros_like(values))


def softmax_rows(query, key):
    scores = nt(query, key) * (HEAD_DIM**-0.5)
    expo = jnp.exp(scores - jnp.max(scores, -1, keepdims=True))
    return expo / jnp.sum(expo, -1, keepdims=True)


def attn_forward_kernel(
    part_ref, recv_ref, table_ref, gain_ref, bias_ref, wqkv_ref, qb_ref, vb_ref, wout_ref,
    x0_ref, a1_ref, qkv_ref, o_ref, opart_ref,
):
    quad = pl.program_id(0)
    rows, width = part_ref.shape

    @pl.when(quad == 0)
    def _():
        side = table_ref.shape[0]
        half = table_ref.shape[1]
        table = table_ref[...]
        by_row = jnp.broadcast_to(table[:, None, :], (side, side, half)).reshape(rows, half)
        by_col = jnp.broadcast_to(table[None, :, :], (side, side, half)).reshape(rows, half)
        left = part_ref[:, :half] + recv_ref[:, :half] + by_row
        right = part_ref[:, half:] + recv_ref[:, half:] + by_col
        x0_ref[:, :half] = left
        x0_ref[:, half:] = right
        normed, _inv = norm_parts(x0_ref[...])
        a1_ref[...] = (normed * gain_ref[...] + bias_ref[...]).astype(BF16)
        opart_ref[...] = jnp.zeros_like(opart_ref)

    a1 = a1_ref[...]
    query = (nn(a1, wqkv_ref[0]) + qb_ref[...]).astype(BF16)
    key = nn(a1, wqkv_ref[1]).astype(BF16)
    value = (nn(a1, wqkv_ref[2]) + vb_ref[...]).astype(BF16)
    qkv_ref[0] = query
    qkv_ref[1] = key
    qkv_ref[2] = value
    masks = pair_masks(rows)
    for pair in range(query.shape[1] // LANES):
        span = slice(pair * LANES, (pair + 1) * LANES)
        q2, k2, v2 = query[:, span], key[:, span], value[:, span]
        mixed = None
        for mask in masks:
            probs = softmax_rows(only(mask, q2), k2).astype(BF16)
            term = nn(probs, only(mask, v2))
            mixed = term if mixed is None else mixed + term
        o_ref[:, span] = mixed.astype(BF16)
    opart_ref[...] += nn(o_ref[...], wout_ref[...])


def attn_forward(part, recv, table, gain, bias, w_qkv, q_bias, v_bias, w_out):
    rows, width = part.shape
    heads_wide = w_out.shape[0]
    steps = heads_wide // QUAD
    return pl.pallas_call(
        attn_forward_kernel,
        grid=(steps,),
        in_specs=[
            whole(part.shape),
            whole(recv.shape),
            whole(table.shape),
            whole(gain.shape),
            whole(bias.shape),
            pl.BlockSpec((3, width, QUAD), lambda n: (0, 0, n)),
            pl.BlockSpec((1, QUAD), lambda n: (0, n)),
            pl.BlockSpec((1, QUAD), lambda n: (0, n)),
            pl.BlockSpec((QUAD, width), lambda n: (n, 0)),
        ],
        out_specs=[
            whole((rows, width)),
            whole((rows, width)),
            pl.BlockSpec((3, rows, QUAD), lambda n: (0, 0, n)),
            pl.BlockSpec((rows, QUAD), lambda n: (0, n)),
            whole((rows, width)),
        ],
        out_shape=[
            jax.ShapeDtypeStruct((rows, width), F32),
            jax.ShapeDtypeStruct((rows, width), BF16),
            jax.ShapeDtypeStruct((3, rows, heads_wide), BF16),
            jax.ShapeDtypeStruct((rows, heads_wide), BF16),
            jax.ShapeDtypeStruct((rows, width), F32),
        ],
        compiler_params=params(10),
        cost_estimate=long_cost(),
        name="attn_forward",
    )(part, recv, table, gain, bias, w_qkv, q_bias, v_bias, w_out)


def put_rows(refs, values, add):
    first = 0
    for ref in refs:
        rows = ref.shape[0]
        if add:
            ref[...] += values[first : first + rows]
        else:
            ref[...] = values[first : first + rows]
        first += rows


def joined(refs):
    values = [ref[...] for ref in refs]
    return values[0] if len(values) == 1 else jnp.concatenate(values, 0)


def attn_backward_kernel(place, *refs, parts):
    gpart_refs, refs = refs[: parts[0]], refs[parts[0] :]
    grecv_refs, refs = refs[: parts[1]], refs[parts[1] :]
    x1_ref, cot_ref, gain_ref, wout_ref, qkv_ref, wqkv_ref, *refs = refs
    dx1_ref, dya_ref, dqkv_ref, sums_ref, qvsum_ref, keep_ref, gone_ref, *da1_refs = refs[:-1]
    turned_ref = refs[-1]
    quad = pl.program_id(0)
    rows = x1_ref.shape[0]

    @pl.when(quad == 0)
    def _():
        normed, inverse = norm_parts(x1_ref[...])
        grad = joined(gpart_refs) + joined(grecv_refs)
        cot = cot_ref[...].astype(F32)
        dx1 = cot + norm_back(normed, inverse, grad, gain_ref[...])
        dx1_ref[...] = dx1
        dya = dx1.astype(BF16)
        dya_ref[...] = dya
        sums_ref[0:1, :] = column_sum(grad * normed)
        sums_ref[1:2, :] = column_sum(grad)
        sums_ref[2:3, :] = column_sum(dya.astype(F32))
        sums_ref[3:4, :] = column_sum(cot)
        sums_ref[4:8, :] = jnp.zeros((4, sums_ref.shape[1]), F32)
        turn(place, dya_ref, turned_ref, slice(None))
        spread(turned_ref, keep_ref, gone_ref)

    dmix = nt(dya_ref[...], wout_ref[...]).astype(BF16)
    scale = HEAD_DIM**-0.5
    masks = pair_masks(rows)
    for pair in range(dmix.shape[1] // LANES):
        span = slice(pair * LANES, (pair + 1) * LANES)
        q2, k2, v2, d2 = qkv_ref[0, :, span], qkv_ref[1, :, span], qkv_ref[2, :, span], dmix[:, span]
        totals = [None, None, None]
        for mask in masks:
            qm, km, dm = only(mask, q2), only(mask, k2), only(mask, d2)
            probs = softmax_rows(qm, k2)
            dprobs = nt(dm, v2)
            dot_row = jnp.sum(probs * dprobs, -1, keepdims=True)
            dscores = (probs * (dprobs - dot_row)).astype(BF16)
            terms = [nn(dscores, km), tn(dscores, qm), tn(probs.astype(BF16), dm)]
            totals = [t if o is None else o + t for o, t in zip(totals, terms)]
        dqkv_ref[0, :, span] = (totals[0] * scale).astype(BF16)
        dqkv_ref[1, :, span] = (totals[1] * scale).astype(BF16)
        dqkv_ref[2, :, span] = totals[2].astype(BF16)
    da1 = nt(dqkv_ref[0], wqkv_ref[0]) + nt(dqkv_ref[1], wqkv_ref[1]) + nt(dqkv_ref[2], wqkv_ref[2])

    @pl.when(quad == 0)
    def _():
        put_rows(da1_refs, da1, False)

    @pl.when(quad != 0)
    def _():
        put_rows(da1_refs, da1, True)

    steps = pl.num_programs(0)
    for plane in range(3):
        gone_ref[2 + plane * steps + quad] = dqkv_ref[plane].astype(F32)
    qvsum_ref[0:1, :] = column_sum(dqkv_ref[0].astype(F32))
    qvsum_ref[1:2, :] = column_sum(dqkv_ref[2].astype(F32))
    qvsum_ref[2:8, :] = jnp.zeros((6, qvsum_ref.shape[1]), F32)


def attn_backward(place, gparts, grecvs, x1, cotangent, gain, w_out, qkv, w_qkv, item, cuts):
    rows, width = x1.shape
    heads_wide = w_out.shape[0]
    steps = heads_wide // QUAD
    return pl.pallas_call(
        functools.partial(attn_backward_kernel, parts=(len(gparts), len(grecvs))),
        grid_spec=pltpu.PrefetchScalarGridSpec(
            num_scalar_prefetch=1,
            grid=(steps,),
            in_specs=[
                *[whole(v.shape) for v in (*gparts, *grecvs)],
                whole(x1.shape),
                pl.BlockSpec((rows, width), lambda n, *_: (item, 0)),
                whole(gain.shape),
                pl.BlockSpec((QUAD, width), lambda n, *_: (n, 0)),
                pl.BlockSpec((3, rows, QUAD), lambda n, *_: (0, 0, n)),
                pl.BlockSpec((3, width, QUAD), lambda n, *_: (0, 0, n)),
            ],
            out_specs=[
                whole((rows, width)),
                whole((rows, width)),
                pl.BlockSpec((3, rows, QUAD), lambda n, *_: (0, 0, n)),
                whole((8, width)),
                pl.BlockSpec((8, QUAD), lambda n, *_: (0, n)),
                whole((width // 2, rows)),
                whole((2 + 3 * steps, PART, rows)),
                *[whole((cut, width)) for cut in cuts],
            ],
            scratch_shapes=[pltpu.VMEM((width, rows), BF16)],
        ),
        out_shape=[
            jax.ShapeDtypeStruct((rows, width), F32),
            jax.ShapeDtypeStruct((rows, width), BF16),
            jax.ShapeDtypeStruct((3, rows, heads_wide), BF16),
            jax.ShapeDtypeStruct((8, width), F32),
            jax.ShapeDtypeStruct((8, heads_wide), F32),
            jax.ShapeDtypeStruct((width // 2, rows), BF16),
            jax.ShapeDtypeStruct((2 + 3 * steps, PART, rows), F32),
            *[jax.ShapeDtypeStruct((cut, width), F32) for cut in cuts],
        ],
        compiler_params=params(16),
        cost_estimate=long_cost(),
        name="attn_backward",
    )(place, *gparts, *grecvs, x1, cotangent, gain, w_out, qkv, w_qkv)


def mlp_kernel(
    place, x0_ref, opart_ref, orecv_ref, obias_ref, gain_ref, bias_ref, wfc1_ref, b1_ref, wfc2_ref, cot_ref,
    x1_ref, a2_ref, act_ref, dpre_ref, b1sum_ref, keep_ref, gact_ref, gpre_ref, *refs,
):
    da2_refs, turned_ref = refs[:-1], refs[-1]
    step = pl.program_id(0)

    @pl.when(step == 0)
    def _():
        x1_ref[...] = x0_ref[...] + (opart_ref[...] + orecv_ref[...] + obias_ref[...])
        normed, _inv = norm_parts(x1_ref[...])
        a2_ref[...] = (normed * gain_ref[...] + bias_ref[...]).astype(BF16)
        turn(place, a2_ref, turned_ref, slice(None))
        spread(turned_ref, keep_ref, gpre_ref)

    pre = nn(a2_ref[...], wfc1_ref[...]) + b1_ref[...]
    dact = nt(cot_ref[...], wfc2_ref[...])
    cdf = 0.5 * (1.0 + lax.erf(pre * (2.0**-0.5)))
    act = (pre * cdf).astype(BF16)
    act_ref[...] = act
    density = jnp.exp(-0.5 * pre * pre) * 0.3989422804014327
    dpre = (dact * (cdf + pre * density)).astype(BF16)
    dpre_ref[...] = dpre
    for part in range(act.shape[1] // PART):
        columns = slice(part * PART, (part + 1) * PART)
        gact_ref[part] = act[:, columns].astype(F32)
        gpre_ref[2 + step * (act.shape[1] // PART) + part] = dpre[:, columns].astype(F32)
    b1sum_ref[...] = column_sum(dpre.astype(F32))
    da2 = nt(dpre, wfc1_ref[...])

    @pl.when(step == 0)
    def _():
        put_rows(da2_refs, da2, False)

    @pl.when(step != 0)
    def _():
        put_rows(da2_refs, da2, True)


def mlp(
    place, x0, opart, orecv, out_bias, gain, bias, w_fc1, fc1_bias, w_fc2, cotangent, item, cuts
):
    rows, width = x0.shape
    hidden = w_fc1.shape[1]
    tile = 512
    parts = tile // PART
    row_tile = pl.BlockSpec((rows, tile), lambda n, *_: (0, n))
    gone = pl.BlockSpec((parts, rows, PART), lambda n, *_: (n, 0, 0))
    return pl.pallas_call(
        mlp_kernel,
        grid_spec=pltpu.PrefetchScalarGridSpec(
            num_scalar_prefetch=1,
            grid=(hidden // tile,),
            in_specs=[
                whole(x0.shape),
                whole(opart.shape),
                whole(orecv.shape),
                whole(out_bias.shape),
                whole(gain.shape),
                whole(bias.shape),
                pl.BlockSpec((width, tile), lambda n, *_: (0, n)),
                pl.BlockSpec((1, tile), lambda n, *_: (0, n)),
                pl.BlockSpec((tile, width), lambda n, *_: (n, 0)),
                pl.BlockSpec((rows, width), lambda n, *_: (item, 0)),
            ],
            out_specs=[
                whole((rows, width)),
                whole((rows, width)),
                row_tile,
                row_tile,
                pl.BlockSpec((1, tile), lambda n, *_: (0, n)),
                whole((width // 2, rows)),
                gone,
                whole((2 + hidden // PART, rows, PART)),
                *[whole((cut, width)) for cut in cuts],
            ],
            scratch_shapes=[pltpu.VMEM((width, rows), BF16)],
        ),
        out_shape=[
            jax.ShapeDtypeStruct((rows, width), F32),
            jax.ShapeDtypeStruct((rows, width), BF16),
            jax.ShapeDtypeStruct((rows, hidden), BF16),
            jax.ShapeDtypeStruct((rows, hidden), BF16),
            jax.ShapeDtypeStruct((1, hidden), F32),
            jax.ShapeDtypeStruct((width // 2, rows), BF16),
            jax.ShapeDtypeStruct((hidden // PART, rows, PART), F32),
            jax.ShapeDtypeStruct((2 + hidden // PART, rows, PART), F32),
            *[jax.ShapeDtypeStruct((cut, width), F32) for cut in cuts],
        ],
        compiler_params=params(14),
        cost_estimate=long_cost(),
        name="mlp",
    )(place, x0, opart, orecv, out_bias, gain, bias, w_fc1, fc1_bias, w_fc2, cotangent)


def mlp_out_kernel(act_ref, wfc2_ref, out_ref):
    out_ref[...] = nn(act_ref[...], wfc2_ref[...])


def mlp_out(act, w_fc2):
    rows, hidden = act.shape
    width = w_fc2.shape[1]
    tile = 512
    return pl.pallas_call(
        mlp_out_kernel,
        grid=(width // tile,),
        in_specs=[whole(act.shape), pl.BlockSpec((hidden, tile), lambda n: (0, n))],
        out_specs=pl.BlockSpec((rows, tile), lambda n: (0, n)),
        out_shape=jax.ShapeDtypeStruct((rows, width), F32),
        compiler_params=params(6),
        cost_estimate=long_cost(),
        name="mlp_out",
    )(act, w_fc2)


def first_norm_back_kernel(place, *refs, parts, riders):
    gpart_refs, refs = refs[: parts[0]], refs[parts[0] :]
    grecv_refs, refs = refs[: parts[1]], refs[parts[1] :]
    rider_refs, refs = refs[:riders], refs[riders:]
    x0_ref, dx1_ref, gain_ref, dx0_ref, sums_ref, keep_ref, gone_ref, block_ref, turned_ref = refs
    normed, inverse = norm_parts(x0_ref[...])
    grad = joined(gpart_refs) + joined(grecv_refs)
    dx0_ref[...] = (dx1_ref[...] + norm_back(normed, inverse, grad, gain_ref[...])).astype(BF16)
    sums_ref[0:1, :] = column_sum(grad * normed)
    sums_ref[1:2, :] = column_sum(grad)
    sums_ref[2:8, :] = jnp.zeros((6, sums_ref.shape[1]), F32)
    turn(place, dx0_ref, turned_ref, slice(None))
    middle = turned_ref.shape[0] // 2
    keep_ref[...] = turned_ref[:middle, :]
    gone_ref[:middle, :] = turned_ref[middle:, :].astype(F32)
    for chip in range(8):
        lanes = pl.ds(pl.multiple_of(place[chip] * LANES, LANES), LANES)
        for row in range(2):
            block_ref[chip : chip + 1, row * LANES : (row + 1) * LANES] = sums_ref[row : row + 1, lanes]
    gone_ref[middle : middle + 8, :] = block_ref[...]
    first = middle + 8
    for rider_ref in rider_refs:
        gone_ref[first : first + rider_ref.shape[0], :] = rider_ref[...]
        first += rider_ref.shape[0]


def first_norm_back(place, gparts, grecvs, x0, dx1, gain, estimate, riders=()):
    rows, width = x0.shape
    operands = (*gparts, *grecvs, *riders, x0, dx1, gain)
    extra = sum(v.shape[0] for v in riders)
    shapes = [
        jax.ShapeDtypeStruct((rows, width), BF16),
        jax.ShapeDtypeStruct((8, width), F32),
        jax.ShapeDtypeStruct((width // 2, rows), BF16),
        jax.ShapeDtypeStruct((width // 2 + 8 + extra, rows), F32),
        jax.ShapeDtypeStruct((8, 2 * LANES), F32),
    ]
    return pl.pallas_call(
        functools.partial(
            first_norm_back_kernel, parts=(len(gparts), len(grecvs)), riders=len(riders)
        ),
        grid_spec=pltpu.PrefetchScalarGridSpec(
            num_scalar_prefetch=1,
            grid=(1,),
            in_specs=[whole(v.shape) for v in operands],
            out_specs=[whole(v.shape) for v in shapes],
            scratch_shapes=[pltpu.VMEM((width, rows), BF16)],
        ),
        out_shape=shapes,
        compiler_params=params(10),
        cost_estimate=estimate,
        name="first_norm_back",
    )(place, *operands)


def pack_vectors_kernel(place, sa_ref, sb_ref, qa_ref, qb_ref, ba_ref, bb_ref, out_ref, *refs):
    sums_ref, qv_ref, hidden_ref = refs
    sums_ref[...] = sa_ref[...] + sb_ref[...]
    qv_ref[...] = qa_ref[...] + qb_ref[...]
    hidden_ref[...] = ba_ref[...] + bb_ref[...]
    out_ref[...] = jnp.zeros_like(out_ref)
    half = LANES // 2
    for pos in range(8):
        chip = place[pos]
        lanes = pl.ds(pl.multiple_of(chip * LANES, LANES), LANES)
        for row in range(4):
            first = row % 2 * LANES
            spot = 4 * pos + row // 2
            out_ref[spot : spot + 1, first : first + LANES] = sums_ref[row : row + 1, lanes]
        both = pl.ds(pl.multiple_of(chip // 2 * LANES, LANES), LANES)
        spot = 4 * pos + 2
        for row in range(2):
            pair = qv_ref[row : row + 1, both]
            own = jnp.where(chip % 2 == 0, pair[:, :half], pair[:, half:])
            out_ref[spot : spot + 1, row * half : (row + 1) * half] = own
        wide = pl.ds(pl.multiple_of(chip * 2 * LANES, 2 * LANES), 2 * LANES)
        out_ref[spot + 1 : spot + 2, :] = hidden_ref[0:1, wide]


def pack_vectors(place, sums, qv, hidden):
    operands = (*sums, *qv, *hidden)
    return pl.pallas_call(
        pack_vectors_kernel,
        grid_spec=pltpu.PrefetchScalarGridSpec(
            num_scalar_prefetch=1,
            grid=(1,),
            in_specs=[whole(v.shape) for v in operands],
            out_specs=whole((32, 2 * LANES)),
            scratch_shapes=[pltpu.VMEM(v[0].shape, F32) for v in (sums, qv, hidden)],
        ),
        out_shape=jax.ShapeDtypeStruct((32, 2 * LANES), F32),
        compiler_params=params(4),
        cost_estimate=short_cost(),
        name="pack_vectors",
    )(place, *operands)


def pixel_grad_kernel(kinds, grad_ref, wspec_ref, wrgb_ref, pick_ref, *refs, item):
    out_ref = refs[-1]
    spectral = kinds[item] == 1
    grad = grad_ref[...]
    wide = wspec_ref.shape[0]
    cut = (wide // 2 + LANES - 1) // LANES * LANES

    @pl.when(spectral)
    def _():
        out_ref[:, :cut] = nt(grad, wspec_ref[:cut, :]).astype(BF16)
        out_ref[:, cut:] = nt(grad, wspec_ref[cut:, :]).astype(BF16)

    @pl.when(jnp.logical_not(spectral))
    def _():
        small = nt(grad, wrgb_ref[...]).astype(BF16)
        out_ref[...] = nt(small, pick_ref[...]).astype(BF16)


def pixel_grad(kinds, grad, w_spectral, w_rgb, pick, item, items, filled=None):
    rows = grad.shape[0]
    wide, width = w_spectral.shape
    more = [] if filled is None else [filled]
    return pl.pallas_call(
        functools.partial(pixel_grad_kernel, item=item),
        grid_spec=pltpu.PrefetchScalarGridSpec(
            num_scalar_prefetch=1,
            grid=(1,),
            in_specs=[
                whole(grad.shape),
                whole(w_spectral.shape),
                whole(w_rgb.shape),
                whole(pick.shape),
            ]
            + [pl.BlockSpec(memory_space=pl.ANY)] * len(more),
            out_specs=pl.BlockSpec((rows, wide), lambda i, *_: (item, 0)),
        ),
        out_shape=jax.ShapeDtypeStruct((items * rows, wide), BF16),
        input_output_aliases={5: 0} if more else {},
        compiler_params=params(12),
        cost_estimate=long_cost(),
        name="pixel_grad",
    )(kinds, grad, w_spectral, w_rgb, pick, *more)


def gather_left(keep_refs, gone_refs, first, left_ref):
    rows = keep_refs[0].shape[-1]
    for pos, keep_ref in enumerate(keep_refs):
        left_ref[:, pos * rows : (pos + 1) * rows] = keep_ref[...]
    base = len(keep_refs) * rows
    for pos, gone_ref in enumerate(gone_refs):
        columns = slice(base + pos * rows, base + (pos + 1) * rows)
        if len(gone_ref.shape) == 2:
            left_ref[:, columns] = gone_ref[: left_ref.shape[0], :].astype(BF16)
            continue
        for part in range(2):
            left_ref[part * PART : (part + 1) * PART, columns] = gone_ref[first + part].astype(BF16)


def emit(left_ref, rights, send_ref, keep_ref, moves, columns=slice(None)):
    right = jnp.concatenate([r.astype(BF16) for r in rights], 0)
    total = nn(left_ref[...], right)
    half = LANES // 2
    for pos, block in enumerate(moves):
        out_ref = send_ref if pos < 4 else keep_ref
        value = total[block * half : (block + 1) * half]
        if len(out_ref.shape) == 4:
            out_ref[pos % 4, 0, :, columns] = value
        else:
            out_ref[pos % 4, :half, columns] = value


def plain_grad_kernel(
    ka_ref, kb_ref, la_ref, lb_ref, ra_ref, rb_ref, oa_ref, ob_ref, *refs, moves, vectors
):
    send_ref, keep_ref, left_ref = refs[-3:]

    @pl.when(pl.program_id(0) == 0)
    def _():
        gather_left((ka_ref, kb_ref), (la_ref, lb_ref), 0, left_ref)

    for part in range(oa_ref.shape[0]):
        columns = slice(part * PART, (part + 1) * PART)
        rights = (ra_ref[:, columns], rb_ref[:, columns], oa_ref[part], ob_ref[part])
        emit(left_ref, rights, send_ref, keep_ref, moves, columns)
    if vectors:
        early_ref, sa_ref, sb_ref = refs[:3]
        half = LANES // 2
        middle = left_ref.shape[0]
        late = sa_ref[...] + sb_ref[...] + (la_ref[middle:, :] + lb_ref[middle:, :])
        for pos, block in enumerate(moves):
            out_ref = send_ref if pos < 4 else keep_ref
            out_ref[pos % 4, half:, :] = early_ref[block]

            @pl.when(pl.program_id(0) == 0)
            def _(out_ref=out_ref, pos=pos, block=block):
                out_ref[pos % 4, half + 1 : half + 2, : late.shape[1]] = late[block : block + 1]


def plain_grad(keeps, lefts, rights, others, moves, name, skip=0, columns=None, lead=0, vectors=(), planes=1):
    half_width, rows = keeps[0][0].shape[-2:]
    columns = columns or rights[0].shape[1]
    wide = WIDE
    base = skip // (wide * PART)
    half = LANES // 2

    def keep_spec(array, item):
        if array.ndim == 2:
            return whole(array.shape)
        return pl.BlockSpec((None,) + array.shape[1:], lambda n: (item, 0, 0))

    right = pl.BlockSpec((rows, wide * PART), lambda n: (0, n + base))
    other = pl.BlockSpec((wide, rows, PART), lambda n: (n + base + lead // wide, 0, 0))
    height = half + 8 if vectors else half
    out = pl.BlockSpec((4, height, wide * PART), lambda n: (0, 0, n))
    shape = jax.ShapeDtypeStruct((4, height, columns), F32)
    if planes > 1:
        per = columns // planes // (wide * PART)
        out = pl.BlockSpec((4, 1, half, wide * PART), lambda n: (0, n // per, 0, n % per))
        shape = jax.ShapeDtypeStruct((4, planes, half, columns // planes), F32)

    def left_spec(array, item):
        if array.ndim == 2:
            return pl.BlockSpec((half_width + 8, rows), lambda n: (item, 0))
        return pl.BlockSpec((2, PART, rows), lambda n: (item, 0, 0))

    vector_specs = []
    if vectors:
        vector_specs = [pl.BlockSpec((8, 8, wide * PART), lambda n: (0, 0, n))]
        vector_specs += [whole(v.shape) for v in vectors[1:]]
    return pl.pallas_call(
        functools.partial(plain_grad_kernel, moves=moves, vectors=bool(vectors)),
        grid=(columns // (wide * PART),),
        in_specs=[keep_spec(*k) for k in keeps]
        + [left_spec(*v) for v in lefts]
        + [right, right, other, other]
        + vector_specs,
        out_specs=[out, out],
        scratch_shapes=[pltpu.VMEM((half_width, 4 * rows), BF16)],
        out_shape=[shape, shape],
        compiler_params=params(14),
        cost_estimate=short_cost(),
        name=name,
    )(*[k for k, _ in keeps], *[v for v, _ in lefts], *rights, *others, *vectors)


def query_key_kernel(
    aa_ref, ab_ref, fa_ref, fb_ref, ba_ref, bb_ref, da_ref, db_ref, send_ref, keep_ref, left_ref,
    *, moves,
):
    plane, step = pl.program_id(0), pl.program_id(1)

    @pl.when((plane == 0) & (step == 0))
    def _():
        gather_left((aa_ref, ab_ref), (fa_ref, fb_ref), 0, left_ref)

    spot = 2 + plane * pl.num_programs(1) + step
    emit(left_ref, (da_ref[...], db_ref[...], ba_ref[spot], bb_ref[spot]), send_ref, keep_ref, moves)


def value_out_kernel(
    aa_ref, ab_ref, fa_ref, fb_ref, ba_ref, bb_ref, da_ref, db_ref, ya_ref, yb_ref, ma_ref, mb_ref,
    send_ref, keep_ref, left_ref, *, moves,
):
    plane, step = pl.program_id(0), pl.program_id(1)

    @pl.when((plane == 0) & (step == 0))
    def _():
        gather_left((aa_ref, ab_ref), (fa_ref, fb_ref), 0, left_ref)

    @pl.when((plane == 1) & (step == 0))
    def _():
        gather_left((ya_ref, yb_ref), (ba_ref, bb_ref), 0, left_ref)

    @pl.when(plane == 0)
    def _():
        spot = 2 + 2 * pl.num_programs(1) + step
        emit(left_ref, (da_ref[...], db_ref[...], ba_ref[spot], bb_ref[spot]), send_ref, keep_ref, moves)

    @pl.when(plane == 1)
    def _():
        spot = 2 + step
        emit(left_ref, (ma_ref[...], mb_ref[...], fa_ref[spot], fb_ref[spot]), send_ref, keep_ref, moves)


def attn_grad(keep_a1, other_f, other_b, dqkv, moves, out_side=None):
    half_width, rows = keep_a1[0].shape
    columns = dqkv[0].shape[2]
    steps = columns // PART
    half = LANES // 2
    side = whole((half_width, rows))
    specs = [side, side] + [whole(v.shape) for v in (*other_f, *other_b)]
    if out_side is None:
        kernel, name, more = query_key_kernel, "query_key_grad", []
        plane = pl.BlockSpec((None, rows, PART), lambda p, n: (p, 0, n))
        specs += [plane, plane]
    else:
        kernel, name, more = value_out_kernel, "value_out_grad", [*out_side[0], *out_side[1]]
        plane = pl.BlockSpec((None, rows, PART), lambda p, n: (2, 0, n))
        mixed = pl.BlockSpec((rows, PART), lambda p, n: (0, n))
        specs += [plane, plane, side, side, mixed, mixed]
    out = pl.BlockSpec((4, half, PART), lambda p, n: (0, 0, p * steps + n))
    shape = jax.ShapeDtypeStruct((4, half, 2 * columns), F32)
    return pl.pallas_call(
        functools.partial(kernel, moves=moves),
        grid=(2, steps),
        in_specs=specs,
        out_specs=[out, out],
        scratch_shapes=[pltpu.VMEM((half_width, 4 * rows), BF16)],
        out_shape=[shape, shape],
        compiler_params=params(12),
        cost_estimate=short_cost(),
        name=name,
    )(*keep_a1, *other_f, *other_b, *dqkv, *more)


def exchange(values, axis, bit, size):
    return lax.ppermute(values, axis, [(i, i ^ bit) for i in range(size)])


def swap(values):
    return exchange(values, "tensor", 1, 2)


def after(first, values):
    return lax.optimization_barrier((first, values))[1]


X_FIRST = (2, 4, 8)
Z_FIRST = (4, 2, 8)


def block_flips(bits):
    return [sum((1 - ((p >> (2 - n)) & 1)) * (bits[n] // 2) for n in range(3)) for p in range(8)]


def block_moves(bits):
    stands = block_flips(X_FIRST)
    return tuple(stands.index(f) for f in block_flips(bits))


def places():
    me = lax.axis_index("dp")
    flips = jnp.array(block_flips(X_FIRST), jnp.int32)
    return jnp.concatenate([(me // 2) ^ flips, (me % 2)[None]]).astype(jnp.int32)


class Halving:
    def __init__(self, send, keep, bits, size, first=True):
        self.keep, self.bits, self.size = keep, bits, size
        self.unit = keep.shape[0] // 4
        self.recvs = [exchange(send, "dp", bits[0], size)] if first else []
        self.left = keep.shape[0]
        self.sent = send

    def value(self, order, tie=True):
        if tie:
            self.recvs[-1] = order.tie(self.recvs[-1])
        left = self.left
        count = max(left // 2, self.unit)
        total = self.keep.shape[0] - left
        value = self.keep[total : total + count]
        for recv in self.recvs:
            first = recv.shape[0] - left
            value = value + recv[first : first + count]
        order.mark(value)
        return value

    def came(self, recv):
        self.recvs.append(recv)
        self.left = self.left // 2

    def step(self, order):
        value = self.value(order)
        if self.left == self.unit:
            return value[0] if self.unit == 1 else value
        self.came(exchange(value, "dp", self.bits[len(self.recvs)], self.size))
        return None


class Order:
    def __init__(self):
        self.last = None

    def tie(self, values):
        return values if self.last is None else after(self.last, values)

    def mark(self, values):
        self.last = values


def local(
    pixels, item_kinds, gsd_codes, w_spectral, w_rgb, ln1_gain, ln1_bias, w_qkv, q_bias, v_bias,
    w_out, out_bias, ln2_gain, ln2_bias, w_fc1, fc1_bias, w_fc2, fc2_bias, cotangent, *, size,
):
    items = item_kinds.shape[0]
    rows = pixels.shape[0] // items
    width = w_out.shape[1]
    wide = pixels.shape[1]
    narrow = w_rgb.shape[0]
    bands = wide // (narrow // 3)
    custom = size == 16

    def row(vector):
        return vector.reshape(1, -1)

    g1, c1, g2, c2 = row(ln1_gain), row(ln1_bias), row(ln2_gain), row(ln2_bias)
    qb, vb, ob, b1 = row(q_bias), row(v_bias), row(out_bias), row(fc1_bias)
    wqkv = jnp.transpose(w_qkv, (1, 0, 2))

    source = np.arange(wide)[:, None]
    target = np.arange(narrow)[None, :]
    pick = jnp.asarray((source == (target // 3) * bands + target % 3).astype(ml_dtypes.bfloat16))

    ratio = (gsd_codes.astype(F32) + 1.0) / 4.0
    quarter = width // 4
    frequency = 1.0 / 10000.0 ** (jnp.arange(quarter).astype(F32) / quarter)
    spot = jnp.arange(GRID).astype(F32)
    angle = ratio[:, None, None] * spot[None, :, None] * frequency[None, None, :]
    tables = jnp.concatenate([jnp.sin(angle), jnp.cos(angle)], -1)

    def scatter(values):
        return lax.psum_scatter(values, "dp", scatter_dimension=0, tiled=True)

    def both(left, right):
        return sum(tn(left[i], right[i]) for i in range(items))

    order = Order()
    gate = None

    def send(values, wait=True):
        nonlocal gate
        if gate is not None:
            values = after(gate, values)
        gate = swap(values)
        return gate

    place = places() if custom else jnp.arange(9, dtype=jnp.int32) % 8
    move_x, move_z = block_moves(X_FIRST), block_moves(Z_FIRST)

    def other(values):
        return exchange(values, "dp", 1, size) if custom else values

    cut = rows * 3 // 8 // 8 * 8
    cuts = [(cut, rows - cut)] + [(rows,)] * (items - 1)

    def settle(values):
        values = order.tie(values)
        order.mark(jax.tree.leaves(values)[0])
        return values

    none = [None] * items
    part, mixed, erecv, fwd, orecv, ffn, grecv, bwd, arecv, last, ycot = (list(none) for _ in range(11))
    gmix, pk, gfwd, gact, gpre, gbwd, gdx0, da1, da2 = (list(none) for _ in range(9))

    for i in range(items):
        part[i], mixed[i] = embed(order.tie(item_kinds), pixels, w_spectral, w_rgb, pick, i, rows)
        order.mark(part[i])
        erecv[i] = send(part[i])
    keep_cot, gone_cot = turn_cot(order.tie(place), cotangent, rows)
    order.mark(gone_cot)
    gone_mix = []
    for i in range(items):
        gone_mix.append(pack(order.tie(mixed[i])))
        order.mark(gone_mix[i])
    gcot = other(gone_cot)
    gmix = [other(v) for v in gone_mix]
    for i in range(items):
        fwd[i] = attn_forward(
            part[i], erecv[i], tables[i], order.tie(g1), c1, wqkv, qb, vb, w_out
        )
        order.mark(fwd[i][4])
        orecv[i] = send(fwd[i][4])
        if i == 0:
            gcot = settle(gcot)
        else:
            gmix = [settle(v) for v in gmix]
        pk[i] = pack_attn(order.tie(place), fwd[i][1], fwd[i][3])
        order.mark(pk[i][1])
        gfwd[i] = other(pk[i][1])
    x0, a1, qkv, mix, _ = zip(*fwd)
    for i in range(items):
        ffn[i] = mlp(
            place, x0[i], fwd[i][4], orecv[i], order.tie(ob), g2, c2, w_fc1, b1, w_fc2, cotangent, i,
            cuts[i],
        )
        da2[i] = ffn[i][8:]
        order.mark(da2[i][0])
        if i == 0:
            grecv[i] = [send(v) for v in da2[i]]
        gact[i] = other(ffn[i][6])
        gpre[i] = other(ffn[i][7])
        if i == 0:
            gfwd = [settle(v) for v in gfwd]
        else:
            grecv[0][0] = settle(grecv[0][0])
            gact[0], gpre[0] = settle((gact[0], gpre[0]))
            ycot[1] = mlp_out(order.tie(ffn[1][2]), w_fc2)
            order.mark(ycot[1])
    x1, a2, act, dpre, b1sum, ka2 = list(zip(*[v[:6] for v in ffn]))
    if custom:
        gact[1] = order.tie(gact[1])
        fc2_h = Halving(
            *plain_grad(
                [(keep_cot, 0), (keep_cot, 1)], [(gcot, 0), (gcot, 1)], act, gact, move_x, "fc2_grad"
            ),
            X_FIRST, size,
        )
        order.mark(fc2_h.sent)
        gpre[1] = order.tie(gpre[1])
        fc1_s = plain_grad(
            [(ka2[0], 0), (ka2[1], 0)], [(gpre[0], 0), (gpre[1], 0)], dpre, gpre, move_z, "fc1_grad",
            lead=2, planes=2,
        )
        fc1_s = [v.reshape(8, *v.shape[2:]) for v in fc1_s]
        fc1_h = Halving(*fc1_s, Z_FIRST, size)
        order.mark(fc1_h.sent)
    grecv[1] = [send(order.tie(da2[1][0]))]
    for i in range(items):
        bwd[i] = attn_backward(
            place, da2[i], grecv[i], x1[i], cotangent, order.tie(g2), w_out, qkv[i], wqkv, i, cuts[i]
        )
        da1[i] = bwd[i][7:]
        order.mark(da1[i][0])
        if i == 0:
            arecv[i] = [send(v) for v in da1[i]]
        else:
            arecv[0][0] = settle(arecv[0][0])
            gbwd = [other(order.tie(bwd[0][6])), other(bwd[1][6])]
            ycot[0] = mlp_out(order.tie(ffn[0][2]), w_fc2)
            order.mark(ycot[0])
    dx1, dya, dqkv, sums2, qvsum, kdya = list(zip(*[v[:6] for v in bwd]))
    if custom:
        fc2_h.step(order)
        gbwd = [order.tie(v) for v in gbwd]
        keep_a1 = [v[0] for v in pk]
        attx_h = Halving(*attn_grad(keep_a1, gfwd, gbwd, dqkv, move_x), X_FIRST, size, first=False)
        order.mark(attx_h.sent)
        both_x = jnp.concatenate([fc1_h.value(order), attx_h.sent], 0)
        order.mark(both_x)
        gbwd[1] = order.tie(gbwd[1])
        both_x = exchange(both_x, "dp", 2, size)
        attz_h = Halving(
            *attn_grad(keep_a1, gfwd, gbwd, dqkv, move_z, (kdya, mix)), Z_FIRST, size
        )
        order.mark(attz_h.sent)
    arecv[1] = [send(order.tie(da1[1][0]))]
    riders = ()
    for i in range(items):
        estimate = long_cost() if i == 0 else short_cost()
        last[i] = first_norm_back(
            place, da1[i], arecv[i], x0[i], dx1[i], order.tie(g1), estimate, riders
        )
        order.mark(last[i][0])
        if custom and i == 0:
            fc2_h.step(order)
        if custom and i == 0:
            cube = pack_vectors(order.tie(place), sums2, qvsum, b1sum)
            order.mark(cube)
            riders = (last[0][3], cube)
    summed = list(none)
    summed[0] = send(order.tie(ycot[0]))
    dx0, sums1, kdx0, gone, blocks = zip(*last)
    pixels_grad = pixel_grad(order.tie(item_kinds), dx0[0], w_spectral, w_rgb, pick, 0, items)
    order.mark(pixels_grad)
    if custom:
        mid = mixed[0].shape[1] // 2
        gdx0 = order.tie(other(gone[1]))
        sides = ([(kdx0[0], 0), (kdx0[1], 0)], [(gdx0, 1), (gdx0, 0)], mixed, gmix)
        cube = (cube + order.tie(gdx0)[-cube.shape[0] :]).reshape(8, 1, -1)
        cube = jnp.pad(cube, ((0, 0), (0, 7), (0, 0)))
        embz_h = Halving(
            *plain_grad(*sides, move_z, "embed_grad_b", mid, mid, vectors=(cube, *blocks)),
            Z_FIRST, size,
        )
        order.mark(embz_h.sent)
        sides[3][1] = order.tie(gmix[1])
        embx_h = Halving(*plain_grad(*sides, move_x, "embed_grad_a", 0, mid), X_FIRST, size)
        order.mark(embx_h.sent)
    pixels_grad = pixel_grad(
        order.tie(item_kinds), dx0[1], w_spectral, w_rgb, pick, 1, items, pixels_grad
    )
    order.mark(pixels_grad)
    if custom:
        both_x = order.tie(both_x)
        fc1_h.came(both_x[:4])
        attx_h.recvs.append(both_x[4:])
        fc1_v = fc1_h.value(order, False)
        attx_v = attx_h.value(order, False)
    summed[0] = settle(summed[0])
    if custom:
        fc1_h.came(exchange(fc1_v, "dp", 8, size))
        attx_h.came(exchange(attx_v, "dp", 4, size))
        attz_h.step(order)
        fc2_g = fc2_h.step(order)
        attz_h.step(order)
        embz_h.step(order)
        fc1_g = fc1_h.step(order)
    summed[1] = send(order.tie(ycot[1]))
    if custom:
        embx_h.step(order)
        attx_h.step(order)
        embz_h.step(order)
        attz_g = attz_h.step(order)
    if custom:
        embx_h.step(order)
        attx_g = attx_h.step(order)
    summed[1] = settle(summed[1])
    block_out = jnp.concatenate(
        [(x1[i] + (ycot[i] + summed[i] + fc2_bias)).astype(BF16) for i in range(items)], 0
    )
    order.mark(block_out)
    if custom:
        embz_g = embz_h.step(order)
        embx_g = embx_h.step(order)
        shard = width // size
        core = lax.axis_index("dp") % 2
        spans = [(shard, row * LANES, LANES) for row in range(4)]
        spans += [(shard, 4 * LANES + row * LANES // 2, LANES // 2) for row in range(2)]
        spans += [(shard, 6 * LANES, 2 * LANES)]
        spans += [(shard + 1, row * LANES, LANES) for row in range(2)]
        outs = []
        for row, first, length in spans:
            low = embz_g[row, first : first + length // 2]
            high = embz_g[row, first + length // 2 : first + length]
            outs.append(jnp.where(core == 0, low, high))
        ln2_g, ln2_b, ob_g, b2_g, q_g, v_g, b1_g, ln1_g, ln1_b = outs
        embz_g = embz_g[:shard]
        emb_g = jnp.concatenate([embx_g, embz_g], 1)
        cut = attx_g.shape[1] // 2
        planes = [attx_g[:, :cut], attx_g[:, cut:], attz_g[:, :cut]]
        qkv_grad = jnp.transpose(jnp.stack(planes), (1, 0, 2))
        out_grad = attz_g[:, cut:].T
        fc1_g = jnp.concatenate([fc1_g[0], fc1_g[1]], 1)
    else:
        cot = [cotangent[i * rows : (i + 1) * rows] for i in range(items)]
        fc2_g = scatter(both(cot, act))
        fc1_g = scatter(both(a2, dpre))
        emb_g = scatter(both(dx0, mixed))
        qkv_grad = scatter(
            sum(
                lax.dot_general(
                    a1[i], dqkv[i], (((0,), (1,)), ((), ())), preferred_element_type=F32
                )
                for i in range(items)
            )
        )
        out_grad = scatter(both(dya, mix)).T
        totals = [v[0] + v[1] for v in (sums2, qvsum, b1sum, sums1)]
        rows_of = [(0, 0), (0, 1), (0, 2), (0, 3), (1, 0), (1, 1), (2, 0), (3, 0), (3, 1)]
        outs = [scatter(totals[n][row]) for n, row in rows_of]
        ln2_g, ln2_b, ob_g, b2_g, q_g, v_g, b1_g, ln1_g, ln1_b = outs
    spectral_grad = emb_g[:, :wide].T
    rgb_grad = emb_g[:, wide:].T
    return (
        block_out, pixels_grad, spectral_grad, rgb_grad, ln1_g, ln1_b, qkv_grad, q_g, v_g, out_grad,
        ob_g, ln2_g, ln2_b, fc1_g, b1_g, fc2_g.T, b2_g,
    )


def solution(mesh):
    in_specs = (
        P("dp", "tensor"),
        P("dp"),
        P("dp"),
        P("tensor", None),
        P("tensor", None),
        P(),
        P(),
        P(None, None, "tensor"),
        P("tensor"),
        P("tensor"),
        P("tensor", None),
        P(),
        P(),
        P(),
        P(None, "tensor"),
        P("tensor"),
        P("tensor", None),
        P(),
        P("dp", None),
    )
    out_specs = (
        P("dp", None),
        P("dp", "tensor"),
        P("tensor", "dp"),
        P("tensor", "dp"),
        P("dp"),
        P("dp"),
        P("dp", None, "tensor"),
        P(("tensor", "dp")),
        P(("tensor", "dp")),
        P("tensor", "dp"),
        P("dp"),
        P("dp"),
        P("dp"),
        P("dp", "tensor"),
        P(("tensor", "dp")),
        P("tensor", "dp"),
        P("dp"),
    )
    body = functools.partial(local, size=mesh.shape["dp"])
    return jax.shard_map(body, mesh=mesh, in_specs=in_specs, out_specs=out_specs, check_vma=False)
```

```python
import functools

import jax
import jax.numpy as jnp
import ml_dtypes
import numpy as np
from jax import lax
from jax.experimental import pallas as pl
from jax.experimental.pallas import tpu as pltpu
from jax.sharding import PartitionSpec as P

HEAD_DIM = 64
GRID = 16
EPS = 1e-06
F32 = jnp.float32
BF16 = jnp.bfloat16
LANES = 128
MIB = 1024 * 1024
QUAD = 256
PART = 256
WIDE = 2


def nn(left, right):
    return lax.dot_general(left, right, (((1,), (0,)), ((), ())), preferred_element_type=F32)


def nt(left, right):
    return lax.dot_general(left, right, (((1,), (1,)), ((), ())), preferred_element_type=F32)


def tn(left, right):
    return lax.dot_general(left, right, (((0,), (0,)), ((), ())), preferred_element_type=F32)


def params(mib):
    return pltpu.CompilerParams(vmem_limit_bytes=mib * MIB)


def short_cost():
    return pl.CostEstimate(flops=1000, bytes_accessed=1000, transcendentals=0)


def long_cost():
    return pl.CostEstimate(flops=int(1e11), bytes_accessed=1000, transcendentals=0)


def whole(shape):
    return pl.BlockSpec(shape, lambda *_: (0,) * len(shape), pipeline_mode=pl.Buffered(1))


def norm_parts(values):
    center = values - jnp.mean(values, -1, keepdims=True)
    spread = jnp.mean(center * center, -1, keepdims=True)
    inverse = lax.rsqrt(spread + EPS)
    return center * inverse, inverse


def norm_back(normed, inverse, grad, gain):
    scaled = grad * gain
    mean_scaled = jnp.mean(scaled, -1, keepdims=True)
    mean_cross = jnp.mean(scaled * normed, -1, keepdims=True)
    return inverse * (scaled - mean_scaled - normed * mean_cross)


def column_sum(values):
    return jnp.sum(values, 0, keepdims=True)


def turn(place, source_ref, turned_ref, columns):
    chips = turned_ref.shape[0] // LANES
    half = LANES // 2
    core = place[chips]
    low = pl.multiple_of(core * (chips * half), half)
    high = pl.multiple_of((1 - core) * (chips * half), half)
    for chip in range(chips):
        lanes = pl.ds(pl.multiple_of(place[chip] * LANES, LANES), LANES)
        block = source_ref[:, lanes].T
        turned_ref[pl.ds(low + chip * half, half), columns] = block[:half]
        turned_ref[pl.ds(high + chip * half, half), columns] = block[half:]


def spread(turned_ref, keep_ref, gone_ref, first=0):
    middle = turned_ref.shape[0] // 2
    keep_ref[...] = turned_ref[:middle, :]
    for part in range(2):
        start = middle + part * PART
        gone_ref[first + part] = turned_ref[start : start + PART, :].astype(F32)


def turn_cot_kernel(place, cot_ref, keep_ref, gone_ref, turned_ref):
    turn(place, cot_ref, turned_ref, slice(None))
    spread(turned_ref, keep_ref, gone_ref)


def turn_cot(place, cotangent, rows):
    width = cotangent.shape[1]
    items = cotangent.shape[0] // rows
    return pl.pallas_call(
        turn_cot_kernel,
        grid_spec=pltpu.PrefetchScalarGridSpec(
            num_scalar_prefetch=1,
            grid=(items,),
            in_specs=[pl.BlockSpec((rows, width), lambda i, *_: (i, 0))],
            out_specs=[
                pl.BlockSpec((None, width // 2, rows), lambda i, *_: (i, 0, 0)),
                pl.BlockSpec((2, PART, rows), lambda i, *_: (i, 0, 0)),
            ],
            scratch_shapes=[pltpu.VMEM((width, rows), BF16)],
        ),
        out_shape=[
            jax.ShapeDtypeStruct((items, width // 2, rows), BF16),
            jax.ShapeDtypeStruct((2 * items, PART, rows), F32),
        ],
        compiler_params=params(4),
        cost_estimate=short_cost(),
        name="turn_cotangent",
    )(place, cotangent)


def pack_kernel(values_ref, out_ref):
    out_ref[0] = values_ref[...].astype(F32)


def pack(values):
    rows, columns = values.shape
    return pl.pallas_call(
        pack_kernel,
        grid=(columns // PART,),
        in_specs=[pl.BlockSpec((rows, PART), lambda n: (0, n))],
        out_specs=pl.BlockSpec((1, rows, PART), lambda n: (n, 0, 0)),
        out_shape=jax.ShapeDtypeStruct((columns // PART, rows, PART), F32),
        compiler_params=params(4),
        cost_estimate=short_cost(),
        name="pack_pixels",
    )(values)


def pack_attn_kernel(place, a1_ref, o_ref, keep_ref, gone_ref, turned_ref):
    turn(place, a1_ref, turned_ref, slice(None))
    spread(turned_ref, keep_ref, gone_ref)
    for part in range(o_ref.shape[1] // PART):
        gone_ref[2 + part] = o_ref[:, part * PART : (part + 1) * PART].astype(F32)


def pack_attn(place, a1, mix):
    rows, width = a1.shape
    parts = 2 + mix.shape[1] // PART
    return pl.pallas_call(
        pack_attn_kernel,
        grid_spec=pltpu.PrefetchScalarGridSpec(
            num_scalar_prefetch=1,
            grid=(1,),
            in_specs=[whole(a1.shape), whole(mix.shape)],
            out_specs=[whole((width // 2, rows)), whole((parts, PART, rows))],
            scratch_shapes=[pltpu.VMEM((width, rows), BF16)],
        ),
        out_shape=[
            jax.ShapeDtypeStruct((width // 2, rows), BF16),
            jax.ShapeDtypeStruct((parts, PART, rows), F32),
        ],
        compiler_params=params(4),
        cost_estimate=short_cost(),
        name="pack_attn",
    )(place, a1, mix)


def pieces_of(length):
    third = length // 3 // LANES * LANES
    return [(0, third), (third, third), (2 * third, length - 2 * third)]


def embed_kernel(
    kinds, pix_ref, wspec_ref, wrgb_ref, pick_ref, part_ref, mixed_ref,
    pix_buf, wspec_buf, wrgb_buf, pick_buf, pix_sem, big_sem, small_sem, *, item,
):
    rows, wide = pix_buf.shape
    spectral = kinds[item] == 1
    pieces = pieces_of(wide)
    own_rows = pl.ds(item * rows, rows)

    @pl.when(spectral)
    def _():
        copies = []
        for n, (first, size) in enumerate(pieces):
            span = pl.ds(first, size)
            copies.append(
                (
                    pltpu.make_async_copy(
                        pix_ref.at[own_rows, span], mixed_ref.at[:, span], pix_sem.at[n]
                    ),
                    pltpu.make_async_copy(wspec_ref.at[span], wspec_buf.at[span], big_sem.at[n]),
                )
            )
        for pair in copies:
            for copy in pair:
                copy.start()
        mixed_ref[:, wide:] = jnp.zeros((rows, wrgb_buf.shape[0]), BF16)
        for n, (first, size) in enumerate(pieces):
            for copy in copies[n]:
                copy.wait()
            term = nn(mixed_ref[:, first : first + size], wspec_buf[first : first + size, :])
            if n == 0:
                part_ref[...] = term
            else:
                part_ref[...] += term

    @pl.when(jnp.logical_not(spectral))
    def _():
        copies = []
        for n, (first, size) in enumerate(pieces):
            span = pl.ds(first, size)
            copies.append(
                (
                    pltpu.make_async_copy(
                        pix_ref.at[own_rows, span], pix_buf.at[:, span], pix_sem.at[n]
                    ),
                    pltpu.make_async_copy(pick_ref.at[span], pick_buf.at[span], big_sem.at[n]),
                )
            )
        for pair in copies:
            for copy in pair:
                copy.start()
        weights = pltpu.make_async_copy(wrgb_ref, wrgb_buf, small_sem)
        weights.start()
        mixed_ref[:, :wide] = jnp.zeros((rows, wide), BF16)
        total = None
        for n, (first, size) in enumerate(pieces):
            for copy in copies[n]:
                copy.wait()
            term = nn(pix_buf[:, first : first + size], pick_buf[first : first + size, :])
            total = term if total is None else total + term
        mixed_ref[:, wide:] = total.astype(BF16)
        weights.wait()
        part_ref[...] = nn(mixed_ref[:, wide:], wrgb_buf[...])


def embed(kinds, pixels, w_spectral, w_rgb, pick, item, rows):
    wide, width = w_spectral.shape
    narrow = w_rgb.shape[0]
    far = pl.BlockSpec(memory_space=pltpu.HBM)
    return pl.pallas_call(
        functools.partial(embed_kernel, item=item),
        grid_spec=pltpu.PrefetchScalarGridSpec(
            num_scalar_prefetch=1,
            grid=(1,),
            in_specs=[far, far, far, far],
            out_specs=[whole((rows, width)), whole((rows, wide + narrow))],
            scratch_shapes=[
                pltpu.VMEM((rows, wide), BF16),
                pltpu.VMEM((wide, width), BF16),
                pltpu.VMEM((narrow, width), BF16),
                pltpu.VMEM((wide, narrow), BF16),
                pltpu.SemaphoreType.DMA((3,)),
                pltpu.SemaphoreType.DMA((3,)),
                pltpu.SemaphoreType.DMA(()),
            ],
        ),
        out_shape=[
            jax.ShapeDtypeStruct((rows, width), F32),
            jax.ShapeDtypeStruct((rows, wide + narrow), BF16),
        ],
        compiler_params=params(58),
        cost_estimate=short_cost(),
        name="embed",
    )(kinds, pixels, w_spectral, w_rgb, pick)


def pair_masks(rows):
    lane = lax.broadcasted_iota(jnp.int32, (rows, LANES), 1)
    return lane < HEAD_DIM, lane >= HEAD_DIM


def only(mask, values):
    return jnp.where(mask, values, jnp.zeros_like(values))


def softmax_rows(query, key):
    scores = nt(query, key) * (HEAD_DIM**-0.5)
    expo = jnp.exp(scores - jnp.max(scores, -1, keepdims=True))
    return expo / jnp.sum(expo, -1, keepdims=True)


def attn_forward_kernel(
    part_ref, recv_ref, table_ref, gain_ref, bias_ref, wqkv_ref, qb_ref, vb_ref, wout_ref,
    x0_ref, a1_ref, qkv_ref, o_ref, opart_ref,
):
    quad = pl.program_id(0)
    rows, width = part_ref.shape

    @pl.when(quad == 0)
    def _():
        side = table_ref.shape[0]
        half = table_ref.shape[1]
        table = table_ref[...]
        by_row = jnp.broadcast_to(table[:, None, :], (side, side, half)).reshape(rows, half)
        by_col = jnp.broadcast_to(table[None, :, :], (side, side, half)).reshape(rows, half)
        left = part_ref[:, :half] + recv_ref[:, :half] + by_row
        right = part_ref[:, half:] + recv_ref[:, half:] + by_col
        x0_ref[:, :half] = left
        x0_ref[:, half:] = right
        normed, _inv = norm_parts(x0_ref[...])
        a1_ref[...] = (normed * gain_ref[...] + bias_ref[...]).astype(BF16)
        opart_ref[...] = jnp.zeros_like(opart_ref)

    a1 = a1_ref[...]
    query = (nn(a1, wqkv_ref[0]) + qb_ref[...]).astype(BF16)
    key = nn(a1, wqkv_ref[1]).astype(BF16)
    value = (nn(a1, wqkv_ref[2]) + vb_ref[...]).astype(BF16)
    qkv_ref[0] = query
    qkv_ref[1] = key
    qkv_ref[2] = value
    masks = pair_masks(rows)
    for pair in range(query.shape[1] // LANES):
        span = slice(pair * LANES, (pair + 1) * LANES)
        q2, k2, v2 = query[:, span], key[:, span], value[:, span]
        mixed = None
        for mask in masks:
            probs = softmax_rows(only(mask, q2), k2).astype(BF16)
            term = nn(probs, only(mask, v2))
            mixed = term if mixed is None else mixed + term
        o_ref[:, span] = mixed.astype(BF16)
    opart_ref[...] += nn(o_ref[...], wout_ref[...])


def attn_forward(part, recv, table, gain, bias, w_qkv, q_bias, v_bias, w_out):
    rows, width = part.shape
    heads_wide = w_out.shape[0]
    steps = heads_wide // QUAD
    return pl.pallas_call(
        attn_forward_kernel,
        grid=(steps,),
        in_specs=[
            whole(part.shape),
            whole(recv.shape),
            whole(table.shape),
            whole(gain.shape),
            whole(bias.shape),
            pl.BlockSpec((3, width, QUAD), lambda n: (0, 0, n)),
            pl.BlockSpec((1, QUAD), lambda n: (0, n)),
            pl.BlockSpec((1, QUAD), lambda n: (0, n)),
            pl.BlockSpec((QUAD, width), lambda n: (n, 0)),
        ],
        out_specs=[
            whole((rows, width)),
            whole((rows, width)),
            pl.BlockSpec((3, rows, QUAD), lambda n: (0, 0, n)),
            pl.BlockSpec((rows, QUAD), lambda n: (0, n)),
            whole((rows, width)),
        ],
        out_shape=[
            jax.ShapeDtypeStruct((rows, width), F32),
            jax.ShapeDtypeStruct((rows, width), BF16),
            jax.ShapeDtypeStruct((3, rows, heads_wide), BF16),
            jax.ShapeDtypeStruct((rows, heads_wide), BF16),
            jax.ShapeDtypeStruct((rows, width), F32),
        ],
        compiler_params=params(10),
        cost_estimate=long_cost(),
        name="attn_forward",
    )(part, recv, table, gain, bias, w_qkv, q_bias, v_bias, w_out)


def put_rows(refs, values, add):
    first = 0
    for ref in refs:
        rows = ref.shape[0]
        if add:
            ref[...] += values[first : first + rows]
        else:
            ref[...] = values[first : first + rows]
        first += rows


def joined(refs):
    values = [ref[...] for ref in refs]
    return values[0] if len(values) == 1 else jnp.concatenate(values, 0)


def attn_backward_kernel(place, *refs, parts):
    gpart_refs, refs = refs[: parts[0]], refs[parts[0] :]
    grecv_refs, refs = refs[: parts[1]], refs[parts[1] :]
    x1_ref, cot_ref, gain_ref, wout_ref, qkv_ref, wqkv_ref, *refs = refs
    dx1_ref, dya_ref, dqkv_ref, sums_ref, qvsum_ref, keep_ref, gone_ref, *da1_refs = refs[:-1]
    turned_ref = refs[-1]
    quad = pl.program_id(0)
    rows = x1_ref.shape[0]

    @pl.when(quad == 0)
    def _():
        normed, inverse = norm_parts(x1_ref[...])
        grad = joined(gpart_refs) + joined(grecv_refs)
        cot = cot_ref[...].astype(F32)
        dx1 = cot + norm_back(normed, inverse, grad, gain_ref[...])
        dx1_ref[...] = dx1
        dya = dx1.astype(BF16)
        dya_ref[...] = dya
        sums_ref[0:1, :] = column_sum(grad * normed)
        sums_ref[1:2, :] = column_sum(grad)
        sums_ref[2:3, :] = column_sum(dya.astype(F32))
        sums_ref[3:4, :] = column_sum(cot)
        sums_ref[4:8, :] = jnp.zeros((4, sums_ref.shape[1]), F32)
        turn(place, dya_ref, turned_ref, slice(None))
        spread(turned_ref, keep_ref, gone_ref)

    dmix = nt(dya_ref[...], wout_ref[...]).astype(BF16)
    scale = HEAD_DIM**-0.5
    masks = pair_masks(rows)
    for pair in range(dmix.shape[1] // LANES):
        span = slice(pair * LANES, (pair + 1) * LANES)
        q2, k2, v2, d2 = qkv_ref[0, :, span], qkv_ref[1, :, span], qkv_ref[2, :, span], dmix[:, span]
        totals = [None, None, None]
        for mask in masks:
            qm, km, dm = only(mask, q2), only(mask, k2), only(mask, d2)
            probs = softmax_rows(qm, k2)
            dprobs = nt(dm, v2)
            dot_row = jnp.sum(probs * dprobs, -1, keepdims=True)
            dscores = (probs * (dprobs - dot_row)).astype(BF16)
            terms = [nn(dscores, km), tn(dscores, qm), tn(probs.astype(BF16), dm)]
            totals = [t if o is None else o + t for o, t in zip(totals, terms)]
        dqkv_ref[0, :, span] = (totals[0] * scale).astype(BF16)
        dqkv_ref[1, :, span] = (totals[1] * scale).astype(BF16)
        dqkv_ref[2, :, span] = totals[2].astype(BF16)
    da1 = nt(dqkv_ref[0], wqkv_ref[0]) + nt(dqkv_ref[1], wqkv_ref[1]) + nt(dqkv_ref[2], wqkv_ref[2])

    @pl.when(quad == 0)
    def _():
        put_rows(da1_refs, da1, False)

    @pl.when(quad != 0)
    def _():
        put_rows(da1_refs, da1, True)

    steps = pl.num_programs(0)
    for plane in range(3):
        gone_ref[2 + plane * steps + quad] = dqkv_ref[plane].astype(F32)
    qvsum_ref[0:1, :] = column_sum(dqkv_ref[0].astype(F32))
    qvsum_ref[1:2, :] = column_sum(dqkv_ref[2].astype(F32))
    qvsum_ref[2:8, :] = jnp.zeros((6, qvsum_ref.shape[1]), F32)


def attn_backward(place, gparts, grecvs, x1, cotangent, gain, w_out, qkv, w_qkv, item, cuts):
    rows, width = x1.shape
    heads_wide = w_out.shape[0]
    steps = heads_wide // QUAD
    return pl.pallas_call(
        functools.partial(attn_backward_kernel, parts=(len(gparts), len(grecvs))),
        grid_spec=pltpu.PrefetchScalarGridSpec(
            num_scalar_prefetch=1,
            grid=(steps,),
            in_specs=[
                *[whole(v.shape) for v in (*gparts, *grecvs)],
                whole(x1.shape),
                pl.BlockSpec((rows, width), lambda n, *_: (item, 0)),
                whole(gain.shape),
                pl.BlockSpec((QUAD, width), lambda n, *_: (n, 0)),
                pl.BlockSpec((3, rows, QUAD), lambda n, *_: (0, 0, n)),
                pl.BlockSpec((3, width, QUAD), lambda n, *_: (0, 0, n)),
            ],
            out_specs=[
                whole((rows, width)),
                whole((rows, width)),
                pl.BlockSpec((3, rows, QUAD), lambda n, *_: (0, 0, n)),
                whole((8, width)),
                pl.BlockSpec((8, QUAD), lambda n, *_: (0, n)),
                whole((width // 2, rows)),
                whole((2 + 3 * steps, PART, rows)),
                *[whole((cut, width)) for cut in cuts],
            ],
            scratch_shapes=[pltpu.VMEM((width, rows), BF16)],
        ),
        out_shape=[
            jax.ShapeDtypeStruct((rows, width), F32),
            jax.ShapeDtypeStruct((rows, width), BF16),
            jax.ShapeDtypeStruct((3, rows, heads_wide), BF16),
            jax.ShapeDtypeStruct((8, width), F32),
            jax.ShapeDtypeStruct((8, heads_wide), F32),
            jax.ShapeDtypeStruct((width // 2, rows), BF16),
            jax.ShapeDtypeStruct((2 + 3 * steps, PART, rows), F32),
            *[jax.ShapeDtypeStruct((cut, width), F32) for cut in cuts],
        ],
        compiler_params=params(16),
        cost_estimate=long_cost(),
        name="attn_backward",
    )(place, *gparts, *grecvs, x1, cotangent, gain, w_out, qkv, w_qkv)


def mlp_kernel(
    place, x0_ref, opart_ref, orecv_ref, obias_ref, gain_ref, bias_ref, wfc1_ref, b1_ref, wfc2_ref, cot_ref,
    x1_ref, a2_ref, act_ref, dpre_ref, b1sum_ref, keep_ref, gact_ref, gpre_ref, *refs,
):
    da2_refs, turned_ref = refs[:-1], refs[-1]
    step = pl.program_id(0)

    @pl.when(step == 0)
    def _():
        x1_ref[...] = x0_ref[...] + (opart_ref[...] + orecv_ref[...] + obias_ref[...])
        normed, _inv = norm_parts(x1_ref[...])
        a2_ref[...] = (normed * gain_ref[...] + bias_ref[...]).astype(BF16)
        turn(place, a2_ref, turned_ref, slice(None))
        spread(turned_ref, keep_ref, gpre_ref)

    pre = nn(a2_ref[...], wfc1_ref[...]) + b1_ref[...]
    dact = nt(cot_ref[...], wfc2_ref[...])
    cdf = 0.5 * (1.0 + lax.erf(pre * (2.0**-0.5)))
    act = (pre * cdf).astype(BF16)
    act_ref[...] = act
    density = jnp.exp(-0.5 * pre * pre) * 0.3989422804014327
    dpre = (dact * (cdf + pre * density)).astype(BF16)
    dpre_ref[...] = dpre
    for part in range(act.shape[1] // PART):
        columns = slice(part * PART, (part + 1) * PART)
        gact_ref[part] = act[:, columns].astype(F32)
        gpre_ref[2 + step * (act.shape[1] // PART) + part] = dpre[:, columns].astype(F32)
    b1sum_ref[...] = column_sum(dpre.astype(F32))
    if not da2_refs:
        return
    da2 = nt(dpre, wfc1_ref[...])

    @pl.when(step == 0)
    def _():
        put_rows(da2_refs, da2, False)

    @pl.when(step != 0)
    def _():
        put_rows(da2_refs, da2, True)


def mlp(
    place, x0, opart, orecv, out_bias, gain, bias, w_fc1, fc1_bias, w_fc2, cotangent, item, cuts
):
    rows, width = x0.shape
    hidden = w_fc1.shape[1]
    tile = 512
    parts = tile // PART
    row_tile = pl.BlockSpec((rows, tile), lambda n, *_: (0, n))
    gone = pl.BlockSpec((parts, rows, PART), lambda n, *_: (n, 0, 0))
    return pl.pallas_call(
        mlp_kernel,
        grid_spec=pltpu.PrefetchScalarGridSpec(
            num_scalar_prefetch=1,
            grid=(hidden // tile,),
            in_specs=[
                whole(x0.shape),
                whole(opart.shape),
                whole(orecv.shape),
                whole(out_bias.shape),
                whole(gain.shape),
                whole(bias.shape),
                pl.BlockSpec((width, tile), lambda n, *_: (0, n)),
                pl.BlockSpec((1, tile), lambda n, *_: (0, n)),
                pl.BlockSpec((tile, width), lambda n, *_: (n, 0)),
                pl.BlockSpec((rows, width), lambda n, *_: (item, 0)),
            ],
            out_specs=[
                whole((rows, width)),
                whole((rows, width)),
                row_tile,
                row_tile,
                pl.BlockSpec((1, tile), lambda n, *_: (0, n)),
                whole((width // 2, rows)),
                gone,
                whole((2 + hidden // PART, rows, PART)),
                *[whole((cut, width)) for cut in cuts],
            ],
            scratch_shapes=[pltpu.VMEM((width, rows), BF16)],
        ),
        out_shape=[
            jax.ShapeDtypeStruct((rows, width), F32),
            jax.ShapeDtypeStruct((rows, width), BF16),
            jax.ShapeDtypeStruct((rows, hidden), BF16),
            jax.ShapeDtypeStruct((rows, hidden), BF16),
            jax.ShapeDtypeStruct((1, hidden), F32),
            jax.ShapeDtypeStruct((width // 2, rows), BF16),
            jax.ShapeDtypeStruct((hidden // PART, rows, PART), F32),
            jax.ShapeDtypeStruct((2 + hidden // PART, rows, PART), F32),
            *[jax.ShapeDtypeStruct((cut, width), F32) for cut in cuts],
        ],
        compiler_params=params(14),
        cost_estimate=long_cost(),
        name="mlp",
    )(place, x0, opart, orecv, out_bias, gain, bias, w_fc1, fc1_bias, w_fc2, cotangent)


def mlp_back_kernel(dpre_ref, wfc1_ref, out_ref):
    out_ref[...] = nt(dpre_ref[...], wfc1_ref[...])


def mlp_back(dpre, w_fc1):
    rows, hidden = dpre.shape
    width = w_fc1.shape[0]
    tile = 512
    return pl.pallas_call(
        mlp_back_kernel,
        grid=(width // tile,),
        in_specs=[whole(dpre.shape), pl.BlockSpec((tile, hidden), lambda n: (n, 0))],
        out_specs=pl.BlockSpec((rows, tile), lambda n: (0, n)),
        out_shape=jax.ShapeDtypeStruct((rows, width), F32),
        compiler_params=params(6),
        cost_estimate=long_cost(),
        name="mlp_back",
    )(dpre, w_fc1)


def mlp_out_kernel(act_ref, wfc2_ref, out_ref):
    out_ref[...] = nn(act_ref[...], wfc2_ref[...])


def mlp_out(act, w_fc2, estimate):
    rows, hidden = act.shape
    width = w_fc2.shape[1]
    tile = 512
    return pl.pallas_call(
        mlp_out_kernel,
        grid=(width // tile,),
        in_specs=[whole(act.shape), pl.BlockSpec((hidden, tile), lambda n: (0, n))],
        out_specs=pl.BlockSpec((rows, tile), lambda n: (0, n)),
        out_shape=jax.ShapeDtypeStruct((rows, width), F32),
        compiler_params=params(6),
        cost_estimate=estimate,
        name="mlp_out",
    )(act, w_fc2)


def first_norm_back_kernel(place, *refs, parts, riders):
    gpart_refs, refs = refs[: parts[0]], refs[parts[0] :]
    grecv_refs, refs = refs[: parts[1]], refs[parts[1] :]
    rider_refs, refs = refs[:riders], refs[riders:]
    x0_ref, dx1_ref, gain_ref, dx0_ref, sums_ref, keep_ref, gone_ref, block_ref, turned_ref = refs
    normed, inverse = norm_parts(x0_ref[...])
    grad = joined(gpart_refs) + joined(grecv_refs)
    dx0_ref[...] = (dx1_ref[...] + norm_back(normed, inverse, grad, gain_ref[...])).astype(BF16)
    sums_ref[0:1, :] = column_sum(grad * normed)
    sums_ref[1:2, :] = column_sum(grad)
    sums_ref[2:8, :] = jnp.zeros((6, sums_ref.shape[1]), F32)
    turn(place, dx0_ref, turned_ref, slice(None))
    middle = turned_ref.shape[0] // 2
    keep_ref[...] = turned_ref[:middle, :]
    gone_ref[:middle, :] = turned_ref[middle:, :].astype(F32)
    for chip in range(8):
        lanes = pl.ds(pl.multiple_of(place[chip] * LANES, LANES), LANES)
        for row in range(2):
            block_ref[chip : chip + 1, row * LANES : (row + 1) * LANES] = sums_ref[row : row + 1, lanes]
    gone_ref[middle : middle + 8, :] = block_ref[...]
    first = middle + 8
    for rider_ref in rider_refs:
        gone_ref[first : first + rider_ref.shape[0], :] = rider_ref[...]
        first += rider_ref.shape[0]


def first_norm_back(place, gparts, grecvs, x0, dx1, gain, estimate, riders=()):
    rows, width = x0.shape
    operands = (*gparts, *grecvs, *riders, x0, dx1, gain)
    extra = sum(v.shape[0] for v in riders)
    shapes = [
        jax.ShapeDtypeStruct((rows, width), BF16),
        jax.ShapeDtypeStruct((8, width), F32),
        jax.ShapeDtypeStruct((width // 2, rows), BF16),
        jax.ShapeDtypeStruct((width // 2 + 8 + extra, rows), F32),
        jax.ShapeDtypeStruct((8, 2 * LANES), F32),
    ]
    return pl.pallas_call(
        functools.partial(
            first_norm_back_kernel, parts=(len(gparts), len(grecvs)), riders=len(riders)
        ),
        grid_spec=pltpu.PrefetchScalarGridSpec(
            num_scalar_prefetch=1,
            grid=(1,),
            in_specs=[whole(v.shape) for v in operands],
            out_specs=[whole(v.shape) for v in shapes],
            scratch_shapes=[pltpu.VMEM((width, rows), BF16)],
        ),
        out_shape=shapes,
        compiler_params=params(10),
        cost_estimate=estimate,
        name="first_norm_back",
    )(place, *operands)


def pack_vectors_kernel(place, sa_ref, sb_ref, qa_ref, qb_ref, ba_ref, bb_ref, out_ref, *refs):
    sums_ref, qv_ref, hidden_ref = refs
    sums_ref[...] = sa_ref[...] + sb_ref[...]
    qv_ref[...] = qa_ref[...] + qb_ref[...]
    hidden_ref[...] = ba_ref[...] + bb_ref[...]
    out_ref[...] = jnp.zeros_like(out_ref)
    half = LANES // 2
    for pos in range(8):
        chip = place[pos]
        lanes = pl.ds(pl.multiple_of(chip * LANES, LANES), LANES)
        for row in range(4):
            first = row % 2 * LANES
            spot = 4 * pos + row // 2
            out_ref[spot : spot + 1, first : first + LANES] = sums_ref[row : row + 1, lanes]
        both = pl.ds(pl.multiple_of(chip // 2 * LANES, LANES), LANES)
        spot = 4 * pos + 2
        for row in range(2):
            pair = qv_ref[row : row + 1, both]
            own = jnp.where(chip % 2 == 0, pair[:, :half], pair[:, half:])
            out_ref[spot : spot + 1, row * half : (row + 1) * half] = own
        wide = pl.ds(pl.multiple_of(chip * 2 * LANES, 2 * LANES), 2 * LANES)
        out_ref[spot + 1 : spot + 2, :] = hidden_ref[0:1, wide]


def pack_vectors(place, sums, qv, hidden):
    operands = (*sums, *qv, *hidden)
    return pl.pallas_call(
        pack_vectors_kernel,
        grid_spec=pltpu.PrefetchScalarGridSpec(
            num_scalar_prefetch=1,
            grid=(1,),
            in_specs=[whole(v.shape) for v in operands],
            out_specs=whole((32, 2 * LANES)),
            scratch_shapes=[pltpu.VMEM(v[0].shape, F32) for v in (sums, qv, hidden)],
        ),
        out_shape=jax.ShapeDtypeStruct((32, 2 * LANES), F32),
        compiler_params=params(4),
        cost_estimate=short_cost(),
        name="pack_vectors",
    )(place, *operands)


def pixel_grad_kernel(kinds, grad_ref, wspec_ref, wrgb_ref, pick_ref, *refs, item):
    out_ref = refs[-1]
    spectral = kinds[item] == 1
    grad = grad_ref[...]
    wide = wspec_ref.shape[0]
    cut = (wide // 2 + LANES - 1) // LANES * LANES

    @pl.when(spectral)
    def _():
        out_ref[:, :cut] = nt(grad, wspec_ref[:cut, :]).astype(BF16)
        out_ref[:, cut:] = nt(grad, wspec_ref[cut:, :]).astype(BF16)

    @pl.when(jnp.logical_not(spectral))
    def _():
        small = nt(grad, wrgb_ref[...]).astype(BF16)
        out_ref[...] = nt(small, pick_ref[...]).astype(BF16)


def pixel_grad(kinds, grad, w_spectral, w_rgb, pick, item, items, filled=None):
    rows = grad.shape[0]
    wide, width = w_spectral.shape
    more = [] if filled is None else [filled]
    return pl.pallas_call(
        functools.partial(pixel_grad_kernel, item=item),
        grid_spec=pltpu.PrefetchScalarGridSpec(
            num_scalar_prefetch=1,
            grid=(1,),
            in_specs=[
                whole(grad.shape),
                whole(w_spectral.shape),
                whole(w_rgb.shape),
                whole(pick.shape),
            ]
            + [pl.BlockSpec(memory_space=pl.ANY)] * len(more),
            out_specs=pl.BlockSpec((rows, wide), lambda i, *_: (item, 0)),
        ),
        out_shape=jax.ShapeDtypeStruct((items * rows, wide), BF16),
        input_output_aliases={5: 0} if more else {},
        compiler_params=params(12),
        cost_estimate=long_cost(),
        name="pixel_grad",
    )(kinds, grad, w_spectral, w_rgb, pick, *more)


def gather_left(keep_refs, gone_refs, first, left_ref):
    rows = keep_refs[0].shape[-1]
    for pos, keep_ref in enumerate(keep_refs):
        left_ref[:, pos * rows : (pos + 1) * rows] = keep_ref[...]
    base = len(keep_refs) * rows
    for pos, gone_ref in enumerate(gone_refs):
        columns = slice(base + pos * rows, base + (pos + 1) * rows)
        if len(gone_ref.shape) == 2:
            left_ref[:, columns] = gone_ref[: left_ref.shape[0], :].astype(BF16)
            continue
        for part in range(2):
            left_ref[part * PART : (part + 1) * PART, columns] = gone_ref[first + part].astype(BF16)


def emit(left_ref, rights, send_ref, keep_ref, moves, columns=slice(None)):
    right = jnp.concatenate([r.astype(BF16) for r in rights], 0)
    total = nn(left_ref[...], right)
    half = LANES // 2
    for pos, block in enumerate(moves):
        out_ref = send_ref if pos < 4 else keep_ref
        value = total[block * half : (block + 1) * half]
        if len(out_ref.shape) == 4:
            out_ref[pos % 4, 0, :, columns] = value
        else:
            out_ref[pos % 4, :half, columns] = value


def plain_grad_kernel(
    ka_ref, kb_ref, la_ref, lb_ref, ra_ref, rb_ref, oa_ref, ob_ref, *refs, moves, vectors
):
    send_ref, keep_ref, left_ref = refs[-3:]

    @pl.when(pl.program_id(0) == 0)
    def _():
        gather_left((ka_ref, kb_ref), (la_ref, lb_ref), 0, left_ref)

    for part in range(oa_ref.shape[0]):
        columns = slice(part * PART, (part + 1) * PART)
        rights = (ra_ref[:, columns], rb_ref[:, columns], oa_ref[part], ob_ref[part])
        emit(left_ref, rights, send_ref, keep_ref, moves, columns)
    if vectors:
        early_ref, sa_ref, sb_ref = refs[:3]
        half = LANES // 2
        middle = left_ref.shape[0]
        late = sa_ref[...] + sb_ref[...] + (la_ref[middle:, :] + lb_ref[middle:, :])
        for pos, block in enumerate(moves):
            out_ref = send_ref if pos < 4 else keep_ref
            out_ref[pos % 4, half:, :] = early_ref[block]

            @pl.when(pl.program_id(0) == 0)
            def _(out_ref=out_ref, pos=pos, block=block):
                out_ref[pos % 4, half + 1 : half + 2, : late.shape[1]] = late[block : block + 1]


def plain_grad(keeps, lefts, rights, others, moves, name, skip=0, columns=None, lead=0, vectors=(), planes=1):
    half_width, rows = keeps[0][0].shape[-2:]
    columns = columns or rights[0].shape[1]
    wide = WIDE
    base = skip // (wide * PART)
    half = LANES // 2

    def keep_spec(array, item):
        if array.ndim == 2:
            return whole(array.shape)
        return pl.BlockSpec((None,) + array.shape[1:], lambda n: (item, 0, 0))

    right = pl.BlockSpec((rows, wide * PART), lambda n: (0, n + base))
    other = pl.BlockSpec((wide, rows, PART), lambda n: (n + base + lead // wide, 0, 0))
    height = half + 8 if vectors else half
    out = pl.BlockSpec((4, height, wide * PART), lambda n: (0, 0, n))
    shape = jax.ShapeDtypeStruct((4, height, columns), F32)
    if planes > 1:
        per = columns // planes // (wide * PART)
        out = pl.BlockSpec((4, 1, half, wide * PART), lambda n: (0, n // per, 0, n % per))
        shape = jax.ShapeDtypeStruct((4, planes, half, columns // planes), F32)

    def left_spec(array, item):
        if array.ndim == 2:
            return pl.BlockSpec((half_width + 8, rows), lambda n: (item, 0))
        return pl.BlockSpec((2, PART, rows), lambda n: (item, 0, 0))

    vector_specs = []
    if vectors:
        vector_specs = [pl.BlockSpec((8, 8, wide * PART), lambda n: (0, 0, n))]
        vector_specs += [whole(v.shape) for v in vectors[1:]]
    return pl.pallas_call(
        functools.partial(plain_grad_kernel, moves=moves, vectors=bool(vectors)),
        grid=(columns // (wide * PART),),
        in_specs=[keep_spec(*k) for k in keeps]
        + [left_spec(*v) for v in lefts]
        + [right, right, other, other]
        + vector_specs,
        out_specs=[out, out],
        scratch_shapes=[pltpu.VMEM((half_width, 4 * rows), BF16)],
        out_shape=[shape, shape],
        compiler_params=params(14),
        cost_estimate=short_cost(),
        name=name,
    )(*[k for k, _ in keeps], *[v for v, _ in lefts], *rights, *others, *vectors)


def query_key_kernel(
    aa_ref, ab_ref, fa_ref, fb_ref, ba_ref, bb_ref, da_ref, db_ref, send_ref, keep_ref, left_ref,
    *, moves,
):
    plane, step = pl.program_id(0), pl.program_id(1)

    @pl.when((plane == 0) & (step == 0))
    def _():
        gather_left((aa_ref, ab_ref), (fa_ref, fb_ref), 0, left_ref)

    spot = 2 + plane * pl.num_programs(1) + step
    emit(left_ref, (da_ref[...], db_ref[...], ba_ref[spot], bb_ref[spot]), send_ref, keep_ref, moves)


def value_out_kernel(
    aa_ref, ab_ref, fa_ref, fb_ref, ba_ref, bb_ref, da_ref, db_ref, ya_ref, yb_ref, ma_ref, mb_ref,
    send_ref, keep_ref, left_ref, *, moves,
):
    plane, step = pl.program_id(0), pl.program_id(1)

    @pl.when((plane == 0) & (step == 0))
    def _():
        gather_left((aa_ref, ab_ref), (fa_ref, fb_ref), 0, left_ref)

    @pl.when((plane == 1) & (step == 0))
    def _():
        gather_left((ya_ref, yb_ref), (ba_ref, bb_ref), 0, left_ref)

    @pl.when(plane == 0)
    def _():
        spot = 2 + 2 * pl.num_programs(1) + step
        emit(left_ref, (da_ref[...], db_ref[...], ba_ref[spot], bb_ref[spot]), send_ref, keep_ref, moves)

    @pl.when(plane == 1)
    def _():
        spot = 2 + step
        emit(left_ref, (ma_ref[...], mb_ref[...], fa_ref[spot], fb_ref[spot]), send_ref, keep_ref, moves)


def attn_grad(keep_a1, other_f, other_b, dqkv, moves, out_side=None):
    half_width, rows = keep_a1[0].shape
    columns = dqkv[0].shape[2]
    steps = columns // PART
    half = LANES // 2
    side = whole((half_width, rows))
    specs = [side, side] + [whole(v.shape) for v in (*other_f, *other_b)]
    if out_side is None:
        kernel, name, more = query_key_kernel, "query_key_grad", []
        plane = pl.BlockSpec((None, rows, PART), lambda p, n: (p, 0, n))
        specs += [plane, plane]
    else:
        kernel, name, more = value_out_kernel, "value_out_grad", [*out_side[0], *out_side[1]]
        plane = pl.BlockSpec((None, rows, PART), lambda p, n: (2, 0, n))
        mixed = pl.BlockSpec((rows, PART), lambda p, n: (0, n))
        specs += [plane, plane, side, side, mixed, mixed]
    out = pl.BlockSpec((4, half, PART), lambda p, n: (0, 0, p * steps + n))
    shape = jax.ShapeDtypeStruct((4, half, 2 * columns), F32)
    return pl.pallas_call(
        functools.partial(kernel, moves=moves),
        grid=(2, steps),
        in_specs=specs,
        out_specs=[out, out],
        scratch_shapes=[pltpu.VMEM((half_width, 4 * rows), BF16)],
        out_shape=[shape, shape],
        compiler_params=params(12),
        cost_estimate=short_cost(),
        name=name,
    )(*keep_a1, *other_f, *other_b, *dqkv, *more)


def exchange(values, axis, bit, size):
    return lax.ppermute(values, axis, [(i, i ^ bit) for i in range(size)])


def swap(values):
    return exchange(values, "tensor", 1, 2)


def after(first, values):
    return lax.optimization_barrier((first, values))[1]


X_FIRST = (2, 4, 8)
Z_FIRST = (4, 2, 8)


def block_flips(bits):
    return [sum((1 - ((p >> (2 - n)) & 1)) * (bits[n] // 2) for n in range(3)) for p in range(8)]


def block_moves(bits):
    stands = block_flips(X_FIRST)
    return tuple(stands.index(f) for f in block_flips(bits))


def places():
    me = lax.axis_index("dp")
    flips = jnp.array(block_flips(X_FIRST), jnp.int32)
    return jnp.concatenate([(me // 2) ^ flips, (me % 2)[None]]).astype(jnp.int32)


class Halving:
    def __init__(self, send, keep, bits, size, first=True):
        self.keep, self.bits, self.size = keep, bits, size
        self.unit = keep.shape[0] // 4
        self.recvs = [exchange(send, "dp", bits[0], size)] if first else []
        self.left = keep.shape[0]
        self.sent = send

    def value(self, order, tie=True):
        if tie:
            self.recvs[-1] = order.tie(self.recvs[-1])
        left = self.left
        count = max(left // 2, self.unit)
        total = self.keep.shape[0] - left
        value = self.keep[total : total + count]
        for recv in self.recvs:
            first = recv.shape[0] - left
            value = value + recv[first : first + count]
        order.mark(value)
        return value

    def came(self, recv):
        self.recvs.append(recv)
        self.left = self.left // 2

    def step(self, order):
        value = self.value(order)
        if self.left == self.unit:
            return value[0] if self.unit == 1 else value
        self.came(exchange(value, "dp", self.bits[len(self.recvs)], self.size))
        return None


class Order:
    def __init__(self):
        self.last = None

    def tie(self, values):
        return values if self.last is None else after(self.last, values)

    def mark(self, values):
        self.last = values


def local(
    pixels, item_kinds, gsd_codes, w_spectral, w_rgb, ln1_gain, ln1_bias, w_qkv, q_bias, v_bias,
    w_out, out_bias, ln2_gain, ln2_bias, w_fc1, fc1_bias, w_fc2, fc2_bias, cotangent, *, size,
):
    items = item_kinds.shape[0]
    rows = pixels.shape[0] // items
    width = w_out.shape[1]
    wide = pixels.shape[1]
    narrow = w_rgb.shape[0]
    bands = wide // (narrow // 3)
    custom = size == 16

    def row(vector):
        return vector.reshape(1, -1)

    g1, c1, g2, c2 = row(ln1_gain), row(ln1_bias), row(ln2_gain), row(ln2_bias)
    qb, vb, ob, b1 = row(q_bias), row(v_bias), row(out_bias), row(fc1_bias)
    wqkv = jnp.transpose(w_qkv, (1, 0, 2))

    source = np.arange(wide)[:, None]
    target = np.arange(narrow)[None, :]
    pick = jnp.asarray((source == (target // 3) * bands + target % 3).astype(ml_dtypes.bfloat16))

    ratio = (gsd_codes.astype(F32) + 1.0) / 4.0
    quarter = width // 4
    frequency = 1.0 / 10000.0 ** (jnp.arange(quarter).astype(F32) / quarter)
    spot = jnp.arange(GRID).astype(F32)
    angle = ratio[:, None, None] * spot[None, :, None] * frequency[None, None, :]
    tables = jnp.concatenate([jnp.sin(angle), jnp.cos(angle)], -1)

    def scatter(values):
        return lax.psum_scatter(values, "dp", scatter_dimension=0, tiled=True)

    def both(left, right):
        return sum(tn(left[i], right[i]) for i in range(items))

    order = Order()
    gate = None

    def send(values, wait=True):
        nonlocal gate
        if gate is not None:
            values = after(gate, values)
        gate = swap(values)
        return gate

    place = places() if custom else jnp.arange(9, dtype=jnp.int32) % 8
    move_x, move_z = block_moves(X_FIRST), block_moves(Z_FIRST)

    def other(values):
        return exchange(values, "dp", 1, size) if custom else values

    cut = rows * 3 // 8 // 8 * 8
    cuts = [(cut, rows - cut)] + [(rows,)] * (items - 1)

    def settle(values):
        values = order.tie(values)
        order.mark(jax.tree.leaves(values)[0])
        return values

    none = [None] * items
    part, mixed, erecv, fwd, orecv, ffn, grecv, bwd, arecv, last, ycot = (list(none) for _ in range(11))
    gmix, pk, gfwd, gact, gpre, gbwd, gdx0, da1, da2 = (list(none) for _ in range(9))

    for i in range(items):
        part[i], mixed[i] = embed(order.tie(item_kinds), pixels, w_spectral, w_rgb, pick, i, rows)
        order.mark(part[i])
        erecv[i] = send(part[i])
    keep_cot, gone_cot = turn_cot(order.tie(place), cotangent, rows)
    order.mark(gone_cot)
    gone_mix = []
    for i in range(items):
        gone_mix.append(pack(order.tie(mixed[i])))
        order.mark(gone_mix[i])
    gcot = other(gone_cot)
    gmix = [other(v) for v in gone_mix]
    for i in range(items):
        fwd[i] = attn_forward(
            part[i], erecv[i], tables[i], order.tie(g1), c1, wqkv, qb, vb, w_out
        )
        order.mark(fwd[i][4])
        orecv[i] = send(fwd[i][4])
        if i == 0:
            gcot = settle(gcot)
        else:
            gmix = [settle(v) for v in gmix]
        pk[i] = pack_attn(order.tie(place), fwd[i][1], fwd[i][3])
        order.mark(pk[i][1])
        gfwd[i] = other(pk[i][1])
    x0, a1, qkv, mix, _ = zip(*fwd)
    for i in range(items):
        ffn[i] = mlp(
            place, x0[i], fwd[i][4], orecv[i], order.tie(ob), g2, c2, w_fc1, b1, w_fc2, cotangent, i,
            cuts[i] if i == 0 else (),
        )
        da2[i] = ffn[i][8:]
        order.mark(da2[i][0] if i == 0 else ffn[i][6])
        if i == 0:
            grecv[i] = [send(v) for v in da2[i]]
        gact[i] = other(ffn[i][6])
        gpre[i] = other(ffn[i][7])
        if i == 0:
            gfwd = [settle(v) for v in gfwd]
        else:
            grecv[0][0] = settle(grecv[0][0])
            gact[0], gpre[0] = settle((gact[0], gpre[0]))
            da2[1] = [mlp_back(order.tie(ffn[1][3]), w_fc1)]
            order.mark(da2[1][0])
    x1, a2, act, dpre, b1sum, ka2 = list(zip(*[v[:6] for v in ffn]))
    if custom:
        gact[1] = order.tie(gact[1])
        fc2_h = Halving(
            *plain_grad(
                [(keep_cot, 0), (keep_cot, 1)], [(gcot, 0), (gcot, 1)], act, gact, move_x, "fc2_grad"
            ),
            X_FIRST, size,
        )
        order.mark(fc2_h.sent)
        gpre[1] = order.tie(gpre[1])
        fc1_s = plain_grad(
            [(ka2[0], 0), (ka2[1], 0)], [(gpre[0], 0), (gpre[1], 0)], dpre, gpre, move_z, "fc1_grad",
            lead=2, planes=2,
        )
        fc1_s = [v.reshape(8, *v.shape[2:]) for v in fc1_s]
        fc1_h = Halving(*fc1_s, Z_FIRST, size)
        order.mark(fc1_h.sent)
    grecv[1] = [send(order.tie(da2[1][0]))]
    for i in range(items):
        bwd[i] = attn_backward(
            place, da2[i], grecv[i], x1[i], cotangent, order.tie(g2), w_out, qkv[i], wqkv, i, cuts[i]
        )
        da1[i] = bwd[i][7:]
        order.mark(da1[i][0])
        if i == 0:
            arecv[i] = [send(v) for v in da1[i]]
            ycot[1] = mlp_out(order.tie(ffn[1][2]), w_fc2, short_cost())
            order.mark(ycot[1])
        else:
            arecv[0][0] = settle(arecv[0][0])
            gbwd = [other(order.tie(bwd[0][6])), other(bwd[1][6])]
            ycot[0] = mlp_out(order.tie(ffn[0][2]), w_fc2, long_cost())
            order.mark(ycot[0])
    dx1, dya, dqkv, sums2, qvsum, kdya = list(zip(*[v[:6] for v in bwd]))
    if custom:
        fc2_h.step(order)
        gbwd = [order.tie(v) for v in gbwd]
        keep_a1 = [v[0] for v in pk]
        attx_h = Halving(*attn_grad(keep_a1, gfwd, gbwd, dqkv, move_x), X_FIRST, size, first=False)
        order.mark(attx_h.sent)
        both_x = jnp.concatenate([fc1_h.value(order), attx_h.sent], 0)
        order.mark(both_x)
        gbwd[1] = order.tie(gbwd[1])
        both_x = exchange(both_x, "dp", 2, size)
        attz_h = Halving(
            *attn_grad(keep_a1, gfwd, gbwd, dqkv, move_z, (kdya, mix)), Z_FIRST, size
        )
        order.mark(attz_h.sent)
    arecv[1] = [send(order.tie(da1[1][0]))]
    riders = ()
    for i in range(items):
        estimate = long_cost() if i == 0 else short_cost()
        last[i] = first_norm_back(
            place, da1[i], arecv[i], x0[i], dx1[i], order.tie(g1), estimate, riders
        )
        order.mark(last[i][0])
        if custom and i == 0:
            fc2_h.step(order)
        if custom and i == 0:
            cube = pack_vectors(order.tie(place), sums2, qvsum, b1sum)
            order.mark(cube)
            riders = (last[0][3], cube)
    summed = list(none)
    summed[0] = send(order.tie(ycot[0]))
    dx0, sums1, kdx0, gone, blocks = zip(*last)
    pixels_grad = pixel_grad(order.tie(item_kinds), dx0[0], w_spectral, w_rgb, pick, 0, items)
    order.mark(pixels_grad)
    if custom:
        mid = mixed[0].shape[1] // 2
        gdx0 = order.tie(other(gone[1]))
        sides = ([(kdx0[0], 0), (kdx0[1], 0)], [(gdx0, 1), (gdx0, 0)], mixed, gmix)
        cube = (cube + order.tie(gdx0)[-cube.shape[0] :]).reshape(8, 1, -1)
        cube = jnp.pad(cube, ((0, 0), (0, 7), (0, 0)))
        embz_h = Halving(
            *plain_grad(*sides, move_z, "embed_grad_b", mid, mid, vectors=(cube, *blocks)),
            Z_FIRST, size,
        )
        order.mark(embz_h.sent)
        sides[3][1] = order.tie(gmix[1])
        embx_h = Halving(*plain_grad(*sides, move_x, "embed_grad_a", 0, mid), X_FIRST, size)
        order.mark(embx_h.sent)
    pixels_grad = pixel_grad(
        order.tie(item_kinds), dx0[1], w_spectral, w_rgb, pick, 1, items, pixels_grad
    )
    order.mark(pixels_grad)
    if custom:
        both_x = order.tie(both_x)
        fc1_h.came(both_x[:4])
        attx_h.recvs.append(both_x[4:])
        fc1_v = fc1_h.value(order, False)
        attx_v = attx_h.value(order, False)
    summed[0] = settle(summed[0])
    if custom:
        fc1_h.came(exchange(fc1_v, "dp", 8, size))
        attx_h.came(exchange(attx_v, "dp", 4, size))
        attz_h.step(order)
        fc2_g = fc2_h.step(order)
        attz_h.step(order)
        embz_h.step(order)
        fc1_g = fc1_h.step(order)
    summed[1] = send(order.tie(ycot[1]))
    if custom:
        embx_h.step(order)
        attx_h.step(order)
        embz_h.step(order)
        attz_g = attz_h.step(order)
    if custom:
        embx_h.step(order)
        attx_g = attx_h.step(order)
    summed[1] = settle(summed[1])
    block_out = jnp.concatenate(
        [(x1[i] + (ycot[i] + summed[i] + fc2_bias)).astype(BF16) for i in range(items)], 0
    )
    order.mark(block_out)
    if custom:
        embz_g = embz_h.step(order)
        embx_g = embx_h.step(order)
        shard = width // size
        core = lax.axis_index("dp") % 2
        spans = [(shard, row * LANES, LANES) for row in range(4)]
        spans += [(shard, 4 * LANES + row * LANES // 2, LANES // 2) for row in range(2)]
        spans += [(shard, 6 * LANES, 2 * LANES)]
        spans += [(shard + 1, row * LANES, LANES) for row in range(2)]
        outs = []
        for row, first, length in spans:
            low = embz_g[row, first : first + length // 2]
            high = embz_g[row, first + length // 2 : first + length]
            outs.append(jnp.where(core == 0, low, high))
        ln2_g, ln2_b, ob_g, b2_g, q_g, v_g, b1_g, ln1_g, ln1_b = outs
        embz_g = embz_g[:shard]
        emb_g = jnp.concatenate([embx_g, embz_g], 1)
        cut = attx_g.shape[1] // 2
        planes = [attx_g[:, :cut], attx_g[:, cut:], attz_g[:, :cut]]
        qkv_grad = jnp.transpose(jnp.stack(planes), (1, 0, 2))
        out_grad = attz_g[:, cut:].T
        fc1_g = jnp.concatenate([fc1_g[0], fc1_g[1]], 1)
    else:
        cot = [cotangent[i * rows : (i + 1) * rows] for i in range(items)]
        fc2_g = scatter(both(cot, act))
        fc1_g = scatter(both(a2, dpre))
        emb_g = scatter(both(dx0, mixed))
        qkv_grad = scatter(
            sum(
                lax.dot_general(
                    a1[i], dqkv[i], (((0,), (1,)), ((), ())), preferred_element_type=F32
                )
                for i in range(items)
            )
        )
        out_grad = scatter(both(dya, mix)).T
        totals = [v[0] + v[1] for v in (sums2, qvsum, b1sum, sums1)]
        rows_of = [(0, 0), (0, 1), (0, 2), (0, 3), (1, 0), (1, 1), (2, 0), (3, 0), (3, 1)]
        outs = [scatter(totals[n][row]) for n, row in rows_of]
        ln2_g, ln2_b, ob_g, b2_g, q_g, v_g, b1_g, ln1_g, ln1_b = outs
    spectral_grad = emb_g[:, :wide].T
    rgb_grad = emb_g[:, wide:].T
    return (
        block_out, pixels_grad, spectral_grad, rgb_grad, ln1_g, ln1_b, qkv_grad, q_g, v_g, out_grad,
        ob_g, ln2_g, ln2_b, fc1_g, b1_g, fc2_g.T, b2_g,
    )


def solution(mesh):
    in_specs = (
        P("dp", "tensor"),
        P("dp"),
        P("dp"),
        P("tensor", None),
        P("tensor", None),
        P(),
        P(),
        P(None, None, "tensor"),
        P("tensor"),
        P("tensor"),
        P("tensor", None),
        P(),
        P(),
        P(),
        P(None, "tensor"),
        P("tensor"),
        P("tensor", None),
        P(),
        P("dp", None),
    )
    out_specs = (
        P("dp", None),
        P("dp", "tensor"),
        P("tensor", "dp"),
        P("tensor", "dp"),
        P("dp"),
        P("dp"),
        P("dp", None, "tensor"),
        P(("tensor", "dp")),
        P(("tensor", "dp")),
        P("tensor", "dp"),
        P("dp"),
        P("dp"),
        P("dp"),
        P("dp", "tensor"),
        P(("tensor", "dp")),
        P("tensor", "dp"),
        P("dp"),
    )
    body = functools.partial(local, size=mesh.shape["dp"])
    return jax.shard_map(body, mesh=mesh, in_specs=in_specs, out_specs=out_specs, check_vma=False)
```

```python
import functools

import jax
import jax.numpy as jnp
import ml_dtypes
import numpy as np
from jax import lax
from jax.experimental import pallas as pl
from jax.experimental.pallas import tpu as pltpu
from jax.sharding import PartitionSpec as P

HEAD_DIM = 64
GRID = 16
EPS = 1e-06
F32 = jnp.float32
BF16 = jnp.bfloat16
LANES = 128
MIB = 1024 * 1024
QUAD = 256
PART = 256
WIDE = 2


def nn(left, right):
    return lax.dot_general(left, right, (((1,), (0,)), ((), ())), preferred_element_type=F32)


def nt(left, right):
    return lax.dot_general(left, right, (((1,), (1,)), ((), ())), preferred_element_type=F32)


def tn(left, right):
    return lax.dot_general(left, right, (((0,), (0,)), ((), ())), preferred_element_type=F32)


def params(mib):
    return pltpu.CompilerParams(vmem_limit_bytes=mib * MIB)


def short_cost():
    return pl.CostEstimate(flops=1000, bytes_accessed=1000, transcendentals=0)


def long_cost():
    return pl.CostEstimate(flops=int(1e11), bytes_accessed=1000, transcendentals=0)


def whole(shape):
    return pl.BlockSpec(shape, lambda *_: (0,) * len(shape), pipeline_mode=pl.Buffered(1))


def norm_parts(values):
    center = values - jnp.mean(values, -1, keepdims=True)
    spread = jnp.mean(center * center, -1, keepdims=True)
    inverse = lax.rsqrt(spread + EPS)
    return center * inverse, inverse


def norm_back(normed, inverse, grad, gain):
    scaled = grad * gain
    mean_scaled = jnp.mean(scaled, -1, keepdims=True)
    mean_cross = jnp.mean(scaled * normed, -1, keepdims=True)
    return inverse * (scaled - mean_scaled - normed * mean_cross)


def column_sum(values):
    return jnp.sum(values, 0, keepdims=True)


def turn(place, source_ref, turned_ref, columns):
    chips = turned_ref.shape[0] // LANES
    half = LANES // 2
    core = place[chips]
    low = pl.multiple_of(core * (chips * half), half)
    high = pl.multiple_of((1 - core) * (chips * half), half)
    for chip in range(chips):
        lanes = pl.ds(pl.multiple_of(place[chip] * LANES, LANES), LANES)
        block = source_ref[:, lanes].T
        turned_ref[pl.ds(low + chip * half, half), columns] = block[:half]
        turned_ref[pl.ds(high + chip * half, half), columns] = block[half:]


def spread(turned_ref, keep_ref, gone_ref, first=0):
    middle = turned_ref.shape[0] // 2
    keep_ref[...] = turned_ref[:middle, :]
    for part in range(2):
        start = middle + part * PART
        gone_ref[first + part] = turned_ref[start : start + PART, :].astype(F32)


def turn_cot_kernel(place, cot_ref, keep_ref, gone_ref, turned_ref):
    turn(place, cot_ref, turned_ref, slice(None))
    spread(turned_ref, keep_ref, gone_ref)


def turn_cot(place, cotangent, rows):
    width = cotangent.shape[1]
    items = cotangent.shape[0] // rows
    return pl.pallas_call(
        turn_cot_kernel,
        grid_spec=pltpu.PrefetchScalarGridSpec(
            num_scalar_prefetch=1,
            grid=(items,),
            in_specs=[pl.BlockSpec((rows, width), lambda i, *_: (i, 0))],
            out_specs=[
                pl.BlockSpec((None, width // 2, rows), lambda i, *_: (i, 0, 0)),
                pl.BlockSpec((2, PART, rows), lambda i, *_: (i, 0, 0)),
            ],
            scratch_shapes=[pltpu.VMEM((width, rows), BF16)],
        ),
        out_shape=[
            jax.ShapeDtypeStruct((items, width // 2, rows), BF16),
            jax.ShapeDtypeStruct((2 * items, PART, rows), F32),
        ],
        compiler_params=params(4),
        cost_estimate=short_cost(),
        name="turn_cotangent",
    )(place, cotangent)


def pack_kernel(values_ref, out_ref):
    out_ref[0] = values_ref[...].astype(F32)


def pack(values):
    rows, columns = values.shape
    return pl.pallas_call(
        pack_kernel,
        grid=(columns // PART,),
        in_specs=[pl.BlockSpec((rows, PART), lambda n: (0, n))],
        out_specs=pl.BlockSpec((1, rows, PART), lambda n: (n, 0, 0)),
        out_shape=jax.ShapeDtypeStruct((columns // PART, rows, PART), F32),
        compiler_params=params(4),
        cost_estimate=short_cost(),
        name="pack_pixels",
    )(values)


def pack_attn_kernel(place, a1_ref, o_ref, keep_ref, gone_ref, turned_ref):
    turn(place, a1_ref, turned_ref, slice(None))
    spread(turned_ref, keep_ref, gone_ref)
    for part in range(o_ref.shape[1] // PART):
        gone_ref[2 + part] = o_ref[:, part * PART : (part + 1) * PART].astype(F32)


def pack_attn(place, a1, mix):
    rows, width = a1.shape
    parts = 2 + mix.shape[1] // PART
    return pl.pallas_call(
        pack_attn_kernel,
        grid_spec=pltpu.PrefetchScalarGridSpec(
            num_scalar_prefetch=1,
            grid=(1,),
            in_specs=[whole(a1.shape), whole(mix.shape)],
            out_specs=[whole((width // 2, rows)), whole((parts, PART, rows))],
            scratch_shapes=[pltpu.VMEM((width, rows), BF16)],
        ),
        out_shape=[
            jax.ShapeDtypeStruct((width // 2, rows), BF16),
            jax.ShapeDtypeStruct((parts, PART, rows), F32),
        ],
        compiler_params=params(4),
        cost_estimate=short_cost(),
        name="pack_attn",
    )(place, a1, mix)


def pieces_of(length):
    third = length // 3 // LANES * LANES
    return [(0, third), (third, third), (2 * third, length - 2 * third)]


def embed_kernel(
    kinds, pix_ref, wspec_ref, wrgb_ref, pick_ref, part_ref, mixed_ref,
    pix_buf, wspec_buf, wrgb_buf, pick_buf, pix_sem, big_sem, small_sem, *, item,
):
    rows, wide = pix_buf.shape
    spectral = kinds[item] == 1
    pieces = pieces_of(wide)
    own_rows = pl.ds(item * rows, rows)

    @pl.when(spectral)
    def _():
        copies = []
        for n, (first, size) in enumerate(pieces):
            span = pl.ds(first, size)
            copies.append(
                (
                    pltpu.make_async_copy(
                        pix_ref.at[own_rows, span], mixed_ref.at[:, span], pix_sem.at[n]
                    ),
                    pltpu.make_async_copy(wspec_ref.at[span], wspec_buf.at[span], big_sem.at[n]),
                )
            )
        for pair in copies:
            for copy in pair:
                copy.start()
        mixed_ref[:, wide:] = jnp.zeros((rows, wrgb_buf.shape[0]), BF16)
        for n, (first, size) in enumerate(pieces):
            for copy in copies[n]:
                copy.wait()
            term = nn(mixed_ref[:, first : first + size], wspec_buf[first : first + size, :])
            if n == 0:
                part_ref[...] = term
            else:
                part_ref[...] += term

    @pl.when(jnp.logical_not(spectral))
    def _():
        copies = []
        for n, (first, size) in enumerate(pieces):
            span = pl.ds(first, size)
            copies.append(
                (
                    pltpu.make_async_copy(
                        pix_ref.at[own_rows, span], pix_buf.at[:, span], pix_sem.at[n]
                    ),
                    pltpu.make_async_copy(pick_ref.at[span], pick_buf.at[span], big_sem.at[n]),
                )
            )
        for pair in copies:
            for copy in pair:
                copy.start()
        weights = pltpu.make_async_copy(wrgb_ref, wrgb_buf, small_sem)
        weights.start()
        mixed_ref[:, :wide] = jnp.zeros((rows, wide), BF16)
        total = None
        for n, (first, size) in enumerate(pieces):
            for copy in copies[n]:
                copy.wait()
            term = nn(pix_buf[:, first : first + size], pick_buf[first : first + size, :])
            total = term if total is None else total + term
        mixed_ref[:, wide:] = total.astype(BF16)
        weights.wait()
        part_ref[...] = nn(mixed_ref[:, wide:], wrgb_buf[...])


def embed(kinds, pixels, w_spectral, w_rgb, pick, item, rows):
    wide, width = w_spectral.shape
    narrow = w_rgb.shape[0]
    far = pl.BlockSpec(memory_space=pltpu.HBM)
    return pl.pallas_call(
        functools.partial(embed_kernel, item=item),
        grid_spec=pltpu.PrefetchScalarGridSpec(
            num_scalar_prefetch=1,
            grid=(1,),
            in_specs=[far, far, far, far],
            out_specs=[whole((rows, width)), whole((rows, wide + narrow))],
            scratch_shapes=[
                pltpu.VMEM((rows, wide), BF16),
                pltpu.VMEM((wide, width), BF16),
                pltpu.VMEM((narrow, width), BF16),
                pltpu.VMEM((wide, narrow), BF16),
                pltpu.SemaphoreType.DMA((3,)),
                pltpu.SemaphoreType.DMA((3,)),
                pltpu.SemaphoreType.DMA(()),
            ],
        ),
        out_shape=[
            jax.ShapeDtypeStruct((rows, width), F32),
            jax.ShapeDtypeStruct((rows, wide + narrow), BF16),
        ],
        compiler_params=params(58),
        cost_estimate=short_cost(),
        name="embed",
    )(kinds, pixels, w_spectral, w_rgb, pick)


def pair_masks(rows):
    lane = lax.broadcasted_iota(jnp.int32, (rows, LANES), 1)
    return lane < HEAD_DIM, lane >= HEAD_DIM


def only(mask, values):
    return jnp.where(mask, values, jnp.zeros_like(values))


def softmax_rows(query, key):
    scores = nt(query, key) * (HEAD_DIM**-0.5)
    expo = jnp.exp(scores - jnp.max(scores, -1, keepdims=True))
    return expo / jnp.sum(expo, -1, keepdims=True)


def attn_forward_kernel(
    part_ref, recv_ref, table_ref, gain_ref, bias_ref, wqkv_ref, qb_ref, vb_ref, wout_ref,
    x0_ref, a1_ref, qkv_ref, o_ref, opart_ref,
):
    quad = pl.program_id(0)
    rows, width = part_ref.shape

    @pl.when(quad == 0)
    def _():
        side = table_ref.shape[0]
        half = table_ref.shape[1]
        table = table_ref[...]
        by_row = jnp.broadcast_to(table[:, None, :], (side, side, half)).reshape(rows, half)
        by_col = jnp.broadcast_to(table[None, :, :], (side, side, half)).reshape(rows, half)
        left = part_ref[:, :half] + recv_ref[:, :half] + by_row
        right = part_ref[:, half:] + recv_ref[:, half:] + by_col
        x0_ref[:, :half] = left
        x0_ref[:, half:] = right
        normed, _inv = norm_parts(x0_ref[...])
        a1_ref[...] = (normed * gain_ref[...] + bias_ref[...]).astype(BF16)
        opart_ref[...] = jnp.zeros_like(opart_ref)

    a1 = a1_ref[...]
    query = (nn(a1, wqkv_ref[0]) + qb_ref[...]).astype(BF16)
    key = nn(a1, wqkv_ref[1]).astype(BF16)
    value = (nn(a1, wqkv_ref[2]) + vb_ref[...]).astype(BF16)
    qkv_ref[0] = query
    qkv_ref[1] = key
    qkv_ref[2] = value
    masks = pair_masks(rows)
    for pair in range(query.shape[1] // LANES):
        span = slice(pair * LANES, (pair + 1) * LANES)
        q2, k2, v2 = query[:, span], key[:, span], value[:, span]
        mixed = None
        for mask in masks:
            probs = softmax_rows(only(mask, q2), k2).astype(BF16)
            term = nn(probs, only(mask, v2))
            mixed = term if mixed is None else mixed + term
        o_ref[:, span] = mixed.astype(BF16)
    opart_ref[...] += nn(o_ref[...], wout_ref[...])


def attn_forward(part, recv, table, gain, bias, w_qkv, q_bias, v_bias, w_out):
    rows, width = part.shape
    heads_wide = w_out.shape[0]
    steps = heads_wide // QUAD
    return pl.pallas_call(
        attn_forward_kernel,
        grid=(steps,),
        in_specs=[
            whole(part.shape),
            whole(recv.shape),
            whole(table.shape),
            whole(gain.shape),
            whole(bias.shape),
            pl.BlockSpec((3, width, QUAD), lambda n: (0, 0, n)),
            pl.BlockSpec((1, QUAD), lambda n: (0, n)),
            pl.BlockSpec((1, QUAD), lambda n: (0, n)),
            pl.BlockSpec((QUAD, width), lambda n: (n, 0)),
        ],
        out_specs=[
            whole((rows, width)),
            whole((rows, width)),
            pl.BlockSpec((3, rows, QUAD), lambda n: (0, 0, n)),
            pl.BlockSpec((rows, QUAD), lambda n: (0, n)),
            whole((rows, width)),
        ],
        out_shape=[
            jax.ShapeDtypeStruct((rows, width), F32),
            jax.ShapeDtypeStruct((rows, width), BF16),
            jax.ShapeDtypeStruct((3, rows, heads_wide), BF16),
            jax.ShapeDtypeStruct((rows, heads_wide), BF16),
            jax.ShapeDtypeStruct((rows, width), F32),
        ],
        compiler_params=params(10),
        cost_estimate=long_cost(),
        name="attn_forward",
    )(part, recv, table, gain, bias, w_qkv, q_bias, v_bias, w_out)


def put_rows(refs, values, add):
    first = 0
    for ref in refs:
        rows = ref.shape[0]
        if add:
            ref[...] += values[first : first + rows]
        else:
            ref[...] = values[first : first + rows]
        first += rows


def joined(refs):
    values = [ref[...] for ref in refs]
    return values[0] if len(values) == 1 else jnp.concatenate(values, 0)


def attn_backward_kernel(place, *refs, parts):
    gpart_refs, refs = refs[: parts[0]], refs[parts[0] :]
    grecv_refs, refs = refs[: parts[1]], refs[parts[1] :]
    x1_ref, cot_ref, gain_ref, wout_ref, qkv_ref, wqkv_ref, *refs = refs
    dx1_ref, dya_ref, dqkv_ref, sums_ref, qvsum_ref, keep_ref, gone_ref, *da1_refs = refs[:-1]
    turned_ref = refs[-1]
    quad = pl.program_id(0)
    rows = x1_ref.shape[0]

    @pl.when(quad == 0)
    def _():
        normed, inverse = norm_parts(x1_ref[...])
        grad = joined(gpart_refs) + joined(grecv_refs)
        cot = cot_ref[...].astype(F32)
        dx1 = cot + norm_back(normed, inverse, grad, gain_ref[...])
        dx1_ref[...] = dx1
        dya = dx1.astype(BF16)
        dya_ref[...] = dya
        sums_ref[0:1, :] = column_sum(grad * normed)
        sums_ref[1:2, :] = column_sum(grad)
        sums_ref[2:3, :] = column_sum(dya.astype(F32))
        sums_ref[3:4, :] = column_sum(cot)
        sums_ref[4:8, :] = jnp.zeros((4, sums_ref.shape[1]), F32)
        turn(place, dya_ref, turned_ref, slice(None))
        spread(turned_ref, keep_ref, gone_ref)

    dmix = nt(dya_ref[...], wout_ref[...]).astype(BF16)
    scale = HEAD_DIM**-0.5
    masks = pair_masks(rows)
    for pair in range(dmix.shape[1] // LANES):
        span = slice(pair * LANES, (pair + 1) * LANES)
        q2, k2, v2, d2 = qkv_ref[0, :, span], qkv_ref[1, :, span], qkv_ref[2, :, span], dmix[:, span]
        totals = [None, None, None]
        for mask in masks:
            qm, km, dm = only(mask, q2), only(mask, k2), only(mask, d2)
            probs = softmax_rows(qm, k2)
            dprobs = nt(dm, v2)
            dot_row = jnp.sum(probs * dprobs, -1, keepdims=True)
            dscores = (probs * (dprobs - dot_row)).astype(BF16)
            terms = [nn(dscores, km), tn(dscores, qm), tn(probs.astype(BF16), dm)]
            totals = [t if o is None else o + t for o, t in zip(totals, terms)]
        dqkv_ref[0, :, span] = (totals[0] * scale).astype(BF16)
        dqkv_ref[1, :, span] = (totals[1] * scale).astype(BF16)
        dqkv_ref[2, :, span] = totals[2].astype(BF16)
    da1 = nt(dqkv_ref[0], wqkv_ref[0]) + nt(dqkv_ref[1], wqkv_ref[1]) + nt(dqkv_ref[2], wqkv_ref[2])

    @pl.when(quad == 0)
    def _():
        put_rows(da1_refs, da1, False)

    @pl.when(quad != 0)
    def _():
        put_rows(da1_refs, da1, True)

    steps = pl.num_programs(0)
    for plane in range(3):
        gone_ref[2 + plane * steps + quad] = dqkv_ref[plane].astype(F32)
    qvsum_ref[0:1, :] = column_sum(dqkv_ref[0].astype(F32))
    qvsum_ref[1:2, :] = column_sum(dqkv_ref[2].astype(F32))
    qvsum_ref[2:8, :] = jnp.zeros((6, qvsum_ref.shape[1]), F32)


def attn_backward(place, gparts, grecvs, x1, cotangent, gain, w_out, qkv, w_qkv, item, cuts):
    rows, width = x1.shape
    heads_wide = w_out.shape[0]
    steps = heads_wide // QUAD
    return pl.pallas_call(
        functools.partial(attn_backward_kernel, parts=(len(gparts), len(grecvs))),
        grid_spec=pltpu.PrefetchScalarGridSpec(
            num_scalar_prefetch=1,
            grid=(steps,),
            in_specs=[
                *[whole(v.shape) for v in (*gparts, *grecvs)],
                whole(x1.shape),
                pl.BlockSpec((rows, width), lambda n, *_: (item, 0)),
                whole(gain.shape),
                pl.BlockSpec((QUAD, width), lambda n, *_: (n, 0)),
                pl.BlockSpec((3, rows, QUAD), lambda n, *_: (0, 0, n)),
                pl.BlockSpec((3, width, QUAD), lambda n, *_: (0, 0, n)),
            ],
            out_specs=[
                whole((rows, width)),
                whole((rows, width)),
                pl.BlockSpec((3, rows, QUAD), lambda n, *_: (0, 0, n)),
                whole((8, width)),
                pl.BlockSpec((8, QUAD), lambda n, *_: (0, n)),
                whole((width // 2, rows)),
                whole((2 + 3 * steps, PART, rows)),
                *[whole((cut, width)) for cut in cuts],
            ],
            scratch_shapes=[pltpu.VMEM((width, rows), BF16)],
        ),
        out_shape=[
            jax.ShapeDtypeStruct((rows, width), F32),
            jax.ShapeDtypeStruct((rows, width), BF16),
            jax.ShapeDtypeStruct((3, rows, heads_wide), BF16),
            jax.ShapeDtypeStruct((8, width), F32),
            jax.ShapeDtypeStruct((8, heads_wide), F32),
            jax.ShapeDtypeStruct((width // 2, rows), BF16),
            jax.ShapeDtypeStruct((2 + 3 * steps, PART, rows), F32),
            *[jax.ShapeDtypeStruct((cut, width), F32) for cut in cuts],
        ],
        compiler_params=params(16),
        cost_estimate=long_cost(),
        name="attn_backward",
    )(place, *gparts, *grecvs, x1, cotangent, gain, w_out, qkv, w_qkv)


def mlp_kernel(
    place, x0_ref, opart_ref, orecv_ref, obias_ref, gain_ref, bias_ref, wfc1_ref, b1_ref, wfc2_ref, cot_ref,
    x1_ref, a2_ref, act_ref, dpre_ref, b1sum_ref, keep_ref, gact_ref, gpre_ref, *refs,
):
    da2_refs, turned_ref = refs[:-1], refs[-1]
    step = pl.program_id(0)

    @pl.when(step == 0)
    def _():
        x1_ref[...] = x0_ref[...] + (opart_ref[...] + orecv_ref[...] + obias_ref[...])
        normed, _inv = norm_parts(x1_ref[...])
        a2_ref[...] = (normed * gain_ref[...] + bias_ref[...]).astype(BF16)
        turn(place, a2_ref, turned_ref, slice(None))
        spread(turned_ref, keep_ref, gpre_ref)

    pre = nn(a2_ref[...], wfc1_ref[...]) + b1_ref[...]
    dact = nt(cot_ref[...], wfc2_ref[...])
    cdf = 0.5 * (1.0 + lax.erf(pre * (2.0**-0.5)))
    act = (pre * cdf).astype(BF16)
    act_ref[...] = act
    density = jnp.exp(-0.5 * pre * pre) * 0.3989422804014327
    dpre = (dact * (cdf + pre * density)).astype(BF16)
    dpre_ref[...] = dpre
    for part in range(act.shape[1] // PART):
        columns = slice(part * PART, (part + 1) * PART)
        gact_ref[part] = act[:, columns].astype(F32)
        gpre_ref[2 + step * (act.shape[1] // PART) + part] = dpre[:, columns].astype(F32)
    b1sum_ref[...] = column_sum(dpre.astype(F32))
    if not da2_refs:
        return
    da2 = nt(dpre, wfc1_ref[...])

    @pl.when(step == 0)
    def _():
        put_rows(da2_refs, da2, False)

    @pl.when(step != 0)
    def _():
        put_rows(da2_refs, da2, True)


def mlp(
    place, x0, opart, orecv, out_bias, gain, bias, w_fc1, fc1_bias, w_fc2, cotangent, item, cuts
):
    rows, width = x0.shape
    hidden = w_fc1.shape[1]
    tile = 512
    parts = tile // PART
    row_tile = pl.BlockSpec((rows, tile), lambda n, *_: (0, n))
    gone = pl.BlockSpec((parts, rows, PART), lambda n, *_: (n, 0, 0))
    return pl.pallas_call(
        mlp_kernel,
        grid_spec=pltpu.PrefetchScalarGridSpec(
            num_scalar_prefetch=1,
            grid=(hidden // tile,),
            in_specs=[
                whole(x0.shape),
                whole(opart.shape),
                whole(orecv.shape),
                whole(out_bias.shape),
                whole(gain.shape),
                whole(bias.shape),
                pl.BlockSpec((width, tile), lambda n, *_: (0, n)),
                pl.BlockSpec((1, tile), lambda n, *_: (0, n)),
                pl.BlockSpec((tile, width), lambda n, *_: (n, 0)),
                pl.BlockSpec((rows, width), lambda n, *_: (item, 0)),
            ],
            out_specs=[
                whole((rows, width)),
                whole((rows, width)),
                row_tile,
                row_tile,
                pl.BlockSpec((1, tile), lambda n, *_: (0, n)),
                whole((width // 2, rows)),
                gone,
                whole((2 + hidden // PART, rows, PART)),
                *[whole((cut, width)) for cut in cuts],
            ],
            scratch_shapes=[pltpu.VMEM((width, rows), BF16)],
        ),
        out_shape=[
            jax.ShapeDtypeStruct((rows, width), F32),
            jax.ShapeDtypeStruct((rows, width), BF16),
            jax.ShapeDtypeStruct((rows, hidden), BF16),
            jax.ShapeDtypeStruct((rows, hidden), BF16),
            jax.ShapeDtypeStruct((1, hidden), F32),
            jax.ShapeDtypeStruct((width // 2, rows), BF16),
            jax.ShapeDtypeStruct((hidden // PART, rows, PART), F32),
            jax.ShapeDtypeStruct((2 + hidden // PART, rows, PART), F32),
            *[jax.ShapeDtypeStruct((cut, width), F32) for cut in cuts],
        ],
        compiler_params=params(14),
        cost_estimate=long_cost(),
        name="mlp",
    )(place, x0, opart, orecv, out_bias, gain, bias, w_fc1, fc1_bias, w_fc2, cotangent)


def mlp_back_kernel(dpre_ref, wfc1_ref, out_ref):
    out_ref[...] = nt(dpre_ref[...], wfc1_ref[...])


def mlp_back(dpre, w_fc1):
    rows, hidden = dpre.shape
    width = w_fc1.shape[0]
    tile = 512
    return pl.pallas_call(
        mlp_back_kernel,
        grid=(width // tile,),
        in_specs=[whole(dpre.shape), pl.BlockSpec((tile, hidden), lambda n: (n, 0))],
        out_specs=pl.BlockSpec((rows, tile), lambda n: (0, n)),
        out_shape=jax.ShapeDtypeStruct((rows, width), F32),
        compiler_params=params(6),
        cost_estimate=long_cost(),
        name="mlp_back",
    )(dpre, w_fc1)


def mlp_out_kernel(act_ref, wfc2_ref, out_ref):
    out_ref[...] = nn(act_ref[...], wfc2_ref[...])


def mlp_out(act, w_fc2, estimate):
    rows, hidden = act.shape
    width = w_fc2.shape[1]
    tile = 512
    return pl.pallas_call(
        mlp_out_kernel,
        grid=(width // tile,),
        in_specs=[whole(act.shape), pl.BlockSpec((hidden, tile), lambda n: (0, n))],
        out_specs=pl.BlockSpec((rows, tile), lambda n: (0, n)),
        out_shape=jax.ShapeDtypeStruct((rows, width), F32),
        compiler_params=params(6),
        cost_estimate=estimate,
        name="mlp_out",
    )(act, w_fc2)


def first_norm_back_kernel(place, *refs, parts, riders):
    gpart_refs, refs = refs[: parts[0]], refs[parts[0] :]
    grecv_refs, refs = refs[: parts[1]], refs[parts[1] :]
    rider_refs, refs = refs[:riders], refs[riders:]
    x0_ref, dx1_ref, gain_ref, dx0_ref, sums_ref, keep_ref, gone_ref, block_ref, turned_ref = refs
    normed, inverse = norm_parts(x0_ref[...])
    grad = joined(gpart_refs) + joined(grecv_refs)
    dx0_ref[...] = (dx1_ref[...] + norm_back(normed, inverse, grad, gain_ref[...])).astype(BF16)
    sums_ref[0:1, :] = column_sum(grad * normed)
    sums_ref[1:2, :] = column_sum(grad)
    sums_ref[2:8, :] = jnp.zeros((6, sums_ref.shape[1]), F32)
    turn(place, dx0_ref, turned_ref, slice(None))
    middle = turned_ref.shape[0] // 2
    keep_ref[...] = turned_ref[:middle, :]
    gone_ref[:middle, :] = turned_ref[middle:, :].astype(F32)
    for chip in range(8):
        lanes = pl.ds(pl.multiple_of(place[chip] * LANES, LANES), LANES)
        for row in range(2):
            block_ref[chip : chip + 1, row * LANES : (row + 1) * LANES] = sums_ref[row : row + 1, lanes]
    gone_ref[middle : middle + 8, :] = block_ref[...]
    first = middle + 8
    for rider_ref in rider_refs:
        gone_ref[first : first + rider_ref.shape[0], :] = rider_ref[...]
        first += rider_ref.shape[0]


def first_norm_back(place, gparts, grecvs, x0, dx1, gain, estimate, riders=()):
    rows, width = x0.shape
    operands = (*gparts, *grecvs, *riders, x0, dx1, gain)
    extra = sum(v.shape[0] for v in riders)
    shapes = [
        jax.ShapeDtypeStruct((rows, width), BF16),
        jax.ShapeDtypeStruct((8, width), F32),
        jax.ShapeDtypeStruct((width // 2, rows), BF16),
        jax.ShapeDtypeStruct((width // 2 + 8 + extra, rows), F32),
        jax.ShapeDtypeStruct((8, 2 * LANES), F32),
    ]
    return pl.pallas_call(
        functools.partial(
            first_norm_back_kernel, parts=(len(gparts), len(grecvs)), riders=len(riders)
        ),
        grid_spec=pltpu.PrefetchScalarGridSpec(
            num_scalar_prefetch=1,
            grid=(1,),
            in_specs=[whole(v.shape) for v in operands],
            out_specs=[whole(v.shape) for v in shapes],
            scratch_shapes=[pltpu.VMEM((width, rows), BF16)],
        ),
        out_shape=shapes,
        compiler_params=params(10),
        cost_estimate=estimate,
        name="first_norm_back",
    )(place, *operands)


def pack_vectors_kernel(place, sa_ref, sb_ref, qa_ref, qb_ref, ba_ref, bb_ref, out_ref, *refs):
    sums_ref, qv_ref, hidden_ref = refs
    sums_ref[...] = sa_ref[...] + sb_ref[...]
    qv_ref[...] = qa_ref[...] + qb_ref[...]
    hidden_ref[...] = ba_ref[...] + bb_ref[...]
    out_ref[...] = jnp.zeros_like(out_ref)
    half = LANES // 2
    for pos in range(8):
        chip = place[pos]
        lanes = pl.ds(pl.multiple_of(chip * LANES, LANES), LANES)
        for row in range(4):
            first = row % 2 * LANES
            spot = 4 * pos + row // 2
            out_ref[spot : spot + 1, first : first + LANES] = sums_ref[row : row + 1, lanes]
        both = pl.ds(pl.multiple_of(chip // 2 * LANES, LANES), LANES)
        spot = 4 * pos + 2
        for row in range(2):
            pair = qv_ref[row : row + 1, both]
            own = jnp.where(chip % 2 == 0, pair[:, :half], pair[:, half:])
            out_ref[spot : spot + 1, row * half : (row + 1) * half] = own
        wide = pl.ds(pl.multiple_of(chip * 2 * LANES, 2 * LANES), 2 * LANES)
        out_ref[spot + 1 : spot + 2, :] = hidden_ref[0:1, wide]


def pack_vectors(place, sums, qv, hidden):
    operands = (*sums, *qv, *hidden)
    return pl.pallas_call(
        pack_vectors_kernel,
        grid_spec=pltpu.PrefetchScalarGridSpec(
            num_scalar_prefetch=1,
            grid=(1,),
            in_specs=[whole(v.shape) for v in operands],
            out_specs=whole((32, 2 * LANES)),
            scratch_shapes=[pltpu.VMEM(v[0].shape, F32) for v in (sums, qv, hidden)],
        ),
        out_shape=jax.ShapeDtypeStruct((32, 2 * LANES), F32),
        compiler_params=params(4),
        cost_estimate=short_cost(),
        name="pack_vectors",
    )(place, *operands)


def pixel_grad_kernel(kinds, grad_ref, wspec_ref, wrgb_ref, pick_ref, *refs, item):
    out_ref = refs[-1]
    spectral = kinds[item] == 1
    grad = grad_ref[...]
    wide = wspec_ref.shape[0]
    cut = (wide // 2 + LANES - 1) // LANES * LANES

    @pl.when(spectral)
    def _():
        out_ref[:, :cut] = nt(grad, wspec_ref[:cut, :]).astype(BF16)
        out_ref[:, cut:] = nt(grad, wspec_ref[cut:, :]).astype(BF16)

    @pl.when(jnp.logical_not(spectral))
    def _():
        small = nt(grad, wrgb_ref[...]).astype(BF16)
        out_ref[...] = nt(small, pick_ref[...]).astype(BF16)


def pixel_grad(kinds, grad, w_spectral, w_rgb, pick, item, items, filled=None):
    rows = grad.shape[0]
    wide, width = w_spectral.shape
    more = [] if filled is None else [filled]
    return pl.pallas_call(
        functools.partial(pixel_grad_kernel, item=item),
        grid_spec=pltpu.PrefetchScalarGridSpec(
            num_scalar_prefetch=1,
            grid=(1,),
            in_specs=[
                whole(grad.shape),
                whole(w_spectral.shape),
                whole(w_rgb.shape),
                whole(pick.shape),
            ]
            + [pl.BlockSpec(memory_space=pl.ANY)] * len(more),
            out_specs=pl.BlockSpec((rows, wide), lambda i, *_: (item, 0)),
        ),
        out_shape=jax.ShapeDtypeStruct((items * rows, wide), BF16),
        input_output_aliases={5: 0} if more else {},
        compiler_params=params(12),
        cost_estimate=long_cost(),
        name="pixel_grad",
    )(kinds, grad, w_spectral, w_rgb, pick, *more)


def gather_left(keep_refs, gone_refs, first, left_ref):
    rows = keep_refs[0].shape[-1]
    for pos, keep_ref in enumerate(keep_refs):
        left_ref[:, pos * rows : (pos + 1) * rows] = keep_ref[...]
    base = len(keep_refs) * rows
    for pos, gone_ref in enumerate(gone_refs):
        columns = slice(base + pos * rows, base + (pos + 1) * rows)
        if len(gone_ref.shape) == 2:
            left_ref[:, columns] = gone_ref[: left_ref.shape[0], :].astype(BF16)
            continue
        for part in range(2):
            left_ref[part * PART : (part + 1) * PART, columns] = gone_ref[first + part].astype(BF16)


def emit(left_ref, rights, send_ref, keep_ref, moves, columns=slice(None)):
    right = jnp.concatenate([r.astype(BF16) for r in rights], 0)
    total = nn(left_ref[...], right)
    half = LANES // 2
    for pos, block in enumerate(moves):
        out_ref = send_ref if pos < 4 else keep_ref
        value = total[block * half : (block + 1) * half]
        if len(out_ref.shape) == 4:
            out_ref[pos % 4, 0, :, columns] = value
        else:
            out_ref[pos % 4, :half, columns] = value


def plain_grad_kernel(
    ka_ref, kb_ref, la_ref, lb_ref, ra_ref, rb_ref, oa_ref, ob_ref, *refs, moves, vectors
):
    send_ref, keep_ref, left_ref = refs[-3:]

    @pl.when(pl.program_id(0) == 0)
    def _():
        gather_left((ka_ref, kb_ref), (la_ref, lb_ref), 0, left_ref)

    for part in range(oa_ref.shape[0]):
        columns = slice(part * PART, (part + 1) * PART)
        rights = (ra_ref[:, columns], rb_ref[:, columns], oa_ref[part], ob_ref[part])
        emit(left_ref, rights, send_ref, keep_ref, moves, columns)
    if vectors:
        early_ref, sa_ref, sb_ref = refs[:3]
        half = LANES // 2
        middle = left_ref.shape[0]
        late = sa_ref[...] + sb_ref[...] + (la_ref[middle:, :] + lb_ref[middle:, :])
        for pos, block in enumerate(moves):
            out_ref = send_ref if pos < 4 else keep_ref
            out_ref[pos % 4, half:, :] = early_ref[block]

            @pl.when(pl.program_id(0) == 0)
            def _(out_ref=out_ref, pos=pos, block=block):
                out_ref[pos % 4, half + 1 : half + 2, : late.shape[1]] = late[block : block + 1]


def plain_grad(keeps, lefts, rights, others, moves, name, skip=0, columns=None, lead=0, vectors=(), planes=1):
    half_width, rows = keeps[0][0].shape[-2:]
    columns = columns or rights[0].shape[1]
    wide = WIDE
    base = skip // (wide * PART)
    half = LANES // 2

    def keep_spec(array, item):
        if array.ndim == 2:
            return whole(array.shape)
        return pl.BlockSpec((None,) + array.shape[1:], lambda n: (item, 0, 0))

    right = pl.BlockSpec((rows, wide * PART), lambda n: (0, n + base))
    other = pl.BlockSpec((wide, rows, PART), lambda n: (n + base + lead // wide, 0, 0))
    height = half + 8 if vectors else half
    out = pl.BlockSpec((4, height, wide * PART), lambda n: (0, 0, n))
    shape = jax.ShapeDtypeStruct((4, height, columns), F32)
    if planes > 1:
        per = columns // planes // (wide * PART)
        out = pl.BlockSpec((4, 1, half, wide * PART), lambda n: (0, n // per, 0, n % per))
        shape = jax.ShapeDtypeStruct((4, planes, half, columns // planes), F32)

    def left_spec(array, item):
        if array.ndim == 2:
            return pl.BlockSpec((half_width + 8, rows), lambda n: (item, 0))
        return pl.BlockSpec((2, PART, rows), lambda n: (item, 0, 0))

    vector_specs = []
    if vectors:
        vector_specs = [pl.BlockSpec((8, 8, wide * PART), lambda n: (0, 0, n))]
        vector_specs += [whole(v.shape) for v in vectors[1:]]
    return pl.pallas_call(
        functools.partial(plain_grad_kernel, moves=moves, vectors=bool(vectors)),
        grid=(columns // (wide * PART),),
        in_specs=[keep_spec(*k) for k in keeps]
        + [left_spec(*v) for v in lefts]
        + [right, right, other, other]
        + vector_specs,
        out_specs=[out, out],
        scratch_shapes=[pltpu.VMEM((half_width, 4 * rows), BF16)],
        out_shape=[shape, shape],
        compiler_params=params(14),
        cost_estimate=short_cost(),
        name=name,
    )(*[k for k, _ in keeps], *[v for v, _ in lefts], *rights, *others, *vectors)


def query_key_kernel(
    aa_ref, ab_ref, fa_ref, fb_ref, ba_ref, bb_ref, da_ref, db_ref, send_ref, keep_ref, left_ref,
    *, moves,
):
    plane, step = pl.program_id(0), pl.program_id(1)

    @pl.when((plane == 0) & (step == 0))
    def _():
        gather_left((aa_ref, ab_ref), (fa_ref, fb_ref), 0, left_ref)

    spot = 2 + plane * pl.num_programs(1) + step
    emit(left_ref, (da_ref[...], db_ref[...], ba_ref[spot], bb_ref[spot]), send_ref, keep_ref, moves)


def value_out_kernel(
    aa_ref, ab_ref, fa_ref, fb_ref, ba_ref, bb_ref, da_ref, db_ref, ya_ref, yb_ref, ma_ref, mb_ref,
    send_ref, keep_ref, left_ref, *, moves,
):
    plane, step = pl.program_id(0), pl.program_id(1)

    @pl.when((plane == 0) & (step == 0))
    def _():
        gather_left((aa_ref, ab_ref), (fa_ref, fb_ref), 0, left_ref)

    @pl.when((plane == 1) & (step == 0))
    def _():
        gather_left((ya_ref, yb_ref), (ba_ref, bb_ref), 0, left_ref)

    @pl.when(plane == 0)
    def _():
        spot = 2 + 2 * pl.num_programs(1) + step
        emit(left_ref, (da_ref[...], db_ref[...], ba_ref[spot], bb_ref[spot]), send_ref, keep_ref, moves)

    @pl.when(plane == 1)
    def _():
        spot = 2 + step
        emit(left_ref, (ma_ref[...], mb_ref[...], fa_ref[spot], fb_ref[spot]), send_ref, keep_ref, moves)


def attn_grad(keep_a1, other_f, other_b, dqkv, moves, out_side=None):
    half_width, rows = keep_a1[0].shape
    columns = dqkv[0].shape[2]
    steps = columns // PART
    half = LANES // 2
    side = whole((half_width, rows))
    specs = [side, side] + [whole(v.shape) for v in (*other_f, *other_b)]
    if out_side is None:
        kernel, name, more = query_key_kernel, "query_key_grad", []
        plane = pl.BlockSpec((None, rows, PART), lambda p, n: (p, 0, n))
        specs += [plane, plane]
    else:
        kernel, name, more = value_out_kernel, "value_out_grad", [*out_side[0], *out_side[1]]
        plane = pl.BlockSpec((None, rows, PART), lambda p, n: (2, 0, n))
        mixed = pl.BlockSpec((rows, PART), lambda p, n: (0, n))
        specs += [plane, plane, side, side, mixed, mixed]
    out = pl.BlockSpec((4, half, PART), lambda p, n: (0, 0, p * steps + n))
    shape = jax.ShapeDtypeStruct((4, half, 2 * columns), F32)
    return pl.pallas_call(
        functools.partial(kernel, moves=moves),
        grid=(2, steps),
        in_specs=specs,
        out_specs=[out, out],
        scratch_shapes=[pltpu.VMEM((half_width, 4 * rows), BF16)],
        out_shape=[shape, shape],
        compiler_params=params(12),
        cost_estimate=short_cost(),
        name=name,
    )(*keep_a1, *other_f, *other_b, *dqkv, *more)


def exchange(values, axis, bit, size):
    return lax.ppermute(values, axis, [(i, i ^ bit) for i in range(size)])


def swap(values):
    return exchange(values, "tensor", 1, 2)


def after(first, values):
    return lax.optimization_barrier((first, values))[1]


X_FIRST = (2, 4, 8)
Z_FIRST = (4, 2, 8)


def block_flips(bits):
    return [sum((1 - ((p >> (2 - n)) & 1)) * (bits[n] // 2) for n in range(3)) for p in range(8)]


def block_moves(bits):
    stands = block_flips(X_FIRST)
    return tuple(stands.index(f) for f in block_flips(bits))


def places():
    me = lax.axis_index("dp")
    flips = jnp.array(block_flips(X_FIRST), jnp.int32)
    return jnp.concatenate([(me // 2) ^ flips, (me % 2)[None]]).astype(jnp.int32)


class Halving:
    def __init__(self, send, keep, bits, size, first=True):
        self.keep, self.bits, self.size = keep, bits, size
        self.unit = keep.shape[0] // 4
        self.recvs = [exchange(send, "dp", bits[0], size)] if first else []
        self.left = keep.shape[0]
        self.sent = send

    def value(self, order, tie=True):
        if tie:
            self.recvs[-1] = order.tie(self.recvs[-1])
        left = self.left
        count = max(left // 2, self.unit)
        total = self.keep.shape[0] - left
        value = self.keep[total : total + count]
        for recv in self.recvs:
            first = recv.shape[0] - left
            value = value + recv[first : first + count]
        order.mark(value)
        return value

    def came(self, recv):
        self.recvs.append(recv)
        self.left = self.left // 2

    def step(self, order):
        value = self.value(order)
        if self.left == self.unit:
            return value[0] if self.unit == 1 else value
        self.came(exchange(value, "dp", self.bits[len(self.recvs)], self.size))
        return None


class Order:
    def __init__(self):
        self.last = None

    def tie(self, values):
        return values if self.last is None else after(self.last, values)

    def mark(self, values):
        self.last = values


def local(
    pixels, item_kinds, gsd_codes, w_spectral, w_rgb, ln1_gain, ln1_bias, w_qkv, q_bias, v_bias,
    w_out, out_bias, ln2_gain, ln2_bias, w_fc1, fc1_bias, w_fc2, fc2_bias, cotangent, *, size,
):
    items = item_kinds.shape[0]
    rows = pixels.shape[0] // items
    width = w_out.shape[1]
    wide = pixels.shape[1]
    narrow = w_rgb.shape[0]
    bands = wide // (narrow // 3)
    custom = size == 16

    def row(vector):
        return vector.reshape(1, -1)

    g1, c1, g2, c2 = row(ln1_gain), row(ln1_bias), row(ln2_gain), row(ln2_bias)
    qb, vb, ob, b1 = row(q_bias), row(v_bias), row(out_bias), row(fc1_bias)
    wqkv = jnp.transpose(w_qkv, (1, 0, 2))

    source = np.arange(wide)[:, None]
    target = np.arange(narrow)[None, :]
    pick = jnp.asarray((source == (target // 3) * bands + target % 3).astype(ml_dtypes.bfloat16))

    ratio = (gsd_codes.astype(F32) + 1.0) / 4.0
    quarter = width // 4
    frequency = 1.0 / 10000.0 ** (jnp.arange(quarter).astype(F32) / quarter)
    spot = jnp.arange(GRID).astype(F32)
    angle = ratio[:, None, None] * spot[None, :, None] * frequency[None, None, :]
    tables = jnp.concatenate([jnp.sin(angle), jnp.cos(angle)], -1)

    def scatter(values):
        return lax.psum_scatter(values, "dp", scatter_dimension=0, tiled=True)

    def both(left, right):
        return sum(tn(left[i], right[i]) for i in range(items))

    order = Order()
    gate = None

    def send(values, wait=True):
        nonlocal gate
        if gate is not None:
            values = after(gate, values)
        gate = swap(values)
        return gate

    place = places() if custom else jnp.arange(9, dtype=jnp.int32) % 8
    move_x, move_z = block_moves(X_FIRST), block_moves(Z_FIRST)

    def other(values):
        return exchange(values, "dp", 1, size) if custom else values

    cut = rows * 3 // 8 // 8 * 8
    cuts = [(cut, rows - cut)] + [(rows,)] * (items - 1)

    def settle(values):
        values = order.tie(values)
        order.mark(jax.tree.leaves(values)[0])
        return values

    none = [None] * items
    part, mixed, erecv, fwd, orecv, ffn, grecv, bwd, arecv, last, ycot = (list(none) for _ in range(11))
    gmix, pk, gfwd, gact, gpre, gbwd, gdx0, da1, da2 = (list(none) for _ in range(9))

    for i in range(items):
        part[i], mixed[i] = embed(order.tie(item_kinds), pixels, w_spectral, w_rgb, pick, i, rows)
        order.mark(part[i])
        erecv[i] = send(part[i])
    keep_cot, gone_cot = turn_cot(order.tie(place), cotangent, rows)
    order.mark(gone_cot)
    gone_mix = []
    for i in range(items):
        gone_mix.append(pack(order.tie(mixed[i])))
        order.mark(gone_mix[i])
    gcot = other(gone_cot)
    gmix = [other(v) for v in gone_mix]
    for i in range(items):
        fwd[i] = attn_forward(
            part[i], erecv[i], tables[i], order.tie(g1), c1, wqkv, qb, vb, w_out
        )
        order.mark(fwd[i][4])
        orecv[i] = send(fwd[i][4])
        if i == 0:
            gcot = settle(gcot)
        else:
            gmix = [settle(v) for v in gmix]
        pk[i] = pack_attn(order.tie(place), fwd[i][1], fwd[i][3])
        order.mark(pk[i][1])
        gfwd[i] = other(pk[i][1])
    x0, a1, qkv, mix, _ = zip(*fwd)
    for i in range(items):
        ffn[i] = mlp(
            place, x0[i], fwd[i][4], orecv[i], order.tie(ob), g2, c2, w_fc1, b1, w_fc2, cotangent, i,
            cuts[i] if i == 0 else (),
        )
        da2[i] = ffn[i][8:]
        order.mark(da2[i][0] if i == 0 else ffn[i][6])
        if i == 0:
            grecv[i] = [send(v) for v in da2[i]]
        gact[i] = other(ffn[i][6])
        gpre[i] = other(ffn[i][7])
        if i == 0:
            gfwd = [settle(v) for v in gfwd]
        else:
            grecv[0][0] = settle(grecv[0][0])
            gact[0], gpre[0] = settle((gact[0], gpre[0]))
            da2[1] = [mlp_back(order.tie(ffn[1][3]), w_fc1)]
            order.mark(da2[1][0])
    x1, a2, act, dpre, b1sum, ka2 = list(zip(*[v[:6] for v in ffn]))
    if custom:
        gact[1] = order.tie(gact[1])
        fc2_h = Halving(
            *plain_grad(
                [(keep_cot, 0), (keep_cot, 1)], [(gcot, 0), (gcot, 1)], act, gact, move_x, "fc2_grad"
            ),
            X_FIRST, size,
        )
        order.mark(fc2_h.sent)
        gpre[1] = order.tie(gpre[1])
        fc1_s = plain_grad(
            [(ka2[0], 0), (ka2[1], 0)], [(gpre[0], 0), (gpre[1], 0)], dpre, gpre, move_z, "fc1_grad",
            lead=2, planes=2,
        )
        fc1_s = [v.reshape(8, *v.shape[2:]) for v in fc1_s]
        fc1_h = Halving(*fc1_s, Z_FIRST, size)
        order.mark(fc1_h.sent)
    grecv[1] = [send(order.tie(da2[1][0]))]
    for i in range(items):
        bwd[i] = attn_backward(
            place, da2[i], grecv[i], x1[i], cotangent, order.tie(g2), w_out, qkv[i], wqkv, i, cuts[i]
        )
        da1[i] = bwd[i][7:]
        order.mark(da1[i][0])
        if i == 0:
            arecv[i] = [send(v) for v in da1[i]]
            ycot[1] = mlp_out(order.tie(ffn[1][2]), w_fc2, short_cost())
            order.mark(ycot[1])
        else:
            arecv[0][0] = settle(arecv[0][0])
            gbwd = [other(order.tie(bwd[0][6])), other(bwd[1][6])]
            ycot[0] = mlp_out(order.tie(ffn[0][2]), w_fc2, long_cost())
            order.mark(ycot[0])
    dx1, dya, dqkv, sums2, qvsum, kdya = list(zip(*[v[:6] for v in bwd]))
    if custom:
        fc2_h.step(order)
        gbwd = [order.tie(v) for v in gbwd]
        keep_a1 = [v[0] for v in pk]
        attx_h = Halving(*attn_grad(keep_a1, gfwd, gbwd, dqkv, move_x), X_FIRST, size, first=False)
        order.mark(attx_h.sent)
        both_x = jnp.concatenate([fc1_h.value(order), attx_h.sent], 0)
        order.mark(both_x)
        gbwd[1] = order.tie(gbwd[1])
        both_x = exchange(both_x, "dp", 2, size)
        attz_h = Halving(
            *attn_grad(keep_a1, gfwd, gbwd, dqkv, move_z, (kdya, mix)), Z_FIRST, size
        )
        order.mark(attz_h.sent)
    arecv[1] = [send(order.tie(da1[1][0]))]
    riders = ()
    for i in range(items):
        estimate = long_cost() if i == 0 else short_cost()
        last[i] = first_norm_back(
            place, da1[i], arecv[i], x0[i], dx1[i], order.tie(g1), estimate, riders
        )
        order.mark(last[i][0])
        if custom and i == 0:
            fc2_h.step(order)
        if custom and i == 0:
            cube = pack_vectors(order.tie(place), sums2, qvsum, b1sum)
            order.mark(cube)
            riders = (last[0][3], cube)
    summed = list(none)
    summed[0] = send(order.tie(ycot[0]))
    dx0, sums1, kdx0, gone, blocks = zip(*last)
    pixels_grad = pixel_grad(order.tie(item_kinds), dx0[0], w_spectral, w_rgb, pick, 0, items)
    order.mark(pixels_grad)
    if custom:
        mid = mixed[0].shape[1] // 2
        gdx0 = order.tie(other(gone[1]))
        sides = ([(kdx0[0], 0), (kdx0[1], 0)], [(gdx0, 1), (gdx0, 0)], mixed, gmix)
        embz_h = Halving(
            *plain_grad(*sides, move_z, "embed_grad_b", mid, mid),
            Z_FIRST, size,
        )
        order.mark(embz_h.sent)
        sides[3][1] = order.tie(gmix[1])
        cube = (cube + order.tie(gdx0)[-cube.shape[0] :]).reshape(8, 1, -1)
        cube = jnp.pad(cube, ((0, 0), (0, 7), (0, 0)))
        embx_h = Halving(
            *plain_grad(*sides, move_x, "embed_grad_a", 0, mid, vectors=(cube, *blocks)),
            X_FIRST, size,
        )
        order.mark(embx_h.sent)
    pixels_grad = pixel_grad(
        order.tie(item_kinds), dx0[1], w_spectral, w_rgb, pick, 1, items, pixels_grad
    )
    order.mark(pixels_grad)
    if custom:
        both_x = order.tie(both_x)
        fc1_h.came(both_x[:4])
        attx_h.recvs.append(both_x[4:])
        fc1_v = fc1_h.value(order, False)
        attx_v = attx_h.value(order, False)
    summed[0] = settle(summed[0])
    if custom:
        fc1_h.came(exchange(fc1_v, "dp", 8, size))
        attx_h.came(exchange(attx_v, "dp", 4, size))
        attz_h.step(order)
        fc2_g = fc2_h.step(order)
        attz_h.step(order)
        embz_h.step(order)
        fc1_g = fc1_h.step(order)
    summed[1] = send(order.tie(ycot[1]))
    if custom:
        embx_h.step(order)
        attx_h.step(order)
        embz_h.step(order)
        attz_g = attz_h.step(order)
    if custom:
        embx_h.step(order)
        attx_g = attx_h.step(order)
    summed[1] = settle(summed[1])
    block_out = jnp.concatenate(
        [(x1[i] + (ycot[i] + summed[i] + fc2_bias)).astype(BF16) for i in range(items)], 0
    )
    order.mark(block_out)
    if custom:
        embz_g = embz_h.step(order)
        embx_g = embx_h.step(order)
        shard = width // size
        core = lax.axis_index("dp") % 2
        spans = [(shard, row * LANES, LANES) for row in range(4)]
        spans += [(shard, 4 * LANES + row * LANES // 2, LANES // 2) for row in range(2)]
        spans += [(shard, 6 * LANES, 2 * LANES)]
        spans += [(shard + 1, row * LANES, LANES) for row in range(2)]
        outs = []
        for row, first, length in spans:
            low = embx_g[row, first : first + length // 2]
            high = embx_g[row, first + length // 2 : first + length]
            outs.append(jnp.where(core == 0, low, high))
        ln2_g, ln2_b, ob_g, b2_g, q_g, v_g, b1_g, ln1_g, ln1_b = outs
        embx_g = embx_g[:shard]
        emb_g = jnp.concatenate([embx_g, embz_g], 1)
        cut = attx_g.shape[1] // 2
        planes = [attx_g[:, :cut], attx_g[:, cut:], attz_g[:, :cut]]
        qkv_grad = jnp.transpose(jnp.stack(planes), (1, 0, 2))
        out_grad = attz_g[:, cut:].T
        fc1_g = jnp.concatenate([fc1_g[0], fc1_g[1]], 1)
    else:
        cot = [cotangent[i * rows : (i + 1) * rows] for i in range(items)]
        fc2_g = scatter(both(cot, act))
        fc1_g = scatter(both(a2, dpre))
        emb_g = scatter(both(dx0, mixed))
        qkv_grad = scatter(
            sum(
                lax.dot_general(
                    a1[i], dqkv[i], (((0,), (1,)), ((), ())), preferred_element_type=F32
                )
                for i in range(items)
            )
        )
        out_grad = scatter(both(dya, mix)).T
        totals = [v[0] + v[1] for v in (sums2, qvsum, b1sum, sums1)]
        rows_of = [(0, 0), (0, 1), (0, 2), (0, 3), (1, 0), (1, 1), (2, 0), (3, 0), (3, 1)]
        outs = [scatter(totals[n][row]) for n, row in rows_of]
        ln2_g, ln2_b, ob_g, b2_g, q_g, v_g, b1_g, ln1_g, ln1_b = outs
    spectral_grad = emb_g[:, :wide].T
    rgb_grad = emb_g[:, wide:].T
    return (
        block_out, pixels_grad, spectral_grad, rgb_grad, ln1_g, ln1_b, qkv_grad, q_g, v_g, out_grad,
        ob_g, ln2_g, ln2_b, fc1_g, b1_g, fc2_g.T, b2_g,
    )


def solution(mesh):
    in_specs = (
        P("dp", "tensor"),
        P("dp"),
        P("dp"),
        P("tensor", None),
        P("tensor", None),
        P(),
        P(),
        P(None, None, "tensor"),
        P("tensor"),
        P("tensor"),
        P("tensor", None),
        P(),
        P(),
        P(),
        P(None, "tensor"),
        P("tensor"),
        P("tensor", None),
        P(),
        P("dp", None),
    )
    out_specs = (
        P("dp", None),
        P("dp", "tensor"),
        P("tensor", "dp"),
        P("tensor", "dp"),
        P("dp"),
        P("dp"),
        P("dp", None, "tensor"),
        P(("tensor", "dp")),
        P(("tensor", "dp")),
        P("tensor", "dp"),
        P("dp"),
        P("dp"),
        P("dp"),
        P("dp", "tensor"),
        P(("tensor", "dp")),
        P("tensor", "dp"),
        P("dp"),
    )
    body = functools.partial(local, size=mesh.shape["dp"])
    return jax.shard_map(body, mesh=mesh, in_specs=in_specs, out_specs=out_specs, check_vma=False)
```

```python
import functools

import jax
import jax.numpy as jnp
import ml_dtypes
import numpy as np
from jax import lax
from jax.experimental import pallas as pl
from jax.experimental.pallas import tpu as pltpu
from jax.sharding import PartitionSpec as P

HEAD_DIM = 64
GRID = 16
EPS = 1e-06
F32 = jnp.float32
BF16 = jnp.bfloat16
LANES = 128
MIB = 1024 * 1024
QUAD = 256
PART = 256
WIDE = 2


def nn(left, right):
    return lax.dot_general(left, right, (((1,), (0,)), ((), ())), preferred_element_type=F32)


def nt(left, right):
    return lax.dot_general(left, right, (((1,), (1,)), ((), ())), preferred_element_type=F32)


def tn(left, right):
    return lax.dot_general(left, right, (((0,), (0,)), ((), ())), preferred_element_type=F32)


def params(mib):
    return pltpu.CompilerParams(vmem_limit_bytes=mib * MIB)


def short_cost():
    return pl.CostEstimate(flops=1000, bytes_accessed=1000, transcendentals=0)


def long_cost():
    return pl.CostEstimate(flops=int(1e11), bytes_accessed=1000, transcendentals=0)


def whole(shape):
    return pl.BlockSpec(shape, lambda *_: (0,) * len(shape), pipeline_mode=pl.Buffered(1))


def norm_parts(values):
    center = values - jnp.mean(values, -1, keepdims=True)
    spread = jnp.mean(center * center, -1, keepdims=True)
    inverse = lax.rsqrt(spread + EPS)
    return center * inverse, inverse


def norm_back(normed, inverse, grad, gain):
    scaled = grad * gain
    mean_scaled = jnp.mean(scaled, -1, keepdims=True)
    mean_cross = jnp.mean(scaled * normed, -1, keepdims=True)
    return inverse * (scaled - mean_scaled - normed * mean_cross)


def column_sum(values):
    return jnp.sum(values, 0, keepdims=True)


def turn(place, source_ref, turned_ref, columns):
    chips = turned_ref.shape[0] // LANES
    half = LANES // 2
    core = place[chips]
    low = pl.multiple_of(core * (chips * half), half)
    high = pl.multiple_of((1 - core) * (chips * half), half)
    for chip in range(chips):
        lanes = pl.ds(pl.multiple_of(place[chip] * LANES, LANES), LANES)
        block = source_ref[:, lanes].T
        turned_ref[pl.ds(low + chip * half, half), columns] = block[:half]
        turned_ref[pl.ds(high + chip * half, half), columns] = block[half:]


def spread(turned_ref, keep_ref, gone_ref, first=0):
    middle = turned_ref.shape[0] // 2
    keep_ref[...] = turned_ref[:middle, :]
    for part in range(2):
        start = middle + part * PART
        gone_ref[first + part] = turned_ref[start : start + PART, :].astype(F32)


def turn_cot_kernel(place, cot_ref, keep_ref, gone_ref, turned_ref):
    turn(place, cot_ref, turned_ref, slice(None))
    spread(turned_ref, keep_ref, gone_ref)


def turn_cot(place, cotangent, rows):
    width = cotangent.shape[1]
    items = cotangent.shape[0] // rows
    return pl.pallas_call(
        turn_cot_kernel,
        grid_spec=pltpu.PrefetchScalarGridSpec(
            num_scalar_prefetch=1,
            grid=(items,),
            in_specs=[pl.BlockSpec((rows, width), lambda i, *_: (i, 0))],
            out_specs=[
                pl.BlockSpec((None, width // 2, rows), lambda i, *_: (i, 0, 0)),
                pl.BlockSpec((2, PART, rows), lambda i, *_: (i, 0, 0)),
            ],
            scratch_shapes=[pltpu.VMEM((width, rows), BF16)],
        ),
        out_shape=[
            jax.ShapeDtypeStruct((items, width // 2, rows), BF16),
            jax.ShapeDtypeStruct((2 * items, PART, rows), F32),
        ],
        compiler_params=params(4),
        cost_estimate=short_cost(),
        name="turn_cotangent",
    )(place, cotangent)


def pack_kernel(values_ref, out_ref):
    out_ref[0] = values_ref[...].astype(F32)


def pack(values):
    rows, columns = values.shape
    return pl.pallas_call(
        pack_kernel,
        grid=(columns // PART,),
        in_specs=[pl.BlockSpec((rows, PART), lambda n: (0, n))],
        out_specs=pl.BlockSpec((1, rows, PART), lambda n: (n, 0, 0)),
        out_shape=jax.ShapeDtypeStruct((columns // PART, rows, PART), F32),
        compiler_params=params(4),
        cost_estimate=short_cost(),
        name="pack_pixels",
    )(values)


def pack_attn_kernel(place, a1_ref, o_ref, keep_ref, gone_ref, turned_ref):
    turn(place, a1_ref, turned_ref, slice(None))
    spread(turned_ref, keep_ref, gone_ref)
    for part in range(o_ref.shape[1] // PART):
        gone_ref[2 + part] = o_ref[:, part * PART : (part + 1) * PART].astype(F32)


def pack_attn(place, a1, mix):
    rows, width = a1.shape
    parts = 2 + mix.shape[1] // PART
    return pl.pallas_call(
        pack_attn_kernel,
        grid_spec=pltpu.PrefetchScalarGridSpec(
            num_scalar_prefetch=1,
            grid=(1,),
            in_specs=[whole(a1.shape), whole(mix.shape)],
            out_specs=[whole((width // 2, rows)), whole((parts, PART, rows))],
            scratch_shapes=[pltpu.VMEM((width, rows), BF16)],
        ),
        out_shape=[
            jax.ShapeDtypeStruct((width // 2, rows), BF16),
            jax.ShapeDtypeStruct((parts, PART, rows), F32),
        ],
        compiler_params=params(4),
        cost_estimate=short_cost(),
        name="pack_attn",
    )(place, a1, mix)


def pieces_of(length):
    third = length // 3 // LANES * LANES
    return [(0, third), (third, third), (2 * third, length - 2 * third)]


def embed_kernel(
    kinds, pix_ref, wspec_ref, wrgb_ref, pick_ref, part_ref, mixed_ref,
    pix_buf, wspec_buf, wrgb_buf, pick_buf, pix_sem, big_sem, small_sem, *, item,
):
    rows, wide = pix_buf.shape
    spectral = kinds[item] == 1
    pieces = pieces_of(wide)
    own_rows = pl.ds(item * rows, rows)

    @pl.when(spectral)
    def _():
        copies = []
        for n, (first, size) in enumerate(pieces):
            span = pl.ds(first, size)
            copies.append(
                (
                    pltpu.make_async_copy(
                        pix_ref.at[own_rows, span], mixed_ref.at[:, span], pix_sem.at[n]
                    ),
                    pltpu.make_async_copy(wspec_ref.at[span], wspec_buf.at[span], big_sem.at[n]),
                )
            )
        for pair in copies:
            for copy in pair:
                copy.start()
        mixed_ref[:, wide:] = jnp.zeros((rows, wrgb_buf.shape[0]), BF16)
        for n, (first, size) in enumerate(pieces):
            for copy in copies[n]:
                copy.wait()
            term = nn(mixed_ref[:, first : first + size], wspec_buf[first : first + size, :])
            if n == 0:
                part_ref[...] = term
            else:
                part_ref[...] += term

    @pl.when(jnp.logical_not(spectral))
    def _():
        copies = []
        for n, (first, size) in enumerate(pieces):
            span = pl.ds(first, size)
            copies.append(
                (
                    pltpu.make_async_copy(
                        pix_ref.at[own_rows, span], pix_buf.at[:, span], pix_sem.at[n]
                    ),
                    pltpu.make_async_copy(pick_ref.at[span], pick_buf.at[span], big_sem.at[n]),
                )
            )
        for pair in copies:
            for copy in pair:
                copy.start()
        weights = pltpu.make_async_copy(wrgb_ref, wrgb_buf, small_sem)
        weights.start()
        mixed_ref[:, :wide] = jnp.zeros((rows, wide), BF16)
        total = None
        for n, (first, size) in enumerate(pieces):
            for copy in copies[n]:
                copy.wait()
            term = nn(pix_buf[:, first : first + size], pick_buf[first : first + size, :])
            total = term if total is None else total + term
        mixed_ref[:, wide:] = total.astype(BF16)
        weights.wait()
        part_ref[...] = nn(mixed_ref[:, wide:], wrgb_buf[...])


def embed(kinds, pixels, w_spectral, w_rgb, pick, item, rows):
    wide, width = w_spectral.shape
    narrow = w_rgb.shape[0]
    far = pl.BlockSpec(memory_space=pltpu.HBM)
    return pl.pallas_call(
        functools.partial(embed_kernel, item=item),
        grid_spec=pltpu.PrefetchScalarGridSpec(
            num_scalar_prefetch=1,
            grid=(1,),
            in_specs=[far, far, far, far],
            out_specs=[whole((rows, width)), whole((rows, wide + narrow))],
            scratch_shapes=[
                pltpu.VMEM((rows, wide), BF16),
                pltpu.VMEM((wide, width), BF16),
                pltpu.VMEM((narrow, width), BF16),
                pltpu.VMEM((wide, narrow), BF16),
                pltpu.SemaphoreType.DMA((3,)),
                pltpu.SemaphoreType.DMA((3,)),
                pltpu.SemaphoreType.DMA(()),
            ],
        ),
        out_shape=[
            jax.ShapeDtypeStruct((rows, width), F32),
            jax.ShapeDtypeStruct((rows, wide + narrow), BF16),
        ],
        compiler_params=params(58),
        cost_estimate=short_cost(),
        name="embed",
    )(kinds, pixels, w_spectral, w_rgb, pick)


def pair_masks(rows):
    lane = lax.broadcasted_iota(jnp.int32, (rows, LANES), 1)
    return lane < HEAD_DIM, lane >= HEAD_DIM


def only(mask, values):
    return jnp.where(mask, values, jnp.zeros_like(values))


def softmax_rows(query, key):
    scores = nt(query, key) * (HEAD_DIM**-0.5)
    expo = jnp.exp(scores - jnp.max(scores, -1, keepdims=True))
    return expo / jnp.sum(expo, -1, keepdims=True)


def attn_forward_kernel(
    part_ref, recv_ref, table_ref, gain_ref, bias_ref, wqkv_ref, qb_ref, vb_ref, wout_ref,
    x0_ref, a1_ref, qkv_ref, o_ref, opart_ref,
):
    quad = pl.program_id(0)
    rows, width = part_ref.shape

    @pl.when(quad == 0)
    def _():
        side = table_ref.shape[0]
        half = table_ref.shape[1]
        table = table_ref[...]
        by_row = jnp.broadcast_to(table[:, None, :], (side, side, half)).reshape(rows, half)
        by_col = jnp.broadcast_to(table[None, :, :], (side, side, half)).reshape(rows, half)
        left = part_ref[:, :half] + recv_ref[:, :half] + by_row
        right = part_ref[:, half:] + recv_ref[:, half:] + by_col
        x0_ref[:, :half] = left
        x0_ref[:, half:] = right
        normed, _inv = norm_parts(x0_ref[...])
        a1_ref[...] = (normed * gain_ref[...] + bias_ref[...]).astype(BF16)
        opart_ref[...] = jnp.zeros_like(opart_ref)

    a1 = a1_ref[...]
    query = (nn(a1, wqkv_ref[0]) + qb_ref[...]).astype(BF16)
    key = nn(a1, wqkv_ref[1]).astype(BF16)
    value = (nn(a1, wqkv_ref[2]) + vb_ref[...]).astype(BF16)
    qkv_ref[0] = query
    qkv_ref[1] = key
    qkv_ref[2] = value
    masks = pair_masks(rows)
    for pair in range(query.shape[1] // LANES):
        span = slice(pair * LANES, (pair + 1) * LANES)
        q2, k2, v2 = query[:, span], key[:, span], value[:, span]
        mixed = None
        for mask in masks:
            probs = softmax_rows(only(mask, q2), k2).astype(BF16)
            term = nn(probs, only(mask, v2))
            mixed = term if mixed is None else mixed + term
        o_ref[:, span] = mixed.astype(BF16)
    opart_ref[...] += nn(o_ref[...], wout_ref[...])


def attn_forward(part, recv, table, gain, bias, w_qkv, q_bias, v_bias, w_out):
    rows, width = part.shape
    heads_wide = w_out.shape[0]
    steps = heads_wide // QUAD
    return pl.pallas_call(
        attn_forward_kernel,
        grid=(steps,),
        in_specs=[
            whole(part.shape),
            whole(recv.shape),
            whole(table.shape),
            whole(gain.shape),
            whole(bias.shape),
            pl.BlockSpec((3, width, QUAD), lambda n: (0, 0, n)),
            pl.BlockSpec((1, QUAD), lambda n: (0, n)),
            pl.BlockSpec((1, QUAD), lambda n: (0, n)),
            pl.BlockSpec((QUAD, width), lambda n: (n, 0)),
        ],
        out_specs=[
            whole((rows, width)),
            whole((rows, width)),
            pl.BlockSpec((3, rows, QUAD), lambda n: (0, 0, n)),
            pl.BlockSpec((rows, QUAD), lambda n: (0, n)),
            whole((rows, width)),
        ],
        out_shape=[
            jax.ShapeDtypeStruct((rows, width), F32),
            jax.ShapeDtypeStruct((rows, width), BF16),
            jax.ShapeDtypeStruct((3, rows, heads_wide), BF16),
            jax.ShapeDtypeStruct((rows, heads_wide), BF16),
            jax.ShapeDtypeStruct((rows, width), F32),
        ],
        compiler_params=params(10),
        cost_estimate=long_cost(),
        name="attn_forward",
    )(part, recv, table, gain, bias, w_qkv, q_bias, v_bias, w_out)


def put_rows(refs, values, add):
    first = 0
    for ref in refs:
        rows = ref.shape[0]
        if add:
            ref[...] += values[first : first + rows]
        else:
            ref[...] = values[first : first + rows]
        first += rows


def joined(refs):
    values = [ref[...] for ref in refs]
    return values[0] if len(values) == 1 else jnp.concatenate(values, 0)


def attn_backward_kernel(place, *refs, parts):
    gpart_refs, refs = refs[: parts[0]], refs[parts[0] :]
    grecv_refs, refs = refs[: parts[1]], refs[parts[1] :]
    x1_ref, cot_ref, gain_ref, wout_ref, qkv_ref, wqkv_ref, *refs = refs
    dx1_ref, dya_ref, dqkv_ref, sums_ref, qvsum_ref, keep_ref, gone_ref, *da1_refs = refs[:-1]
    turned_ref = refs[-1]
    quad = pl.program_id(0)
    rows = x1_ref.shape[0]

    @pl.when(quad == 0)
    def _():
        normed, inverse = norm_parts(x1_ref[...])
        grad = joined(gpart_refs) + joined(grecv_refs)
        cot = cot_ref[...].astype(F32)
        dx1 = cot + norm_back(normed, inverse, grad, gain_ref[...])
        dx1_ref[...] = dx1
        dya = dx1.astype(BF16)
        dya_ref[...] = dya
        sums_ref[0:1, :] = column_sum(grad * normed)
        sums_ref[1:2, :] = column_sum(grad)
        sums_ref[2:3, :] = column_sum(dya.astype(F32))
        sums_ref[3:4, :] = column_sum(cot)
        sums_ref[4:8, :] = jnp.zeros((4, sums_ref.shape[1]), F32)
        turn(place, dya_ref, turned_ref, slice(None))
        spread(turned_ref, keep_ref, gone_ref)

    dmix = nt(dya_ref[...], wout_ref[...]).astype(BF16)
    scale = HEAD_DIM**-0.5
    masks = pair_masks(rows)
    for pair in range(dmix.shape[1] // LANES):
        span = slice(pair * LANES, (pair + 1) * LANES)
        q2, k2, v2, d2 = qkv_ref[0, :, span], qkv_ref[1, :, span], qkv_ref[2, :, span], dmix[:, span]
        totals = [None, None, None]
        for mask in masks:
            qm, km, dm = only(mask, q2), only(mask, k2), only(mask, d2)
            probs = softmax_rows(qm, k2)
            dprobs = nt(dm, v2)
            dot_row = jnp.sum(probs * dprobs, -1, keepdims=True)
            dscores = (probs * (dprobs - dot_row)).astype(BF16)
            terms = [nn(dscores, km), tn(dscores, qm), tn(probs.astype(BF16), dm)]
            totals = [t if o is None else o + t for o, t in zip(totals, terms)]
        dqkv_ref[0, :, span] = (totals[0] * scale).astype(BF16)
        dqkv_ref[1, :, span] = (totals[1] * scale).astype(BF16)
        dqkv_ref[2, :, span] = totals[2].astype(BF16)
    steps = pl.num_programs(0)
    for plane in range(3):
        gone_ref[2 + plane * steps + quad] = dqkv_ref[plane].astype(F32)
    qvsum_ref[0:1, :] = column_sum(dqkv_ref[0].astype(F32))
    qvsum_ref[1:2, :] = column_sum(dqkv_ref[2].astype(F32))
    qvsum_ref[2:8, :] = jnp.zeros((6, qvsum_ref.shape[1]), F32)
    if not da1_refs:
        return
    da1 = nt(dqkv_ref[0], wqkv_ref[0]) + nt(dqkv_ref[1], wqkv_ref[1]) + nt(dqkv_ref[2], wqkv_ref[2])

    @pl.when(quad == 0)
    def _():
        put_rows(da1_refs, da1, False)

    @pl.when(quad != 0)
    def _():
        put_rows(da1_refs, da1, True)


def attn_backward(place, gparts, grecvs, x1, cotangent, gain, w_out, qkv, w_qkv, item, cuts):
    rows, width = x1.shape
    heads_wide = w_out.shape[0]
    steps = heads_wide // QUAD
    return pl.pallas_call(
        functools.partial(attn_backward_kernel, parts=(len(gparts), len(grecvs))),
        grid_spec=pltpu.PrefetchScalarGridSpec(
            num_scalar_prefetch=1,
            grid=(steps,),
            in_specs=[
                *[whole(v.shape) for v in (*gparts, *grecvs)],
                whole(x1.shape),
                pl.BlockSpec((rows, width), lambda n, *_: (item, 0)),
                whole(gain.shape),
                pl.BlockSpec((QUAD, width), lambda n, *_: (n, 0)),
                pl.BlockSpec((3, rows, QUAD), lambda n, *_: (0, 0, n)),
                pl.BlockSpec((3, width, QUAD), lambda n, *_: (0, 0, n)),
            ],
            out_specs=[
                whole((rows, width)),
                whole((rows, width)),
                pl.BlockSpec((3, rows, QUAD), lambda n, *_: (0, 0, n)),
                whole((8, width)),
                pl.BlockSpec((8, QUAD), lambda n, *_: (0, n)),
                whole((width // 2, rows)),
                whole((2 + 3 * steps, PART, rows)),
                *[whole((cut, width)) for cut in cuts],
            ],
            scratch_shapes=[pltpu.VMEM((width, rows), BF16)],
        ),
        out_shape=[
            jax.ShapeDtypeStruct((rows, width), F32),
            jax.ShapeDtypeStruct((rows, width), BF16),
            jax.ShapeDtypeStruct((3, rows, heads_wide), BF16),
            jax.ShapeDtypeStruct((8, width), F32),
            jax.ShapeDtypeStruct((8, heads_wide), F32),
            jax.ShapeDtypeStruct((width // 2, rows), BF16),
            jax.ShapeDtypeStruct((2 + 3 * steps, PART, rows), F32),
            *[jax.ShapeDtypeStruct((cut, width), F32) for cut in cuts],
        ],
        compiler_params=params(16),
        cost_estimate=long_cost(),
        name="attn_backward",
    )(place, *gparts, *grecvs, x1, cotangent, gain, w_out, qkv, w_qkv)


def attn_in_back_kernel(dqkv_ref, wqkv_ref, out_ref):
    out_ref[...] = (
        nt(dqkv_ref[0], wqkv_ref[0]) + nt(dqkv_ref[1], wqkv_ref[1]) + nt(dqkv_ref[2], wqkv_ref[2])
    )


def attn_in_back(dqkv, w_qkv):
    rows, columns = dqkv.shape[1:]
    width = w_qkv.shape[1]
    tile = 512
    return pl.pallas_call(
        attn_in_back_kernel,
        grid=(width // tile,),
        in_specs=[whole(dqkv.shape), pl.BlockSpec((3, tile, columns), lambda n: (0, n, 0))],
        out_specs=pl.BlockSpec((rows, tile), lambda n: (0, n)),
        out_shape=jax.ShapeDtypeStruct((rows, width), F32),
        compiler_params=params(8),
        cost_estimate=long_cost(),
        name="attn_in_back",
    )(dqkv, w_qkv)


def mlp_kernel(
    place, x0_ref, opart_ref, orecv_ref, obias_ref, gain_ref, bias_ref, wfc1_ref, b1_ref, wfc2_ref, cot_ref,
    x1_ref, a2_ref, act_ref, dpre_ref, b1sum_ref, keep_ref, gact_ref, gpre_ref, *refs,
):
    da2_refs, turned_ref = refs[:-1], refs[-1]
    step = pl.program_id(0)

    @pl.when(step == 0)
    def _():
        x1_ref[...] = x0_ref[...] + (opart_ref[...] + orecv_ref[...] + obias_ref[...])
        normed, _inv = norm_parts(x1_ref[...])
        a2_ref[...] = (normed * gain_ref[...] + bias_ref[...]).astype(BF16)
        turn(place, a2_ref, turned_ref, slice(None))
        spread(turned_ref, keep_ref, gpre_ref)

    pre = nn(a2_ref[...], wfc1_ref[...]) + b1_ref[...]
    dact = nt(cot_ref[...], wfc2_ref[...])
    cdf = 0.5 * (1.0 + lax.erf(pre * (2.0**-0.5)))
    act = (pre * cdf).astype(BF16)
    act_ref[...] = act
    density = jnp.exp(-0.5 * pre * pre) * 0.3989422804014327
    dpre = (dact * (cdf + pre * density)).astype(BF16)
    dpre_ref[...] = dpre
    for part in range(act.shape[1] // PART):
        columns = slice(part * PART, (part + 1) * PART)
        gact_ref[part] = act[:, columns].astype(F32)
        gpre_ref[2 + step * (act.shape[1] // PART) + part] = dpre[:, columns].astype(F32)
    b1sum_ref[...] = column_sum(dpre.astype(F32))
    if not da2_refs:
        return
    da2 = nt(dpre, wfc1_ref[...])

    @pl.when(step == 0)
    def _():
        put_rows(da2_refs, da2, False)

    @pl.when(step != 0)
    def _():
        put_rows(da2_refs, da2, True)


def mlp(
    place, x0, opart, orecv, out_bias, gain, bias, w_fc1, fc1_bias, w_fc2, cotangent, item, cuts
):
    rows, width = x0.shape
    hidden = w_fc1.shape[1]
    tile = 512
    parts = tile // PART
    row_tile = pl.BlockSpec((rows, tile), lambda n, *_: (0, n))
    gone = pl.BlockSpec((parts, rows, PART), lambda n, *_: (n, 0, 0))
    return pl.pallas_call(
        mlp_kernel,
        grid_spec=pltpu.PrefetchScalarGridSpec(
            num_scalar_prefetch=1,
            grid=(hidden // tile,),
            in_specs=[
                whole(x0.shape),
                whole(opart.shape),
                whole(orecv.shape),
                whole(out_bias.shape),
                whole(gain.shape),
                whole(bias.shape),
                pl.BlockSpec((width, tile), lambda n, *_: (0, n)),
                pl.BlockSpec((1, tile), lambda n, *_: (0, n)),
                pl.BlockSpec((tile, width), lambda n, *_: (n, 0)),
                pl.BlockSpec((rows, width), lambda n, *_: (item, 0)),
            ],
            out_specs=[
                whole((rows, width)),
                whole((rows, width)),
                row_tile,
                row_tile,
                pl.BlockSpec((1, tile), lambda n, *_: (0, n)),
                whole((width // 2, rows)),
                gone,
                whole((2 + hidden // PART, rows, PART)),
                *[whole((cut, width)) for cut in cuts],
            ],
            scratch_shapes=[pltpu.VMEM((width, rows), BF16)],
        ),
        out_shape=[
            jax.ShapeDtypeStruct((rows, width), F32),
            jax.ShapeDtypeStruct((rows, width), BF16),
            jax.ShapeDtypeStruct((rows, hidden), BF16),
            jax.ShapeDtypeStruct((rows, hidden), BF16),
            jax.ShapeDtypeStruct((1, hidden), F32),
            jax.ShapeDtypeStruct((width // 2, rows), BF16),
            jax.ShapeDtypeStruct((hidden // PART, rows, PART), F32),
            jax.ShapeDtypeStruct((2 + hidden // PART, rows, PART), F32),
            *[jax.ShapeDtypeStruct((cut, width), F32) for cut in cuts],
        ],
        compiler_params=params(14),
        cost_estimate=long_cost(),
        name="mlp",
    )(place, x0, opart, orecv, out_bias, gain, bias, w_fc1, fc1_bias, w_fc2, cotangent)


def mlp_back_kernel(dpre_ref, wfc1_ref, out_ref):
    out_ref[...] = nt(dpre_ref[...], wfc1_ref[...])


def mlp_back(dpre, w_fc1):
    rows, hidden = dpre.shape
    width = w_fc1.shape[0]
    tile = 512
    return pl.pallas_call(
        mlp_back_kernel,
        grid=(width // tile,),
        in_specs=[whole(dpre.shape), pl.BlockSpec((tile, hidden), lambda n: (n, 0))],
        out_specs=pl.BlockSpec((rows, tile), lambda n: (0, n)),
        out_shape=jax.ShapeDtypeStruct((rows, width), F32),
        compiler_params=params(6),
        cost_estimate=long_cost(),
        name="mlp_back",
    )(dpre, w_fc1)


def mlp_out_kernel(act_ref, wfc2_ref, out_ref):
    out_ref[...] = nn(act_ref[...], wfc2_ref[...])


def mlp_out(act, w_fc2, estimate):
    rows, hidden = act.shape
    width = w_fc2.shape[1]
    tile = 512
    return pl.pallas_call(
        mlp_out_kernel,
        grid=(width // tile,),
        in_specs=[whole(act.shape), pl.BlockSpec((hidden, tile), lambda n: (0, n))],
        out_specs=pl.BlockSpec((rows, tile), lambda n: (0, n)),
        out_shape=jax.ShapeDtypeStruct((rows, width), F32),
        compiler_params=params(6),
        cost_estimate=estimate,
        name="mlp_out",
    )(act, w_fc2)


def first_norm_back_kernel(place, *refs, parts, riders):
    gpart_refs, refs = refs[: parts[0]], refs[parts[0] :]
    grecv_refs, refs = refs[: parts[1]], refs[parts[1] :]
    rider_refs, refs = refs[:riders], refs[riders:]
    x0_ref, dx1_ref, gain_ref, dx0_ref, sums_ref, keep_ref, gone_ref, block_ref, turned_ref = refs
    normed, inverse = norm_parts(x0_ref[...])
    grad = joined(gpart_refs) + joined(grecv_refs)
    dx0_ref[...] = (dx1_ref[...] + norm_back(normed, inverse, grad, gain_ref[...])).astype(BF16)
    sums_ref[0:1, :] = column_sum(grad * normed)
    sums_ref[1:2, :] = column_sum(grad)
    sums_ref[2:8, :] = jnp.zeros((6, sums_ref.shape[1]), F32)
    turn(place, dx0_ref, turned_ref, slice(None))
    middle = turned_ref.shape[0] // 2
    keep_ref[...] = turned_ref[:middle, :]
    gone_ref[:middle, :] = turned_ref[middle:, :].astype(F32)
    for chip in range(8):
        lanes = pl.ds(pl.multiple_of(place[chip] * LANES, LANES), LANES)
        for row in range(2):
            block_ref[chip : chip + 1, row * LANES : (row + 1) * LANES] = sums_ref[row : row + 1, lanes]
    gone_ref[middle : middle + 8, :] = block_ref[...]
    first = middle + 8
    for rider_ref in rider_refs:
        gone_ref[first : first + rider_ref.shape[0], :] = rider_ref[...]
        first += rider_ref.shape[0]


def first_norm_back(place, gparts, grecvs, x0, dx1, gain, estimate, riders=()):
    rows, width = x0.shape
    operands = (*gparts, *grecvs, *riders, x0, dx1, gain)
    extra = sum(v.shape[0] for v in riders)
    shapes = [
        jax.ShapeDtypeStruct((rows, width), BF16),
        jax.ShapeDtypeStruct((8, width), F32),
        jax.ShapeDtypeStruct((width // 2, rows), BF16),
        jax.ShapeDtypeStruct((width // 2 + 8 + extra, rows), F32),
        jax.ShapeDtypeStruct((8, 2 * LANES), F32),
    ]
    return pl.pallas_call(
        functools.partial(
            first_norm_back_kernel, parts=(len(gparts), len(grecvs)), riders=len(riders)
        ),
        grid_spec=pltpu.PrefetchScalarGridSpec(
            num_scalar_prefetch=1,
            grid=(1,),
            in_specs=[whole(v.shape) for v in operands],
            out_specs=[whole(v.shape) for v in shapes],
            scratch_shapes=[pltpu.VMEM((width, rows), BF16)],
        ),
        out_shape=shapes,
        compiler_params=params(10),
        cost_estimate=estimate,
        name="first_norm_back",
    )(place, *operands)


def pack_vectors_kernel(place, sa_ref, sb_ref, qa_ref, qb_ref, ba_ref, bb_ref, out_ref, *refs):
    sums_ref, qv_ref, hidden_ref = refs
    sums_ref[...] = sa_ref[...] + sb_ref[...]
    qv_ref[...] = qa_ref[...] + qb_ref[...]
    hidden_ref[...] = ba_ref[...] + bb_ref[...]
    out_ref[...] = jnp.zeros_like(out_ref)
    half = LANES // 2
    for pos in range(8):
        chip = place[pos]
        lanes = pl.ds(pl.multiple_of(chip * LANES, LANES), LANES)
        for row in range(4):
            first = row % 2 * LANES
            spot = 4 * pos + row // 2
            out_ref[spot : spot + 1, first : first + LANES] = sums_ref[row : row + 1, lanes]
        both = pl.ds(pl.multiple_of(chip // 2 * LANES, LANES), LANES)
        spot = 4 * pos + 2
        for row in range(2):
            pair = qv_ref[row : row + 1, both]
            own = jnp.where(chip % 2 == 0, pair[:, :half], pair[:, half:])
            out_ref[spot : spot + 1, row * half : (row + 1) * half] = own
        wide = pl.ds(pl.multiple_of(chip * 2 * LANES, 2 * LANES), 2 * LANES)
        out_ref[spot + 1 : spot + 2, :] = hidden_ref[0:1, wide]


def pack_vectors(place, sums, qv, hidden):
    operands = (*sums, *qv, *hidden)
    return pl.pallas_call(
        pack_vectors_kernel,
        grid_spec=pltpu.PrefetchScalarGridSpec(
            num_scalar_prefetch=1,
            grid=(1,),
            in_specs=[whole(v.shape) for v in operands],
            out_specs=whole((32, 2 * LANES)),
            scratch_shapes=[pltpu.VMEM(v[0].shape, F32) for v in (sums, qv, hidden)],
        ),
        out_shape=jax.ShapeDtypeStruct((32, 2 * LANES), F32),
        compiler_params=params(4),
        cost_estimate=short_cost(),
        name="pack_vectors",
    )(place, *operands)


def pixel_grad_kernel(kinds, grad_ref, wspec_ref, wrgb_ref, pick_ref, *refs, item):
    out_ref = refs[-1]
    spectral = kinds[item] == 1
    grad = grad_ref[...]
    wide = wspec_ref.shape[0]
    cut = (wide // 2 + LANES - 1) // LANES * LANES

    @pl.when(spectral)
    def _():
        out_ref[:, :cut] = nt(grad, wspec_ref[:cut, :]).astype(BF16)
        out_ref[:, cut:] = nt(grad, wspec_ref[cut:, :]).astype(BF16)

    @pl.when(jnp.logical_not(spectral))
    def _():
        small = nt(grad, wrgb_ref[...]).astype(BF16)
        out_ref[...] = nt(small, pick_ref[...]).astype(BF16)


def pixel_grad(kinds, grad, w_spectral, w_rgb, pick, item, items, filled=None):
    rows = grad.shape[0]
    wide, width = w_spectral.shape
    more = [] if filled is None else [filled]
    return pl.pallas_call(
        functools.partial(pixel_grad_kernel, item=item),
        grid_spec=pltpu.PrefetchScalarGridSpec(
            num_scalar_prefetch=1,
            grid=(1,),
            in_specs=[
                whole(grad.shape),
                whole(w_spectral.shape),
                whole(w_rgb.shape),
                whole(pick.shape),
            ]
            + [pl.BlockSpec(memory_space=pl.ANY)] * len(more),
            out_specs=pl.BlockSpec((rows, wide), lambda i, *_: (item, 0)),
        ),
        out_shape=jax.ShapeDtypeStruct((items * rows, wide), BF16),
        input_output_aliases={5: 0} if more else {},
        compiler_params=params(12),
        cost_estimate=long_cost(),
        name="pixel_grad",
    )(kinds, grad, w_spectral, w_rgb, pick, *more)


def gather_left(keep_refs, gone_refs, first, left_ref):
    rows = keep_refs[0].shape[-1]
    for pos, keep_ref in enumerate(keep_refs):
        left_ref[:, pos * rows : (pos + 1) * rows] = keep_ref[...]
    base = len(keep_refs) * rows
    for pos, gone_ref in enumerate(gone_refs):
        columns = slice(base + pos * rows, base + (pos + 1) * rows)
        if len(gone_ref.shape) == 2:
            left_ref[:, columns] = gone_ref[: left_ref.shape[0], :].astype(BF16)
            continue
        for part in range(2):
            left_ref[part * PART : (part + 1) * PART, columns] = gone_ref[first + part].astype(BF16)


def emit(left_ref, rights, send_ref, keep_ref, moves, columns=slice(None)):
    right = jnp.concatenate([r.astype(BF16) for r in rights], 0)
    total = nn(left_ref[...], right)
    half = LANES // 2
    for pos, block in enumerate(moves):
        out_ref = send_ref if pos < 4 else keep_ref
        value = total[block * half : (block + 1) * half]
        if len(out_ref.shape) == 4:
            out_ref[pos % 4, 0, :, columns] = value
        else:
            out_ref[pos % 4, :half, columns] = value


def plain_grad_kernel(
    ka_ref, kb_ref, la_ref, lb_ref, ra_ref, rb_ref, oa_ref, ob_ref, *refs, moves, vectors
):
    send_ref, keep_ref, left_ref = refs[-3:]

    @pl.when(pl.program_id(0) == 0)
    def _():
        gather_left((ka_ref, kb_ref), (la_ref, lb_ref), 0, left_ref)

    for part in range(oa_ref.shape[0]):
        columns = slice(part * PART, (part + 1) * PART)
        rights = (ra_ref[:, columns], rb_ref[:, columns], oa_ref[part], ob_ref[part])
        emit(left_ref, rights, send_ref, keep_ref, moves, columns)
    if vectors:
        early_ref, sa_ref, sb_ref = refs[:3]
        half = LANES // 2
        middle = left_ref.shape[0]
        late = sa_ref[...] + sb_ref[...] + (la_ref[middle:, :] + lb_ref[middle:, :])
        for pos, block in enumerate(moves):
            out_ref = send_ref if pos < 4 else keep_ref
            out_ref[pos % 4, half:, :] = early_ref[block]

            @pl.when(pl.program_id(0) == 0)
            def _(out_ref=out_ref, pos=pos, block=block):
                out_ref[pos % 4, half + 1 : half + 2, : late.shape[1]] = late[block : block + 1]


def plain_grad(keeps, lefts, rights, others, moves, name, skip=0, columns=None, lead=0, vectors=(), planes=1):
    half_width, rows = keeps[0][0].shape[-2:]
    columns = columns or rights[0].shape[1]
    wide = WIDE
    base = skip // (wide * PART)
    half = LANES // 2

    def keep_spec(array, item):
        if array.ndim == 2:
            return whole(array.shape)
        return pl.BlockSpec((None,) + array.shape[1:], lambda n: (item, 0, 0))

    right = pl.BlockSpec((rows, wide * PART), lambda n: (0, n + base))
    other = pl.BlockSpec((wide, rows, PART), lambda n: (n + base + lead // wide, 0, 0))
    height = half + 8 if vectors else half
    out = pl.BlockSpec((4, height, wide * PART), lambda n: (0, 0, n))
    shape = jax.ShapeDtypeStruct((4, height, columns), F32)
    if planes > 1:
        per = columns // planes // (wide * PART)
        out = pl.BlockSpec((4, 1, half, wide * PART), lambda n: (0, n // per, 0, n % per))
        shape = jax.ShapeDtypeStruct((4, planes, half, columns // planes), F32)

    def left_spec(array, item):
        if array.ndim == 2:
            return pl.BlockSpec((half_width + 8, rows), lambda n: (item, 0))
        return pl.BlockSpec((2, PART, rows), lambda n: (item, 0, 0))

    vector_specs = []
    if vectors:
        vector_specs = [pl.BlockSpec((8, 8, wide * PART), lambda n: (0, 0, n))]
        vector_specs += [whole(v.shape) for v in vectors[1:]]
    return pl.pallas_call(
        functools.partial(plain_grad_kernel, moves=moves, vectors=bool(vectors)),
        grid=(columns // (wide * PART),),
        in_specs=[keep_spec(*k) for k in keeps]
        + [left_spec(*v) for v in lefts]
        + [right, right, other, other]
        + vector_specs,
        out_specs=[out, out],
        scratch_shapes=[pltpu.VMEM((half_width, 4 * rows), BF16)],
        out_shape=[shape, shape],
        compiler_params=params(14),
        cost_estimate=short_cost(),
        name=name,
    )(*[k for k, _ in keeps], *[v for v, _ in lefts], *rights, *others, *vectors)


def query_key_kernel(
    aa_ref, ab_ref, fa_ref, fb_ref, ba_ref, bb_ref, da_ref, db_ref, send_ref, keep_ref, left_ref,
    *, moves,
):
    plane, step = pl.program_id(0), pl.program_id(1)

    @pl.when((plane == 0) & (step == 0))
    def _():
        gather_left((aa_ref, ab_ref), (fa_ref, fb_ref), 0, left_ref)

    spot = 2 + plane * pl.num_programs(1) + step
    emit(left_ref, (da_ref[...], db_ref[...], ba_ref[spot], bb_ref[spot]), send_ref, keep_ref, moves)


def value_out_kernel(
    aa_ref, ab_ref, fa_ref, fb_ref, ba_ref, bb_ref, da_ref, db_ref, ya_ref, yb_ref, ma_ref, mb_ref,
    send_ref, keep_ref, left_ref, *, moves,
):
    plane, step = pl.program_id(0), pl.program_id(1)

    @pl.when((plane == 0) & (step == 0))
    def _():
        gather_left((aa_ref, ab_ref), (fa_ref, fb_ref), 0, left_ref)

    @pl.when((plane == 1) & (step == 0))
    def _():
        gather_left((ya_ref, yb_ref), (ba_ref, bb_ref), 0, left_ref)

    @pl.when(plane == 0)
    def _():
        spot = 2 + 2 * pl.num_programs(1) + step
        emit(left_ref, (da_ref[...], db_ref[...], ba_ref[spot], bb_ref[spot]), send_ref, keep_ref, moves)

    @pl.when(plane == 1)
    def _():
        spot = 2 + step
        emit(left_ref, (ma_ref[...], mb_ref[...], fa_ref[spot], fb_ref[spot]), send_ref, keep_ref, moves)


def attn_grad(keep_a1, other_f, other_b, dqkv, moves, out_side=None):
    half_width, rows = keep_a1[0].shape
    columns = dqkv[0].shape[2]
    steps = columns // PART
    half = LANES // 2
    side = whole((half_width, rows))
    specs = [side, side] + [whole(v.shape) for v in (*other_f, *other_b)]
    if out_side is None:
        kernel, name, more = query_key_kernel, "query_key_grad", []
        plane = pl.BlockSpec((None, rows, PART), lambda p, n: (p, 0, n))
        specs += [plane, plane]
    else:
        kernel, name, more = value_out_kernel, "value_out_grad", [*out_side[0], *out_side[1]]
        plane = pl.BlockSpec((None, rows, PART), lambda p, n: (2, 0, n))
        mixed = pl.BlockSpec((rows, PART), lambda p, n: (0, n))
        specs += [plane, plane, side, side, mixed, mixed]
    out = pl.BlockSpec((4, half, PART), lambda p, n: (0, 0, p * steps + n))
    shape = jax.ShapeDtypeStruct((4, half, 2 * columns), F32)
    return pl.pallas_call(
        functools.partial(kernel, moves=moves),
        grid=(2, steps),
        in_specs=specs,
        out_specs=[out, out],
        scratch_shapes=[pltpu.VMEM((half_width, 4 * rows), BF16)],
        out_shape=[shape, shape],
        compiler_params=params(12),
        cost_estimate=short_cost(),
        name=name,
    )(*keep_a1, *other_f, *other_b, *dqkv, *more)


def exchange(values, axis, bit, size):
    return lax.ppermute(values, axis, [(i, i ^ bit) for i in range(size)])


def swap(values):
    return exchange(values, "tensor", 1, 2)


def after(first, values):
    return lax.optimization_barrier((first, values))[1]


X_FIRST = (2, 4, 8)
Z_FIRST = (4, 2, 8)


def block_flips(bits):
    return [sum((1 - ((p >> (2 - n)) & 1)) * (bits[n] // 2) for n in range(3)) for p in range(8)]


def block_moves(bits):
    stands = block_flips(X_FIRST)
    return tuple(stands.index(f) for f in block_flips(bits))


def places():
    me = lax.axis_index("dp")
    flips = jnp.array(block_flips(X_FIRST), jnp.int32)
    return jnp.concatenate([(me // 2) ^ flips, (me % 2)[None]]).astype(jnp.int32)


class Halving:
    def __init__(self, send, keep, bits, size, first=True):
        self.keep, self.bits, self.size = keep, bits, size
        self.unit = keep.shape[0] // 4
        self.recvs = [exchange(send, "dp", bits[0], size)] if first else []
        self.left = keep.shape[0]
        self.sent = send

    def value(self, order, tie=True):
        if tie:
            self.recvs[-1] = order.tie(self.recvs[-1])
        left = self.left
        count = max(left // 2, self.unit)
        total = self.keep.shape[0] - left
        value = self.keep[total : total + count]
        for recv in self.recvs:
            first = recv.shape[0] - left
            value = value + recv[first : first + count]
        order.mark(value)
        return value

    def came(self, recv):
        self.recvs.append(recv)
        self.left = self.left // 2

    def step(self, order):
        value = self.value(order)
        if self.left == self.unit:
            return value[0] if self.unit == 1 else value
        self.came(exchange(value, "dp", self.bits[len(self.recvs)], self.size))
        return None


class Order:
    def __init__(self):
        self.last = None

    def tie(self, values):
        return values if self.last is None else after(self.last, values)

    def mark(self, values):
        self.last = values


def local(
    pixels, item_kinds, gsd_codes, w_spectral, w_rgb, ln1_gain, ln1_bias, w_qkv, q_bias, v_bias,
    w_out, out_bias, ln2_gain, ln2_bias, w_fc1, fc1_bias, w_fc2, fc2_bias, cotangent, *, size,
):
    items = item_kinds.shape[0]
    rows = pixels.shape[0] // items
    width = w_out.shape[1]
    wide = pixels.shape[1]
    narrow = w_rgb.shape[0]
    bands = wide // (narrow // 3)
    custom = size == 16

    def row(vector):
        return vector.reshape(1, -1)

    g1, c1, g2, c2 = row(ln1_gain), row(ln1_bias), row(ln2_gain), row(ln2_bias)
    qb, vb, ob, b1 = row(q_bias), row(v_bias), row(out_bias), row(fc1_bias)
    wqkv = jnp.transpose(w_qkv, (1, 0, 2))

    source = np.arange(wide)[:, None]
    target = np.arange(narrow)[None, :]
    pick = jnp.asarray((source == (target // 3) * bands + target % 3).astype(ml_dtypes.bfloat16))

    ratio = (gsd_codes.astype(F32) + 1.0) / 4.0
    quarter = width // 4
    frequency = 1.0 / 10000.0 ** (jnp.arange(quarter).astype(F32) / quarter)
    spot = jnp.arange(GRID).astype(F32)
    angle = ratio[:, None, None] * spot[None, :, None] * frequency[None, None, :]
    tables = jnp.concatenate([jnp.sin(angle), jnp.cos(angle)], -1)

    def scatter(values):
        return lax.psum_scatter(values, "dp", scatter_dimension=0, tiled=True)

    def both(left, right):
        return sum(tn(left[i], right[i]) for i in range(items))

    order = Order()
    gate = None

    def send(values, wait=True):
        nonlocal gate
        if gate is not None:
            values = after(gate, values)
        gate = swap(values)
        return gate

    place = places() if custom else jnp.arange(9, dtype=jnp.int32) % 8
    move_x, move_z = block_moves(X_FIRST), block_moves(Z_FIRST)

    def other(values):
        return exchange(values, "dp", 1, size) if custom else values

    cut = rows * 3 // 8 // 8 * 8
    cuts = [(cut, rows - cut)] + [(rows,)] * (items - 1)

    def settle(values):
        values = order.tie(values)
        order.mark(jax.tree.leaves(values)[0])
        return values

    none = [None] * items
    part, mixed, erecv, fwd, orecv, ffn, grecv, bwd, arecv, last, ycot = (list(none) for _ in range(11))
    gmix, pk, gfwd, gact, gpre, gbwd, gdx0, da1, da2 = (list(none) for _ in range(9))

    for i in range(items):
        part[i], mixed[i] = embed(order.tie(item_kinds), pixels, w_spectral, w_rgb, pick, i, rows)
        order.mark(part[i])
        erecv[i] = send(part[i])
    keep_cot, gone_cot = turn_cot(order.tie(place), cotangent, rows)
    order.mark(gone_cot)
    gone_mix = []
    for i in range(items):
        gone_mix.append(pack(order.tie(mixed[i])))
        order.mark(gone_mix[i])
    gcot = other(gone_cot)
    gmix = [other(v) for v in gone_mix]
    for i in range(items):
        fwd[i] = attn_forward(
            part[i], erecv[i], tables[i], order.tie(g1), c1, wqkv, qb, vb, w_out
        )
        order.mark(fwd[i][4])
        orecv[i] = send(fwd[i][4])
        if i == 0:
            gcot = settle(gcot)
        else:
            gmix = [settle(v) for v in gmix]
        pk[i] = pack_attn(order.tie(place), fwd[i][1], fwd[i][3])
        order.mark(pk[i][1])
        gfwd[i] = other(pk[i][1])
    x0, a1, qkv, mix, _ = zip(*fwd)
    for i in range(items):
        ffn[i] = mlp(
            place, x0[i], fwd[i][4], orecv[i], order.tie(ob), g2, c2, w_fc1, b1, w_fc2, cotangent, i,
            cuts[i] if i == 0 else (),
        )
        da2[i] = ffn[i][8:]
        order.mark(da2[i][0] if i == 0 else ffn[i][6])
        if i == 0:
            grecv[i] = [send(v) for v in da2[i]]
        gact[i] = other(ffn[i][6])
        gpre[i] = other(ffn[i][7])
        if i == 0:
            gfwd = [settle(v) for v in gfwd]
        else:
            grecv[0][0] = settle(grecv[0][0])
            gact[0], gpre[0] = settle((gact[0], gpre[0]))
            da2[1] = [mlp_back(order.tie(ffn[1][3]), w_fc1)]
            order.mark(da2[1][0])
    x1, a2, act, dpre, b1sum, ka2 = list(zip(*[v[:6] for v in ffn]))
    if custom:
        gact[1] = order.tie(gact[1])
        fc2_h = Halving(
            *plain_grad(
                [(keep_cot, 0), (keep_cot, 1)], [(gcot, 0), (gcot, 1)], act, gact, move_x, "fc2_grad"
            ),
            X_FIRST, size,
        )
        order.mark(fc2_h.sent)
        gpre[1] = order.tie(gpre[1])
        fc1_s = plain_grad(
            [(ka2[0], 0), (ka2[1], 0)], [(gpre[0], 0), (gpre[1], 0)], dpre, gpre, move_z, "fc1_grad",
            lead=2, planes=2,
        )
        fc1_s = [v.reshape(8, *v.shape[2:]) for v in fc1_s]
        fc1_h = Halving(*fc1_s, Z_FIRST, size)
        order.mark(fc1_h.sent)
    grecv[1] = [send(order.tie(da2[1][0]))]
    for i in range(items):
        bwd[i] = attn_backward(
            place, da2[i], grecv[i], x1[i], cotangent, order.tie(g2), w_out, qkv[i], wqkv, i,
            cuts[i] if i == 0 else (),
        )
        da1[i] = bwd[i][7:]
        order.mark(da1[i][0] if i == 0 else bwd[i][6])
        if i == 0:
            arecv[i] = [send(v) for v in da1[i]]
            for n in range(items):
                ycot[n] = mlp_out(order.tie(ffn[n][2]), w_fc2, short_cost())
                order.mark(ycot[n])
        else:
            arecv[0][0] = settle(arecv[0][0])
            gbwd = [other(order.tie(bwd[0][6])), other(bwd[1][6])]
            da1[1] = [attn_in_back(order.tie(bwd[1][2]), wqkv)]
            order.mark(da1[1][0])
    dx1, dya, dqkv, sums2, qvsum, kdya = list(zip(*[v[:6] for v in bwd]))
    if custom:
        fc2_h.step(order)
        gbwd = [order.tie(v) for v in gbwd]
        keep_a1 = [v[0] for v in pk]
        attx_h = Halving(*attn_grad(keep_a1, gfwd, gbwd, dqkv, move_x), X_FIRST, size, first=False)
        order.mark(attx_h.sent)
        both_x = jnp.concatenate([fc1_h.value(order), attx_h.sent], 0)
        order.mark(both_x)
        gbwd[1] = order.tie(gbwd[1])
        both_x = exchange(both_x, "dp", 2, size)
        attz_h = Halving(
            *attn_grad(keep_a1, gfwd, gbwd, dqkv, move_z, (kdya, mix)), Z_FIRST, size
        )
        order.mark(attz_h.sent)
    arecv[1] = [send(order.tie(da1[1][0]))]
    riders = ()
    for i in range(items):
        estimate = long_cost() if i == 0 else short_cost()
        last[i] = first_norm_back(
            place, da1[i], arecv[i], x0[i], dx1[i], order.tie(g1), estimate, riders
        )
        order.mark(last[i][0])
        if custom and i == 0:
            fc2_h.step(order)
        if custom and i == 0:
            cube = pack_vectors(order.tie(place), sums2, qvsum, b1sum)
            order.mark(cube)
            riders = (last[0][3], cube)
    summed = list(none)
    summed[0] = send(order.tie(ycot[0]))
    dx0, sums1, kdx0, gone, blocks = zip(*last)
    pixels_grad = pixel_grad(order.tie(item_kinds), dx0[0], w_spectral, w_rgb, pick, 0, items)
    order.mark(pixels_grad)
    if custom:
        mid = mixed[0].shape[1] // 2
        gdx0 = order.tie(other(gone[1]))
        sides = ([(kdx0[0], 0), (kdx0[1], 0)], [(gdx0, 1), (gdx0, 0)], mixed, gmix)
        embz_h = Halving(
            *plain_grad(*sides, move_z, "embed_grad_b", mid, mid),
            Z_FIRST, size,
        )
        order.mark(embz_h.sent)
        sides[3][1] = order.tie(gmix[1])
        cube = (cube + order.tie(gdx0)[-cube.shape[0] :]).reshape(8, 1, -1)
        cube = jnp.pad(cube, ((0, 0), (0, 7), (0, 0)))
        embx_h = Halving(
            *plain_grad(*sides, move_x, "embed_grad_a", 0, mid, vectors=(cube, *blocks)),
            X_FIRST, size,
        )
        order.mark(embx_h.sent)
    pixels_grad = pixel_grad(
        order.tie(item_kinds), dx0[1], w_spectral, w_rgb, pick, 1, items, pixels_grad
    )
    order.mark(pixels_grad)
    if custom:
        both_x = order.tie(both_x)
        fc1_h.came(both_x[:4])
        attx_h.recvs.append(both_x[4:])
        fc1_v = fc1_h.value(order, False)
        attx_v = attx_h.value(order, False)
    summed[0] = settle(summed[0])
    if custom:
        fc1_h.came(exchange(fc1_v, "dp", 8, size))
        attx_h.came(exchange(attx_v, "dp", 4, size))
        attz_h.step(order)
        fc2_g = fc2_h.step(order)
        attz_h.step(order)
        embz_h.step(order)
        fc1_g = fc1_h.step(order)
    summed[1] = send(order.tie(ycot[1]))
    if custom:
        embx_h.step(order)
        attx_h.step(order)
        embz_h.step(order)
        attz_g = attz_h.step(order)
    if custom:
        embx_h.step(order)
        attx_g = attx_h.step(order)
    summed[1] = settle(summed[1])
    block_out = jnp.concatenate(
        [(x1[i] + (ycot[i] + summed[i] + fc2_bias)).astype(BF16) for i in range(items)], 0
    )
    order.mark(block_out)
    if custom:
        embz_g = embz_h.step(order)
        embx_g = embx_h.step(order)
        shard = width // size
        core = lax.axis_index("dp") % 2
        spans = [(shard, row * LANES, LANES) for row in range(4)]
        spans += [(shard, 4 * LANES + row * LANES // 2, LANES // 2) for row in range(2)]
        spans += [(shard, 6 * LANES, 2 * LANES)]
        spans += [(shard + 1, row * LANES, LANES) for row in range(2)]
        outs = []
        for row, first, length in spans:
            low = embx_g[row, first : first + length // 2]
            high = embx_g[row, first + length // 2 : first + length]
            outs.append(jnp.where(core == 0, low, high))
        ln2_g, ln2_b, ob_g, b2_g, q_g, v_g, b1_g, ln1_g, ln1_b = outs
        embx_g = embx_g[:shard]
        emb_g = jnp.concatenate([embx_g, embz_g], 1)
        cut = attx_g.shape[1] // 2
        planes = [attx_g[:, :cut], attx_g[:, cut:], attz_g[:, :cut]]
        qkv_grad = jnp.transpose(jnp.stack(planes), (1, 0, 2))
        out_grad = attz_g[:, cut:].T
        fc1_g = jnp.concatenate([fc1_g[0], fc1_g[1]], 1)
    else:
        cot = [cotangent[i * rows : (i + 1) * rows] for i in range(items)]
        fc2_g = scatter(both(cot, act))
        fc1_g = scatter(both(a2, dpre))
        emb_g = scatter(both(dx0, mixed))
        qkv_grad = scatter(
            sum(
                lax.dot_general(
                    a1[i], dqkv[i], (((0,), (1,)), ((), ())), preferred_element_type=F32
                )
                for i in range(items)
            )
        )
        out_grad = scatter(both(dya, mix)).T
        totals = [v[0] + v[1] for v in (sums2, qvsum, b1sum, sums1)]
        rows_of = [(0, 0), (0, 1), (0, 2), (0, 3), (1, 0), (1, 1), (2, 0), (3, 0), (3, 1)]
        outs = [scatter(totals[n][row]) for n, row in rows_of]
        ln2_g, ln2_b, ob_g, b2_g, q_g, v_g, b1_g, ln1_g, ln1_b = outs
    spectral_grad = emb_g[:, :wide].T
    rgb_grad = emb_g[:, wide:].T
    return (
        block_out, pixels_grad, spectral_grad, rgb_grad, ln1_g, ln1_b, qkv_grad, q_g, v_g, out_grad,
        ob_g, ln2_g, ln2_b, fc1_g, b1_g, fc2_g.T, b2_g,
    )


def solution(mesh):
    in_specs = (
        P("dp", "tensor"),
        P("dp"),
        P("dp"),
        P("tensor", None),
        P("tensor", None),
        P(),
        P(),
        P(None, None, "tensor"),
        P("tensor"),
        P("tensor"),
        P("tensor", None),
        P(),
        P(),
        P(),
        P(None, "tensor"),
        P("tensor"),
        P("tensor", None),
        P(),
        P("dp", None),
    )
    out_specs = (
        P("dp", None),
        P("dp", "tensor"),
        P("tensor", "dp"),
        P("tensor", "dp"),
        P("dp"),
        P("dp"),
        P("dp", None, "tensor"),
        P(("tensor", "dp")),
        P(("tensor", "dp")),
        P("tensor", "dp"),
        P("dp"),
        P("dp"),
        P("dp"),
        P("dp", "tensor"),
        P(("tensor", "dp")),
        P("tensor", "dp"),
        P("dp"),
    )
    body = functools.partial(local, size=mesh.shape["dp"])
    return jax.shard_map(body, mesh=mesh, in_specs=in_specs, out_specs=out_specs, check_vma=False)
```
